32 devices in a mesh: dp: 8 (over z, y), fsdp: 4 (over x, core).
Axes of the slice: x: 2, y: 2, z: 4, core: 2. Of those that a mesh axis runs over, the one named last changes fastest.
Arguments:
- tokens: bfloat16 [131072, 384], P(('dp', 'fsdp')), may hold values from -6 to 6
- centres: float32 [3, 131072], P(None, ('dp', 'fsdp')), may hold values from -1 to 1
- lengths: int32 [512], P(('dp', 'fsdp')), may hold values from 32 to 256, as said below
- cotangent: bfloat16 [131072, 384], P(('dp', 'fsdp')), may hold values from -6 to 6
- smalls: float32 [4736], P(('dp', 'fsdp')), may hold values from -1.5 to 1.5
- master_qkv: float32 [384, 1152], P(('dp', 'fsdp')), may hold values from -0.3125 to 0.3125
- master_out: float32 [384, 384], P(('dp', 'fsdp')), may hold values from -0.875 to 0.875
- master_up: float32 [384, 1536], P(('dp', 'fsdp')), may hold values from -0.3125 to 0.3125
- master_down: float32 [1536, 384], P(('dp', 'fsdp')), may hold values from -0.15625 to 0.15625
- master_pos: float32 [128, 384], P(('dp', 'fsdp')), may hold values from -0.5 to 0.5
- first_qkv: float32 [384, 1152], P(('dp', 'fsdp')), may hold values from -868.8928 to 868.8928
- first_out: float32 [384, 384], P(('dp', 'fsdp')), may hold values from -868.8928 to 868.8928
- first_up: float32 [384, 1536], P(('dp', 'fsdp')), may hold values from -868.8928 to 868.8928
- first_down: float32 [1536, 384], P(('dp', 'fsdp')), may hold values from -868.8928 to 868.8928
- first_pos: float32 [128, 384], P(('dp', 'fsdp')), may hold values from -868.8928 to 868.8928
- second_qkv: float32 [384, 1152], P(('dp', 'fsdp')), may hold values from 20971.52 to 83886.08
- second_out: float32 [384, 384], P(('dp', 'fsdp')), may hold values from 20971.52 to 83886.08
- second_up: float32 [384, 1536], P(('dp', 'fsdp')), may hold values from 20971.52 to 83886.08
- second_down: float32 [1536, 384], P(('dp', 'fsdp')), may hold values from 20971.52 to 83886.08
- second_pos: float32 [128, 384], P(('dp', 'fsdp')), may hold values from 20971.52 to 83886.08
- left_qkv: float32 [384, 384], P(('dp', 'fsdp')), may hold values from -1 to 1, as said below
- left_out: float32 [384, 384], P(('dp', 'fsdp')), may hold values from -1 to 1, as said below
- left_up: float32 [384, 384], P(('dp', 'fsdp')), may hold values from -1 to 1, as said below
- left_down: float32 [1536, 1536], P(('dp', 'fsdp')), may hold values from -1 to 1, as said below
- left_pos: float32 [128, 128], P(('dp', 'fsdp')), may hold values from -1 to 1, as said below
- right_qkv: float32 [1152, 1152], replicated, may hold values from -1 to 1, as said below
- right_out: float32 [384, 384], replicated, may hold values from -1 to 1, as said below
- right_up: float32 [1536, 1536], replicated, may hold values from -1 to 1, as said below
- right_down: float32 [384, 384], replicated, may hold values from -1 to 1, as said below
- right_pos: float32 [384, 384], replicated, may hold values from -1 to 1, as said below
Outputs:
- layer_out: bfloat16 [131072, 384], P(('dp', 'fsdp'))
- grad_tokens: bfloat16 [131072, 384], P(('dp', 'fsdp'))
- grad_smalls: float32 [4736], P(('dp', 'fsdp'))
- grad_qkv: float32 [384, 1152], P(('dp', 'fsdp'))
- grad_out: float32 [384, 384], P(('dp', 'fsdp'))
- grad_up: float32 [384, 1536], P(('dp', 'fsdp'))
- grad_down: float32 [1536, 384], P(('dp', 'fsdp'))
- grad_pos: float32 [128, 384], P(('dp', 'fsdp'))
- first_qkv_next: float32 [384, 1152], P(('dp', 'fsdp'))
- first_out_next: float32 [384, 384], P(('dp', 'fsdp'))
- first_up_next: float32 [384, 1536], P(('dp', 'fsdp'))
- first_down_next: float32 [1536, 384], P(('dp', 'fsdp'))
- first_pos_next: float32 [128, 384], P(('dp', 'fsdp'))
- second_qkv_next: float32 [384, 1152], P(('dp', 'fsdp'))
- second_out_next: float32 [384, 384], P(('dp', 'fsdp'))
- second_up_next: float32 [384, 1536], P(('dp', 'fsdp'))
- second_down_next: float32 [1536, 384], P(('dp', 'fsdp'))
- second_pos_next: float32 [128, 384], P(('dp', 'fsdp'))
- master_qkv_next: float32 [384, 1152], P(('dp', 'fsdp'))
- master_out_next: float32 [384, 384], P(('dp', 'fsdp'))
- master_up_next: float32 [384, 1536], P(('dp', 'fsdp'))
- master_down_next: float32 [1536, 384], P(('dp', 'fsdp'))
- master_pos_next: float32 [128, 384], P(('dp', 'fsdp'))
- weight_qkv_low: bfloat16 [384, 1152], P(('dp', 'fsdp'))
- weight_out_low: bfloat16 [384, 384], P(('dp', 'fsdp'))
- weight_up_low: bfloat16 [384, 1536], P(('dp', 'fsdp'))
- weight_down_low: bfloat16 [1536, 384], P(('dp', 'fsdp'))
- weight_pos_low: bfloat16 [128, 384], P(('dp', 'fsdp'))
The draws below stay inside these ranges and needn't reach their ends.
Inputs may be any that keep to these rules, and one draw needn't show every extreme that they name: `lengths`: on every device one of its 16 clouds has exactly 256 patches. `left_qkv`: an orthogonal matrix. `left_out`: an orthogonal matrix. `left_up`: an orthogonal matrix. `left_down`: an orthogonal matrix. `left_pos`: an orthogonal matrix. `right_qkv`: an orthogonal matrix. `right_out`: an orthogonal matrix. `right_up`: an orthogonal matrix. `right_down`: an orthogonal matrix. `right_pos`: an orthogonal matrix.
All inputs are finite; a program needn't handle non-finite values.
Results may differ from the reference program's by a relative error of at most 0.011.
Values may be sent and summed in bfloat16 or wider, within the bound.
A program may use at most 320 MiB of HBM per device.

```python
import math
import jax
import jax.numpy as jnp
from jax import lax

D = 384
HEADS = 6
HEAD = 64
FF = 1536
PH = 128
LMAX = 256
MIN_LEN = 32
CLOUDS_DEV = 16
CLOUDS = 512
TOKENS = 131072


def orthogonal(key, order):
    keys = jax.random.split(key, 3)
    row_order = jax.random.permutation(keys[0], order).astype(jnp.int32)
    col_order = jax.random.permutation(keys[1], order).astype(jnp.int32)
    row_signs = (2 * jax.random.randint(keys[2], (order,), 0, 2) - 1).astype(jnp.float32)
    phase = (2 * col_order[None, :] + 1) * row_order[:, None] % (4 * order)
    angle = phase.astype(jnp.float32) * (math.pi / (2.0 * order))
    scales = jnp.where(row_order == 0, math.sqrt(1.0 / order), math.sqrt(2.0 / order)).astype(jnp.float32)
    return (row_signs * scales)[:, None] * jnp.cos(angle)


def draw_lengths(key, part):
    key = jax.random.fold_in(key, 101)
    first_key, second_key = jax.random.split(key)
    raw_lengths = jax.random.randint(first_key, (CLOUDS // CLOUDS_DEV, CLOUDS_DEV), MIN_LEN, LMAX + 1)
    chosen = jax.random.randint(second_key, (CLOUDS // CLOUDS_DEV, 1), 0, CLOUDS_DEV)
    filled = jnp.arange(CLOUDS_DEV)[None, :] == chosen
    return jnp.where(filled, LMAX, raw_lengths).reshape(CLOUDS).astype(jnp.int32)


def draw_smalls(key, part):
    key = jax.random.fold_in(key, 102)
    keys = jax.random.split(key, 5)
    gains = jax.random.uniform(keys[0], (2, D), jnp.float32, 0.5, 1.5)
    biases = jax.random.uniform(keys[1], (5, D), jnp.float32, -0.5, 0.5)
    up_bias = jax.random.uniform(keys[2], (FF,), jnp.float32, -0.5, 0.5)
    hidden_bias = jax.random.uniform(keys[3], (PH,), jnp.float32, -0.8, 0.8)
    pos_first = jax.random.uniform(keys[4], (3 * PH,), jnp.float32, -1.5, 1.5)
    return jnp.concatenate([gains[0], biases[0], gains[1], biases[1], biases[2], biases[3], biases[4], up_bias, hidden_bias, pos_first])


def draw_left_qkv(key, part):
    return orthogonal(jax.random.fold_in(key, 201), D)


def draw_left_out(key, part):
    return orthogonal(jax.random.fold_in(key, 202), D)


def draw_left_up(key, part):
    return orthogonal(jax.random.fold_in(key, 203), D)


def draw_left_down(key, part):
    return orthogonal(jax.random.fold_in(key, 204), FF)


def draw_left_pos(key, part):
    return orthogonal(jax.random.fold_in(key, 205), PH)


def draw_right_qkv(key, part):
    return orthogonal(jax.random.fold_in(key, 301), 3 * D)


def draw_right_out(key, part):
    return orthogonal(jax.random.fold_in(key, 302), D)


def draw_right_up(key, part):
    return orthogonal(jax.random.fold_in(key, 303), FF)


def draw_right_down(key, part):
    return orthogonal(jax.random.fold_in(key, 304), D)


def draw_right_pos(key, part):
    return orthogonal(jax.random.fold_in(key, 305), D)


def block_levels(stream_key, shape, cuts, low, top_value):
    level, own = 1.0, jax.random.fold_in(stream_key, 6)
    for axis_at, parts in cuts:
        heights = jnp.exp(jax.random.uniform(jax.random.fold_in(own, axis_at), (parts,), jnp.float32, low / len(cuts), top_value / len(cuts)))
        level = level * jnp.repeat(heights, shape[axis_at] // parts).reshape([-1 if axis == axis_at else 1 for axis in range(len(shape))])
    return level


def scatter_about(key, extent, scale, most, cuts=(), kind=jnp.bfloat16):
    gain = block_levels(key, extent, cuts, -0.22, 0.18) if cuts else 1.0
    entries = jax.random.normal(key, extent, jnp.float32) * scale * gain
    return jnp.minimum(jnp.maximum(entries, -most), most).astype(kind)


def setup_inputs(seed: int = 0) -> dict:
    arg_keys = jax.random.split(jax.random.key(seed), 31)
    tokens = scatter_about(arg_keys[0], (TOKENS, D), 1.0, 6.0, ((0, 32),))
    centres = jnp.clip(jax.random.uniform(arg_keys[1], (3, TOKENS), jnp.float32, -1.0, 1.0) * block_levels(arg_keys[1], (3, TOKENS), ((1, 32),), -0.4, 0.0), -1.0, 1.0)
    lengths = draw_lengths(jax.random.fold_in(arg_keys[30], 71), 0)
    cotangent = scatter_about(arg_keys[3], (TOKENS, D), 1.0, 6.0, ((0, 32),))
    smalls = draw_smalls(jax.random.fold_in(arg_keys[30], 71), 0)
    master_qkv = scatter_about(arg_keys[5], (D, 3 * D), D ** -0.5, 0.3125, ((0, 32),), jnp.float32)
    master_out = scatter_about(arg_keys[6], (D, D), (D // 8) ** -0.5, 0.875, ((0, 32),), jnp.float32)
    master_up = scatter_about(arg_keys[7], (D, FF), D ** -0.5, 0.3125, ((0, 32),), jnp.float32)
    master_down = scatter_about(arg_keys[8], (FF, D), FF ** -0.5, 0.15625, ((0, 32),), jnp.float32)
    master_pos = scatter_about(arg_keys[9], (PH, D), PH ** -0.5, 0.5, ((0, 32),), jnp.float32)
    first_qkv = scatter_about(arg_keys[10], (D, 3 * D), (0.4 * TOKENS ** 0.5), 868.8928, ((0, 32),), jnp.float32)
    first_out = scatter_about(arg_keys[11], (D, D), (0.4 * TOKENS ** 0.5), 868.8928, ((0, 32),), jnp.float32)
    first_up = scatter_about(arg_keys[12], (D, FF), (0.4 * TOKENS ** 0.5), 868.8928, ((0, 32),), jnp.float32)
    first_down = scatter_about(arg_keys[13], (FF, D), (0.4 * TOKENS ** 0.5), 868.8928, ((0, 32),), jnp.float32)
    first_pos = scatter_about(arg_keys[14], (PH, D), (0.4 * TOKENS ** 0.5), 868.8928, ((0, 32),), jnp.float32)
    second_qkv = jnp.clip(jnp.exp(math.log(83886.08) - 1.3862944 * jax.random.uniform(arg_keys[15], (D, 3 * D), jnp.float32) ** block_levels(arg_keys[15], (D, 3 * D), ((0, 32),), -0.2, 0.2)), 20971.52, 83886.08)
    second_out = jnp.clip(jnp.exp(math.log(83886.08) - 1.3862944 * jax.random.uniform(arg_keys[16], (D, D), jnp.float32) ** block_levels(arg_keys[16], (D, D), ((0, 32),), -0.2, 0.2)), 20971.52, 83886.08)
    second_up = jnp.clip(jnp.exp(math.log(83886.08) - 1.3862944 * jax.random.uniform(arg_keys[17], (D, FF), jnp.float32) ** block_levels(arg_keys[17], (D, FF), ((0, 32),), -0.2, 0.2)), 20971.52, 83886.08)
    second_down = jnp.clip(jnp.exp(math.log(83886.08) - 1.3862944 * jax.random.uniform(arg_keys[18], (FF, D), jnp.float32) ** block_levels(arg_keys[18], (FF, D), ((0, 32),), -0.2, 0.2)), 20971.52, 83886.08)
    second_pos = jnp.clip(jnp.exp(math.log(83886.08) - 1.3862944 * jax.random.uniform(arg_keys[19], (PH, D), jnp.float32) ** block_levels(arg_keys[19], (PH, D), ((0, 32),), -0.2, 0.2)), 20971.52, 83886.08)
    left_qkv = draw_left_qkv(jax.random.fold_in(arg_keys[30], 71), 0)
    left_out = draw_left_out(jax.random.fold_in(arg_keys[30], 71), 0)
    left_up = draw_left_up(jax.random.fold_in(arg_keys[30], 71), 0)
    left_down = draw_left_down(jax.random.fold_in(arg_keys[30], 71), 0)
    left_pos = draw_left_pos(jax.random.fold_in(arg_keys[30], 71), 0)
    right_qkv = draw_right_qkv(jax.random.fold_in(arg_keys[30], 71), 0)
    right_out = draw_right_out(jax.random.fold_in(arg_keys[30], 71), 0)
    right_up = draw_right_up(jax.random.fold_in(arg_keys[30], 71), 0)
    right_down = draw_right_down(jax.random.fold_in(arg_keys[30], 71), 0)
    right_pos = draw_right_pos(jax.random.fold_in(arg_keys[30], 71), 0)
    return dict(tokens=tokens, centres=centres, lengths=lengths, cotangent=cotangent, smalls=smalls, master_qkv=master_qkv, master_out=master_out, master_up=master_up, master_down=master_down, master_pos=master_pos, first_qkv=first_qkv, first_out=first_out, first_up=first_up, first_down=first_down, first_pos=first_pos, second_qkv=second_qkv, second_out=second_out, second_up=second_up, second_down=second_down, second_pos=second_pos, left_qkv=left_qkv, left_out=left_out, left_up=left_up, left_down=left_down, left_pos=left_pos, right_qkv=right_qkv, right_out=right_out, right_up=right_up, right_down=right_down, right_pos=right_pos)


HIGHEST = lax.Precision.HIGHEST
EPSILON = 1e-05
ADAM_EPSILON = 1e-08
WEIGHT_DECAY = 0.05
DECAY = 0.5
NEG_FILL = -1e+30

@jax.custom_vjp
def low(v):
    return lax.optimization_barrier(v.astype(jnp.bfloat16)).astype(jnp.float32)

@jax.custom_vjp
def low_back(v):
    return v

def low_keep(v):
    return (low(v), None)

def low_pass(kept, grad):
    return (grad,)

def back_keep(v):
    return (v, None)

def back_low(kept, grad):
    return (low(grad),)
low.defvjp(low_keep, low_pass)
low_back.defvjp(back_keep, back_low)

def hdot(left_side, right_side):
    return jnp.dot(left_side, right_side, precision=HIGHEST)

def layer_norm(inputs, gain_vec, shift_vec):
    centred = inputs - lax.optimization_barrier(jnp.mean(inputs, axis=-1, keepdims=True))
    spread = lax.optimization_barrier(jnp.mean(centred * centred, axis=-1, keepdims=True))
    return centred * lax.rsqrt(spread + EPSILON) * gain_vec + shift_vec

def gelu_exact(inputs):
    return jax.nn.gelu(inputs, approximate=False)

def unpack_smalls(flat_params):
    pieces = [flat_params[place * D:(place + 1) * D] for place in range(7)]
    offset = 7 * D
    up_bias = flat_params[offset:offset + FF]
    hidden_bias = flat_params[offset + FF:offset + FF + PH]
    pos_first = flat_params[offset + FF + PH:].reshape(3, PH)
    return pieces + [up_bias, hidden_bias, pos_first]

def forward(params, tok_rows, cen_rows, key_mask):
    w_qkv, w_out, w_up, w_down, w_pos, small_vec = params
    gain_one, shift_one, gain_two, shift_two, attn_bias, down_bias, embed_bias, up_bias, hidden_bias, pos_first = unpack_smalls(small_vec)
    clouds = key_mask.shape[0]
    row_count = tok_rows.shape[0]
    score_scale = HEAD ** (-0.5)
    pos_hidden = hdot(cen_rows, pos_first) + hidden_bias
    pos_act = low(gelu_exact(pos_hidden))
    embedded = tok_rows + low_back(hdot(pos_act, w_pos)) + embed_bias
    normed_one = low(layer_norm(embedded, gain_one, shift_one))
    qkv = low(low_back(hdot(normed_one, w_qkv))).reshape(clouds, LMAX, 3, HEADS, HEAD)
    queries = qkv[:, :, 0]
    key_heads = qkv[:, :, 1]
    value_heads = qkv[:, :, 2]
    scores = low_back(jnp.einsum('cqhd,ckhd->chqk', queries, key_heads, precision=HIGHEST) * score_scale)
    scores = jnp.where(key_mask[:, None, None, :], scores, NEG_FILL)
    row_top = lax.optimization_barrier(jnp.max(scores, axis=-1, keepdims=True))
    exponent = jnp.exp(scores - row_top)
    softmax_probs = exponent / lax.optimization_barrier(jnp.sum(exponent, axis=-1, keepdims=True))
    probs_low = low(softmax_probs)
    attended = jnp.einsum('chqk,ckhd->cqhd', probs_low, value_heads, precision=HIGHEST).reshape(row_count, D)
    attended = low(low_back(attended))
    branch_in = embedded + low_back(hdot(attended, w_out)) + attn_bias
    normed_two = low(layer_norm(branch_in, gain_two, shift_two))
    hidden = low_back(hdot(normed_two, w_up) + up_bias)
    activation = low(gelu_exact(hidden))
    return branch_in + low_back(hdot(activation, w_down)) + down_bias

def add_pair(first_term, second_term):
    return first_term + second_term

def reference(tokens, centres, lengths, cotangent, smalls, master_qkv, master_out, master_up, master_down, master_pos, first_qkv, first_out, first_up, first_down, first_pos, second_qkv, second_out, second_up, second_down, second_pos, left_qkv, left_out, left_up, left_down, left_pos, right_qkv, right_out, right_up, right_down, right_pos):
    masters = (master_qkv, master_out, master_up, master_down, master_pos)
    firsts = (first_qkv, first_out, first_up, first_down, first_pos)
    seconds = (second_qkv, second_out, second_up, second_down, second_pos)
    left_bases = (left_qkv, left_out, left_up, left_down, left_pos)
    right_bases = (right_qkv, right_out, right_up, right_down, right_pos)
    group = min(CLOUDS, max(1, 4096 // LMAX))
    blocks = CLOUDS // group
    row_count = group * LMAX
    lowered = tuple((low(weight) for weight in masters)) + (low(smalls),)
    tok_blocks = tokens.astype(jnp.float32).reshape(blocks, row_count, D)
    cen_blocks = jnp.transpose(centres).reshape(blocks, row_count, 3)
    len_blocks = lengths.reshape(blocks, group)
    cot_blocks = cotangent.astype(jnp.float32).reshape(blocks, row_count, D)
    positions = jnp.arange(LMAX, dtype=jnp.int32)

    def one_block(carry, inputs):
        tok_rows, cen_rows, len_rows, cot_rows = inputs
        key_mask = positions[None, :] < len_rows[:, None]
        live_rows = key_mask.reshape(row_count).astype(jnp.float32)

        def run_layer(params, tok_in):
            return forward(params, tok_in, cen_rows, key_mask)
        output, pull = jax.vjp(run_layer, lowered, tok_rows)
        param_grads, tok_grad = pull(cot_rows * live_rows[:, None])
        carry = jax.tree.map(add_pair, carry, param_grads)
        return (carry, (output, tok_grad))
    start_carry = tuple((jnp.zeros_like(weight) for weight in lowered))
    grads, stacked = lax.scan(one_block, start_carry, (tok_blocks, cen_blocks, len_blocks, cot_blocks))
    layer_out = stacked[0].reshape(TOKENS, D).astype(jnp.bfloat16)
    grad_tokens = stacked[1].reshape(TOKENS, D).astype(jnp.bfloat16)
    firsts_next = []
    seconds_next = []
    masters_next = []
    lows_next = []
    for place in range(5):
        rotated = hdot(hdot(jnp.transpose(left_bases[place]), grads[place]), right_bases[place])
        first_next = DECAY * firsts[place] + (1.0 - DECAY) * rotated
        second_next = DECAY * seconds[place] + (1.0 - DECAY) * rotated * rotated
        direction = first_next / (jnp.sqrt(second_next) + ADAM_EPSILON)
        update = hdot(hdot(left_bases[place], direction), jnp.transpose(right_bases[place]))
        rate = left_bases[place].shape[0] ** (-0.5)
        master_next = masters[place] * (1.0 - rate * WEIGHT_DECAY) - rate * update
        firsts_next.append(first_next)
        seconds_next.append(second_next)
        masters_next.append(master_next)
        lows_next.append(master_next.astype(jnp.bfloat16))
    return (layer_out, grad_tokens, grads[5], grads[0], grads[1], grads[2], grads[3], grads[4], firsts_next[0], firsts_next[1], firsts_next[2], firsts_next[3], firsts_next[4], seconds_next[0], seconds_next[1], seconds_next[2], seconds_next[3], seconds_next[4], masters_next[0], masters_next[1], masters_next[2], masters_next[3], masters_next[4], lows_next[0], lows_next[1], lows_next[2], lows_next[3], lows_next[4])
```

```python
import functools
import jax
import jax.numpy as jnp
from jax import lax
from jax.experimental import pallas as pl
from jax.experimental.pallas import tpu as pltpu
from jax.sharding import PartitionSpec as P

D = 384
HEADS = 6
HEAD = 64
FF = 1536
PH = 128
LMAX = 256
LANES = 128
EPSILON = 1e-05
NEG_FILL = -1e30
HIGHEST = lax.Precision.HIGHEST
BF = jnp.bfloat16
F32 = jnp.float32

QKV_AT, UP_AT, OUT_AT, DOWN_AT, POS_AT, BLOCKS = 0, 9, 21, 24, 36, 37
FLAT_ROWS = 14336
SMALL_ROWS = 37


def nn(a, b):
    return jnp.dot(a, b, preferred_element_type=F32)


def nt(a, b):
    return lax.dot_general(a, b, (((1,), (1,)), ((), ())), preferred_element_type=F32)


def tn(a, b):
    return lax.dot_general(a, b, (((0,), (0,)), ((), ())), preferred_element_type=F32)


INV_SQRT2 = 0.7071067811865476
INV_SQRT_2PI = 0.3989422804014327


def gelu_pair(x):
    cdf = 0.5 * (1.0 + lax.erf(x * INV_SQRT2))
    pdf = jnp.exp(-0.5 * x * x) * INV_SQRT_2PI
    return x * cdf, cdf + x * pdf


def norm_parts(x):
    mean = jnp.mean(x, axis=-1, keepdims=True)
    centred = x - mean
    spread = jnp.mean(centred * centred, axis=-1, keepdims=True)
    inv = lax.rsqrt(spread + EPSILON)
    return centred * inv, inv


def col8(x):
    rows, cols = x.shape
    return jnp.sum(x.reshape(rows // 8, 8, cols), axis=0)


def layer_kernel(
    len_ref,
    tok_ref,
    cen_ref,
    cot_ref,
    small_ref,
    wqkv_ref,
    wout_ref,
    wup_ref,
    wdown_ref,
    wpos_ref,
    out_ref,
    gtok_ref,
    grad_ref,
    sgrad_ref,
    sacc,
    posh_s,
    emb_s,
    xh1_s,
    n1_s,
    qkv_s,
    p_s,
    att_s,
    bin_s,
    n2g_s,
    ff_s,
    qg_s,
    *,
    fc,
):
    step = pl.program_id(0)
    last = pl.num_programs(0) - 1

    @pl.when(step == 0)
    def _():
        grad_ref[...] = jnp.zeros_like(grad_ref)
        sacc[...] = jnp.zeros_like(sacc)

    length = len_ref[step]

    def vec(at, blocks):
        return jnp.concatenate([small_ref[at + i : at + i + 1, :] for i in range(blocks)], axis=1)

    def add_small(at, value):
        cols = value.shape[1]
        sacc[:, at * LANES : at * LANES + cols] += value

    def add_grad(block, value):
        for i in range(value.shape[1] // LANES):
            rows = slice((block + i) * D, (block + i + 1) * D)
            grad_ref[rows, :] += value[:, i * LANES : (i + 1) * LANES]

    gain_one, shift_one, gain_two, shift_two, attn_bias, down_bias, embed_bias = (
        vec(3 * i, 3) for i in range(7)
    )
    hidden_bias = small_ref[33:34, :]
    pos_first = small_ref[34:37, :]
    cen = cen_ref[...]

    pos_hidden = (
        lax.dot_general(
            cen, pos_first, (((0,), (0,)), ((), ())), precision=HIGHEST, preferred_element_type=F32
        )
        + hidden_bias
    )
    pos_act, pos_slope = gelu_pair(pos_hidden)
    pos_low = pos_act.astype(BF)
    posh_s[...] = pos_slope
    embedded = tok_ref[...].astype(F32) + nn(pos_low, wpos_ref[...]) + embed_bias
    emb_s[...] = embedded
    xhat_one, inv_one = norm_parts(embedded)
    xh1_s[...] = xhat_one
    n1 = (xhat_one * gain_one + shift_one).astype(BF)
    n1_s[...] = n1
    qkv_s[...] = nn(n1, wqkv_ref[...]).astype(BF)

    key_live = lax.broadcasted_iota(jnp.int32, (LMAX, LMAX), 0) < length
    lane = lax.broadcasted_iota(jnp.int32, (1, LANES), 1)
    halves = [(lane < HEAD).astype(F32).astype(BF), (lane >= HEAD).astype(F32).astype(BF)]
    scale = HEAD ** (-0.5)
    scaled = [(h.astype(F32) * scale).astype(BF) for h in halves]

    for pair in range(HEADS // 2):
        cols = slice(pair * LANES, (pair + 1) * LANES)
        q = qkv_s[:, cols]
        k = qkv_s[:, D + pair * LANES : D + (pair + 1) * LANES]
        v = qkv_s[:, 2 * D + pair * LANES : 2 * D + (pair + 1) * LANES]
        v_t = v.T
        for h in range(2):
            s = nt(k, q * scaled[h])
            s = jnp.where(key_live, s, NEG_FILL)
            top = jnp.max(s, axis=0, keepdims=True)
            e = jnp.exp(s - top)
            total = jnp.sum(e, axis=0, keepdims=True)
            p = (e * (1.0 / total)).astype(BF)
            p_s[2 * pair + h] = p
            o_t = nn(v_t[h * HEAD : (h + 1) * HEAD, :], p)
            att_s[pair * LANES + h * HEAD : pair * LANES + (h + 1) * HEAD, :] = o_t.astype(BF)

    branch_in = emb_s[...] + tn(att_s[...], wout_ref[...]) + attn_bias
    bin_s[...] = branch_in
    xhat_two, inv_two = norm_parts(branch_in)
    n2 = (xhat_two * gain_two + shift_two).astype(BF)
    n2_t = n2.T
    row_live = lax.broadcasted_iota(jnp.int32, (LMAX, D), 0) < length
    gy = jnp.where(row_live, cot_ref[...].astype(F32), 0.0)
    gy_low = gy.astype(BF)
    gy_t = gy_low.T
    add_small(15, col8(gy))

    for c in range(FF // fc):
        cols = slice(c * fc, (c + 1) * fc)
        up_bias = vec(21 + c * (fc // LANES), fc // LANES)
        hidden = nn(n2, wup_ref[:, cols]) + up_bias
        act, slope = gelu_pair(hidden)
        act_low = act.astype(BF)
        part = nn(act_low, wdown_ref[cols, :])
        act_grad = nt(gy_low, wdown_ref[cols, :])
        hg = (act_grad * slope).astype(BF)
        add_small(21 + c * (fc // LANES), col8(hg.astype(F32)))
        back = nt(hg, wup_ref[:, cols])
        if c == 0:
            ff_s[...] = part
            n2g_s[...] = back
        else:
            ff_s[...] += part
            n2g_s[...] += back
        add_grad(UP_AT + c * (fc // LANES), nn(n2_t, hg))
        add_grad(DOWN_AT + c * (fc // LANES), nn(gy_t, act_low))

    out_ref[...] = (bin_s[...] + ff_s[...] + down_bias).astype(BF)

    n2g = n2g_s[...]
    add_small(6, col8(n2g * xhat_two))
    add_small(9, col8(n2g))
    u = n2g * gain_two
    bg = gy + inv_two * (
        u
        - jnp.mean(u, axis=-1, keepdims=True)
        - xhat_two * jnp.mean(u * xhat_two, axis=-1, keepdims=True)
    )
    bin_s[...] = bg
    add_small(12, col8(bg))
    bg_low = bg.astype(BF)
    add_grad(OUT_AT, nn(att_s[...], bg_low))
    ag = nt(bg_low, wout_ref[...]).astype(BF)

    for pair in range(HEADS // 2):
        cols = slice(pair * LANES, (pair + 1) * LANES)
        q = qkv_s[:, cols]
        k = qkv_s[:, D + pair * LANES : D + (pair + 1) * LANES]
        v = qkv_s[:, 2 * D + pair * LANES : 2 * D + (pair + 1) * LANES]
        k_t = k.T
        ago = ag[:, cols]
        dq_t = []
        dk = None
        dv = None
        for h in range(2):
            p_low = p_s[2 * pair + h]
            p = p_low.astype(F32)
            ago_h = ago * halves[h]
            dp = nt(v, ago_h)
            rd = jnp.sum(p * dp, axis=0, keepdims=True)
            ds = (p * (dp - rd)).astype(BF)
            dv_h = nn(p_low, ago_h)
            dk_h = nn(ds, q * scaled[h])
            dv = dv_h if dv is None else dv + dv_h
            dk = dk_h if dk is None else dk + dk_h
            dq_t.append((nn(k_t[h * HEAD : (h + 1) * HEAD, :], ds) * scale).astype(BF))
        qg_s[:, cols] = jnp.concatenate(dq_t, axis=0).T
        qg_s[:, D + pair * LANES : D + (pair + 1) * LANES] = dk.astype(BF)
        qg_s[:, 2 * D + pair * LANES : 2 * D + (pair + 1) * LANES] = dv.astype(BF)

    qg = qg_s[...]
    add_grad(QKV_AT, nn(n1_s[...].T, qg))
    n1g = nt(qg, wqkv_ref[...])
    xhat = xh1_s[...]
    add_small(0, col8(n1g * xhat))
    add_small(3, col8(n1g))
    u = n1g * gain_one
    eg = bin_s[...] + inv_one * (
        u
        - jnp.mean(u, axis=-1, keepdims=True)
        - xhat * jnp.mean(u * xhat, axis=-1, keepdims=True)
    )
    add_small(18, col8(eg))
    eg_low = eg.astype(BF)
    gtok_ref[...] = eg_low
    add_grad(POS_AT, tn(eg_low, pos_low))
    phg = nt(eg_low, wpos_ref[...]) * posh_s[...]
    add_small(33, col8(phg))
    pf_grad = jnp.dot(cen, phg, precision=HIGHEST, preferred_element_type=F32)
    for i in range(3):
        sacc[0:1, (34 + i) * LANES : (35 + i) * LANES] += pf_grad[i : i + 1, :]

    @pl.when(step == last)
    def _():
        for i in range(SMALL_ROWS):
            sgrad_ref[i : i + 1, :] = jnp.sum(
                sacc[:, i * LANES : (i + 1) * LANES], axis=0, keepdims=True
            )


def layer_pass(tokens, centres, lengths, cotangent, small_rows, wqkv, wout, wup, wdown, wpos, fc=512):
    clouds = lengths.shape[0]
    rows = clouds * LMAX
    whole = lambda shape: pl.BlockSpec(shape, lambda i, *_: (0, 0), pipeline_mode=pl.Buffered(1))
    tile = lambda: pl.BlockSpec((LMAX, D), lambda i, *_: (i, 0))
    return pl.pallas_call(
        functools.partial(layer_kernel, fc=fc),
        out_shape=(
            jax.ShapeDtypeStruct((rows, D), BF),
            jax.ShapeDtypeStruct((rows, D), BF),
            jax.ShapeDtypeStruct((FLAT_ROWS, LANES), F32),
            jax.ShapeDtypeStruct((SMALL_ROWS, LANES), F32),
        ),
        grid_spec=pltpu.PrefetchScalarGridSpec(
            num_scalar_prefetch=1,
            grid=(clouds,),
            in_specs=[
                tile(),
                pl.BlockSpec((3, LMAX), lambda i, *_: (0, i)),
                tile(),
                whole((SMALL_ROWS, LANES)),
                whole((D, 3 * D)),
                whole((D, D)),
                whole((D, FF)),
                whole((FF, D)),
                whole((PH, D)),
            ],
            out_specs=[
                tile(),
                tile(),
                whole((FLAT_ROWS, LANES)),
                whole((SMALL_ROWS, LANES)),
            ],
            scratch_shapes=[
                pltpu.VMEM((8, SMALL_ROWS * LANES), F32),
                pltpu.VMEM((LMAX, PH), F32),
                pltpu.VMEM((LMAX, D), F32),
                pltpu.VMEM((LMAX, D), F32),
                pltpu.VMEM((LMAX, D), BF),
                pltpu.VMEM((LMAX, 3 * D), BF),
                pltpu.VMEM((HEADS, LMAX, LMAX), BF),
                pltpu.VMEM((D, LMAX), BF),
                pltpu.VMEM((LMAX, D), F32),
                pltpu.VMEM((LMAX, D), F32),
                pltpu.VMEM((LMAX, D), F32),
                pltpu.VMEM((LMAX, 3 * D), BF),
            ],
        ),
        compiler_params=pltpu.CompilerParams(vmem_limit_bytes=60 * 1024 * 1024),
        name="layer",
    )(lengths, tokens, centres, cotangent, small_rows, wqkv, wout, wup, wdown, wpos)


MESH_ID = pl.DeviceIdType.MESH


def mesh_roles(mesh):
    dp, fs = mesh.shape["dp"], mesh.shape["fsdp"]
    if dp >= 32:
        return {
            "z": ("dp", dp // 4 // 2, 4) if dp == 32 else ("dp", 8, dp // 8),
            "y": ("dp", 2, 4),
            "c": ("dp", 1, 2),
            "x": ("fsdp", 1, fs),
        }
    return {
        "z": ("dp", 2, dp // 2),
        "y": ("dp", 1, 2),
        "x": ("fsdp", 2, fs // 2),
        "c": ("fsdp", 1, 2),
    }


def flipped(coord, offset, size):
    if offset == 0:
        return coord
    if size == 2:
        return 1 - coord
    return {1: coord + 1 - 2 * (coord % 2), 2: (coord + 2) % 4, 3: 3 - coord}[offset]


class Grid:
    def __init__(self, roles, sizes):
        self.roles, self.sizes = roles, sizes
        self.index = {axis: lax.axis_index(axis) for axis in sizes}
        self.coord = {
            role: (self.index[axis] // stride) % size
            for role, (axis, stride, size) in roles.items()
        }

    def place(self, **offsets):
        at = dict(self.index)
        for role, offset in offsets.items():
            axis, stride, size = self.roles[role]
            other = flipped(self.coord[role], offset, size)
            at[axis] = at[axis] + (other - self.coord[role]) * stride
        return at

    def slot(self, **offsets):
        at = self.place(**offsets)
        return at["dp"] * self.sizes["fsdp"] + at["fsdp"]

    def size(self, role):
        return self.roles[role][2]

    def offsets(self, role):
        return range(1, self.size(role))


class Wire:
    def __init__(self, grid, send_sems, recv_sems):
        self.grid, self.send_sems, self.recv_sems = grid, send_sems, recv_sems
        self.copies = {}

    def send(self, key, source, target, **offsets):
        number = len(self.copies)
        copy = pltpu.make_async_remote_copy(
            src_ref=source,
            dst_ref=target,
            send_sem=self.send_sems.at[number],
            recv_sem=self.recv_sems.at[number],
            device_id=self.grid.place(**offsets),
            device_id_type=MESH_ID,
        )
        copy.start()
        assert key not in self.copies
        self.copies[key] = copy

    def arrived(self, key):
        self.copies[key].wait_recv()

    def finish(self):
        for copy in self.copies.values():
            copy.wait_send()


def meet(grid):
    barrier = pltpu.get_barrier_semaphore()
    count = 0
    for role in ("z", "y", "x", "c"):
        for offset in grid.offsets(role):
            pl.semaphore_signal(
                barrier,
                inc=1,
                device_id=grid.place(**{role: offset}),
                device_id_type=MESH_ID,
            )
            count += 1
    pl.semaphore_wait(barrier, count)


def gather_copies(roles):
    nz, ny, nx, nc = (roles[role][2] for role in ("z", "y", "x", "c"))
    plane = (ny - 1) + (nx - 1) + 2 * (ny - 1) * (nx - 1)
    core = (nc - 1) * (1 + plane)
    return (nz - 1) + nz * (plane + core)


def gather_all(grid, wire, buf):
    rows = buf.shape[1]
    half = rows // 32 * 16
    parts = {"a": pl.ds(0, half), "b": pl.ds(half, rows - half)}

    def pass_on(key, slot, part, **offsets):
        ref = buf.at[slot] if part is None else buf.at[slot, parts[part]]
        wire.send(("gather",) + key, ref, ref, **offsets)

    zs, ys, xs, cs = ([*grid.offsets(role)] for role in ("z", "y", "x", "c"))

    def to_core(key, slot, part=None):
        for c in cs:
            pass_on(("c", c) + key, slot, part, c=c)

    def have(b):
        slot = grid.slot(z=b)
        for y in ys:
            pass_on(("y", b, y), slot, None, y=y)
        for x in xs:
            pass_on(("x", b, x), slot, None, x=x)
        to_core((b, 0, 0, 0), slot)

    def relay(b):
        for y in ys:
            wire.arrived(("gather", "y", b, y))
            for x in xs:
                pass_on(("a", b, y, x), grid.slot(z=b, y=y), "a", x=x)
            to_core((b, y, 0, 0), grid.slot(z=b, y=y))
        for x in xs:
            wire.arrived(("gather", "x", b, x))
            for y in ys:
                pass_on(("b", b, y, x), grid.slot(z=b, x=x), "b", y=y)
            to_core((b, 0, x, 0), grid.slot(z=b, x=x))

    for z in zs:
        pass_on(("z", z), grid.slot(), None, z=z)
    have(0)
    for b in zs:
        wire.arrived(("gather", "z", b))
        have(b)
        relay(b - 1)
    relay(len(zs))
    for b in [0] + zs:
        for y in ys:
            for x in xs:
                for part in ("a", "b"):
                    wire.arrived(("gather", part, b, y, x))
                    to_core((b, y, x, part), grid.slot(z=b, y=y, x=x), part)
    for key in list(wire.copies):
        if key[:2] == ("gather", "c"):
            wire.arrived(key)


def reduce_copies(roles):
    nz, ny, nx, nc = (roles[role][2] for role in ("z", "y", "x", "c"))
    plane = (ny - 1) + (nx - 1) + 2 * (ny - 1) * (nx - 1)
    return (nc - 1) * nz * ny * nx + nz * plane + (nz - 1)


def small_copies(roles):
    return sum(roles[role][2] - 1 for role in ("z", "y", "x", "c"))


def reduce_scatter(grid, wire, full, small, acc, out_c, in_c, out_p, in_p, out_z, in_z, s_out, s_in, extra):
    rows = full.shape[1]
    half = rows // 32 * 16
    first, second = pl.ds(0, half), pl.ds(half, rows - half)
    zs, ys, xs, cs = ([*grid.offsets(role)] for role in ("z", "y", "x", "c"))
    order = zs + [0]

    small_order = ["c", "y", "x", "z"]
    small_state = {"value": small[...], "stage": 0}

    def small_send():
        stage = small_state["stage"]
        role = small_order[stage]
        s_out[stage] = small_state["value"]
        for offset in grid.offsets(role):
            number = extra[(role, offset)]
            wire.send(("s", role, offset), s_out.at[stage], s_in.at[number], **{role: offset})

    def small_take():
        stage = small_state["stage"]
        role = small_order[stage]
        value = small_state["value"]
        for offset in grid.offsets(role):
            wire.arrived(("s", role, offset))
            value = value + s_in[extra[(role, offset)]]
        small_state["value"] = value
        small_state["stage"] = stage + 1

    small_send()
    for b in order:
        for y in [0] + ys:
            for x in [0] + xs:
                for c in cs:
                    out_c[c - 1, b, y, x] = full[grid.slot(z=b, y=y, x=x, c=c)].astype(BF)
                    wire.send(
                        ("c", c, b, y, x), out_c.at[c - 1, b, y, x], in_c.at[c - 1, b, y, x], c=c
                    )

    def core_sum(b, y, x):
        value = full[grid.slot(z=b, y=y, x=x)]
        for c in cs:
            wire.arrived(("c", c, b, y, x))
            value = value + in_c[c - 1, b, y, x].astype(F32)
        return value

    def diagonal(b):
        for y in ys:
            for x in xs:
                out_p[b, y, x] = core_sum(b, y, x).astype(BF)
                wire.send(("a", b, y, x), out_p.at[b, y, x, first], in_p.at[b, y, x, first], x=x)
                wire.send(("b", b, y, x), out_p.at[b, y, x, second], in_p.at[b, y, x, second], y=y)

    def neighbour(b):
        for y in ys:
            acc[...] = core_sum(b, y, 0)
            for x in xs:
                wire.arrived(("a", b, y, x))
                acc[first, :] += in_p[b, y, x, first].astype(F32)
            out_p[b, y, 0] = acc[...].astype(BF)
            wire.send(("y", b, y), out_p.at[b, y, 0], in_p.at[b, y, 0], y=y)
        for x in xs:
            acc[...] = core_sum(b, 0, x)
            for y in ys:
                wire.arrived(("b", b, y, x))
                acc[second, :] += in_p[b, y, x, second].astype(F32)
            out_p[b, 0, x] = acc[...].astype(BF)
            wire.send(("x", b, x), out_p.at[b, 0, x], in_p.at[b, 0, x], x=x)

    def plane_sum(b):
        value = core_sum(b, 0, 0)
        for y in ys:
            wire.arrived(("y", b, y))
            value = value + in_p[b, y, 0].astype(F32)
        for x in xs:
            wire.arrived(("x", b, x))
            value = value + in_p[b, 0, x].astype(F32)
        return value

    total = None
    for turn in range(len(order) + 2):
        if turn < len(order):
            diagonal(order[turn])
        if 1 <= turn <= len(order):
            neighbour(order[turn - 1])
            if small_state["stage"] < 3:
                small_take()
                small_send()
        if turn >= 2:
            b = order[turn - 2]
            value = plane_sum(b)
            if b:
                out_z[b - 1] = value.astype(BF)
                wire.send(("z", b), out_z.at[b - 1], in_z.at[b - 1], z=b)
            else:
                total = value
    small_take()
    for b in zs:
        wire.arrived(("z", b))
        total = total + in_z[b - 1].astype(F32)
    return total, small_state["value"]


DECAY = 0.5
ADAM_EPSILON = 1e-08
WEIGHT_DECAY = 0.05
VMEM_LIMIT = 60 * 1024 * 1024
NAMES = ("qkv", "out", "up", "down", "pos")
HEIGHT = {"qkv": D, "out": D, "up": D, "down": FF, "pos": PH}
WIDTH = {"qkv": 3 * D, "out": D, "up": FF, "down": D, "pos": D}
SMALLS = SMALL_ROWS * LANES


def pad16(rows):
    return -(-rows // 16) * 16


class Layout:
    def __init__(self, count, smalls):
        self.count = count
        self.rows = {name: HEIGHT[name] // count for name in NAMES}
        self.padded = {name: pad16(self.rows[name]) for name in NAMES}
        self.start = {}
        at = 0
        for name in NAMES:
            self.start[name] = at
            at += self.padded[name] * (WIDTH[name] // LANES)
        self.small_at = at
        self.small_len = SMALLS // count
        if smalls:
            at += 16
        self.total = at

    def span(self, name, block):
        at = self.start[name] + block * self.padded[name]
        return slice(at, at + self.padded[name])

    def spread(self, name):
        rows, padded = self.rows[name], self.padded[name]
        shape = (HEIGHT[name], self.count * padded)
        row = lax.broadcasted_iota(jnp.int32, shape, 0)
        col = lax.broadcasted_iota(jnp.int32, shape, 1)
        own, owner = col % padded, col // padded
        hit = (own < rows) & (owner * rows + own == row)
        return hit.astype(F32).astype(BF)


def pad_rows(value, rows):
    have = value.shape[0]
    if have == rows:
        return value
    return jnp.concatenate([value, jnp.zeros((rows - have, value.shape[1]), value.dtype)], axis=0)


def head_kernel(roles, sizes, lay, *refs):
    masters = dict(zip(NAMES, refs[:5]))
    small_ref = refs[5]
    outs = dict(zip(NAMES, refs[6:11]))
    flat_ref, buf, send_sems, recv_sems = refs[11:]
    grid = Grid(roles, sizes)
    wire = Wire(grid, send_sems, recv_sems)
    own = grid.slot()
    for name in NAMES:
        for block in range(WIDTH[name] // LANES):
            piece = masters[name][:, block * LANES : (block + 1) * LANES]
            buf[own, lay.span(name, block), :] = pad_rows(piece, lay.padded[name]).astype(BF)
    buf[own, lay.small_at : lay.small_at + 16, :] = pad_rows(small_ref[...], 16).astype(BF)
    meet(grid)
    gather_all(grid, wire, buf)
    for name in NAMES:
        spread = None if lay.rows[name] == lay.padded[name] else lay.spread(name)
        for block in range(WIDTH[name] // LANES):
            piece = buf[:, lay.span(name, block), :].reshape(lay.count * lay.padded[name], LANES)
            if spread is not None:
                piece = nn(spread, piece).astype(BF)
            outs[name][:, block * LANES : (block + 1) * LANES] = piece
    lane = lax.broadcasted_iota(jnp.int32, (1, LANES), 1)
    for row in range(SMALL_ROWS):
        line = jnp.zeros((1, LANES), F32)
        at = row * LANES
        while at < (row + 1) * LANES:
            owner, place = at // lay.small_len, at % lay.small_len
            source_row, source_lane = place // LANES, place % LANES
            take = min(
                (row + 1) * LANES - at, lay.small_len - place, LANES - source_lane
            )
            target = at - row * LANES
            piece = buf[owner, lay.small_at : lay.small_at + 16, :].astype(F32)
            piece = piece[source_row : source_row + 1, :]
            shift = (target - source_lane) % LANES
            if shift:
                piece = pltpu.roll(piece, shift, 1)
            line = jnp.where((lane >= target) & (lane < target + take), piece, line)
            at += take
        flat_ref[row : row + 1, :] = line
    wire.finish()


def vmem():
    return pl.BlockSpec(memory_space=pltpu.VMEM)


def gather_weights(roles, sizes, lay, masters, smalls):
    count = gather_copies(roles)
    lines = -(-lay.small_len // LANES)
    padded = jnp.pad(smalls, (0, lines * LANES - lay.small_len)).reshape(lines, LANES)
    return pl.pallas_call(
        functools.partial(head_kernel, roles, sizes, lay),
        out_shape=tuple(jax.ShapeDtypeStruct((HEIGHT[n], WIDTH[n]), BF) for n in NAMES)
        + (jax.ShapeDtypeStruct((SMALL_ROWS, LANES), F32),),
        in_specs=[vmem()] * 6,
        out_specs=tuple([vmem()] * 6),
        scratch_shapes=[
            pltpu.VMEM((lay.count, lay.total, LANES), BF),
            pltpu.SemaphoreType.DMA((count,)),
            pltpu.SemaphoreType.DMA((count,)),
        ],
        compiler_params=pltpu.CompilerParams(
            collective_id=0, has_side_effects=True, vmem_limit_bytes=VMEM_LIMIT
        ),
        name="gather_weights",
    )(*masters, padded)


def reduce_kernel(roles, sizes, extra, full, small, out, small_out, acc, out_c, in_c, out_p, in_p, out_z, in_z, s_out, s_in, send_sems, recv_sems):
    grid = Grid(roles, sizes)
    wire = Wire(grid, send_sems, recv_sems)
    meet(grid)
    total, smalls = reduce_scatter(
        grid, wire, full, small, acc, out_c, in_c, out_p, in_p, out_z, in_z, s_out, s_in, extra
    )
    small_out[...] = smalls
    out[grid.slot()] = total.astype(BF)
    gather_all(grid, wire, out)
    wire.finish()


def reduce_all(roles, sizes, full, small):
    slots, rows, _ = full.shape
    nz, ny, nx, nc = (roles[role][2] for role in ("z", "y", "x", "c"))
    count = reduce_copies(roles) + small_copies(roles) + gather_copies(roles)
    extra = {}
    for role in ("c", "y", "x", "z"):
        for offset in range(1, roles[role][2]):
            extra[(role, offset)] = len(extra)
    return pl.pallas_call(
        functools.partial(reduce_kernel, roles, sizes, extra),
        out_shape=(
            jax.ShapeDtypeStruct((slots, rows, LANES), BF),
            jax.ShapeDtypeStruct((SMALL_ROWS, LANES), F32),
        ),
        in_specs=[vmem()] * 2,
        out_specs=(vmem(), vmem()),
        scratch_shapes=[
            pltpu.VMEM((rows, LANES), F32),
            pltpu.VMEM((nc - 1, nz, ny, nx, rows, LANES), BF),
            pltpu.VMEM((nc - 1, nz, ny, nx, rows, LANES), BF),
            pltpu.VMEM((nz, ny, nx, rows, LANES), BF),
            pltpu.VMEM((nz, ny, nx, rows, LANES), BF),
            pltpu.VMEM((nz - 1, rows, LANES), BF),
            pltpu.VMEM((nz - 1, rows, LANES), BF),
            pltpu.VMEM((4, SMALL_ROWS, LANES), F32),
            pltpu.VMEM((len(extra), SMALL_ROWS, LANES), F32),
            pltpu.SemaphoreType.DMA((count,)),
            pltpu.SemaphoreType.DMA((count,)),
        ],
        compiler_params=pltpu.CompilerParams(
            collective_id=1, has_side_effects=True, vmem_limit_bytes=VMEM_LIMIT
        ),
        name="reduce_all",
    )(full, small)


def split(value):
    high = value.astype(BF)
    return jnp.concatenate([high, (value - high.astype(F32)).astype(BF)], axis=0)


def joined(value):
    half = value.shape[0] // 2
    return value[:half] + value[half:]


def turn_kernel(lay, chunk, index_ref, flat, *refs):
    lefts, rights, firsts, seconds, grads, firsts_next, seconds_next = (
        dict(zip(NAMES, refs[5 * i : 5 * i + 5])) for i in range(7)
    )
    slot = refs[35]
    me = index_ref[0]
    starts = {"qkv": QKV_AT, "up": UP_AT, "out": OUT_AT, "down": DOWN_AT, "pos": POS_AT}
    for name in NAMES:
        height, width = HEIGHT[name], WIDTH[name]
        rows, padded = lay.rows[name], lay.padded[name]
        row = lax.broadcasted_iota(jnp.int32, (padded, height), 0)
        col = lax.broadcasted_iota(jnp.int32, (padded, height), 1)
        pick = ((row < rows) & (col == me * rows + row)).astype(F32).astype(BF)
        left_rows = nt(pick, lefts[name][...]).astype(BF)
        lhs = jnp.concatenate([left_rows, pick], axis=0)
        blocks = []
        if name in ("down", "pos"):
            both = None
            for block in range(height // LANES):
                at = (starts[name] + block) * D
                part = nt(lhs[:, block * LANES : (block + 1) * LANES], flat[at : at + D, :])
                both = part if both is None else both + part
        else:
            for block in range(width // LANES):
                at = (starts[name] + block) * D
                blocks.append(nn(lhs, flat[at : at + D, :]))
            both = jnp.concatenate(blocks, axis=1)
        grads[name][...] = both[padded : padded + rows]
        terms = split(both[:padded])
        for at in range(0, width, chunk):
            cols = slice(at, at + chunk)
            rotated = joined(nn(terms, rights[name][:, cols].astype(BF)))[:rows]
            first = DECAY * firsts[name][:, cols] + (1.0 - DECAY) * rotated
            second = DECAY * seconds[name][:, cols] + (1.0 - DECAY) * rotated * rotated
            firsts_next[name][:, cols] = first
            seconds_next[name][:, cols] = second
            direction = pad_rows(first / (jnp.sqrt(second) + ADAM_EPSILON), padded).astype(BF)
            for i in range(chunk // LANES):
                slot[lay.span(name, at // LANES + i), :] = direction[:, i * LANES : (i + 1) * LANES]


def turn_in(lay, index, flat, lefts, rights, firsts, seconds):
    shapes = [jax.ShapeDtypeStruct((lay.rows[n], WIDTH[n]), F32) for n in NAMES]
    return pl.pallas_call(
        functools.partial(turn_kernel, lay, D),
        out_shape=tuple(shapes * 3) + (jax.ShapeDtypeStruct((lay.total, LANES), BF),),
        in_specs=[pl.BlockSpec(memory_space=pltpu.SMEM)] + [vmem()] * 21,
        out_specs=tuple([vmem()] * 16),
        compiler_params=pltpu.CompilerParams(vmem_limit_bytes=VMEM_LIMIT),
        name="turn_in",
    )(index, flat, *lefts, *rights, *firsts, *seconds)


def steps_kernel(roles, sizes, slot, buf, send_sems, recv_sems):
    grid = Grid(roles, sizes)
    wire = Wire(grid, send_sems, recv_sems)
    buf[grid.slot()] = slot[...]
    meet(grid)
    gather_all(grid, wire, buf)
    wire.finish()


def gather_steps(roles, sizes, lay, slot):
    count = gather_copies(roles)
    return pl.pallas_call(
        functools.partial(steps_kernel, roles, sizes),
        out_shape=jax.ShapeDtypeStruct((lay.count, lay.total, LANES), BF),
        in_specs=[vmem()],
        out_specs=vmem(),
        scratch_shapes=[
            pltpu.SemaphoreType.DMA((count,)),
            pltpu.SemaphoreType.DMA((count,)),
        ],
        compiler_params=pltpu.CompilerParams(
            collective_id=2, has_side_effects=True, vmem_limit_bytes=VMEM_LIMIT
        ),
        name="gather_steps",
    )(slot)


def back_kernel(lay, chunk, steps, *refs):
    lefts, rights, masters, nexts, lows = (
        dict(zip(NAMES, refs[5 * i : 5 * i + 5])) for i in range(5)
    )
    for name in NAMES:
        height, width = HEIGHT[name], WIDTH[name]
        rows, padded = lay.rows[name], lay.padded[name]
        left = split(pad_rows(lefts[name][...], padded))
        if rows != padded:
            left = nn(left, lay.spread(name)).astype(BF)
        parts = []
        for block in range(width // LANES):
            piece = steps[:, lay.span(name, block), :].reshape(lay.count * padded, LANES)
            parts.append(joined(nn(left, piece)))
        partway = split(jnp.concatenate(parts, axis=1))
        rate = height ** (-0.5)
        for at in range(0, width, chunk):
            cols = slice(at, at + chunk)
            update = joined(nt(partway, rights[name][cols, :].astype(BF)))[:rows]
            master = masters[name][:, cols] * (1.0 - rate * WEIGHT_DECAY) - rate * update
            nexts[name][:, cols] = master
            lows[name][:, cols] = master.astype(BF)


def turn_back(lay, steps, lefts, rights, masters):
    shapes = [(lay.rows[n], WIDTH[n]) for n in NAMES]
    return pl.pallas_call(
        functools.partial(back_kernel, lay, D),
        out_shape=tuple(jax.ShapeDtypeStruct(s, F32) for s in shapes)
        + tuple(jax.ShapeDtypeStruct(s, BF) for s in shapes),
        in_specs=[vmem()] * 16,
        out_specs=tuple([vmem()] * 10),
        compiler_params=pltpu.CompilerParams(vmem_limit_bytes=VMEM_LIMIT),
        name="turn_back",
    )(steps, *lefts, *rights, *masters)


AXES = ("dp", "fsdp")


def on_device(roles, sizes, tokens, centres, lengths, cotangent, smalls, *matrices):
    masters, firsts, seconds, lefts, rights = (matrices[5 * i : 5 * i + 5] for i in range(5))
    count = sizes["dp"] * sizes["fsdp"]
    heads = Layout(count, True)
    lay = Layout(count, False)
    *weights, small_rows = gather_weights(roles, sizes, heads, masters, smalls)
    w_qkv, w_out, w_up, w_down, w_pos = weights
    later = lax.optimization_barrier((small_rows,) + tuple(left.astype(BF) for left in lefts))
    small_rows = later[0]
    whole_lefts = [lax.all_gather(left, AXES, axis=0, tiled=True) for left in later[1:]]
    layer_out, grad_tokens, full, small_grads = layer_pass(
        tokens, centres, lengths, cotangent, small_rows, w_qkv, w_out, w_up, w_down, w_pos
    )
    flat, small_total = reduce_all(
        roles, sizes, full.reshape(count, FLAT_ROWS // count, LANES), small_grads
    )
    me = lax.axis_index("dp") * sizes["fsdp"] + lax.axis_index("fsdp")
    grad_smalls = lax.dynamic_slice(
        small_total.reshape(SMALLS), (me * heads.small_len,), (heads.small_len,)
    )
    *turned, slot = turn_in(
        lay,
        me.reshape(1),
        flat.reshape(FLAT_ROWS, LANES),
        whole_lefts,
        rights,
        firsts,
        seconds,
    )
    steps = gather_steps(roles, sizes, lay, slot)
    updated = turn_back(lay, steps, lefts, rights, masters)
    return (layer_out, grad_tokens, grad_smalls, *turned, *updated)


def solution(mesh):
    sizes = {axis: mesh.shape[axis] for axis in AXES}
    rows, flat = P(AXES, None), P(AXES)
    return jax.shard_map(
        functools.partial(on_device, mesh_roles(mesh), sizes),
        mesh=mesh,
        in_specs=(rows, P(None, AXES), flat, rows, flat) + (rows,) * 20 + (P(),) * 5,
        out_specs=(rows, rows, flat) + (rows,) * 25,
        check_vma=False,
    )
```

```python
import functools
import jax
import jax.numpy as jnp
from jax import lax
from jax.experimental import pallas as pl
from jax.experimental.pallas import tpu as pltpu
from jax.sharding import PartitionSpec as P

D = 384
HEADS = 6
HEAD = 64
FF = 1536
PH = 128
LMAX = 256
LANES = 128
EPSILON = 1e-05
NEG_FILL = -1e30
HIGHEST = lax.Precision.HIGHEST
BF = jnp.bfloat16
F32 = jnp.float32

QKV_AT, UP_AT, OUT_AT, DOWN_AT, POS_AT, BLOCKS = 0, 9, 21, 24, 36, 37
FLAT_ROWS = 14336
SMALL_ROWS = 37


def nn(a, b):
    return jnp.dot(a, b, preferred_element_type=F32)


def nt(a, b):
    return lax.dot_general(a, b, (((1,), (1,)), ((), ())), preferred_element_type=F32)


def tn(a, b):
    return lax.dot_general(a, b, (((0,), (0,)), ((), ())), preferred_element_type=F32)


INV_SQRT2 = 0.7071067811865476
INV_SQRT_2PI = 0.3989422804014327


def gelu_pair(x):
    cdf = 0.5 * (1.0 + lax.erf(x * INV_SQRT2))
    pdf = jnp.exp(-0.5 * x * x) * INV_SQRT_2PI
    return x * cdf, cdf + x * pdf


def norm_parts(x):
    mean = jnp.mean(x, axis=-1, keepdims=True)
    centred = x - mean
    spread = jnp.mean(centred * centred, axis=-1, keepdims=True)
    inv = lax.rsqrt(spread + EPSILON)
    return centred * inv, inv


def col8(x):
    rows, cols = x.shape
    return jnp.sum(x.reshape(rows // 8, 8, cols), axis=0)


def layer_kernel(
    len_ref,
    tok_ref,
    cen_ref,
    cot_ref,
    small_ref,
    wqkv_ref,
    wout_ref,
    wup_ref,
    wdown_ref,
    wpos_ref,
    out_ref,
    gtok_ref,
    grad_ref,
    sgrad_ref,
    sacc,
    posh_s,
    emb_s,
    xh1_s,
    n1_s,
    qkv_s,
    p_s,
    att_s,
    bin_s,
    n2g_s,
    ff_s,
    qg_s,
    *,
    fc,
):
    step = pl.program_id(0)
    last = pl.num_programs(0) - 1

    @pl.when(step == 0)
    def _():
        grad_ref[...] = jnp.zeros_like(grad_ref)
        sacc[...] = jnp.zeros_like(sacc)

    length = len_ref[step]

    def vec(at, blocks):
        return jnp.concatenate([small_ref[at + i : at + i + 1, :] for i in range(blocks)], axis=1)

    def add_small(at, value):
        cols = value.shape[1]
        sacc[:, at * LANES : at * LANES + cols] += value

    def add_grad(block, value):
        for i in range(value.shape[1] // LANES):
            rows = slice((block + i) * D, (block + i + 1) * D)
            grad_ref[rows, :] += value[:, i * LANES : (i + 1) * LANES]

    gain_one, shift_one, gain_two, shift_two, attn_bias, down_bias, embed_bias = (
        vec(3 * i, 3) for i in range(7)
    )
    hidden_bias = small_ref[33:34, :]
    pos_first = small_ref[34:37, :]
    cen = cen_ref[...]

    pos_hidden = (
        lax.dot_general(
            cen, pos_first, (((0,), (0,)), ((), ())), precision=HIGHEST, preferred_element_type=F32
        )
        + hidden_bias
    )
    pos_act, pos_slope = gelu_pair(pos_hidden)
    pos_low = pos_act.astype(BF)
    posh_s[...] = pos_slope
    embedded = tok_ref[...].astype(F32) + nn(pos_low, wpos_ref[...]) + embed_bias
    emb_s[...] = embedded
    xhat_one, inv_one = norm_parts(embedded)
    xh1_s[...] = xhat_one
    n1 = (xhat_one * gain_one + shift_one).astype(BF)
    n1_s[...] = n1
    qkv_s[...] = nn(n1, wqkv_ref[...]).astype(BF)

    key_live = lax.broadcasted_iota(jnp.int32, (LMAX, LMAX), 0) < length
    lane = lax.broadcasted_iota(jnp.int32, (1, LANES), 1)
    halves = [(lane < HEAD).astype(F32).astype(BF), (lane >= HEAD).astype(F32).astype(BF)]
    scale = HEAD ** (-0.5)
    scaled = [(h.astype(F32) * scale).astype(BF) for h in halves]

    for pair in range(HEADS // 2):
        cols = slice(pair * LANES, (pair + 1) * LANES)
        q = qkv_s[:, cols]
        k = qkv_s[:, D + pair * LANES : D + (pair + 1) * LANES]
        v = qkv_s[:, 2 * D + pair * LANES : 2 * D + (pair + 1) * LANES]
        v_t = v.T
        for h in range(2):
            s = nt(k, q * scaled[h])
            s = jnp.where(key_live, s, NEG_FILL)
            top = jnp.max(s, axis=0, keepdims=True)
            e = jnp.exp(s - top)
            total = jnp.sum(e, axis=0, keepdims=True)
            p = (e * (1.0 / total)).astype(BF)
            p_s[2 * pair + h] = p
            o_t = nn(v_t[h * HEAD : (h + 1) * HEAD, :], p)
            att_s[pair * LANES + h * HEAD : pair * LANES + (h + 1) * HEAD, :] = o_t.astype(BF)

    branch_in = emb_s[...] + tn(att_s[...], wout_ref[...]) + attn_bias
    bin_s[...] = branch_in
    xhat_two, inv_two = norm_parts(branch_in)
    n2 = (xhat_two * gain_two + shift_two).astype(BF)
    n2_t = n2.T
    row_live = lax.broadcasted_iota(jnp.int32, (LMAX, D), 0) < length
    gy = jnp.where(row_live, cot_ref[...].astype(F32), 0.0)
    gy_low = gy.astype(BF)
    gy_t = gy_low.T
    add_small(15, col8(gy))

    for c in range(FF // fc):
        cols = slice(c * fc, (c + 1) * fc)
        up_bias = vec(21 + c * (fc // LANES), fc // LANES)
        hidden = nn(n2, wup_ref[:, cols]) + up_bias
        act, slope = gelu_pair(hidden)
        act_low = act.astype(BF)
        part = nn(act_low, wdown_ref[cols, :])
        act_grad = nt(gy_low, wdown_ref[cols, :])
        hg = (act_grad * slope).astype(BF)
        add_small(21 + c * (fc // LANES), col8(hg.astype(F32)))
        back = nt(hg, wup_ref[:, cols])
        if c == 0:
            ff_s[...] = part
            n2g_s[...] = back
        else:
            ff_s[...] += part
            n2g_s[...] += back
        add_grad(UP_AT + c * (fc // LANES), nn(n2_t, hg))
        add_grad(DOWN_AT + c * (fc // LANES), nn(gy_t, act_low))

    out_ref[...] = (bin_s[...] + ff_s[...] + down_bias).astype(BF)

    n2g = n2g_s[...]
    add_small(6, col8(n2g * xhat_two))
    add_small(9, col8(n2g))
    u = n2g * gain_two
    bg = gy + inv_two * (
        u
        - jnp.mean(u, axis=-1, keepdims=True)
        - xhat_two * jnp.mean(u * xhat_two, axis=-1, keepdims=True)
    )
    bin_s[...] = bg
    add_small(12, col8(bg))
    bg_low = bg.astype(BF)
    add_grad(OUT_AT, nn(att_s[...], bg_low))
    ag = nt(bg_low, wout_ref[...]).astype(BF)

    for pair in range(HEADS // 2):
        cols = slice(pair * LANES, (pair + 1) * LANES)
        q = qkv_s[:, cols]
        k = qkv_s[:, D + pair * LANES : D + (pair + 1) * LANES]
        v = qkv_s[:, 2 * D + pair * LANES : 2 * D + (pair + 1) * LANES]
        k_t = k.T
        ago = ag[:, cols]
        dq_t = []
        dk = None
        dv = None
        for h in range(2):
            p_low = p_s[2 * pair + h]
            p = p_low.astype(F32)
            ago_h = ago * halves[h]
            dp = nt(v, ago_h)
            rd = jnp.sum(p * dp, axis=0, keepdims=True)
            ds = (p * (dp - rd)).astype(BF)
            dv_h = nn(p_low, ago_h)
            dk_h = nn(ds, q * scaled[h])
            dv = dv_h if dv is None else dv + dv_h
            dk = dk_h if dk is None else dk + dk_h
            dq_t.append((nn(k_t[h * HEAD : (h + 1) * HEAD, :], ds) * scale).astype(BF))
        qg_s[:, cols] = jnp.concatenate(dq_t, axis=0).T
        qg_s[:, D + pair * LANES : D + (pair + 1) * LANES] = dk.astype(BF)
        qg_s[:, 2 * D + pair * LANES : 2 * D + (pair + 1) * LANES] = dv.astype(BF)

    qg = qg_s[...]
    add_grad(QKV_AT, nn(n1_s[...].T, qg))
    n1g = nt(qg, wqkv_ref[...])
    xhat = xh1_s[...]
    add_small(0, col8(n1g * xhat))
    add_small(3, col8(n1g))
    u = n1g * gain_one
    eg = bin_s[...] + inv_one * (
        u
        - jnp.mean(u, axis=-1, keepdims=True)
        - xhat * jnp.mean(u * xhat, axis=-1, keepdims=True)
    )
    add_small(18, col8(eg))
    eg_low = eg.astype(BF)
    gtok_ref[...] = eg_low
    add_grad(POS_AT, tn(eg_low, pos_low))
    phg = nt(eg_low, wpos_ref[...]) * posh_s[...]
    add_small(33, col8(phg))
    pf_grad = jnp.dot(cen, phg, precision=HIGHEST, preferred_element_type=F32)
    for i in range(3):
        sacc[0:1, (34 + i) * LANES : (35 + i) * LANES] += pf_grad[i : i + 1, :]

    @pl.when(step == last)
    def _():
        for i in range(SMALL_ROWS):
            sgrad_ref[i : i + 1, :] = jnp.sum(
                sacc[:, i * LANES : (i + 1) * LANES], axis=0, keepdims=True
            )


def layer_pass(tokens, centres, lengths, cotangent, small_rows, wqkv, wout, wup, wdown, wpos, fc=512):
    clouds = lengths.shape[0]
    rows = clouds * LMAX
    whole = lambda shape: pl.BlockSpec(shape, lambda i, *_: (0, 0), pipeline_mode=pl.Buffered(1))
    tile = lambda: pl.BlockSpec((LMAX, D), lambda i, *_: (i, 0))
    return pl.pallas_call(
        functools.partial(layer_kernel, fc=fc),
        out_shape=(
            jax.ShapeDtypeStruct((rows, D), BF),
            jax.ShapeDtypeStruct((rows, D), BF),
            jax.ShapeDtypeStruct((FLAT_ROWS, LANES), F32),
            jax.ShapeDtypeStruct((SMALL_ROWS, LANES), F32),
        ),
        grid_spec=pltpu.PrefetchScalarGridSpec(
            num_scalar_prefetch=1,
            grid=(clouds,),
            in_specs=[
                tile(),
                pl.BlockSpec((3, LMAX), lambda i, *_: (0, i)),
                tile(),
                whole((SMALL_ROWS, LANES)),
                whole((D, 3 * D)),
                whole((D, D)),
                whole((D, FF)),
                whole((FF, D)),
                whole((PH, D)),
            ],
            out_specs=[
                tile(),
                tile(),
                whole((FLAT_ROWS, LANES)),
                whole((SMALL_ROWS, LANES)),
            ],
            scratch_shapes=[
                pltpu.VMEM((8, SMALL_ROWS * LANES), F32),
                pltpu.VMEM((LMAX, PH), F32),
                pltpu.VMEM((LMAX, D), F32),
                pltpu.VMEM((LMAX, D), F32),
                pltpu.VMEM((LMAX, D), BF),
                pltpu.VMEM((LMAX, 3 * D), BF),
                pltpu.VMEM((HEADS, LMAX, LMAX), BF),
                pltpu.VMEM((D, LMAX), BF),
                pltpu.VMEM((LMAX, D), F32),
                pltpu.VMEM((LMAX, D), F32),
                pltpu.VMEM((LMAX, D), F32),
                pltpu.VMEM((LMAX, 3 * D), BF),
            ],
        ),
        compiler_params=pltpu.CompilerParams(vmem_limit_bytes=60 * 1024 * 1024),
        name="layer",
    )(lengths, tokens, centres, cotangent, small_rows, wqkv, wout, wup, wdown, wpos)


MESH_ID = pl.DeviceIdType.MESH


def mesh_roles(mesh):
    dp, fs = mesh.shape["dp"], mesh.shape["fsdp"]
    if dp >= 32:
        return {
            "z": ("dp", dp // 4 // 2, 4) if dp == 32 else ("dp", 8, dp // 8),
            "y": ("dp", 2, 4),
            "c": ("dp", 1, 2),
            "x": ("fsdp", 1, fs),
        }
    return {
        "z": ("dp", 2, dp // 2),
        "y": ("dp", 1, 2),
        "x": ("fsdp", 2, fs // 2),
        "c": ("fsdp", 1, 2),
    }


def flipped(coord, offset, size):
    if offset == 0:
        return coord
    if size == 2:
        return 1 - coord
    return {1: coord + 1 - 2 * (coord % 2), 2: (coord + 2) % 4, 3: 3 - coord}[offset]


class Grid:
    def __init__(self, roles, sizes):
        self.roles, self.sizes = roles, sizes
        self.index = {axis: lax.axis_index(axis) for axis in sizes}
        self.coord = {
            role: (self.index[axis] // stride) % size
            for role, (axis, stride, size) in roles.items()
        }

    def place(self, **offsets):
        at = dict(self.index)
        for role, offset in offsets.items():
            axis, stride, size = self.roles[role]
            other = flipped(self.coord[role], offset, size)
            at[axis] = at[axis] + (other - self.coord[role]) * stride
        return at

    def slot(self, **offsets):
        at = self.place(**offsets)
        return at["dp"] * self.sizes["fsdp"] + at["fsdp"]

    def size(self, role):
        return self.roles[role][2]

    def offsets(self, role):
        return range(1, self.size(role))


class Wire:
    def __init__(self, grid, send_sems, recv_sems):
        self.grid, self.send_sems, self.recv_sems = grid, send_sems, recv_sems
        self.copies = {}

    def send(self, key, source, target, **offsets):
        number = len(self.copies)
        copy = pltpu.make_async_remote_copy(
            src_ref=source,
            dst_ref=target,
            send_sem=self.send_sems.at[number],
            recv_sem=self.recv_sems.at[number],
            device_id=self.grid.place(**offsets),
            device_id_type=MESH_ID,
        )
        copy.start()
        assert key not in self.copies
        self.copies[key] = copy

    def arrived(self, key):
        self.copies[key].wait_recv()

    def finish(self):
        for copy in self.copies.values():
            copy.wait_send()


def meet(grid):
    barrier = pltpu.get_barrier_semaphore()
    count = 0
    for role in ("z", "y", "x", "c"):
        for offset in grid.offsets(role):
            pl.semaphore_signal(
                barrier,
                inc=1,
                device_id=grid.place(**{role: offset}),
                device_id_type=MESH_ID,
            )
            count += 1
    pl.semaphore_wait(barrier, count)


def gather_copies(roles):
    nz, ny, nx, nc = (roles[role][2] for role in ("z", "y", "x", "c"))
    plane = (ny - 1) + (nx - 1) + 2 * (ny - 1) * (nx - 1)
    core = (nc - 1) * (1 + plane)
    return (nz - 1) + nz * (plane + core)


def gather_all(grid, wire, buf, meanwhile=None):
    rows = buf.shape[1]
    half = rows // 32 * 16
    parts = {"a": pl.ds(0, half), "b": pl.ds(half, rows - half)}

    def pass_on(key, slot, part, **offsets):
        ref = buf.at[slot] if part is None else buf.at[slot, parts[part]]
        wire.send(("gather",) + key, ref, ref, **offsets)

    zs, ys, xs, cs = ([*grid.offsets(role)] for role in ("z", "y", "x", "c"))

    def to_core(key, slot, part=None):
        for c in cs:
            pass_on(("c", c) + key, slot, part, c=c)

    def have(b):
        slot = grid.slot(z=b)
        for y in ys:
            pass_on(("y", b, y), slot, None, y=y)
        for x in xs:
            pass_on(("x", b, x), slot, None, x=x)
        to_core((b, 0, 0, 0), slot)

    def relay(b):
        for y in ys:
            wire.arrived(("gather", "y", b, y))
            for x in xs:
                pass_on(("a", b, y, x), grid.slot(z=b, y=y), "a", x=x)
            to_core((b, y, 0, 0), grid.slot(z=b, y=y))
        for x in xs:
            wire.arrived(("gather", "x", b, x))
            for y in ys:
                pass_on(("b", b, y, x), grid.slot(z=b, x=x), "b", y=y)
            to_core((b, 0, x, 0), grid.slot(z=b, x=x))

    for z in zs:
        pass_on(("z", z), grid.slot(), None, z=z)
    have(0)
    if meanwhile is not None:
        meanwhile()
    for b in zs:
        wire.arrived(("gather", "z", b))
        have(b)
        relay(b - 1)
    relay(len(zs))
    for b in [0] + zs:
        for y in ys:
            for x in xs:
                for part in ("a", "b"):
                    wire.arrived(("gather", part, b, y, x))
                    to_core((b, y, x, part), grid.slot(z=b, y=y, x=x), part)
    for key in list(wire.copies):
        if key[:2] == ("gather", "c"):
            wire.arrived(key)


def reduce_copies(roles):
    nz, ny, nx, nc = (roles[role][2] for role in ("z", "y", "x", "c"))
    plane = (ny - 1) + (nx - 1) + 2 * (ny - 1) * (nx - 1)
    return (nc - 1) * nz * ny * nx + nz * plane + (nz - 1)


def small_copies(roles):
    return sum(roles[role][2] - 1 for role in ("z", "y", "x", "c"))


def reduce_scatter(grid, wire, full, small, acc, out_c, in_c, out_p, in_p, out_z, in_z, s_out, s_in, extra):
    rows = full.shape[1]
    half = rows // 32 * 16
    first, second = pl.ds(0, half), pl.ds(half, rows - half)
    zs, ys, xs, cs = ([*grid.offsets(role)] for role in ("z", "y", "x", "c"))
    order = zs + [0]

    small_order = ["c", "y", "x", "z"]
    small_state = {"value": small[...], "stage": 0}

    def small_send():
        stage = small_state["stage"]
        role = small_order[stage]
        s_out[stage] = small_state["value"]
        for offset in grid.offsets(role):
            number = extra[(role, offset)]
            wire.send(("s", role, offset), s_out.at[stage], s_in.at[number], **{role: offset})

    def small_take():
        stage = small_state["stage"]
        role = small_order[stage]
        value = small_state["value"]
        for offset in grid.offsets(role):
            wire.arrived(("s", role, offset))
            value = value + s_in[extra[(role, offset)]]
        small_state["value"] = value
        small_state["stage"] = stage + 1

    small_send()
    for b in order:
        for y in [0] + ys:
            for x in [0] + xs:
                for c in cs:
                    out_c[c - 1, b, y, x] = full[grid.slot(z=b, y=y, x=x, c=c)].astype(BF)
                    wire.send(
                        ("c", c, b, y, x), out_c.at[c - 1, b, y, x], in_c.at[c - 1, b, y, x], c=c
                    )

    def core_sum(b, y, x):
        value = full[grid.slot(z=b, y=y, x=x)]
        for c in cs:
            wire.arrived(("c", c, b, y, x))
            value = value + in_c[c - 1, b, y, x].astype(F32)
        return value

    def diagonal(b):
        for y in ys:
            for x in xs:
                out_p[b, y, x] = core_sum(b, y, x).astype(BF)
                wire.send(("a", b, y, x), out_p.at[b, y, x, first], in_p.at[b, y, x, first], x=x)
                wire.send(("b", b, y, x), out_p.at[b, y, x, second], in_p.at[b, y, x, second], y=y)

    def neighbour(b):
        for y in ys:
            acc[...] = core_sum(b, y, 0)
            for x in xs:
                wire.arrived(("a", b, y, x))
                acc[first, :] += in_p[b, y, x, first].astype(F32)
            out_p[b, y, 0] = acc[...].astype(BF)
            wire.send(("y", b, y), out_p.at[b, y, 0], in_p.at[b, y, 0], y=y)
        for x in xs:
            acc[...] = core_sum(b, 0, x)
            for y in ys:
                wire.arrived(("b", b, y, x))
                acc[second, :] += in_p[b, y, x, second].astype(F32)
            out_p[b, 0, x] = acc[...].astype(BF)
            wire.send(("x", b, x), out_p.at[b, 0, x], in_p.at[b, 0, x], x=x)

    def plane_sum(b):
        value = core_sum(b, 0, 0)
        for y in ys:
            wire.arrived(("y", b, y))
            value = value + in_p[b, y, 0].astype(F32)
        for x in xs:
            wire.arrived(("x", b, x))
            value = value + in_p[b, 0, x].astype(F32)
        return value

    total = None
    for turn in range(len(order) + 2):
        if turn < len(order):
            diagonal(order[turn])
        if 1 <= turn <= len(order):
            neighbour(order[turn - 1])
            if small_state["stage"] < 3:
                small_take()
                small_send()
        if turn >= 2:
            b = order[turn - 2]
            value = plane_sum(b)
            if b:
                out_z[b - 1] = value.astype(BF)
                wire.send(("z", b), out_z.at[b - 1], in_z.at[b - 1], z=b)
            else:
                total = value
    small_take()
    for b in zs:
        wire.arrived(("z", b))
        total = total + in_z[b - 1].astype(F32)
    return total, small_state["value"]


DECAY = 0.5
ADAM_EPSILON = 1e-08
WEIGHT_DECAY = 0.05
VMEM_LIMIT = 60 * 1024 * 1024
NAMES = ("qkv", "out", "up", "down", "pos")
HEIGHT = {"qkv": D, "out": D, "up": D, "down": FF, "pos": PH}
WIDTH = {"qkv": 3 * D, "out": D, "up": FF, "down": D, "pos": D}
SMALLS = SMALL_ROWS * LANES


def pad16(rows):
    return -(-rows // 16) * 16


class Layout:
    def __init__(self, count, smalls):
        self.count = count
        self.rows = {name: HEIGHT[name] // count for name in NAMES}
        self.padded = {name: pad16(self.rows[name]) for name in NAMES}
        self.start = {}
        at = 0
        for name in NAMES:
            self.start[name] = at
            at += self.padded[name] * (WIDTH[name] // LANES)
        self.small_at = at
        self.small_len = SMALLS // count
        if smalls:
            at += 16
        self.total = at

    @property
    def base_rows(self):
        return self.padded["down"] + 16

    def base_place(self, name):
        if name == "down":
            return slice(0, self.padded["down"]), slice(0, FF)
        at = {"qkv": 0, "out": D, "up": 2 * D, "pos": 3 * D}[name]
        return slice(self.padded["down"], self.base_rows), slice(at, at + HEIGHT[name])

    def span(self, name, block):
        at = self.start[name] + block * self.padded[name]
        return slice(at, at + self.padded[name])

    def spread(self, name):
        rows, padded = self.rows[name], self.padded[name]
        shape = (HEIGHT[name], self.count * padded)
        row = lax.broadcasted_iota(jnp.int32, shape, 0)
        col = lax.broadcasted_iota(jnp.int32, shape, 1)
        own, owner = col % padded, col // padded
        hit = (own < rows) & (owner * rows + own == row)
        return hit.astype(F32).astype(BF)


def pad_rows(value, rows):
    have = value.shape[0]
    if have == rows:
        return value
    return jnp.concatenate([value, jnp.zeros((rows - have, value.shape[1]), value.dtype)], axis=0)


def head_kernel(roles, sizes, lay, *refs):
    masters = dict(zip(NAMES, refs[:5]))
    small_ref = refs[5]
    lefts = dict(zip(NAMES, refs[6:11]))
    outs = dict(zip(NAMES, refs[11:16]))
    flat_ref, bases, buf, send_sems, recv_sems = refs[16:]
    grid = Grid(roles, sizes)
    wire = Wire(grid, send_sems, recv_sems)
    own = grid.slot()
    for name in NAMES:
        for block in range(WIDTH[name] // LANES):
            piece = masters[name][:, block * LANES : (block + 1) * LANES]
            buf[own, lay.span(name, block), :] = pad_rows(piece, lay.padded[name]).astype(BF)
    buf[own, lay.small_at : lay.small_at + 16, :] = pad_rows(small_ref[...], 16).astype(BF)

    def pack_bases():
        bases[lay.padded["down"] :, :] = jnp.zeros((16, FF), BF)
        for name in NAMES:
            rows, cols = lay.base_place(name)
            bases[rows, cols] = pad_rows(lefts[name][...], rows.stop - rows.start).astype(BF)

    meet(grid)
    gather_all(grid, wire, buf, pack_bases)
    for name in NAMES:
        spread = None if lay.rows[name] == lay.padded[name] else lay.spread(name)
        for block in range(WIDTH[name] // LANES):
            piece = buf[:, lay.span(name, block), :].reshape(lay.count * lay.padded[name], LANES)
            if spread is not None:
                piece = nn(spread, piece).astype(BF)
            outs[name][:, block * LANES : (block + 1) * LANES] = piece
    lane = lax.broadcasted_iota(jnp.int32, (1, LANES), 1)
    for row in range(SMALL_ROWS):
        line = jnp.zeros((1, LANES), F32)
        at = row * LANES
        while at < (row + 1) * LANES:
            owner, place = at // lay.small_len, at % lay.small_len
            source_row, source_lane = place // LANES, place % LANES
            take = min(
                (row + 1) * LANES - at, lay.small_len - place, LANES - source_lane
            )
            target = at - row * LANES
            piece = buf[owner, lay.small_at : lay.small_at + 16, :].astype(F32)
            piece = piece[source_row : source_row + 1, :]
            shift = (target - source_lane) % LANES
            if shift:
                piece = pltpu.roll(piece, shift, 1)
            line = jnp.where((lane >= target) & (lane < target + take), piece, line)
            at += take
        flat_ref[row : row + 1, :] = line
    wire.finish()


def vmem():
    return pl.BlockSpec(memory_space=pltpu.VMEM)


def gather_weights(roles, sizes, lay, masters, smalls, lefts):
    count = gather_copies(roles)
    lines = -(-lay.small_len // LANES)
    padded = jnp.pad(smalls, (0, lines * LANES - lay.small_len)).reshape(lines, LANES)
    return pl.pallas_call(
        functools.partial(head_kernel, roles, sizes, lay),
        out_shape=tuple(jax.ShapeDtypeStruct((HEIGHT[n], WIDTH[n]), BF) for n in NAMES)
        + (
            jax.ShapeDtypeStruct((SMALL_ROWS, LANES), F32),
            jax.ShapeDtypeStruct((lay.base_rows, FF), BF),
        ),
        in_specs=[vmem()] * 11,
        out_specs=tuple([vmem()] * 7),
        scratch_shapes=[
            pltpu.VMEM((lay.count, lay.total, LANES), BF),
            pltpu.SemaphoreType.DMA((count,)),
            pltpu.SemaphoreType.DMA((count,)),
        ],
        compiler_params=pltpu.CompilerParams(
            collective_id=0, has_side_effects=True, vmem_limit_bytes=VMEM_LIMIT
        ),
        name="gather_weights",
    )(*masters, padded, *lefts)


def reduce_kernel(roles, sizes, extra, full, small, out, small_out, acc, out_c, in_c, out_p, in_p, out_z, in_z, s_out, s_in, send_sems, recv_sems):
    grid = Grid(roles, sizes)
    wire = Wire(grid, send_sems, recv_sems)
    meet(grid)
    total, smalls = reduce_scatter(
        grid, wire, full, small, acc, out_c, in_c, out_p, in_p, out_z, in_z, s_out, s_in, extra
    )
    small_out[...] = smalls
    out[grid.slot()] = total.astype(BF)
    gather_all(grid, wire, out)
    wire.finish()


def reduce_all(roles, sizes, full, small):
    slots, rows, _ = full.shape
    nz, ny, nx, nc = (roles[role][2] for role in ("z", "y", "x", "c"))
    count = reduce_copies(roles) + small_copies(roles) + gather_copies(roles)
    extra = {}
    for role in ("c", "y", "x", "z"):
        for offset in range(1, roles[role][2]):
            extra[(role, offset)] = len(extra)
    return pl.pallas_call(
        functools.partial(reduce_kernel, roles, sizes, extra),
        out_shape=(
            jax.ShapeDtypeStruct((slots, rows, LANES), BF),
            jax.ShapeDtypeStruct((SMALL_ROWS, LANES), F32),
        ),
        in_specs=[vmem()] * 2,
        out_specs=(vmem(), vmem()),
        scratch_shapes=[
            pltpu.VMEM((rows, LANES), F32),
            pltpu.VMEM((nc - 1, nz, ny, nx, rows, LANES), BF),
            pltpu.VMEM((nc - 1, nz, ny, nx, rows, LANES), BF),
            pltpu.VMEM((nz, ny, nx, rows, LANES), BF),
            pltpu.VMEM((nz, ny, nx, rows, LANES), BF),
            pltpu.VMEM((nz - 1, rows, LANES), BF),
            pltpu.VMEM((nz - 1, rows, LANES), BF),
            pltpu.VMEM((4, SMALL_ROWS, LANES), F32),
            pltpu.VMEM((len(extra), SMALL_ROWS, LANES), F32),
            pltpu.SemaphoreType.DMA((count,)),
            pltpu.SemaphoreType.DMA((count,)),
        ],
        compiler_params=pltpu.CompilerParams(
            collective_id=1, has_side_effects=True, vmem_limit_bytes=VMEM_LIMIT
        ),
        name="reduce_all",
    )(full, small)


def split(value):
    high = value.astype(BF)
    return jnp.concatenate([high, (value - high.astype(F32)).astype(BF)], axis=0)


def joined(value):
    half = value.shape[0] // 2
    return value[:half] + value[half:]


def turn_kernel(lay, chunk, index_ref, flat, bases, *refs):
    rights, firsts, seconds, grads, firsts_next, seconds_next = (
        dict(zip(NAMES, refs[5 * i : 5 * i + 5])) for i in range(6)
    )
    slot = refs[30]
    me = index_ref[0]
    starts = {"qkv": QKV_AT, "up": UP_AT, "out": OUT_AT, "down": DOWN_AT, "pos": POS_AT}
    for name in NAMES:
        height, width = HEIGHT[name], WIDTH[name]
        rows, padded = lay.rows[name], lay.padded[name]
        row = lax.broadcasted_iota(jnp.int32, (padded, height), 0)
        col = lax.broadcasted_iota(jnp.int32, (padded, height), 1)
        pick = ((row < rows) & (col == me * rows + row)).astype(F32).astype(BF)
        base_rows, base_cols = lay.base_place(name)
        base = bases[:, base_rows, base_cols]
        left_rows = nt(pick, base.reshape(base.shape[0] * base.shape[1], height)).astype(BF)
        if rows != padded:
            left_rows = nt(left_rows, lay.spread(name)).astype(BF)
        lhs = jnp.concatenate([left_rows, pick], axis=0)
        blocks = []
        if name in ("down", "pos"):
            both = None
            for block in range(height // LANES):
                at = (starts[name] + block) * D
                part = nt(lhs[:, block * LANES : (block + 1) * LANES], flat[at : at + D, :])
                both = part if both is None else both + part
        else:
            for block in range(width // LANES):
                at = (starts[name] + block) * D
                blocks.append(nn(lhs, flat[at : at + D, :]))
            both = jnp.concatenate(blocks, axis=1)
        grads[name][...] = both[padded : padded + rows]
        terms = split(both[:padded])
        for at in range(0, width, chunk):
            cols = slice(at, at + chunk)
            rotated = joined(nn(terms, rights[name][:, cols].astype(BF)))[:rows]
            first = DECAY * firsts[name][:, cols] + (1.0 - DECAY) * rotated
            second = DECAY * seconds[name][:, cols] + (1.0 - DECAY) * rotated * rotated
            firsts_next[name][:, cols] = first
            seconds_next[name][:, cols] = second
            direction = pad_rows(first / (jnp.sqrt(second) + ADAM_EPSILON), padded).astype(BF)
            for i in range(chunk // LANES):
                slot[lay.span(name, at // LANES + i), :] = direction[:, i * LANES : (i + 1) * LANES]


def turn_in(lay, index, flat, bases, rights, firsts, seconds):
    shapes = [jax.ShapeDtypeStruct((lay.rows[n], WIDTH[n]), F32) for n in NAMES]
    return pl.pallas_call(
        functools.partial(turn_kernel, lay, D),
        out_shape=tuple(shapes * 3) + (jax.ShapeDtypeStruct((lay.total, LANES), BF),),
        in_specs=[pl.BlockSpec(memory_space=pltpu.SMEM)] + [vmem()] * 17,
        out_specs=tuple([vmem()] * 16),
        compiler_params=pltpu.CompilerParams(vmem_limit_bytes=VMEM_LIMIT),
        name="turn_in",
    )(index, flat, bases, *rights, *firsts, *seconds)


def steps_kernel(roles, sizes, slot, buf, send_sems, recv_sems):
    grid = Grid(roles, sizes)
    wire = Wire(grid, send_sems, recv_sems)
    buf[grid.slot()] = slot[...]
    meet(grid)
    gather_all(grid, wire, buf)
    wire.finish()


def gather_steps(roles, sizes, lay, slot):
    count = gather_copies(roles)
    return pl.pallas_call(
        functools.partial(steps_kernel, roles, sizes),
        out_shape=jax.ShapeDtypeStruct((lay.count, lay.total, LANES), BF),
        in_specs=[vmem()],
        out_specs=vmem(),
        scratch_shapes=[
            pltpu.SemaphoreType.DMA((count,)),
            pltpu.SemaphoreType.DMA((count,)),
        ],
        compiler_params=pltpu.CompilerParams(
            collective_id=2, has_side_effects=True, vmem_limit_bytes=VMEM_LIMIT
        ),
        name="gather_steps",
    )(slot)


def back_kernel(lay, chunk, steps, *refs):
    lefts, rights, masters, nexts, lows = (
        dict(zip(NAMES, refs[5 * i : 5 * i + 5])) for i in range(5)
    )
    for name in NAMES:
        height, width = HEIGHT[name], WIDTH[name]
        rows, padded = lay.rows[name], lay.padded[name]
        left = split(pad_rows(lefts[name][...], padded))
        if rows != padded:
            left = nn(left, lay.spread(name)).astype(BF)
        parts = []
        for block in range(width // LANES):
            piece = steps[:, lay.span(name, block), :].reshape(lay.count * padded, LANES)
            parts.append(joined(nn(left, piece)))
        partway = split(jnp.concatenate(parts, axis=1))
        rate = height ** (-0.5)
        for at in range(0, width, chunk):
            cols = slice(at, at + chunk)
            update = joined(nt(partway, rights[name][cols, :].astype(BF)))[:rows]
            master = masters[name][:, cols] * (1.0 - rate * WEIGHT_DECAY) - rate * update
            nexts[name][:, cols] = master
            lows[name][:, cols] = master.astype(BF)


def turn_back(lay, steps, lefts, rights, masters):
    shapes = [(lay.rows[n], WIDTH[n]) for n in NAMES]
    return pl.pallas_call(
        functools.partial(back_kernel, lay, D),
        out_shape=tuple(jax.ShapeDtypeStruct(s, F32) for s in shapes)
        + tuple(jax.ShapeDtypeStruct(s, BF) for s in shapes),
        in_specs=[vmem()] * 16,
        out_specs=tuple([vmem()] * 10),
        compiler_params=pltpu.CompilerParams(vmem_limit_bytes=VMEM_LIMIT),
        name="turn_back",
    )(steps, *lefts, *rights, *masters)


AXES = ("dp", "fsdp")


def on_device(roles, sizes, tokens, centres, lengths, cotangent, smalls, *matrices):
    masters, firsts, seconds, lefts, rights = (matrices[5 * i : 5 * i + 5] for i in range(5))
    count = sizes["dp"] * sizes["fsdp"]
    heads = Layout(count, True)
    lay = Layout(count, False)
    *weights, small_rows, bases = gather_weights(roles, sizes, heads, masters, smalls, lefts)
    w_qkv, w_out, w_up, w_down, w_pos = weights
    whole_bases = lax.all_gather(bases, AXES, axis=0, tiled=True)
    layer_out, grad_tokens, full, small_grads = layer_pass(
        tokens, centres, lengths, cotangent, small_rows, w_qkv, w_out, w_up, w_down, w_pos
    )
    flat, small_total = reduce_all(
        roles, sizes, full.reshape(count, FLAT_ROWS // count, LANES), small_grads
    )
    me = lax.axis_index("dp") * sizes["fsdp"] + lax.axis_index("fsdp")
    grad_smalls = lax.dynamic_slice(
        small_total.reshape(SMALLS), (me * heads.small_len,), (heads.small_len,)
    )
    *turned, slot = turn_in(
        lay,
        me.reshape(1),
        flat.reshape(FLAT_ROWS, LANES),
        whole_bases.reshape(count, heads.base_rows, FF),
        rights,
        firsts,
        seconds,
    )
    steps = gather_steps(roles, sizes, lay, slot)
    updated = turn_back(lay, steps, lefts, rights, masters)
    return (layer_out, grad_tokens, grad_smalls, *turned, *updated)


def solution(mesh):
    sizes = {axis: mesh.shape[axis] for axis in AXES}
    rows, flat = P(AXES, None), P(AXES)
    return jax.shard_map(
        functools.partial(on_device, mesh_roles(mesh), sizes),
        mesh=mesh,
        in_specs=(rows, P(None, AXES), flat, rows, flat) + (rows,) * 20 + (P(),) * 5,
        out_specs=(rows, rows, flat) + (rows,) * 25,
        check_vma=False,
    )
```

```python
import functools
import jax
import jax.numpy as jnp
from jax import lax
from jax.experimental import pallas as pl
from jax.experimental.pallas import tpu as pltpu
from jax.sharding import PartitionSpec as P

D = 384
HEADS = 6
HEAD = 64
FF = 1536
PH = 128
LMAX = 256
LANES = 128
EPSILON = 1e-05
NEG_FILL = -1e30
HIGHEST = lax.Precision.HIGHEST
BF = jnp.bfloat16
F32 = jnp.float32

QKV_AT, UP_AT, OUT_AT, DOWN_AT, POS_AT, BLOCKS = 0, 9, 21, 24, 36, 37
FLAT_ROWS = 14336
SMALL_ROWS = 37


def nn(a, b):
    return jnp.dot(a, b, preferred_element_type=F32)


def nt(a, b):
    return lax.dot_general(a, b, (((1,), (1,)), ((), ())), preferred_element_type=F32)


def tn(a, b):
    return lax.dot_general(a, b, (((0,), (0,)), ((), ())), preferred_element_type=F32)


INV_SQRT2 = 0.7071067811865476
INV_SQRT_2PI = 0.3989422804014327


def gelu_pair(x):
    cdf = 0.5 * (1.0 + lax.erf(x * INV_SQRT2))
    pdf = jnp.exp(-0.5 * x * x) * INV_SQRT_2PI
    return x * cdf, cdf + x * pdf


def norm_parts(x):
    mean = jnp.mean(x, axis=-1, keepdims=True)
    centred = x - mean
    spread = jnp.mean(centred * centred, axis=-1, keepdims=True)
    inv = lax.rsqrt(spread + EPSILON)
    return centred * inv, inv


def col8(x):
    rows, cols = x.shape
    return jnp.sum(x.reshape(rows // 8, 8, cols), axis=0)


def layer_kernel(
    len_ref,
    tok_ref,
    cen_ref,
    cot_ref,
    small_ref,
    wqkv_ref,
    wout_ref,
    wup_ref,
    wdown_ref,
    wpos_ref,
    out_ref,
    gtok_ref,
    grad_ref,
    sgrad_ref,
    sacc,
    posh_s,
    emb_s,
    xh1_s,
    n1_s,
    qkv_s,
    p_s,
    att_s,
    bin_s,
    n2g_s,
    ff_s,
    qg_s,
    wide_s,
    ds_s,
    dq_s,
    ag_s,
    *,
    fc,
    group,
):
    step = pl.program_id(0)
    last = pl.num_programs(0) - 1

    @pl.when(step == 0)
    def _():
        grad_ref[...] = jnp.zeros_like(grad_ref)
        sacc[...] = jnp.zeros_like(sacc)

    rows = group * LMAX
    lengths = [len_ref[step * group + i] for i in range(group)]

    def live(width):
        return jnp.concatenate(
            [lax.broadcasted_iota(jnp.int32, (LMAX, width), 0) < length for length in lengths], axis=0
        )

    def vec(at, blocks):
        return jnp.concatenate([small_ref[at + i : at + i + 1, :] for i in range(blocks)], axis=1)

    def add_small(at, value):
        cols = value.shape[1]
        sacc[:, at * LANES : at * LANES + cols] += value

    def add_grad(block, value):
        for i in range(value.shape[1] // LANES):
            rows = slice((block + i) * D, (block + i + 1) * D)
            grad_ref[rows, :] += value[:, i * LANES : (i + 1) * LANES]

    gain_one, shift_one, gain_two, shift_two, attn_bias, down_bias, embed_bias = (
        vec(3 * i, 3) for i in range(7)
    )
    hidden_bias = small_ref[33:34, :]
    pos_first = small_ref[34:37, :]
    cen = cen_ref[...]

    pos_hidden = (
        lax.dot_general(
            cen, pos_first, (((0,), (0,)), ((), ())), precision=HIGHEST, preferred_element_type=F32
        )
        + hidden_bias
    )
    pos_act, pos_slope = gelu_pair(pos_hidden)
    pos_low = pos_act.astype(BF)
    posh_s[...] = pos_slope
    embedded = tok_ref[...].astype(F32) + nn(pos_low, wpos_ref[...]) + embed_bias
    emb_s[...] = embedded
    xhat_one, inv_one = norm_parts(embedded)
    xh1_s[...] = xhat_one
    n1 = (xhat_one * gain_one + shift_one).astype(BF)
    n1_s[...] = n1
    qkv_s[...] = nn(n1, wqkv_ref[...]).astype(BF)

    lane = lax.broadcasted_iota(jnp.int32, (1, LANES), 1)
    halves = [(lane < HEAD).astype(F32).astype(BF), (lane >= HEAD).astype(F32).astype(BF)]
    scale = HEAD ** (-0.5)
    scaled = [(h.astype(F32) * scale).astype(BF) for h in halves]

    key_live = [
        lax.broadcasted_iota(jnp.int32, (LMAX, LMAX), 0) < length for length in lengths
    ]
    spans = [slice(i * LMAX, (i + 1) * LMAX) for i in range(group)]

    heads = [(i, head) for head in range(HEADS) for i in range(group)]

    def lanes_of(which, i, head):
        at = which * D + head // 2 * LANES
        return qkv_s[spans[i], at : at + LANES]

    def staged(*stages):
        for turn in range(len(heads) + len(stages) - 1):
            for lag, stage in enumerate(stages):
                if 0 <= turn - lag < len(heads):
                    stage(turn - lag, *heads[turn - lag])

    def scores(number, i, head):
        wide_s[number % 3] = nt(lanes_of(1, i, head), lanes_of(0, i, head) * scaled[head % 2])

    def soften(number, i, head):
        s = jnp.where(key_live[i], wide_s[number % 3], NEG_FILL)
        e = jnp.exp(s - jnp.max(s, axis=0, keepdims=True))
        p_s[i * HEADS + head] = (e * (1.0 / jnp.sum(e, axis=0, keepdims=True))).astype(BF)

    def attend(number, i, head):
        at = head % 2 * HEAD
        o_t = nn(lanes_of(2, i, head).T[at : at + HEAD, :], p_s[i * HEADS + head])
        att_s[head * HEAD : (head + 1) * HEAD, spans[i]] = o_t.astype(BF)

    staged(scores, soften, attend)

    branch_in = emb_s[...] + tn(att_s[...], wout_ref[...]) + attn_bias
    bin_s[...] = branch_in
    xhat_two, inv_two = norm_parts(branch_in)
    n2 = (xhat_two * gain_two + shift_two).astype(BF)
    n2_t = n2.T
    gy = jnp.where(live(D), cot_ref[...].astype(F32), 0.0)
    gy_low = gy.astype(BF)
    gy_t = gy_low.T
    add_small(15, col8(gy))

    for c in range(FF // fc):
        cols = slice(c * fc, (c + 1) * fc)
        up_bias = vec(21 + c * (fc // LANES), fc // LANES)
        hidden = nn(n2, wup_ref[:, cols]) + up_bias
        act, slope = gelu_pair(hidden)
        act_low = act.astype(BF)
        part = nn(act_low, wdown_ref[cols, :])
        act_grad = nt(gy_low, wdown_ref[cols, :])
        hg = (act_grad * slope).astype(BF)
        add_small(21 + c * (fc // LANES), col8(hg.astype(F32)))
        back = nt(hg, wup_ref[:, cols])
        if c == 0:
            ff_s[...] = part
            n2g_s[...] = back
        else:
            ff_s[...] += part
            n2g_s[...] += back
        add_grad(UP_AT + c * (fc // LANES), nn(n2_t, hg))
        add_grad(DOWN_AT + c * (fc // LANES), nn(gy_t, act_low))

    out_ref[...] = (bin_s[...] + ff_s[...] + down_bias).astype(BF)

    n2g = n2g_s[...]
    add_small(6, col8(n2g * xhat_two))
    add_small(9, col8(n2g))
    u = n2g * gain_two
    bg = gy + inv_two * (
        u
        - jnp.mean(u, axis=-1, keepdims=True)
        - xhat_two * jnp.mean(u * xhat_two, axis=-1, keepdims=True)
    )
    bin_s[...] = bg
    add_small(12, col8(bg))
    bg_low = bg.astype(BF)
    add_grad(OUT_AT, nn(att_s[...], bg_low))
    ag = nt(bg_low, wout_ref[...]).astype(BF)

    ag_s[...] = ag
    dk, dv = {}, {}

    def ago_of(i, head):
        at = head // 2 * LANES
        return ag_s[spans[i], at : at + LANES] * halves[head % 2]

    def probs_back(number, i, head):
        wide_s[number % 3] = nt(lanes_of(2, i, head), ago_of(i, head))

    def scores_back(number, i, head):
        p = p_s[i * HEADS + head].astype(F32)
        dp = wide_s[number % 3]
        rd = jnp.sum(p * dp, axis=0, keepdims=True)
        ds_s[number % 2] = (p * (dp - rd)).astype(BF)

    def heads_back(number, i, head):
        ds = ds_s[number % 2]
        at = head % 2 * HEAD
        dv[i, head] = nn(p_s[i * HEADS + head], ago_of(i, head))
        dk[i, head] = nn(ds, lanes_of(0, i, head) * scaled[head % 2])
        dq_t = nn(lanes_of(1, i, head).T[at : at + HEAD, :], ds) * scale
        dq_s[head * HEAD : (head + 1) * HEAD, spans[i]] = dq_t.astype(BF)
        if head % 2:
            at = head // 2 * LANES
            qg_s[spans[i], at : at + LANES] = dq_s[at : at + LANES, spans[i]].T
            for which, terms in ((1, dk), (2, dv)):
                total = terms.pop((i, head - 1)) + terms.pop((i, head))
                qg_s[spans[i], which * D + at : which * D + at + LANES] = total.astype(BF)

    staged(probs_back, scores_back, heads_back)

    qg = qg_s[...]
    add_grad(QKV_AT, nn(n1_s[...].T, qg))
    n1g = nt(qg, wqkv_ref[...])
    xhat = xh1_s[...]
    add_small(0, col8(n1g * xhat))
    add_small(3, col8(n1g))
    u = n1g * gain_one
    eg = bin_s[...] + inv_one * (
        u
        - jnp.mean(u, axis=-1, keepdims=True)
        - xhat * jnp.mean(u * xhat, axis=-1, keepdims=True)
    )
    add_small(18, col8(eg))
    eg_low = eg.astype(BF)
    gtok_ref[...] = eg_low
    add_grad(POS_AT, tn(eg_low, pos_low))
    phg = nt(eg_low, wpos_ref[...]) * posh_s[...]
    add_small(33, col8(phg))
    pf_grad = jnp.dot(cen, phg, precision=HIGHEST, preferred_element_type=F32)
    for i in range(3):
        sacc[0:1, (34 + i) * LANES : (35 + i) * LANES] += pf_grad[i : i + 1, :]

    @pl.when(step == last)
    def _():
        for i in range(SMALL_ROWS):
            sgrad_ref[i : i + 1, :] = jnp.sum(
                sacc[:, i * LANES : (i + 1) * LANES], axis=0, keepdims=True
            )


def layer_pass(tokens, centres, lengths, cotangent, small_rows, wqkv, wout, wup, wdown, wpos, fc=768, group=2):
    clouds = lengths.shape[0]
    rows = clouds * LMAX
    span = group * LMAX
    whole = lambda shape: pl.BlockSpec(shape, lambda i, *_: (0, 0), pipeline_mode=pl.Buffered(1))
    tile = lambda: pl.BlockSpec((span, D), lambda i, *_: (i, 0))
    return pl.pallas_call(
        functools.partial(layer_kernel, fc=fc, group=group),
        out_shape=(
            jax.ShapeDtypeStruct((rows, D), BF),
            jax.ShapeDtypeStruct((rows, D), BF),
            jax.ShapeDtypeStruct((FLAT_ROWS, LANES), F32),
            jax.ShapeDtypeStruct((SMALL_ROWS, LANES), F32),
        ),
        grid_spec=pltpu.PrefetchScalarGridSpec(
            num_scalar_prefetch=1,
            grid=(clouds // group,),
            in_specs=[
                tile(),
                pl.BlockSpec((3, span), lambda i, *_: (0, i)),
                tile(),
                whole((SMALL_ROWS, LANES)),
                whole((D, 3 * D)),
                whole((D, D)),
                whole((D, FF)),
                whole((FF, D)),
                whole((PH, D)),
            ],
            out_specs=[
                tile(),
                tile(),
                whole((FLAT_ROWS, LANES)),
                whole((SMALL_ROWS, LANES)),
            ],
            scratch_shapes=[
                pltpu.VMEM((8, SMALL_ROWS * LANES), F32),
                pltpu.VMEM((span, PH), F32),
                pltpu.VMEM((span, D), F32),
                pltpu.VMEM((span, D), F32),
                pltpu.VMEM((span, D), BF),
                pltpu.VMEM((span, 3 * D), BF),
                pltpu.VMEM((group * HEADS, LMAX, LMAX), BF),
                pltpu.VMEM((D, span), BF),
                pltpu.VMEM((span, D), F32),
                pltpu.VMEM((span, D), F32),
                pltpu.VMEM((span, D), F32),
                pltpu.VMEM((span, 3 * D), BF),
                pltpu.VMEM((3, LMAX, LMAX), F32),
                pltpu.VMEM((2, LMAX, LMAX), BF),
                pltpu.VMEM((D, span), BF),
                pltpu.VMEM((span, D), BF),
            ],
        ),
        compiler_params=pltpu.CompilerParams(vmem_limit_bytes=60 * 1024 * 1024),
        name="layer",
    )(lengths, tokens, centres, cotangent, small_rows, wqkv, wout, wup, wdown, wpos)


MESH_ID = pl.DeviceIdType.MESH


def mesh_roles(mesh):
    dp, fs = mesh.shape["dp"], mesh.shape["fsdp"]
    if dp >= 32:
        return {
            "z": ("dp", dp // 4 // 2, 4) if dp == 32 else ("dp", 8, dp // 8),
            "y": ("dp", 2, 4),
            "c": ("dp", 1, 2),
            "x": ("fsdp", 1, fs),
        }
    return {
        "z": ("dp", 2, dp // 2),
        "y": ("dp", 1, 2),
        "x": ("fsdp", 2, fs // 2),
        "c": ("fsdp", 1, 2),
    }


def flipped(coord, offset, size):
    if offset == 0:
        return coord
    if size == 2:
        return 1 - coord
    return {1: coord + 1 - 2 * (coord % 2), 2: (coord + 2) % 4, 3: 3 - coord}[offset]


class Grid:
    def __init__(self, roles, sizes):
        self.roles, self.sizes = roles, sizes
        self.index = {axis: lax.axis_index(axis) for axis in sizes}
        self.coord = {
            role: (self.index[axis] // stride) % size
            for role, (axis, stride, size) in roles.items()
        }

    def place(self, **offsets):
        at = dict(self.index)
        for role, offset in offsets.items():
            axis, stride, size = self.roles[role]
            other = flipped(self.coord[role], offset, size)
            at[axis] = at[axis] + (other - self.coord[role]) * stride
        return at

    def slot(self, **offsets):
        at = self.place(**offsets)
        return at["dp"] * self.sizes["fsdp"] + at["fsdp"]

    def size(self, role):
        return self.roles[role][2]

    def offsets(self, role):
        return range(1, self.size(role))


class Wire:
    def __init__(self, grid, send_sems, recv_sems):
        self.grid, self.send_sems, self.recv_sems = grid, send_sems, recv_sems
        self.copies = {}

    def send(self, key, source, target, **offsets):
        number = len(self.copies)
        copy = pltpu.make_async_remote_copy(
            src_ref=source,
            dst_ref=target,
            send_sem=self.send_sems.at[number],
            recv_sem=self.recv_sems.at[number],
            device_id=self.grid.place(**offsets),
            device_id_type=MESH_ID,
        )
        copy.start()
        assert key not in self.copies
        self.copies[key] = copy

    def arrived(self, key):
        self.copies[key].wait_recv()

    def finish(self):
        for copy in self.copies.values():
            copy.wait_send()


def meet(grid):
    barrier = pltpu.get_barrier_semaphore()
    count = 0
    for role in ("z", "y", "x", "c"):
        for offset in grid.offsets(role):
            pl.semaphore_signal(
                barrier,
                inc=1,
                device_id=grid.place(**{role: offset}),
                device_id_type=MESH_ID,
            )
            count += 1
    pl.semaphore_wait(barrier, count)


def gather_copies(roles):
    nz, ny, nx, nc = (roles[role][2] for role in ("z", "y", "x", "c"))
    plane = (ny - 1) + (nx - 1) + 2 * (ny - 1) * (nx - 1)
    core = (nc - 1) * (1 + plane)
    return (nz - 1) + nz * (plane + core)


def gather_all(grid, wire, buf, meanwhile=None):
    rows = buf.shape[1]
    half = rows // 32 * 16
    parts = {"a": pl.ds(0, half), "b": pl.ds(half, rows - half)}

    def pass_on(key, slot, part, **offsets):
        ref = buf.at[slot] if part is None else buf.at[slot, parts[part]]
        wire.send(("gather",) + key, ref, ref, **offsets)

    zs, ys, xs, cs = ([*grid.offsets(role)] for role in ("z", "y", "x", "c"))

    def to_core(key, slot, part=None):
        for c in cs:
            pass_on(("c", c) + key, slot, part, c=c)

    def have(b):
        slot = grid.slot(z=b)
        for y in ys:
            pass_on(("y", b, y), slot, None, y=y)
        for x in xs:
            pass_on(("x", b, x), slot, None, x=x)
        to_core((b, 0, 0, 0), slot)

    def relay(b):
        for y in ys:
            wire.arrived(("gather", "y", b, y))
            for x in xs:
                pass_on(("a", b, y, x), grid.slot(z=b, y=y), "a", x=x)
            to_core((b, y, 0, 0), grid.slot(z=b, y=y))
        for x in xs:
            wire.arrived(("gather", "x", b, x))
            for y in ys:
                pass_on(("b", b, y, x), grid.slot(z=b, x=x), "b", y=y)
            to_core((b, 0, x, 0), grid.slot(z=b, x=x))

    for z in zs:
        pass_on(("z", z), grid.slot(), None, z=z)
    have(0)
    if meanwhile is not None:
        meanwhile()
    for b in zs:
        wire.arrived(("gather", "z", b))
        have(b)
        relay(b - 1)
    relay(len(zs))
    for b in [0] + zs:
        for y in ys:
            for x in xs:
                for part in ("a", "b"):
                    wire.arrived(("gather", part, b, y, x))
                    to_core((b, y, x, part), grid.slot(z=b, y=y, x=x), part)
    for key in list(wire.copies):
        if key[:2] == ("gather", "c"):
            wire.arrived(key)


def reduce_copies(roles):
    nz, ny, nx, nc = (roles[role][2] for role in ("z", "y", "x", "c"))
    plane = (ny - 1) + (nx - 1) + 2 * (ny - 1) * (nx - 1)
    return (nc - 1) * nz * ny * nx + nz * plane + (nz - 1)


def small_copies(roles):
    return sum(roles[role][2] - 1 for role in ("z", "y", "x", "c"))


def reduce_scatter(grid, wire, full, small, acc, out_c, in_c, out_p, in_p, out_z, in_z, s_out, s_in, extra):
    rows = full.shape[1]
    half = rows // 32 * 16
    first, second = pl.ds(0, half), pl.ds(half, rows - half)
    zs, ys, xs, cs = ([*grid.offsets(role)] for role in ("z", "y", "x", "c"))
    order = zs + [0]

    small_order = ["c", "y", "x", "z"]
    small_state = {"value": small[...], "stage": 0}

    def small_send():
        stage = small_state["stage"]
        role = small_order[stage]
        s_out[stage] = small_state["value"]
        for offset in grid.offsets(role):
            number = extra[(role, offset)]
            wire.send(("s", role, offset), s_out.at[stage], s_in.at[number], **{role: offset})

    def small_take():
        stage = small_state["stage"]
        role = small_order[stage]
        value = small_state["value"]
        for offset in grid.offsets(role):
            wire.arrived(("s", role, offset))
            value = value + s_in[extra[(role, offset)]]
        small_state["value"] = value
        small_state["stage"] = stage + 1

    small_send()
    for b in order:
        for y in [0] + ys:
            for x in [0] + xs:
                for c in cs:
                    out_c[c - 1, b, y, x] = full[grid.slot(z=b, y=y, x=x, c=c)].astype(BF)
                    wire.send(
                        ("c", c, b, y, x), out_c.at[c - 1, b, y, x], in_c.at[c - 1, b, y, x], c=c
                    )

    def core_sum(b, y, x):
        value = full[grid.slot(z=b, y=y, x=x)]
        for c in cs:
            wire.arrived(("c", c, b, y, x))
            value = value + in_c[c - 1, b, y, x].astype(F32)
        return value

    def diagonal(b):
        for y in ys:
            for x in xs:
                out_p[b, y, x] = core_sum(b, y, x).astype(BF)
                wire.send(("a", b, y, x), out_p.at[b, y, x, first], in_p.at[b, y, x, first], x=x)
                wire.send(("b", b, y, x), out_p.at[b, y, x, second], in_p.at[b, y, x, second], y=y)

    def neighbour(b):
        for y in ys:
            acc[...] = core_sum(b, y, 0)
            for x in xs:
                wire.arrived(("a", b, y, x))
                acc[first, :] += in_p[b, y, x, first].astype(F32)
            out_p[b, y, 0] = acc[...].astype(BF)
            wire.send(("y", b, y), out_p.at[b, y, 0], in_p.at[b, y, 0], y=y)
        for x in xs:
            acc[...] = core_sum(b, 0, x)
            for y in ys:
                wire.arrived(("b", b, y, x))
                acc[second, :] += in_p[b, y, x, second].astype(F32)
            out_p[b, 0, x] = acc[...].astype(BF)
            wire.send(("x", b, x), out_p.at[b, 0, x], in_p.at[b, 0, x], x=x)

    def plane_sum(b):
        value = core_sum(b, 0, 0)
        for y in ys:
            wire.arrived(("y", b, y))
            value = value + in_p[b, y, 0].astype(F32)
        for x in xs:
            wire.arrived(("x", b, x))
            value = value + in_p[b, 0, x].astype(F32)
        return value

    total = None
    for turn in range(len(order) + 2):
        if turn < len(order):
            diagonal(order[turn])
        if 1 <= turn <= len(order):
            neighbour(order[turn - 1])
            if small_state["stage"] < 3:
                small_take()
                small_send()
        if turn >= 2:
            b = order[turn - 2]
            value = plane_sum(b)
            if b:
                out_z[b - 1] = value.astype(BF)
                wire.send(("z", b), out_z.at[b - 1], in_z.at[b - 1], z=b)
            else:
                total = value
    small_take()
    for b in zs:
        wire.arrived(("z", b))
        total = total + in_z[b - 1].astype(F32)
    return total, small_state["value"]


DECAY = 0.5
ADAM_EPSILON = 1e-08
WEIGHT_DECAY = 0.05
VMEM_LIMIT = 60 * 1024 * 1024
NAMES = ("qkv", "out", "up", "down", "pos")
HEIGHT = {"qkv": D, "out": D, "up": D, "down": FF, "pos": PH}
WIDTH = {"qkv": 3 * D, "out": D, "up": FF, "down": D, "pos": D}
SMALLS = SMALL_ROWS * LANES


def pad16(rows):
    return -(-rows // 16) * 16


class Layout:
    def __init__(self, count, smalls):
        self.count = count
        self.rows = {name: HEIGHT[name] // count for name in NAMES}
        self.padded = {name: pad16(self.rows[name]) for name in NAMES}
        self.start = {}
        at = 0
        for name in NAMES:
            self.start[name] = at
            at += self.padded[name] * (WIDTH[name] // LANES)
        self.small_at = at
        self.small_len = SMALLS // count
        if smalls:
            at += 16
        self.total = at

    @property
    def base_rows(self):
        return self.padded["down"] + 16

    def base_place(self, name):
        if name == "down":
            return slice(0, self.padded["down"]), slice(0, FF)
        at = {"qkv": 0, "out": D, "up": 2 * D, "pos": 3 * D}[name]
        return slice(self.padded["down"], self.base_rows), slice(at, at + HEIGHT[name])

    def span(self, name, block):
        at = self.start[name] + block * self.padded[name]
        return slice(at, at + self.padded[name])

    def spread(self, name):
        rows, padded = self.rows[name], self.padded[name]
        shape = (HEIGHT[name], self.count * padded)
        row = lax.broadcasted_iota(jnp.int32, shape, 0)
        col = lax.broadcasted_iota(jnp.int32, shape, 1)
        own, owner = col % padded, col // padded
        hit = (own < rows) & (owner * rows + own == row)
        return hit.astype(F32).astype(BF)


def pad_rows(value, rows):
    have = value.shape[0]
    if have == rows:
        return value
    return jnp.concatenate([value, jnp.zeros((rows - have, value.shape[1]), value.dtype)], axis=0)


def head_kernel(roles, sizes, lay, *refs):
    masters = dict(zip(NAMES, refs[:5]))
    small_ref = refs[5]
    lefts = dict(zip(NAMES, refs[6:11]))
    outs = dict(zip(NAMES, refs[11:16]))
    flat_ref, bases, buf, send_sems, recv_sems = refs[16:]
    grid = Grid(roles, sizes)
    wire = Wire(grid, send_sems, recv_sems)
    own = grid.slot()
    for name in NAMES:
        for block in range(WIDTH[name] // LANES):
            piece = masters[name][:, block * LANES : (block + 1) * LANES]
            buf[own, lay.span(name, block), :] = pad_rows(piece, lay.padded[name]).astype(BF)
    buf[own, lay.small_at : lay.small_at + 16, :] = pad_rows(small_ref[...], 16).astype(BF)

    def pack_bases():
        bases[lay.padded["down"] :, :] = jnp.zeros((16, FF), BF)
        for name in NAMES:
            rows, cols = lay.base_place(name)
            bases[rows, cols] = pad_rows(lefts[name][...], rows.stop - rows.start).astype(BF)

    meet(grid)
    gather_all(grid, wire, buf, pack_bases)
    for name in NAMES:
        spread = None if lay.rows[name] == lay.padded[name] else lay.spread(name)
        for block in range(WIDTH[name] // LANES):
            piece = buf[:, lay.span(name, block), :].reshape(lay.count * lay.padded[name], LANES)
            if spread is not None:
                piece = nn(spread, piece).astype(BF)
            outs[name][:, block * LANES : (block + 1) * LANES] = piece
    lane = lax.broadcasted_iota(jnp.int32, (1, LANES), 1)
    for row in range(SMALL_ROWS):
        line = jnp.zeros((1, LANES), F32)
        at = row * LANES
        while at < (row + 1) * LANES:
            owner, place = at // lay.small_len, at % lay.small_len
            source_row, source_lane = place // LANES, place % LANES
            take = min(
                (row + 1) * LANES - at, lay.small_len - place, LANES - source_lane
            )
            target = at - row * LANES
            piece = buf[owner, lay.small_at : lay.small_at + 16, :].astype(F32)
            piece = piece[source_row : source_row + 1, :]
            shift = (target - source_lane) % LANES
            if shift:
                piece = pltpu.roll(piece, shift, 1)
            line = jnp.where((lane >= target) & (lane < target + take), piece, line)
            at += take
        flat_ref[row : row + 1, :] = line
    wire.finish()


def vmem():
    return pl.BlockSpec(memory_space=pltpu.VMEM)


def gather_weights(roles, sizes, lay, masters, smalls, lefts):
    count = gather_copies(roles)
    lines = -(-lay.small_len // LANES)
    padded = jnp.pad(smalls, (0, lines * LANES - lay.small_len)).reshape(lines, LANES)
    return pl.pallas_call(
        functools.partial(head_kernel, roles, sizes, lay),
        out_shape=tuple(jax.ShapeDtypeStruct((HEIGHT[n], WIDTH[n]), BF) for n in NAMES)
        + (
            jax.ShapeDtypeStruct((SMALL_ROWS, LANES), F32),
            jax.ShapeDtypeStruct((lay.base_rows, FF), BF),
        ),
        in_specs=[vmem()] * 11,
        out_specs=tuple([vmem()] * 7),
        scratch_shapes=[
            pltpu.VMEM((lay.count, lay.total, LANES), BF),
            pltpu.SemaphoreType.DMA((count,)),
            pltpu.SemaphoreType.DMA((count,)),
        ],
        compiler_params=pltpu.CompilerParams(
            collective_id=0, has_side_effects=True, vmem_limit_bytes=VMEM_LIMIT
        ),
        name="gather_weights",
    )(*masters, padded, *lefts)


def reduce_kernel(roles, sizes, extra, full, small, out, small_out, acc, out_c, in_c, out_p, in_p, out_z, in_z, s_out, s_in, send_sems, recv_sems):
    grid = Grid(roles, sizes)
    wire = Wire(grid, send_sems, recv_sems)
    meet(grid)
    total, smalls = reduce_scatter(
        grid, wire, full, small, acc, out_c, in_c, out_p, in_p, out_z, in_z, s_out, s_in, extra
    )
    small_out[...] = smalls
    out[grid.slot()] = total.astype(BF)
    gather_all(grid, wire, out)
    wire.finish()


def reduce_all(roles, sizes, full, small):
    slots, rows, _ = full.shape
    nz, ny, nx, nc = (roles[role][2] for role in ("z", "y", "x", "c"))
    count = reduce_copies(roles) + small_copies(roles) + gather_copies(roles)
    extra = {}
    for role in ("c", "y", "x", "z"):
        for offset in range(1, roles[role][2]):
            extra[(role, offset)] = len(extra)
    return pl.pallas_call(
        functools.partial(reduce_kernel, roles, sizes, extra),
        out_shape=(
            jax.ShapeDtypeStruct((slots, rows, LANES), BF),
            jax.ShapeDtypeStruct((SMALL_ROWS, LANES), F32),
        ),
        in_specs=[vmem()] * 2,
        out_specs=(vmem(), vmem()),
        scratch_shapes=[
            pltpu.VMEM((rows, LANES), F32),
            pltpu.VMEM((nc - 1, nz, ny, nx, rows, LANES), BF),
            pltpu.VMEM((nc - 1, nz, ny, nx, rows, LANES), BF),
            pltpu.VMEM((nz, ny, nx, rows, LANES), BF),
            pltpu.VMEM((nz, ny, nx, rows, LANES), BF),
            pltpu.VMEM((nz - 1, rows, LANES), BF),
            pltpu.VMEM((nz - 1, rows, LANES), BF),
            pltpu.VMEM((4, SMALL_ROWS, LANES), F32),
            pltpu.VMEM((len(extra), SMALL_ROWS, LANES), F32),
            pltpu.SemaphoreType.DMA((count,)),
            pltpu.SemaphoreType.DMA((count,)),
        ],
        compiler_params=pltpu.CompilerParams(
            collective_id=1, has_side_effects=True, vmem_limit_bytes=VMEM_LIMIT
        ),
        name="reduce_all",
    )(full, small)


def split(value):
    high = value.astype(BF)
    return jnp.concatenate([high, (value - high.astype(F32)).astype(BF)], axis=0)


def joined(value):
    half = value.shape[0] // 2
    return value[:half] + value[half:]


def turn_kernel(lay, chunk, index_ref, flat, bases, *refs):
    rights, firsts, seconds, grads, firsts_next, seconds_next = (
        dict(zip(NAMES, refs[5 * i : 5 * i + 5])) for i in range(6)
    )
    slot = refs[30]
    me = index_ref[0]
    starts = {"qkv": QKV_AT, "up": UP_AT, "out": OUT_AT, "down": DOWN_AT, "pos": POS_AT}
    for name in NAMES:
        height, width = HEIGHT[name], WIDTH[name]
        rows, padded = lay.rows[name], lay.padded[name]
        row = lax.broadcasted_iota(jnp.int32, (padded, height), 0)
        col = lax.broadcasted_iota(jnp.int32, (padded, height), 1)
        pick = ((row < rows) & (col == me * rows + row)).astype(F32).astype(BF)
        base_rows, base_cols = lay.base_place(name)
        base = bases[:, base_rows, base_cols]
        left_rows = nt(pick, base.reshape(base.shape[0] * base.shape[1], height)).astype(BF)
        if rows != padded:
            left_rows = nt(left_rows, lay.spread(name)).astype(BF)
        lhs = jnp.concatenate([left_rows, pick], axis=0)
        blocks = []
        if name in ("down", "pos"):
            both = None
            for block in range(height // LANES):
                at = (starts[name] + block) * D
                part = nt(lhs[:, block * LANES : (block + 1) * LANES], flat[at : at + D, :])
                both = part if both is None else both + part
        else:
            for block in range(width // LANES):
                at = (starts[name] + block) * D
                blocks.append(nn(lhs, flat[at : at + D, :]))
            both = jnp.concatenate(blocks, axis=1)
        grads[name][...] = both[padded : padded + rows]
        terms = split(both[:padded])
        for at in range(0, width, chunk):
            cols = slice(at, at + chunk)
            rotated = joined(nn(terms, rights[name][:, cols].astype(BF)))[:rows]
            first = DECAY * firsts[name][:, cols] + (1.0 - DECAY) * rotated
            second = DECAY * seconds[name][:, cols] + (1.0 - DECAY) * rotated * rotated
            firsts_next[name][:, cols] = first
            seconds_next[name][:, cols] = second
            direction = pad_rows(first / (jnp.sqrt(second) + ADAM_EPSILON), padded).astype(BF)
            for i in range(chunk // LANES):
                slot[lay.span(name, at // LANES + i), :] = direction[:, i * LANES : (i + 1) * LANES]


def turn_in(lay, index, flat, bases, rights, firsts, seconds):
    shapes = [jax.ShapeDtypeStruct((lay.rows[n], WIDTH[n]), F32) for n in NAMES]
    return pl.pallas_call(
        functools.partial(turn_kernel, lay, D),
        out_shape=tuple(shapes * 3) + (jax.ShapeDtypeStruct((lay.total, LANES), BF),),
        in_specs=[pl.BlockSpec(memory_space=pltpu.SMEM)] + [vmem()] * 17,
        out_specs=tuple([vmem()] * 16),
        compiler_params=pltpu.CompilerParams(vmem_limit_bytes=VMEM_LIMIT),
        name="turn_in",
    )(index, flat, bases, *rights, *firsts, *seconds)


def steps_kernel(roles, sizes, slot, buf, send_sems, recv_sems):
    grid = Grid(roles, sizes)
    wire = Wire(grid, send_sems, recv_sems)
    buf[grid.slot()] = slot[...]
    meet(grid)
    gather_all(grid, wire, buf)
    wire.finish()


def gather_steps(roles, sizes, lay, slot):
    count = gather_copies(roles)
    return pl.pallas_call(
        functools.partial(steps_kernel, roles, sizes),
        out_shape=jax.ShapeDtypeStruct((lay.count, lay.total, LANES), BF),
        in_specs=[vmem()],
        out_specs=vmem(),
        scratch_shapes=[
            pltpu.SemaphoreType.DMA((count,)),
            pltpu.SemaphoreType.DMA((count,)),
        ],
        compiler_params=pltpu.CompilerParams(
            collective_id=2, has_side_effects=True, vmem_limit_bytes=VMEM_LIMIT
        ),
        name="gather_steps",
    )(slot)


def back_kernel(lay, chunk, steps, *refs):
    lefts, rights, masters, nexts, lows = (
        dict(zip(NAMES, refs[5 * i : 5 * i + 5])) for i in range(5)
    )
    for name in NAMES:
        height, width = HEIGHT[name], WIDTH[name]
        rows, padded = lay.rows[name], lay.padded[name]
        left = split(pad_rows(lefts[name][...], padded))
        if rows != padded:
            left = nn(left, lay.spread(name)).astype(BF)
        parts = []
        for block in range(width // LANES):
            piece = steps[:, lay.span(name, block), :].reshape(lay.count * padded, LANES)
            parts.append(joined(nn(left, piece)))
        partway = split(jnp.concatenate(parts, axis=1))
        rate = height ** (-0.5)
        for at in range(0, width, chunk):
            cols = slice(at, at + chunk)
            update = joined(nt(partway, rights[name][cols, :].astype(BF)))[:rows]
            master = masters[name][:, cols] * (1.0 - rate * WEIGHT_DECAY) - rate * update
            nexts[name][:, cols] = master
            lows[name][:, cols] = master.astype(BF)


def turn_back(lay, steps, lefts, rights, masters):
    shapes = [(lay.rows[n], WIDTH[n]) for n in NAMES]
    return pl.pallas_call(
        functools.partial(back_kernel, lay, D),
        out_shape=tuple(jax.ShapeDtypeStruct(s, F32) for s in shapes)
        + tuple(jax.ShapeDtypeStruct(s, BF) for s in shapes),
        in_specs=[vmem()] * 16,
        out_specs=tuple([vmem()] * 10),
        compiler_params=pltpu.CompilerParams(vmem_limit_bytes=VMEM_LIMIT),
        name="turn_back",
    )(steps, *lefts, *rights, *masters)


AXES = ("dp", "fsdp")


def on_device(roles, sizes, tokens, centres, lengths, cotangent, smalls, *matrices):
    masters, firsts, seconds, lefts, rights = (matrices[5 * i : 5 * i + 5] for i in range(5))
    count = sizes["dp"] * sizes["fsdp"]
    heads = Layout(count, True)
    lay = Layout(count, False)
    *weights, small_rows, bases = gather_weights(roles, sizes, heads, masters, smalls, lefts)
    w_qkv, w_out, w_up, w_down, w_pos = weights
    whole_bases = lax.all_gather(bases, AXES, axis=0, tiled=True)
    layer_out, grad_tokens, full, small_grads = layer_pass(
        tokens, centres, lengths, cotangent, small_rows, w_qkv, w_out, w_up, w_down, w_pos
    )
    flat, small_total = reduce_all(
        roles, sizes, full.reshape(count, FLAT_ROWS // count, LANES), small_grads
    )
    me = lax.axis_index("dp") * sizes["fsdp"] + lax.axis_index("fsdp")
    grad_smalls = lax.dynamic_slice(
        small_total.reshape(SMALLS), (me * heads.small_len,), (heads.small_len,)
    )
    *turned, slot = turn_in(
        lay,
        me.reshape(1),
        flat.reshape(FLAT_ROWS, LANES),
        whole_bases.reshape(count, heads.base_rows, FF),
        rights,
        firsts,
        seconds,
    )
    steps = gather_steps(roles, sizes, lay, slot)
    updated = turn_back(lay, steps, lefts, rights, masters)
    return (layer_out, grad_tokens, grad_smalls, *turned, *updated)


def solution(mesh):
    sizes = {axis: mesh.shape[axis] for axis in AXES}
    rows, flat = P(AXES, None), P(AXES)
    return jax.shard_map(
        functools.partial(on_device, mesh_roles(mesh), sizes),
        mesh=mesh,
        in_specs=(rows, P(None, AXES), flat, rows, flat) + (rows,) * 20 + (P(),) * 5,
        out_specs=(rows, rows, flat) + (rows,) * 25,
        check_vma=False,
    )
```

```python
import functools
import jax
import jax.numpy as jnp
from jax import lax
from jax.experimental import pallas as pl
from jax.experimental.pallas import tpu as pltpu
from jax.sharding import PartitionSpec as P

D = 384
HEADS = 6
HEAD = 64
FF = 1536
PH = 128
LMAX = 256
LANES = 128
EPSILON = 1e-05
NEG_FILL = -1e30
HIGHEST = lax.Precision.HIGHEST
BF = jnp.bfloat16
F32 = jnp.float32

QKV_AT, UP_AT, OUT_AT, DOWN_AT, POS_AT, BLOCKS = 0, 9, 21, 24, 36, 37
FLAT_ROWS = 14336
SMALL_ROWS = 37


def nn(a, b):
    return jnp.dot(a, b, preferred_element_type=F32)


def nt(a, b):
    return lax.dot_general(a, b, (((1,), (1,)), ((), ())), preferred_element_type=F32)


def tn(a, b):
    return lax.dot_general(a, b, (((0,), (0,)), ((), ())), preferred_element_type=F32)


INV_SQRT2 = 0.7071067811865476
INV_SQRT_2PI = 0.3989422804014327


def gelu_pair(x):
    cdf = 0.5 * (1.0 + lax.erf(x * INV_SQRT2))
    pdf = jnp.exp(-0.5 * x * x) * INV_SQRT_2PI
    return x * cdf, cdf + x * pdf


def norm_parts(x):
    mean = jnp.mean(x, axis=-1, keepdims=True)
    centred = x - mean
    spread = jnp.mean(centred * centred, axis=-1, keepdims=True)
    inv = lax.rsqrt(spread + EPSILON)
    return centred * inv, inv


def col8(x):
    rows, cols = x.shape
    return jnp.sum(x.reshape(rows // 8, 8, cols), axis=0)


def layer_kernel(
    len_ref,
    tok_ref,
    cen_ref,
    cot_ref,
    small_ref,
    wqkv_ref,
    wout_ref,
    wup_ref,
    wdown_ref,
    wpos_ref,
    out_ref,
    gtok_ref,
    grad_ref,
    sgrad_ref,
    sacc,
    posh_s,
    emb_s,
    xh1_s,
    n1_s,
    qkv_s,
    p_s,
    att_s,
    bin_s,
    n2g_s,
    ff_s,
    qg_s,
    wide_s,
    ds_s,
    dq_s,
    ag_s,
    *,
    fc,
    group,
):
    step = pl.program_id(0)
    last = pl.num_programs(0) - 1

    @pl.when(step == 0)
    def _():
        grad_ref[...] = jnp.zeros_like(grad_ref)
        sacc[...] = jnp.zeros_like(sacc)

    rows = group * LMAX
    lengths = [len_ref[step * group + i] for i in range(group)]

    def live(width):
        return jnp.concatenate(
            [lax.broadcasted_iota(jnp.int32, (LMAX, width), 0) < length for length in lengths], axis=0
        )

    def vec(at, blocks):
        return jnp.concatenate([small_ref[at + i : at + i + 1, :] for i in range(blocks)], axis=1)

    def add_small(at, value):
        cols = value.shape[1]
        sacc[:, at * LANES : at * LANES + cols] += value

    def add_grad(block, value):
        for i in range(value.shape[1] // LANES):
            rows = slice((block + i) * D, (block + i + 1) * D)
            grad_ref[rows, :] += value[:, i * LANES : (i + 1) * LANES]

    gain_one, shift_one, gain_two, shift_two, attn_bias, down_bias, embed_bias = (
        vec(3 * i, 3) for i in range(7)
    )
    hidden_bias = small_ref[33:34, :]
    pos_first = small_ref[34:37, :]
    cen = cen_ref[...]

    pos_hidden = (
        lax.dot_general(
            cen, pos_first, (((0,), (0,)), ((), ())), precision=HIGHEST, preferred_element_type=F32
        )
        + hidden_bias
    )
    pos_act, pos_slope = gelu_pair(pos_hidden)
    pos_low = pos_act.astype(BF)
    posh_s[...] = pos_slope
    embedded = tok_ref[...].astype(F32) + nn(pos_low, wpos_ref[...]) + embed_bias
    emb_s[...] = embedded
    xhat_one, inv_one = norm_parts(embedded)
    xh1_s[...] = xhat_one
    n1 = (xhat_one * gain_one + shift_one).astype(BF)
    n1_s[...] = n1
    qkv_s[...] = nn(n1, wqkv_ref[...]).astype(BF)

    lane = lax.broadcasted_iota(jnp.int32, (1, LANES), 1)
    halves = [(lane < HEAD).astype(F32).astype(BF), (lane >= HEAD).astype(F32).astype(BF)]
    scale = HEAD ** (-0.5)
    scaled = [(h.astype(F32) * scale).astype(BF) for h in halves]

    key_live = [
        lax.broadcasted_iota(jnp.int32, (LMAX, LMAX), 0) < length for length in lengths
    ]
    spans = [slice(i * LMAX, (i + 1) * LMAX) for i in range(group)]

    heads = [(i, head) for head in range(HEADS) for i in range(group)]

    def lanes_of(which, i, head):
        at = which * D + head // 2 * LANES
        return qkv_s[spans[i], at : at + LANES]

    def staged(*stages):
        for turn in range(len(heads) + len(stages) - 1):
            for lag, stage in enumerate(stages):
                if 0 <= turn - lag < len(heads):
                    stage(turn - lag, *heads[turn - lag])

    def scores(number, i, head):
        wide_s[number % 3] = nt(lanes_of(1, i, head), lanes_of(0, i, head) * scaled[head % 2])

    def soften(number, i, head):
        s = jnp.where(key_live[i], wide_s[number % 3], NEG_FILL)
        e = jnp.exp(s - jnp.max(s, axis=0, keepdims=True))
        p_s[i * HEADS + head] = (e * (1.0 / jnp.sum(e, axis=0, keepdims=True))).astype(BF)

    def attend(number, i, head):
        at = head % 2 * HEAD
        o_t = nn(lanes_of(2, i, head).T[at : at + HEAD, :], p_s[i * HEADS + head])
        att_s[head * HEAD : (head + 1) * HEAD, spans[i]] = o_t.astype(BF)

    staged(scores, soften, attend)

    branch_in = emb_s[...] + tn(att_s[...], wout_ref[...]) + attn_bias
    bin_s[...] = branch_in
    xhat_two, inv_two = norm_parts(branch_in)
    n2 = (xhat_two * gain_two + shift_two).astype(BF)
    n2_t = n2.T
    gy = jnp.where(live(D), cot_ref[...].astype(F32), 0.0)
    gy_low = gy.astype(BF)
    gy_t = gy_low.T
    add_small(15, col8(gy))

    for c in range(FF // fc):
        cols = slice(c * fc, (c + 1) * fc)
        up_bias = vec(21 + c * (fc // LANES), fc // LANES)
        hidden = nn(n2, wup_ref[:, cols]) + up_bias
        act, slope = gelu_pair(hidden)
        act_low = act.astype(BF)
        part = nn(act_low, wdown_ref[cols, :])
        act_grad = nt(gy_low, wdown_ref[cols, :])
        hg = (act_grad * slope).astype(BF)
        add_small(21 + c * (fc // LANES), col8(hg.astype(F32)))
        back = nt(hg, wup_ref[:, cols])
        if c == 0:
            ff_s[...] = part
            n2g_s[...] = back
        else:
            ff_s[...] += part
            n2g_s[...] += back
        add_grad(UP_AT + c * (fc // LANES), nn(n2_t, hg))
        add_grad(DOWN_AT + c * (fc // LANES), nn(gy_t, act_low))

    out_ref[...] = (bin_s[...] + ff_s[...] + down_bias).astype(BF)

    n2g = n2g_s[...]
    add_small(6, col8(n2g * xhat_two))
    add_small(9, col8(n2g))
    u = n2g * gain_two
    bg = gy + inv_two * (
        u
        - jnp.mean(u, axis=-1, keepdims=True)
        - xhat_two * jnp.mean(u * xhat_two, axis=-1, keepdims=True)
    )
    bin_s[...] = bg
    add_small(12, col8(bg))
    bg_low = bg.astype(BF)
    add_grad(OUT_AT, nn(att_s[...], bg_low))
    ag = nt(bg_low, wout_ref[...]).astype(BF)

    ag_s[...] = ag
    dk, dv = {}, {}

    def ago_of(i, head):
        at = head // 2 * LANES
        return ag_s[spans[i], at : at + LANES] * halves[head % 2]

    def probs_back(number, i, head):
        wide_s[number % 3] = nt(lanes_of(2, i, head), ago_of(i, head))

    def scores_back(number, i, head):
        p = p_s[i * HEADS + head].astype(F32)
        dp = wide_s[number % 3]
        rd = jnp.sum(p * dp, axis=0, keepdims=True)
        ds_s[number % 2] = (p * (dp - rd)).astype(BF)

    def heads_back(number, i, head):
        ds = ds_s[number % 2]
        at = head % 2 * HEAD
        dv[i, head] = nn(p_s[i * HEADS + head], ago_of(i, head))
        dk[i, head] = nn(ds, lanes_of(0, i, head) * scaled[head % 2])
        dq_t = nn(lanes_of(1, i, head).T[at : at + HEAD, :], ds) * scale
        dq_s[head * HEAD : (head + 1) * HEAD, spans[i]] = dq_t.astype(BF)
        if head % 2:
            at = head // 2 * LANES
            qg_s[spans[i], at : at + LANES] = dq_s[at : at + LANES, spans[i]].T
            for which, terms in ((1, dk), (2, dv)):
                total = terms.pop((i, head - 1)) + terms.pop((i, head))
                qg_s[spans[i], which * D + at : which * D + at + LANES] = total.astype(BF)

    staged(probs_back, scores_back, heads_back)

    qg = qg_s[...]
    add_grad(QKV_AT, nn(n1_s[...].T, qg))
    n1g = nt(qg, wqkv_ref[...])
    xhat = xh1_s[...]
    add_small(0, col8(n1g * xhat))
    add_small(3, col8(n1g))
    u = n1g * gain_one
    eg = bin_s[...] + inv_one * (
        u
        - jnp.mean(u, axis=-1, keepdims=True)
        - xhat * jnp.mean(u * xhat, axis=-1, keepdims=True)
    )
    add_small(18, col8(eg))
    eg_low = eg.astype(BF)
    gtok_ref[...] = eg_low
    add_grad(POS_AT, tn(eg_low, pos_low))
    phg = nt(eg_low, wpos_ref[...]) * posh_s[...]
    add_small(33, col8(phg))
    pf_grad = jnp.dot(cen, phg, precision=HIGHEST, preferred_element_type=F32)
    for i in range(3):
        sacc[0:1, (34 + i) * LANES : (35 + i) * LANES] += pf_grad[i : i + 1, :]

    @pl.when(step == last)
    def _():
        for i in range(SMALL_ROWS):
            sgrad_ref[i : i + 1, :] = jnp.sum(
                sacc[:, i * LANES : (i + 1) * LANES], axis=0, keepdims=True
            )


def layer_pass(tokens, centres, lengths, cotangent, small_rows, wqkv, wout, wup, wdown, wpos, fc=768, group=2):
    clouds = lengths.shape[0]
    rows = clouds * LMAX
    span = group * LMAX
    whole = lambda shape: pl.BlockSpec(shape, lambda i, *_: (0, 0), pipeline_mode=pl.Buffered(1))
    tile = lambda: pl.BlockSpec((span, D), lambda i, *_: (i, 0))
    return pl.pallas_call(
        functools.partial(layer_kernel, fc=fc, group=group),
        out_shape=(
            jax.ShapeDtypeStruct((rows, D), BF),
            jax.ShapeDtypeStruct((rows, D), BF),
            jax.ShapeDtypeStruct((FLAT_ROWS, LANES), F32),
            jax.ShapeDtypeStruct((SMALL_ROWS, LANES), F32),
        ),
        grid_spec=pltpu.PrefetchScalarGridSpec(
            num_scalar_prefetch=1,
            grid=(clouds // group,),
            in_specs=[
                tile(),
                pl.BlockSpec((3, span), lambda i, *_: (0, i)),
                tile(),
                whole((SMALL_ROWS, LANES)),
                whole((D, 3 * D)),
                whole((D, D)),
                whole((D, FF)),
                whole((FF, D)),
                whole((PH, D)),
            ],
            out_specs=[
                tile(),
                tile(),
                whole((FLAT_ROWS, LANES)),
                whole((SMALL_ROWS, LANES)),
            ],
            scratch_shapes=[
                pltpu.VMEM((8, SMALL_ROWS * LANES), F32),
                pltpu.VMEM((span, PH), F32),
                pltpu.VMEM((span, D), F32),
                pltpu.VMEM((span, D), F32),
                pltpu.VMEM((span, D), BF),
                pltpu.VMEM((span, 3 * D), BF),
                pltpu.VMEM((group * HEADS, LMAX, LMAX), BF),
                pltpu.VMEM((D, span), BF),
                pltpu.VMEM((span, D), F32),
                pltpu.VMEM((span, D), F32),
                pltpu.VMEM((span, D), F32),
                pltpu.VMEM((span, 3 * D), BF),
                pltpu.VMEM((3, LMAX, LMAX), F32),
                pltpu.VMEM((2, LMAX, LMAX), BF),
                pltpu.VMEM((D, span), BF),
                pltpu.VMEM((span, D), BF),
            ],
        ),
        compiler_params=pltpu.CompilerParams(vmem_limit_bytes=60 * 1024 * 1024),
        name="layer",
    )(lengths, tokens, centres, cotangent, small_rows, wqkv, wout, wup, wdown, wpos)


MESH_ID = pl.DeviceIdType.MESH


def mesh_roles(mesh):
    dp, fs = mesh.shape["dp"], mesh.shape["fsdp"]
    if dp >= 32:
        return {
            "z": ("dp", dp // 4 // 2, 4) if dp == 32 else ("dp", 8, dp // 8),
            "y": ("dp", 2, 4),
            "c": ("dp", 1, 2),
            "x": ("fsdp", 1, fs),
        }
    return {
        "z": ("dp", 2, dp // 2),
        "y": ("dp", 1, 2),
        "x": ("fsdp", 2, fs // 2),
        "c": ("fsdp", 1, 2),
    }


def flipped(coord, offset, size):
    if offset == 0:
        return coord
    if size == 2:
        return 1 - coord
    return {1: coord + 1 - 2 * (coord % 2), 2: (coord + 2) % 4, 3: 3 - coord}[offset]


class Grid:
    def __init__(self, roles, sizes):
        self.roles, self.sizes = roles, sizes
        self.index = {axis: lax.axis_index(axis) for axis in sizes}
        self.coord = {
            role: (self.index[axis] // stride) % size
            for role, (axis, stride, size) in roles.items()
        }

    def place(self, **offsets):
        at = dict(self.index)
        for role, offset in offsets.items():
            axis, stride, size = self.roles[role]
            other = flipped(self.coord[role], offset, size)
            at[axis] = at[axis] + (other - self.coord[role]) * stride
        return at

    def slot(self, **offsets):
        at = self.place(**offsets)
        return at["dp"] * self.sizes["fsdp"] + at["fsdp"]

    def size(self, role):
        return self.roles[role][2]

    def offsets(self, role):
        return range(1, self.size(role))


class Wire:
    def __init__(self, grid, send_sems, recv_sems):
        self.grid, self.send_sems, self.recv_sems = grid, send_sems, recv_sems
        self.copies = {}

    def send(self, key, source, target, **offsets):
        number = len(self.copies)
        copy = pltpu.make_async_remote_copy(
            src_ref=source,
            dst_ref=target,
            send_sem=self.send_sems.at[number],
            recv_sem=self.recv_sems.at[number],
            device_id=self.grid.place(**offsets),
            device_id_type=MESH_ID,
        )
        copy.start()
        assert key not in self.copies
        self.copies[key] = copy

    def arrived(self, key):
        self.copies[key].wait_recv()

    def finish(self):
        for copy in self.copies.values():
            copy.wait_send()


def meet(grid):
    barrier = pltpu.get_barrier_semaphore()
    count = 0
    for role in ("z", "y", "x", "c"):
        for offset in grid.offsets(role):
            pl.semaphore_signal(
                barrier,
                inc=1,
                device_id=grid.place(**{role: offset}),
                device_id_type=MESH_ID,
            )
            count += 1
    pl.semaphore_wait(barrier, count)


def gather_copies(roles):
    nz, ny, nx, nc = (roles[role][2] for role in ("z", "y", "x", "c"))
    plane = (ny - 1) + (nx - 1) + 2 * (ny - 1) * (nx - 1)
    core = (nc - 1) * (1 + plane)
    return (nz - 1) + nz * (plane + core)


def nothing():
    pass


def gather_all(grid, wire, buf, tag, idle=nothing):
    rows = buf.shape[1]
    half = rows // 32 * 16
    parts = {"a": pl.ds(0, half), "b": pl.ds(half, rows - half)}

    def pass_on(key, slot, part, **offsets):
        ref = buf.at[slot] if part is None else buf.at[slot, parts[part]]
        wire.send((tag,) + key, ref, ref, **offsets)

    zs, ys, xs, cs = ([*grid.offsets(role)] for role in ("z", "y", "x", "c"))

    def to_core(key, slot, part=None):
        for c in cs:
            pass_on(("c", c) + key, slot, part, c=c)

    def have(b):
        slot = grid.slot(z=b)
        for y in ys:
            pass_on(("y", b, y), slot, None, y=y)
        for x in xs:
            pass_on(("x", b, x), slot, None, x=x)
        to_core((b, 0, 0, 0), slot)

    def relay(b):
        for y in ys:
            wire.arrived((tag, "y", b, y))
            for x in xs:
                pass_on(("a", b, y, x), grid.slot(z=b, y=y), "a", x=x)
            to_core((b, y, 0, 0), grid.slot(z=b, y=y))
        for x in xs:
            wire.arrived((tag, "x", b, x))
            for y in ys:
                pass_on(("b", b, y, x), grid.slot(z=b, x=x), "b", y=y)
            to_core((b, 0, x, 0), grid.slot(z=b, x=x))

    for z in zs:
        pass_on(("z", z), grid.slot(), None, z=z)
    have(0)
    idle()
    for b in zs:
        wire.arrived((tag, "z", b))
        have(b)
        idle()
        relay(b - 1)
        idle()
    relay(len(zs))
    for b in [0] + zs:
        for y in ys:
            for x in xs:
                for part in ("a", "b"):
                    wire.arrived((tag, part, b, y, x))
                    to_core((b, y, x, part), grid.slot(z=b, y=y, x=x), part)
    for key in list(wire.copies):
        if key[:2] == (tag, "c"):
            wire.arrived(key)


def reduce_copies(roles):
    nz, ny, nx, nc = (roles[role][2] for role in ("z", "y", "x", "c"))
    plane = (ny - 1) + (nx - 1) + 2 * (ny - 1) * (nx - 1)
    return (nc - 1) * nz * ny * nx + nz * plane + (nz - 1)


def small_copies(roles):
    return sum(roles[role][2] - 1 for role in ("z", "y", "x", "c"))


def reduce_scatter(grid, wire, full, small, acc, out_c, in_c, out_p, in_p, out_z, in_z, s_out, s_in, extra, ready=lambda b: None, idle=nothing):
    rows = full.shape[1]
    half = rows // 32 * 16
    first, second = pl.ds(0, half), pl.ds(half, rows - half)
    zs, ys, xs, cs = ([*grid.offsets(role)] for role in ("z", "y", "x", "c"))
    order = zs[::-1] + [0]

    small_order = ["c", "y", "x", "z"]
    small_state = {"value": small[...], "stage": 0}

    def small_send():
        stage = small_state["stage"]
        role = small_order[stage]
        s_out[stage] = small_state["value"]
        for offset in grid.offsets(role):
            number = extra[(role, offset)]
            wire.send(("s", role, offset), s_out.at[stage], s_in.at[number], **{role: offset})

    def small_take():
        stage = small_state["stage"]
        role = small_order[stage]
        value = small_state["value"]
        for offset in grid.offsets(role):
            wire.arrived(("s", role, offset))
            value = value + s_in[extra[(role, offset)]]
        small_state["value"] = value
        small_state["stage"] = stage + 1

    small_send()
    for b in order:
        ready(b)
        for y in [0] + ys:
            for x in [0] + xs:
                for c in cs:
                    out_c[c - 1, b, y, x] = full[grid.slot(z=b, y=y, x=x, c=c)].astype(BF)
                    wire.send(
                        ("c", c, b, y, x), out_c.at[c - 1, b, y, x], in_c.at[c - 1, b, y, x], c=c
                    )

    def core_sum(b, y, x):
        value = full[grid.slot(z=b, y=y, x=x)]
        for c in cs:
            wire.arrived(("c", c, b, y, x))
            value = value + in_c[c - 1, b, y, x].astype(F32)
        return value

    def diagonal(b):
        for y in ys:
            for x in xs:
                out_p[b, y, x] = core_sum(b, y, x).astype(BF)
                wire.send(("a", b, y, x), out_p.at[b, y, x, first], in_p.at[b, y, x, first], x=x)
                wire.send(("b", b, y, x), out_p.at[b, y, x, second], in_p.at[b, y, x, second], y=y)

    def neighbour(b):
        for y in ys:
            acc[...] = core_sum(b, y, 0)
            for x in xs:
                wire.arrived(("a", b, y, x))
                acc[first, :] += in_p[b, y, x, first].astype(F32)
            out_p[b, y, 0] = acc[...].astype(BF)
            wire.send(("y", b, y), out_p.at[b, y, 0], in_p.at[b, y, 0], y=y)
        for x in xs:
            acc[...] = core_sum(b, 0, x)
            for y in ys:
                wire.arrived(("b", b, y, x))
                acc[second, :] += in_p[b, y, x, second].astype(F32)
            out_p[b, 0, x] = acc[...].astype(BF)
            wire.send(("x", b, x), out_p.at[b, 0, x], in_p.at[b, 0, x], x=x)

    def plane_sum(b):
        value = core_sum(b, 0, 0)
        for y in ys:
            wire.arrived(("y", b, y))
            value = value + in_p[b, y, 0].astype(F32)
        for x in xs:
            wire.arrived(("x", b, x))
            value = value + in_p[b, 0, x].astype(F32)
        return value

    total = None
    for turn in range(len(order) + 2):
        idle()
        if turn < len(order):
            diagonal(order[turn])
        if 1 <= turn <= len(order):
            neighbour(order[turn - 1])
            if small_state["stage"] < 3:
                small_take()
                small_send()
        idle()
        if turn >= 2:
            b = order[turn - 2]
            value = plane_sum(b)
            if b:
                out_z[b - 1] = value.astype(BF)
                wire.send(("z", b), out_z.at[b - 1], in_z.at[b - 1], z=b)
            else:
                total = value
    small_take()
    for b in zs:
        wire.arrived(("z", b))
        total = total + in_z[b - 1].astype(F32)
    return total, small_state["value"]


DECAY = 0.5
ADAM_EPSILON = 1e-08
WEIGHT_DECAY = 0.05
VMEM_LIMIT = 60 * 1024 * 1024
NAMES = ("qkv", "out", "up", "down", "pos")
HEIGHT = {"qkv": D, "out": D, "up": D, "down": FF, "pos": PH}
WIDTH = {"qkv": 3 * D, "out": D, "up": FF, "down": D, "pos": D}
SMALLS = SMALL_ROWS * LANES


def pad16(rows):
    return -(-rows // 16) * 16


class Layout:
    def __init__(self, count, smalls):
        self.count = count
        self.rows = {name: HEIGHT[name] // count for name in NAMES}
        self.padded = {name: pad16(self.rows[name]) for name in NAMES}
        self.start = {}
        at = 0
        for name in NAMES:
            self.start[name] = at
            at += self.padded[name] * (WIDTH[name] // LANES)
        self.small_at = at
        self.small_len = SMALLS // count
        if smalls:
            at += 16
        self.total = at

    @property
    def base_rows(self):
        return self.padded["down"] + 16

    def base_place(self, name):
        if name == "down":
            return slice(0, self.padded["down"]), slice(0, FF)
        at = {"qkv": 0, "out": D, "up": 2 * D, "pos": 3 * D}[name]
        return slice(self.padded["down"], self.base_rows), slice(at, at + HEIGHT[name])

    def span(self, name, block):
        at = self.start[name] + block * self.padded[name]
        return slice(at, at + self.padded[name])

    def spread(self, name):
        rows, padded = self.rows[name], self.padded[name]
        shape = (HEIGHT[name], self.count * padded)
        row = lax.broadcasted_iota(jnp.int32, shape, 0)
        col = lax.broadcasted_iota(jnp.int32, shape, 1)
        own, owner = col % padded, col // padded
        hit = (own < rows) & (owner * rows + own == row)
        return hit.astype(F32).astype(BF)


def pad_rows(value, rows):
    have = value.shape[0]
    if have == rows:
        return value
    return jnp.concatenate([value, jnp.zeros((rows - have, value.shape[1]), value.dtype)], axis=0)


def once(action):
    pending = [action]

    def run():
        if pending:
            pending.pop()()

    return run


def head_kernel(roles, sizes, lay, *refs):
    masters = dict(zip(NAMES, refs[:5]))
    small_ref = refs[5]
    lefts = dict(zip(NAMES, refs[6:11]))
    outs = dict(zip(NAMES, refs[11:16]))
    flat_ref, bases, buf, send_sems, recv_sems = refs[16:]
    grid = Grid(roles, sizes)
    wire = Wire(grid, send_sems, recv_sems)
    own = grid.slot()
    for name in NAMES:
        for block in range(WIDTH[name] // LANES):
            piece = masters[name][:, block * LANES : (block + 1) * LANES]
            buf[own, lay.span(name, block), :] = pad_rows(piece, lay.padded[name]).astype(BF)
    buf[own, lay.small_at : lay.small_at + 16, :] = pad_rows(small_ref[...], 16).astype(BF)

    def pack_bases():
        bases[lay.padded["down"] :, :] = jnp.zeros((16, FF), BF)
        for name in NAMES:
            rows, cols = lay.base_place(name)
            bases[rows, cols] = pad_rows(lefts[name][...], rows.stop - rows.start).astype(BF)

    meet(grid)
    gather_all(grid, wire, buf, "w", once(pack_bases))
    for name in NAMES:
        spread = None if lay.rows[name] == lay.padded[name] else lay.spread(name)
        for block in range(WIDTH[name] // LANES):
            piece = buf[:, lay.span(name, block), :].reshape(lay.count * lay.padded[name], LANES)
            if spread is not None:
                piece = nn(spread, piece).astype(BF)
            outs[name][:, block * LANES : (block + 1) * LANES] = piece
    lane = lax.broadcasted_iota(jnp.int32, (1, LANES), 1)
    for row in range(SMALL_ROWS):
        line = jnp.zeros((1, LANES), F32)
        at = row * LANES
        while at < (row + 1) * LANES:
            owner, place = at // lay.small_len, at % lay.small_len
            source_row, source_lane = place // LANES, place % LANES
            take = min(
                (row + 1) * LANES - at, lay.small_len - place, LANES - source_lane
            )
            target = at - row * LANES
            piece = buf[owner, lay.small_at : lay.small_at + 16, :].astype(F32)
            piece = piece[source_row : source_row + 1, :]
            shift = (target - source_lane) % LANES
            if shift:
                piece = pltpu.roll(piece, shift, 1)
            line = jnp.where((lane >= target) & (lane < target + take), piece, line)
            at += take
        flat_ref[row : row + 1, :] = line
    wire.finish()


def vmem():
    return pl.BlockSpec(memory_space=pltpu.VMEM)


def gather_weights(roles, sizes, lay, masters, smalls, lefts):
    count = gather_copies(roles)
    lines = -(-lay.small_len // LANES)
    padded = jnp.pad(smalls, (0, lines * LANES - lay.small_len)).reshape(lines, LANES)
    return pl.pallas_call(
        functools.partial(head_kernel, roles, sizes, lay),
        out_shape=tuple(jax.ShapeDtypeStruct((HEIGHT[n], WIDTH[n]), BF) for n in NAMES)
        + (
            jax.ShapeDtypeStruct((SMALL_ROWS, LANES), F32),
            jax.ShapeDtypeStruct((lay.base_rows, FF), BF),
        ),
        in_specs=[vmem()] * 11,
        out_specs=tuple([vmem()] * 7),
        scratch_shapes=[
            pltpu.VMEM((lay.count, lay.total, LANES), BF),
            pltpu.SemaphoreType.DMA((count,)),
            pltpu.SemaphoreType.DMA((count,)),
        ],
        compiler_params=pltpu.CompilerParams(
            collective_id=0, has_side_effects=True, vmem_limit_bytes=VMEM_LIMIT
        ),
        name="gather_weights",
    )(*masters, padded, *lefts)


def split(value):
    high = value.astype(BF)
    return jnp.concatenate([high, (value - high.astype(F32)).astype(BF)], axis=0)


def joined(value):
    half = value.shape[0] // 2
    return value[:half] + value[half:]


class Groups:
    def __init__(self, lay):
        self.lay = lay
        wide = [(name, i) for name in ("qkv", "out", "up") for i in range(WIDTH[name] // LANES)]
        self.members = [wide[i : i + 4] for i in range(0, len(wide), 4)]
        self.members += [[("down", i)] for i in range(WIDTH["down"] // LANES)]
        self.members += [[("pos", i) for i in range(WIDTH["pos"] // LANES)]]
        self.rows = [pad16(sum(lay.rows[name] for name, _ in group)) for group in self.members]
        self.starts = [sum(self.rows[:i]) for i in range(len(self.rows))]
        self.total = sum(self.rows)
        self.kinds = []
        self.kind_of = []
        for group, rows in zip(self.members, self.rows):
            kind = (tuple(name for name, _ in group), rows)
            if kind not in self.kinds:
                self.kinds.append(kind)
            self.kind_of.append(self.kinds.index(kind))

    def span(self, number):
        return slice(self.starts[number], self.starts[number] + self.rows[number])

    def spread(self, name, rows, place):
        own_rows = self.lay.rows[name]
        shape = (HEIGHT[name], self.lay.count * rows)
        row = lax.broadcasted_iota(jnp.int32, shape, 0)
        col = lax.broadcasted_iota(jnp.int32, shape, 1)
        owner = col // rows
        own = col - owner * rows - place * own_rows
        hit = (own >= 0) & (own < own_rows) & (owner * own_rows + own == row)
        return hit.astype(F32).astype(BF)

    def thin(self, number):
        names, rows = self.kinds[number]
        return sum(2 * self.lay.padded[name] for name in names), self.lay.count * rows


RIGHT_CHUNK = 384
STARTS = {"qkv": QKV_AT, "up": UP_AT, "out": OUT_AT, "down": DOWN_AT, "pos": POS_AT}


def tail_kernel(roles, sizes, lay, groups, extra, full_hbm, small, bases_hbm, *refs):
    rights_hbm, lefts, masters, firsts, seconds = (
        dict(zip(NAMES, refs[5 * i : 5 * i + 5])) for i in range(5)
    )
    small_out = refs[25]
    grads, firsts_next, seconds_next, nexts, lows = (
        dict(zip(NAMES, refs[26 + 5 * i : 31 + 5 * i])) for i in range(5)
    )
    rest = refs[51:]
    full, acc, out_c, in_c, out_p, in_p, out_z, in_z, s_out, s_in = rest[:10]
    flat, steps, bases, coarse = rest[10:14]
    rights = dict(zip(NAMES, rest[14:19]))
    picks = dict(zip(NAMES, rest[19:24]))
    thins = rest[24 : 24 + len(groups.kinds)]
    send_sems, recv_sems, full_sems, base_sem, right_sems = rest[24 + len(groups.kinds) :]
    grid = Grid(roles, sizes)
    wire = Wire(grid, send_sems, recv_sems)
    me = grid.slot()

    plane = lay.count // grid.size("z")

    def full_copy(b):
        at = pl.multiple_of(flipped(grid.coord["z"], b, grid.size("z")) * plane, plane)
        part = pl.ds(at, plane)
        return pltpu.make_async_copy(full_hbm.at[part], full.at[part], full_sems.at[b])

    for b in [*grid.offsets("z")][::-1] + [0]:
        full_copy(b).start()
    base_copy = pltpu.make_async_copy(bases_hbm, bases, base_sem)
    base_copy.start()

    chunks = [(name, at) for name in NAMES for at in range(0, WIDTH[name], RIGHT_CHUNK)]

    def right_copy(number):
        name, at = chunks[number]
        return pltpu.make_async_copy(
            rights_hbm[name].at[pl.ds(at, RIGHT_CHUNK), :],
            coarse.at[number % 2, :, pl.ds(0, WIDTH[name])],
            right_sems.at[number],
        )

    right_copy(0).start()
    right_copy(1).start()

    def round_right(number):
        name, at = chunks[number]
        right_copy(number).wait()
        rights[name][at : at + RIGHT_CHUNK, :] = coarse[number % 2, :, : WIDTH[name]].astype(BF)
        if number + 2 < len(chunks):
            right_copy(number + 2).start()

    def make_pick(name):
        height, rows, padded = HEIGHT[name], lay.rows[name], lay.padded[name]
        row = lax.broadcasted_iota(jnp.int32, (padded, height), 0)
        col = lax.broadcasted_iota(jnp.int32, (padded, height), 1)
        pick = ((row < rows) & (col == me * rows + row)).astype(F32).astype(BF)
        base_rows, base_cols = lay.base_place(name)
        base = bases[:, base_rows, base_cols]
        left_rows = nt(pick, base.reshape(base.shape[0] * base.shape[1], height)).astype(BF)
        if rows != padded:
            left_rows = nt(left_rows, lay.spread(name)).astype(BF)
        picks[name][:padded, :] = left_rows
        picks[name][padded:, :] = pick

    def make_thin(number):
        names, rows = groups.kinds[number]
        at = 0
        for place, name in enumerate(names):
            padded = lay.padded[name]
            left = split(pad_rows(lefts[name][...], padded))
            if len(names) > 1 or rows != lay.rows[name]:
                left = nn(left, groups.spread(name, rows, place)).astype(BF)
            thins[number][at : at + 2 * padded, :] = left
            at += 2 * padded

    duties = [functools.partial(round_right, i) for i in range(len(chunks))]
    duties += [base_copy.wait]
    duties += [functools.partial(make_pick, name) for name in NAMES]
    duties += [functools.partial(make_thin, i) for i in range(len(groups.kinds))]

    def idle():
        if duties:
            duties.pop(0)()

    meet(grid)
    total, smalls = reduce_scatter(
        grid, wire, full, small, acc, out_c, in_c, out_p, in_p, out_z, in_z, s_out, s_in, extra,
        lambda b: full_copy(b).wait(), idle,
    )
    small_out[...] = smalls
    flat[me] = total.astype(BF)
    gather_all(grid, wire, flat, "flat", idle)
    while duties:
        idle()

    def flat_block(block):
        height = flat.shape[1]
        pieces, at = [], block * D
        while at < (block + 1) * D:
            slot, row = at // height, at % height
            take = min((block + 1) * D - at, height - row)
            pieces.append(flat[slot, row : row + take, :])
            at += take
        return pieces[0] if len(pieces) == 1 else jnp.concatenate(pieces, axis=0)

    directions = {}
    for name in NAMES:
        height, width = HEIGHT[name], WIDTH[name]
        rows, padded = lay.rows[name], lay.padded[name]
        lhs = picks[name][...]
        if name in ("down", "pos"):
            both = None
            for block in range(height // LANES):
                part = nt(
                    lhs[:, block * LANES : (block + 1) * LANES], flat_block(STARTS[name] + block)
                )
                both = part if both is None else both + part
        else:
            both = jnp.concatenate(
                [nn(lhs, flat_block(STARTS[name] + i)) for i in range(width // LANES)], axis=1
            )
        grads[name][...] = both[padded : padded + rows]
        terms = split(both[:padded])
        for at in range(0, width, D):
            cols = slice(at, at + D)
            rotated = joined(nn(terms, rights[name][:, cols]))[:rows]
            first = DECAY * firsts[name][:, cols] + (1.0 - DECAY) * rotated
            second = DECAY * seconds[name][:, cols] + (1.0 - DECAY) * rotated * rotated
            firsts_next[name][:, cols] = first
            seconds_next[name][:, cols] = second
            direction = first / (jnp.sqrt(second) + ADAM_EPSILON)
            for i in range(D // LANES):
                directions[name, at // LANES + i] = direction[:, i * LANES : (i + 1) * LANES]
    for number, group in enumerate(groups.members):
        piece = jnp.concatenate([directions[member] for member in group], axis=0)
        steps[me, groups.span(number), :] = pad_rows(piece, groups.rows[number]).astype(BF)

    gather_all(grid, wire, steps, "steps")

    partway = {}
    for number, group in enumerate(groups.members):
        rows = groups.rows[number]
        piece = steps[:, groups.span(number), :].reshape(lay.count * rows, LANES)
        whole = nn(thins[groups.kind_of[number]][...], piece)
        at = 0
        for name, block in group:
            padded = lay.padded[name]
            partway[name, block] = joined(whole[at : at + 2 * padded])
            at += 2 * padded
    for name in NAMES:
        height, width = HEIGHT[name], WIDTH[name]
        terms = split(
            jnp.concatenate([partway[name, i] for i in range(width // LANES)], axis=1)
        )
        rate = height ** (-0.5)
        for at in range(0, width, D):
            cols = slice(at, at + D)
            update = joined(nt(terms, rights[name][cols, :]))[: lay.rows[name]]
            master = masters[name][:, cols] * (1.0 - rate * WEIGHT_DECAY) - rate * update
            nexts[name][:, cols] = master
            lows[name][:, cols] = master.astype(BF)
    wire.finish()


def finish_step(roles, sizes, lay, full, small, bases, rights, lefts, masters, firsts, seconds):
    slots, rows, _ = full.shape
    nz, ny, nx, nc = (roles[role][2] for role in ("z", "y", "x", "c"))
    count = reduce_copies(roles) + small_copies(roles) + 2 * gather_copies(roles)
    extra = {}
    for role in ("c", "y", "x", "z"):
        for offset in range(1, roles[role][2]):
            extra[(role, offset)] = len(extra)
    groups = Groups(lay)
    chunks = sum(WIDTH[name] // RIGHT_CHUNK for name in NAMES)
    shapes = [(lay.rows[n], WIDTH[n]) for n in NAMES]
    anywhere = pl.BlockSpec(memory_space=pl.ANY)
    return pl.pallas_call(
        functools.partial(tail_kernel, roles, sizes, lay, groups, extra),
        out_shape=(jax.ShapeDtypeStruct((SMALL_ROWS, LANES), F32),)
        + tuple(jax.ShapeDtypeStruct(s, F32) for s in shapes * 4)
        + tuple(jax.ShapeDtypeStruct(s, BF) for s in shapes),
        in_specs=[anywhere, vmem(), anywhere] + [anywhere] * 5 + [vmem()] * 20,
        out_specs=tuple([vmem()] * 26),
        scratch_shapes=[
            pltpu.VMEM((slots, rows, LANES), F32),
            pltpu.VMEM((rows, LANES), F32),
            pltpu.VMEM((nc - 1, nz, ny, nx, rows, LANES), BF),
            pltpu.VMEM((nc - 1, nz, ny, nx, rows, LANES), BF),
            pltpu.VMEM((nz, ny, nx, rows, LANES), BF),
            pltpu.VMEM((nz, ny, nx, rows, LANES), BF),
            pltpu.VMEM((nz - 1, rows, LANES), BF),
            pltpu.VMEM((nz - 1, rows, LANES), BF),
            pltpu.VMEM((4, SMALL_ROWS, LANES), F32),
            pltpu.VMEM((len(extra), SMALL_ROWS, LANES), F32),
            pltpu.VMEM((slots, rows, LANES), BF),
            pltpu.VMEM((slots, groups.total, LANES), BF),
            pltpu.VMEM(bases.shape, BF),
            pltpu.VMEM((2, RIGHT_CHUNK, FF), F32),
        ]
        + [pltpu.VMEM((WIDTH[name], WIDTH[name]), BF) for name in NAMES]
        + [pltpu.VMEM((2 * lay.padded[name], HEIGHT[name]), BF) for name in NAMES]
        + [pltpu.VMEM(groups.thin(i), BF) for i in range(len(groups.kinds))]
        + [
            pltpu.SemaphoreType.DMA((count,)),
            pltpu.SemaphoreType.DMA((count,)),
            pltpu.SemaphoreType.DMA((nz,)),
            pltpu.SemaphoreType.DMA,
            pltpu.SemaphoreType.DMA((chunks,)),
        ],
        compiler_params=pltpu.CompilerParams(
            collective_id=1, has_side_effects=True, vmem_limit_bytes=VMEM_LIMIT
        ),
        name="finish_step",
    )(full, small, bases, *rights, *lefts, *masters, *firsts, *seconds)


AXES = ("dp", "fsdp")


def on_device(roles, sizes, tokens, centres, lengths, cotangent, smalls, *matrices):
    masters, firsts, seconds, lefts, rights = (matrices[5 * i : 5 * i + 5] for i in range(5))
    count = sizes["dp"] * sizes["fsdp"]
    heads = Layout(count, True)
    lay = Layout(count, False)
    *weights, small_rows, bases = gather_weights(roles, sizes, heads, masters, smalls, lefts)
    w_qkv, w_out, w_up, w_down, w_pos = weights
    whole_bases = lax.all_gather(bases, AXES, axis=0, tiled=True)
    layer_out, grad_tokens, full, small_grads = layer_pass(
        tokens, centres, lengths, cotangent, small_rows, w_qkv, w_out, w_up, w_down, w_pos
    )
    small_total, *finished = finish_step(
        roles,
        sizes,
        lay,
        full.reshape(count, FLAT_ROWS // count, LANES),
        small_grads,
        whole_bases.reshape(count, heads.base_rows, FF),
        rights,
        lefts,
        masters,
        firsts,
        seconds,
    )
    me = lax.axis_index("dp") * sizes["fsdp"] + lax.axis_index("fsdp")
    grad_smalls = lax.dynamic_slice(
        small_total.reshape(SMALLS), (me * heads.small_len,), (heads.small_len,)
    )
    return (layer_out, grad_tokens, grad_smalls, *finished)


def solution(mesh):
    sizes = {axis: mesh.shape[axis] for axis in AXES}
    rows, flat = P(AXES, None), P(AXES)
    return jax.shard_map(
        functools.partial(on_device, mesh_roles(mesh), sizes),
        mesh=mesh,
        in_specs=(rows, P(None, AXES), flat, rows, flat) + (rows,) * 20 + (P(),) * 5,
        out_specs=(rows, rows, flat) + (rows,) * 25,
        check_vma=False,
    )
```

```python
import functools
import jax
import jax.numpy as jnp
from jax import lax
from jax.experimental import pallas as pl
from jax.experimental.pallas import tpu as pltpu
from jax.sharding import PartitionSpec as P

D = 384
HEADS = 6
HEAD = 64
FF = 1536
PH = 128
LMAX = 256
LANES = 128
EPSILON = 1e-05
NEG_FILL = -1e30
HIGHEST = lax.Precision.HIGHEST
BF = jnp.bfloat16
F32 = jnp.float32

QKV_AT, UP_AT, OUT_AT, DOWN_AT, POS_AT, BLOCKS = 0, 9, 21, 24, 36, 37
FLAT_ROWS = 14336
SMALL_ROWS = 37


def nn(a, b):
    return jnp.dot(a, b, preferred_element_type=F32)


def nt(a, b):
    return lax.dot_general(a, b, (((1,), (1,)), ((), ())), preferred_element_type=F32)


def tn(a, b):
    return lax.dot_general(a, b, (((0,), (0,)), ((), ())), preferred_element_type=F32)


INV_SQRT2 = 0.7071067811865476
INV_SQRT_2PI = 0.3989422804014327


def gelu_pair(x):
    cdf = 0.5 * (1.0 + lax.erf(x * INV_SQRT2))
    pdf = jnp.exp(-0.5 * x * x) * INV_SQRT_2PI
    return x * cdf, cdf + x * pdf


def norm_parts(x):
    mean = jnp.mean(x, axis=-1, keepdims=True)
    centred = x - mean
    spread = jnp.mean(centred * centred, axis=-1, keepdims=True)
    inv = lax.rsqrt(spread + EPSILON)
    return centred * inv, inv


def col8(x):
    rows, cols = x.shape
    return jnp.sum(x.reshape(rows // 8, 8, cols), axis=0)


def layer_kernel(
    len_ref,
    tok_ref,
    cen_ref,
    cot_ref,
    small_ref,
    wqkv_ref,
    wout_ref,
    wup_ref,
    wdown_ref,
    wpos_ref,
    out_ref,
    gtok_ref,
    grad_ref,
    sgrad_ref,
    sacc,
    posh_s,
    emb_s,
    xh1_s,
    n1_s,
    qkv_s,
    p_s,
    att_s,
    bin_s,
    n2g_s,
    ff_s,
    qg_s,
    wide_s,
    ds_s,
    dq_s,
    ag_s,
    *,
    fc,
    group,
):
    step = pl.program_id(0)
    last = pl.num_programs(0) - 1

    @pl.when(step == 0)
    def _():
        grad_ref[...] = jnp.zeros_like(grad_ref)
        sacc[...] = jnp.zeros_like(sacc)

    rows = group * LMAX
    lengths = [len_ref[step * group + i] for i in range(group)]

    def live(width):
        return jnp.concatenate(
            [lax.broadcasted_iota(jnp.int32, (LMAX, width), 0) < length for length in lengths], axis=0
        )

    def vec(at, blocks):
        return jnp.concatenate([small_ref[at + i : at + i + 1, :] for i in range(blocks)], axis=1)

    def add_small(at, value):
        cols = value.shape[1]
        sacc[:, at * LANES : at * LANES + cols] += value

    def add_grad(block, value):
        for i in range(value.shape[1] // LANES):
            rows = slice((block + i) * D, (block + i + 1) * D)
            grad_ref[rows, :] += value[:, i * LANES : (i + 1) * LANES]

    gain_one, shift_one, gain_two, shift_two, attn_bias, down_bias, embed_bias = (
        vec(3 * i, 3) for i in range(7)
    )
    hidden_bias = small_ref[33:34, :]
    pos_first = small_ref[34:37, :]
    cen = cen_ref[...]

    pos_hidden = (
        lax.dot_general(
            cen, pos_first, (((0,), (0,)), ((), ())), precision=HIGHEST, preferred_element_type=F32
        )
        + hidden_bias
    )
    pos_act, pos_slope = gelu_pair(pos_hidden)
    pos_low = pos_act.astype(BF)
    posh_s[...] = pos_slope
    embedded = tok_ref[...].astype(F32) + nn(pos_low, wpos_ref[...]) + embed_bias
    emb_s[...] = embedded
    xhat_one, inv_one = norm_parts(embedded)
    xh1_s[...] = xhat_one
    n1 = (xhat_one * gain_one + shift_one).astype(BF)
    n1_s[...] = n1
    qkv_s[...] = nn(n1, wqkv_ref[...]).astype(BF)

    lane = lax.broadcasted_iota(jnp.int32, (1, LANES), 1)
    halves = [(lane < HEAD).astype(F32).astype(BF), (lane >= HEAD).astype(F32).astype(BF)]
    scale = HEAD ** (-0.5)
    scaled = [(h.astype(F32) * scale).astype(BF) for h in halves]

    key_live = [
        lax.broadcasted_iota(jnp.int32, (LMAX, LMAX), 0) < length for length in lengths
    ]
    spans = [slice(i * LMAX, (i + 1) * LMAX) for i in range(group)]

    heads = [(i, head) for head in range(HEADS) for i in range(group)]

    def lanes_of(which, i, head):
        at = which * D + head // 2 * LANES
        return qkv_s[spans[i], at : at + LANES]

    def staged(*stages):
        for turn in range(len(heads) + len(stages) - 1):
            for lag, stage in enumerate(stages):
                if 0 <= turn - lag < len(heads):
                    stage(turn - lag, *heads[turn - lag])

    def scores(number, i, head):
        wide_s[number % 3] = nt(lanes_of(1, i, head), lanes_of(0, i, head) * scaled[head % 2])

    def soften(number, i, head):
        s = jnp.where(key_live[i], wide_s[number % 3], NEG_FILL)
        e = jnp.exp(s - jnp.max(s, axis=0, keepdims=True))
        p_s[i * HEADS + head] = (e * (1.0 / jnp.sum(e, axis=0, keepdims=True))).astype(BF)

    def attend(number, i, head):
        at = head % 2 * HEAD
        o_t = nn(lanes_of(2, i, head).T[at : at + HEAD, :], p_s[i * HEADS + head])
        att_s[head * HEAD : (head + 1) * HEAD, spans[i]] = o_t.astype(BF)

    staged(scores, soften, attend)

    branch_in = emb_s[...] + tn(att_s[...], wout_ref[...]) + attn_bias
    bin_s[...] = branch_in
    xhat_two, inv_two = norm_parts(branch_in)
    n2 = (xhat_two * gain_two + shift_two).astype(BF)
    n2_t = n2.T
    gy = jnp.where(live(D), cot_ref[...].astype(F32), 0.0)
    gy_low = gy.astype(BF)
    gy_t = gy_low.T
    add_small(15, col8(gy))

    for c in range(FF // fc):
        cols = slice(c * fc, (c + 1) * fc)
        up_bias = vec(21 + c * (fc // LANES), fc // LANES)
        hidden = nn(n2, wup_ref[:, cols]) + up_bias
        act, slope = gelu_pair(hidden)
        act_low = act.astype(BF)
        part = nn(act_low, wdown_ref[cols, :])
        act_grad = nt(gy_low, wdown_ref[cols, :])
        hg = (act_grad * slope).astype(BF)
        add_small(21 + c * (fc // LANES), col8(hg.astype(F32)))
        back = nt(hg, wup_ref[:, cols])
        if c == 0:
            ff_s[...] = part
            n2g_s[...] = back
        else:
            ff_s[...] += part
            n2g_s[...] += back
        add_grad(UP_AT + c * (fc // LANES), nn(n2_t, hg))
        add_grad(DOWN_AT + c * (fc // LANES), nn(gy_t, act_low))

    out_ref[...] = (bin_s[...] + ff_s[...] + down_bias).astype(BF)

    n2g = n2g_s[...]
    add_small(6, col8(n2g * xhat_two))
    add_small(9, col8(n2g))
    u = n2g * gain_two
    bg = gy + inv_two * (
        u
        - jnp.mean(u, axis=-1, keepdims=True)
        - xhat_two * jnp.mean(u * xhat_two, axis=-1, keepdims=True)
    )
    bin_s[...] = bg
    add_small(12, col8(bg))
    bg_low = bg.astype(BF)
    add_grad(OUT_AT, nn(att_s[...], bg_low))
    ag = nt(bg_low, wout_ref[...]).astype(BF)

    ag_s[...] = ag
    dk, dv = {}, {}

    def ago_of(i, head):
        at = head // 2 * LANES
        return ag_s[spans[i], at : at + LANES] * halves[head % 2]

    def probs_back(number, i, head):
        wide_s[number % 3] = nt(lanes_of(2, i, head), ago_of(i, head))

    def scores_back(number, i, head):
        p = p_s[i * HEADS + head].astype(F32)
        dp = wide_s[number % 3]
        rd = jnp.sum(p * dp, axis=0, keepdims=True)
        ds_s[number % 2] = (p * (dp - rd)).astype(BF)

    def heads_back(number, i, head):
        ds = ds_s[number % 2]
        at = head % 2 * HEAD
        dv[i, head] = nn(p_s[i * HEADS + head], ago_of(i, head))
        dk[i, head] = nn(ds, lanes_of(0, i, head) * scaled[head % 2])
        dq_t = nn(lanes_of(1, i, head).T[at : at + HEAD, :], ds) * scale
        dq_s[head * HEAD : (head + 1) * HEAD, spans[i]] = dq_t.astype(BF)
        if head % 2:
            at = head // 2 * LANES
            qg_s[spans[i], at : at + LANES] = dq_s[at : at + LANES, spans[i]].T
            for which, terms in ((1, dk), (2, dv)):
                total = terms.pop((i, head - 1)) + terms.pop((i, head))
                qg_s[spans[i], which * D + at : which * D + at + LANES] = total.astype(BF)

    staged(probs_back, scores_back, heads_back)

    qg = qg_s[...]
    add_grad(QKV_AT, nn(n1_s[...].T, qg))
    n1g = nt(qg, wqkv_ref[...])
    xhat = xh1_s[...]
    add_small(0, col8(n1g * xhat))
    add_small(3, col8(n1g))
    u = n1g * gain_one
    eg = bin_s[...] + inv_one * (
        u
        - jnp.mean(u, axis=-1, keepdims=True)
        - xhat * jnp.mean(u * xhat, axis=-1, keepdims=True)
    )
    add_small(18, col8(eg))
    eg_low = eg.astype(BF)
    gtok_ref[...] = eg_low
    add_grad(POS_AT, tn(eg_low, pos_low))
    phg = nt(eg_low, wpos_ref[...]) * posh_s[...]
    add_small(33, col8(phg))
    pf_grad = jnp.dot(cen, phg, precision=HIGHEST, preferred_element_type=F32)
    for i in range(3):
        sacc[0:1, (34 + i) * LANES : (35 + i) * LANES] += pf_grad[i : i + 1, :]

    @pl.when(step == last)
    def _():
        for i in range(SMALL_ROWS):
            sgrad_ref[i : i + 1, :] = jnp.sum(
                sacc[:, i * LANES : (i + 1) * LANES], axis=0, keepdims=True
            )


def layer_pass(tokens, centres, lengths, cotangent, small_rows, wqkv, wout, wup, wdown, wpos, fc=768, group=2):
    clouds = lengths.shape[0]
    rows = clouds * LMAX
    span = group * LMAX
    whole = lambda shape: pl.BlockSpec(shape, lambda i, *_: (0, 0), pipeline_mode=pl.Buffered(1))
    tile = lambda: pl.BlockSpec((span, D), lambda i, *_: (i, 0))
    return pl.pallas_call(
        functools.partial(layer_kernel, fc=fc, group=group),
        out_shape=(
            jax.ShapeDtypeStruct((rows, D), BF),
            jax.ShapeDtypeStruct((rows, D), BF),
            jax.ShapeDtypeStruct((FLAT_ROWS, LANES), F32),
            jax.ShapeDtypeStruct((SMALL_ROWS, LANES), F32),
        ),
        grid_spec=pltpu.PrefetchScalarGridSpec(
            num_scalar_prefetch=1,
            grid=(clouds // group,),
            in_specs=[
                tile(),
                pl.BlockSpec((3, span), lambda i, *_: (0, i)),
                tile(),
                whole((SMALL_ROWS, LANES)),
                whole((D, 3 * D)),
                whole((D, D)),
                whole((D, FF)),
                whole((FF, D)),
                whole((PH, D)),
            ],
            out_specs=[
                tile(),
                tile(),
                whole((FLAT_ROWS, LANES)),
                whole((SMALL_ROWS, LANES)),
            ],
            scratch_shapes=[
                pltpu.VMEM((8, SMALL_ROWS * LANES), F32),
                pltpu.VMEM((span, PH), F32),
                pltpu.VMEM((span, D), F32),
                pltpu.VMEM((span, D), F32),
                pltpu.VMEM((span, D), BF),
                pltpu.VMEM((span, 3 * D), BF),
                pltpu.VMEM((group * HEADS, LMAX, LMAX), BF),
                pltpu.VMEM((D, span), BF),
                pltpu.VMEM((span, D), F32),
                pltpu.VMEM((span, D), F32),
                pltpu.VMEM((span, D), F32),
                pltpu.VMEM((span, 3 * D), BF),
                pltpu.VMEM((3, LMAX, LMAX), F32),
                pltpu.VMEM((2, LMAX, LMAX), BF),
                pltpu.VMEM((D, span), BF),
                pltpu.VMEM((span, D), BF),
            ],
        ),
        compiler_params=pltpu.CompilerParams(vmem_limit_bytes=60 * 1024 * 1024),
        name="layer",
    )(lengths, tokens, centres, cotangent, small_rows, wqkv, wout, wup, wdown, wpos)


MESH_ID = pl.DeviceIdType.MESH


def mesh_roles(mesh):
    dp, fs = mesh.shape["dp"], mesh.shape["fsdp"]
    if dp >= 32:
        return {
            "z": ("dp", dp // 4 // 2, 4) if dp == 32 else ("dp", 8, dp // 8),
            "y": ("dp", 2, 4),
            "c": ("dp", 1, 2),
            "x": ("fsdp", 1, fs),
        }
    return {
        "z": ("dp", 2, dp // 2),
        "y": ("dp", 1, 2),
        "x": ("fsdp", 2, fs // 2),
        "c": ("fsdp", 1, 2),
    }


def flipped(coord, offset, size):
    if offset == 0:
        return coord
    if size == 2:
        return 1 - coord
    return {1: coord + 1 - 2 * (coord % 2), 2: (coord + 2) % 4, 3: 3 - coord}[offset]


class Grid:
    def __init__(self, roles, sizes):
        self.roles, self.sizes = roles, sizes
        self.index = {axis: lax.axis_index(axis) for axis in sizes}
        self.coord = {
            role: (self.index[axis] // stride) % size
            for role, (axis, stride, size) in roles.items()
        }

    def place(self, **offsets):
        at = dict(self.index)
        for role, offset in offsets.items():
            axis, stride, size = self.roles[role]
            other = flipped(self.coord[role], offset, size)
            at[axis] = at[axis] + (other - self.coord[role]) * stride
        return at

    def slot(self, **offsets):
        at = self.place(**offsets)
        return at["dp"] * self.sizes["fsdp"] + at["fsdp"]

    def size(self, role):
        return self.roles[role][2]

    def offsets(self, role):
        return range(1, self.size(role))


class Wire:
    def __init__(self, grid, send_sems, recv_sems):
        self.grid, self.send_sems, self.recv_sems = grid, send_sems, recv_sems
        self.copies = {}

    def send(self, key, source, target, **offsets):
        number = len(self.copies)
        copy = pltpu.make_async_remote_copy(
            src_ref=source,
            dst_ref=target,
            send_sem=self.send_sems.at[number],
            recv_sem=self.recv_sems.at[number],
            device_id=self.grid.place(**offsets),
            device_id_type=MESH_ID,
        )
        copy.start()
        assert key not in self.copies
        self.copies[key] = copy

    def arrived(self, key):
        self.copies[key].wait_recv()

    def finish(self):
        for copy in self.copies.values():
            copy.wait_send()


def meet(grid):
    barrier = pltpu.get_barrier_semaphore()
    count = 0
    for role in ("z", "y", "x", "c"):
        for offset in grid.offsets(role):
            pl.semaphore_signal(
                barrier,
                inc=1,
                device_id=grid.place(**{role: offset}),
                device_id_type=MESH_ID,
            )
            count += 1
    pl.semaphore_wait(barrier, count)


def gather_copies(roles):
    nz, ny, nx, nc = (roles[role][2] for role in ("z", "y", "x", "c"))
    plane = (ny - 1) + (nx - 1) + 2 * (ny - 1) * (nx - 1)
    core = (nc - 1) * (1 + plane)
    return (nz - 1) + nz * (plane + core)


def nothing():
    pass


def gather_all(grid, wire, buf, tag, idle=nothing):
    rows = buf.shape[1]
    half = rows // 32 * 16
    parts = {"a": pl.ds(0, half), "b": pl.ds(half, rows - half)}

    def pass_on(key, slot, part, **offsets):
        ref = buf.at[slot] if part is None else buf.at[slot, parts[part]]
        wire.send((tag,) + key, ref, ref, **offsets)

    zs, ys, xs, cs = ([*grid.offsets(role)] for role in ("z", "y", "x", "c"))

    def to_core(key, slot, part=None):
        for c in cs:
            pass_on(("c", c) + key, slot, part, c=c)

    def have(b):
        slot = grid.slot(z=b)
        for y in ys:
            pass_on(("y", b, y), slot, None, y=y)
        for x in xs:
            pass_on(("x", b, x), slot, None, x=x)
        to_core((b, 0, 0, 0), slot)

    def relay(b):
        for y in ys:
            wire.arrived((tag, "y", b, y))
            for x in xs:
                pass_on(("a", b, y, x), grid.slot(z=b, y=y), "a", x=x)
            to_core((b, y, 0, 0), grid.slot(z=b, y=y))
        for x in xs:
            wire.arrived((tag, "x", b, x))
            for y in ys:
                pass_on(("b", b, y, x), grid.slot(z=b, x=x), "b", y=y)
            to_core((b, 0, x, 0), grid.slot(z=b, x=x))

    for z in zs:
        pass_on(("z", z), grid.slot(), None, z=z)
    have(0)
    idle()
    for b in zs:
        wire.arrived((tag, "z", b))
        have(b)
        idle()
        relay(b - 1)
        idle()
    relay(len(zs))
    for b in [0] + zs:
        for y in ys:
            for x in xs:
                for part in ("a", "b"):
                    wire.arrived((tag, part, b, y, x))
                    to_core((b, y, x, part), grid.slot(z=b, y=y, x=x), part)
    for key in list(wire.copies):
        if key[:2] == (tag, "c"):
            wire.arrived(key)


def reduce_copies(roles):
    nz, ny, nx, nc = (roles[role][2] for role in ("z", "y", "x", "c"))
    plane = (ny - 1) + (nx - 1) + 2 * (ny - 1) * (nx - 1)
    return (nc - 1) * nz * ny * nx + nz * plane + (nz - 1)


def small_copies(roles):
    return sum(roles[role][2] - 1 for role in ("z", "y", "x", "c"))


def reduce_scatter(grid, wire, full, small, acc, out_c, in_c, out_p, in_p, out_z, in_z, s_out, s_in, extra, ready=lambda b: None, idle=nothing):
    rows = full.shape[1]
    half = rows // 32 * 16
    first, second = pl.ds(0, half), pl.ds(half, rows - half)
    zs, ys, xs, cs = ([*grid.offsets(role)] for role in ("z", "y", "x", "c"))
    order = zs[::-1] + [0]

    small_order = ["c", "y", "x", "z"]
    small_state = {"value": small[...], "stage": 0}

    def small_send():
        stage = small_state["stage"]
        role = small_order[stage]
        s_out[stage] = small_state["value"]
        for offset in grid.offsets(role):
            number = extra[(role, offset)]
            wire.send(("s", role, offset), s_out.at[stage], s_in.at[number], **{role: offset})

    def small_take():
        stage = small_state["stage"]
        role = small_order[stage]
        value = small_state["value"]
        for offset in grid.offsets(role):
            wire.arrived(("s", role, offset))
            value = value + s_in[extra[(role, offset)]]
        small_state["value"] = value
        small_state["stage"] = stage + 1

    small_send()
    for b in order:
        ready(b)
        for y in [0] + ys:
            for x in [0] + xs:
                for c in cs:
                    out_c[c - 1, b, y, x] = full[grid.slot(z=b, y=y, x=x, c=c)].astype(BF)
                    wire.send(
                        ("c", c, b, y, x), out_c.at[c - 1, b, y, x], in_c.at[c - 1, b, y, x], c=c
                    )

    def core_sum(b, y, x):
        value = full[grid.slot(z=b, y=y, x=x)]
        for c in cs:
            wire.arrived(("c", c, b, y, x))
            value = value + in_c[c - 1, b, y, x].astype(F32)
        return value

    def diagonal(b):
        for y in ys:
            for x in xs:
                out_p[b, y, x] = core_sum(b, y, x).astype(BF)
                wire.send(("a", b, y, x), out_p.at[b, y, x, first], in_p.at[b, y, x, first], x=x)
                wire.send(("b", b, y, x), out_p.at[b, y, x, second], in_p.at[b, y, x, second], y=y)

    def neighbour(b):
        for y in ys:
            acc[...] = core_sum(b, y, 0)
            for x in xs:
                wire.arrived(("a", b, y, x))
                acc[first, :] += in_p[b, y, x, first].astype(F32)
            out_p[b, y, 0] = acc[...].astype(BF)
            wire.send(("y", b, y), out_p.at[b, y, 0], in_p.at[b, y, 0], y=y)
        for x in xs:
            acc[...] = core_sum(b, 0, x)
            for y in ys:
                wire.arrived(("b", b, y, x))
                acc[second, :] += in_p[b, y, x, second].astype(F32)
            out_p[b, 0, x] = acc[...].astype(BF)
            wire.send(("x", b, x), out_p.at[b, 0, x], in_p.at[b, 0, x], x=x)

    def plane_sum(b):
        value = core_sum(b, 0, 0)
        for y in ys:
            wire.arrived(("y", b, y))
            value = value + in_p[b, y, 0].astype(F32)
        for x in xs:
            wire.arrived(("x", b, x))
            value = value + in_p[b, 0, x].astype(F32)
        return value

    total = None
    for turn in range(len(order) + 2):
        idle()
        if turn < len(order):
            diagonal(order[turn])
        if 1 <= turn <= len(order):
            neighbour(order[turn - 1])
            if small_state["stage"] < 3:
                small_take()
                small_send()
        idle()
        if turn >= 2:
            b = order[turn - 2]
            value = plane_sum(b)
            if b:
                out_z[b - 1] = value.astype(BF)
                wire.send(("z", b), out_z.at[b - 1], in_z.at[b - 1], z=b)
            else:
                total = value
    small_take()
    for b in zs:
        wire.arrived(("z", b))
        total = total + in_z[b - 1].astype(F32)
    return total, small_state["value"]


DECAY = 0.5
ADAM_EPSILON = 1e-08
WEIGHT_DECAY = 0.05
VMEM_LIMIT = 60 * 1024 * 1024
NAMES = ("qkv", "out", "up", "down", "pos")
HEIGHT = {"qkv": D, "out": D, "up": D, "down": FF, "pos": PH}
WIDTH = {"qkv": 3 * D, "out": D, "up": FF, "down": D, "pos": D}
SMALLS = SMALL_ROWS * LANES


def pad16(rows):
    return -(-rows // 16) * 16


class Layout:
    def __init__(self, count, smalls):
        self.count = count
        self.rows = {name: HEIGHT[name] // count for name in NAMES}
        self.padded = {name: pad16(self.rows[name]) for name in NAMES}
        self.start = {}
        at = 0
        for name in NAMES:
            self.start[name] = at
            at += self.padded[name] * (WIDTH[name] // LANES)
        self.small_at = at
        self.small_len = SMALLS // count
        if smalls:
            at += 16
        self.total = at

    @property
    def base_rows(self):
        return self.padded["down"] + 16

    def base_place(self, name):
        if name == "down":
            return slice(0, self.padded["down"]), slice(0, FF)
        at = {"qkv": 0, "out": D, "up": 2 * D, "pos": 3 * D}[name]
        return slice(self.padded["down"], self.base_rows), slice(at, at + HEIGHT[name])

    def span(self, name, block):
        at = self.start[name] + block * self.padded[name]
        return slice(at, at + self.padded[name])

    def spread(self, name):
        rows, padded = self.rows[name], self.padded[name]
        shape = (HEIGHT[name], self.count * padded)
        row = lax.broadcasted_iota(jnp.int32, shape, 0)
        col = lax.broadcasted_iota(jnp.int32, shape, 1)
        own, owner = col % padded, col // padded
        hit = (own < rows) & (owner * rows + own == row)
        return hit.astype(F32).astype(BF)


def pad_rows(value, rows):
    have = value.shape[0]
    if have == rows:
        return value
    return jnp.concatenate([value, jnp.zeros((rows - have, value.shape[1]), value.dtype)], axis=0)


def once(action):
    pending = [action]

    def run():
        if pending:
            pending.pop()()

    return run


def head_kernel(roles, sizes, lay, *refs):
    masters = dict(zip(NAMES, refs[:5]))
    small_ref = refs[5]
    lefts = dict(zip(NAMES, refs[6:11]))
    outs = dict(zip(NAMES, refs[11:16]))
    flat_ref, bases, buf, send_sems, recv_sems = refs[16:]
    grid = Grid(roles, sizes)
    wire = Wire(grid, send_sems, recv_sems)
    own = grid.slot()
    for name in NAMES:
        for block in range(WIDTH[name] // LANES):
            piece = masters[name][:, block * LANES : (block + 1) * LANES]
            buf[own, lay.span(name, block), :] = pad_rows(piece, lay.padded[name]).astype(BF)
    lines = []
    for at in range(0, lay.small_len, LANES):
        line = small_ref[:, at : min(at + LANES, lay.small_len)]
        if line.shape[1] < LANES:
            line = jnp.concatenate([line, jnp.zeros((1, LANES - line.shape[1]), F32)], axis=1)
        lines.append(line)
    lines = jnp.concatenate(lines, axis=0)
    buf[own, lay.small_at : lay.small_at + 16, :] = pad_rows(lines, 16).astype(BF)

    def pack_bases():
        bases[lay.padded["down"] :, :] = jnp.zeros((16, FF), BF)
        for name in NAMES:
            rows, cols = lay.base_place(name)
            bases[rows, cols] = pad_rows(lefts[name][...], rows.stop - rows.start).astype(BF)

    meet(grid)
    gather_all(grid, wire, buf, "w", once(pack_bases))
    for name in NAMES:
        spread = None if lay.rows[name] == lay.padded[name] else lay.spread(name)
        for block in range(WIDTH[name] // LANES):
            piece = buf[:, lay.span(name, block), :].reshape(lay.count * lay.padded[name], LANES)
            if spread is not None:
                piece = nn(spread, piece).astype(BF)
            outs[name][:, block * LANES : (block + 1) * LANES] = piece
    lane = lax.broadcasted_iota(jnp.int32, (1, LANES), 1)
    for row in range(SMALL_ROWS):
        line = jnp.zeros((1, LANES), F32)
        at = row * LANES
        while at < (row + 1) * LANES:
            owner, place = at // lay.small_len, at % lay.small_len
            source_row, source_lane = place // LANES, place % LANES
            take = min(
                (row + 1) * LANES - at, lay.small_len - place, LANES - source_lane
            )
            target = at - row * LANES
            piece = buf[owner, lay.small_at : lay.small_at + 16, :].astype(F32)
            piece = piece[source_row : source_row + 1, :]
            shift = (target - source_lane) % LANES
            if shift:
                piece = pltpu.roll(piece, shift, 1)
            line = jnp.where((lane >= target) & (lane < target + take), piece, line)
            at += take
        flat_ref[row : row + 1, :] = line
    wire.finish()


def vmem():
    return pl.BlockSpec(memory_space=pltpu.VMEM)


def gather_weights(roles, sizes, lay, masters, smalls, lefts):
    count = gather_copies(roles)
    return pl.pallas_call(
        functools.partial(head_kernel, roles, sizes, lay),
        out_shape=tuple(jax.ShapeDtypeStruct((HEIGHT[n], WIDTH[n]), BF) for n in NAMES)
        + (
            jax.ShapeDtypeStruct((SMALL_ROWS, LANES), F32),
            jax.ShapeDtypeStruct((lay.base_rows, FF), BF),
        ),
        in_specs=[vmem()] * 11,
        out_specs=tuple([vmem()] * 7),
        scratch_shapes=[
            pltpu.VMEM((lay.count, lay.total, LANES), BF),
            pltpu.SemaphoreType.DMA((count,)),
            pltpu.SemaphoreType.DMA((count,)),
        ],
        compiler_params=pltpu.CompilerParams(
            collective_id=0, has_side_effects=True, vmem_limit_bytes=VMEM_LIMIT
        ),
        name="gather_weights",
    )(*masters, smalls.reshape(1, lay.small_len), *lefts)


def split(value):
    high = value.astype(BF)
    return jnp.concatenate([high, (value - high.astype(F32)).astype(BF)], axis=0)


def joined(value):
    half = value.shape[0] // 2
    return value[:half] + value[half:]


class Groups:
    def __init__(self, lay):
        self.lay = lay
        wide = [(name, i) for name in ("qkv", "out", "up") for i in range(WIDTH[name] // LANES)]
        self.members = [wide[i : i + 4] for i in range(0, len(wide), 4)]
        self.members += [[("down", i)] for i in range(WIDTH["down"] // LANES)]
        self.members += [[("pos", i) for i in range(WIDTH["pos"] // LANES)]]
        self.rows = [pad16(sum(lay.rows[name] for name, _ in group)) for group in self.members]
        self.starts = [sum(self.rows[:i]) for i in range(len(self.rows))]
        self.total = sum(self.rows)
        self.kinds = []
        self.kind_of = []
        for group, rows in zip(self.members, self.rows):
            kind = (tuple(name for name, _ in group), rows)
            if kind not in self.kinds:
                self.kinds.append(kind)
            self.kind_of.append(self.kinds.index(kind))

    def span(self, number):
        return slice(self.starts[number], self.starts[number] + self.rows[number])

    def spread(self, name, rows, place):
        own_rows = self.lay.rows[name]
        shape = (HEIGHT[name], self.lay.count * rows)
        row = lax.broadcasted_iota(jnp.int32, shape, 0)
        col = lax.broadcasted_iota(jnp.int32, shape, 1)
        owner = col // rows
        own = col - owner * rows - place * own_rows
        hit = (own >= 0) & (own < own_rows) & (owner * own_rows + own == row)
        return hit.astype(F32).astype(BF)

    def thin(self, number):
        names, rows = self.kinds[number]
        return sum(2 * self.lay.padded[name] for name in names), self.lay.count * rows


RIGHT_CHUNK = 384
STARTS = {"qkv": QKV_AT, "up": UP_AT, "out": OUT_AT, "down": DOWN_AT, "pos": POS_AT}


WIDE_AT = {"qkv": 0, "out": 3 * D, "up": 4 * D}


def packed_place(packed, name):
    if name in WIDE_AT:
        return packed[0], WIDE_AT[name]
    return packed[1 if name == "down" else 2], 0


def hand_out_kernel(lay, index_ref, small, *refs):
    packed, small_out = refs[:3], refs[3]
    outs = [dict(zip(NAMES, refs[4 + 5 * i : 9 + 5 * i])) for i in range(5)]
    at = index_ref[0] * lay.small_len
    row, shift = at // LANES, at % LANES
    lane = lax.broadcasted_iota(jnp.int32, (1, LANES), 1)
    for start in range(0, lay.small_len, LANES):
        near, far = (
            pltpu.roll(small[pl.ds(row + start // LANES + i, 1), :], LANES - shift, 1)
            for i in range(2)
        )
        take = min(LANES, lay.small_len - start)
        line = jnp.where(lane < LANES - shift, near, far)
        small_out[:, start : start + take] = line[:, :take]
    for name in NAMES:
        source, at = packed_place(packed, name)
        for kind in range(4):
            value = source[kind, : lay.rows[name], at : at + WIDTH[name]]
            outs[kind][name][...] = value
            if kind == 3:
                outs[4][name][...] = value.astype(BF)


def hand_out(lay, index, small, packed):
    shapes = [(lay.rows[n], WIDTH[n]) for n in NAMES]
    return pl.pallas_call(
        functools.partial(hand_out_kernel, lay),
        out_shape=(jax.ShapeDtypeStruct((1, lay.small_len), F32),)
        + tuple(jax.ShapeDtypeStruct(s, F32) for s in shapes * 4)
        + tuple(jax.ShapeDtypeStruct(s, BF) for s in shapes),
        in_specs=[pl.BlockSpec(memory_space=pltpu.SMEM)] + [vmem()] * 4,
        out_specs=tuple([vmem()] * 26),
        name="hand_out",
    )(index, small, *packed)


def tail_kernel(roles, sizes, lay, groups, extra, full_hbm, small, bases_hbm, *refs):
    rights_hbm, lefts, masters, firsts, seconds = (
        dict(zip(NAMES, refs[5 * i : 5 * i + 5])) for i in range(5)
    )
    small_out = refs[25]
    packed = refs[26:29]
    rest = refs[29:]

    def keep(kind, name, cols, value):
        target, at = packed_place(packed, name)
        target[kind, : value.shape[0], at + cols.start : at + cols.stop] = value

    full, acc, out_c, in_c, out_p, in_p, out_z, in_z, s_out, s_in = rest[:10]
    flat, steps, bases, coarse = rest[10:14]
    rights = dict(zip(NAMES, rest[14:19]))
    picks = dict(zip(NAMES, rest[19:24]))
    thins = rest[24 : 24 + len(groups.kinds)]
    send_sems, recv_sems, full_sems, base_sem, right_sems = rest[24 + len(groups.kinds) :]
    grid = Grid(roles, sizes)
    wire = Wire(grid, send_sems, recv_sems)
    me = grid.slot()

    plane = lay.count // grid.size("z")

    def full_copy(b):
        at = pl.multiple_of(flipped(grid.coord["z"], b, grid.size("z")) * plane, plane)
        part = pl.ds(at, plane)
        return pltpu.make_async_copy(full_hbm.at[part], full.at[part], full_sems.at[b])

    for b in [*grid.offsets("z")][::-1] + [0]:
        full_copy(b).start()
    base_copy = pltpu.make_async_copy(bases_hbm, bases, base_sem)
    base_copy.start()

    chunks = [(name, at) for name in NAMES for at in range(0, WIDTH[name], RIGHT_CHUNK)]

    def right_copy(number):
        name, at = chunks[number]
        return pltpu.make_async_copy(
            rights_hbm[name].at[pl.ds(at, RIGHT_CHUNK), :],
            coarse.at[number % 2, :, pl.ds(0, WIDTH[name])],
            right_sems.at[number],
        )

    right_copy(0).start()
    right_copy(1).start()

    def round_right(number):
        name, at = chunks[number]
        right_copy(number).wait()
        rights[name][at : at + RIGHT_CHUNK, :] = coarse[number % 2, :, : WIDTH[name]].astype(BF)
        if number + 2 < len(chunks):
            right_copy(number + 2).start()

    def make_pick(name):
        height, rows, padded = HEIGHT[name], lay.rows[name], lay.padded[name]
        row = lax.broadcasted_iota(jnp.int32, (padded, height), 0)
        col = lax.broadcasted_iota(jnp.int32, (padded, height), 1)
        pick = ((row < rows) & (col == me * rows + row)).astype(F32).astype(BF)
        base_rows, base_cols = lay.base_place(name)
        base = bases[:, base_rows, base_cols]
        left_rows = nt(pick, base.reshape(base.shape[0] * base.shape[1], height)).astype(BF)
        if rows != padded:
            left_rows = nt(left_rows, lay.spread(name)).astype(BF)
        picks[name][:padded, :] = left_rows
        picks[name][padded:, :] = pick

    def make_thin(number):
        names, rows = groups.kinds[number]
        at = 0
        for place, name in enumerate(names):
            padded = lay.padded[name]
            left = split(pad_rows(lefts[name][...], padded))
            if len(names) > 1 or rows != lay.rows[name]:
                left = nn(left, groups.spread(name, rows, place)).astype(BF)
            thins[number][at : at + 2 * padded, :] = left
            at += 2 * padded

    duties = [functools.partial(round_right, i) for i in range(len(chunks))]
    duties += [base_copy.wait]
    duties += [functools.partial(make_pick, name) for name in NAMES]
    duties += [functools.partial(make_thin, i) for i in range(len(groups.kinds))]

    def idle():
        if duties:
            duties.pop(0)()

    meet(grid)
    total, smalls = reduce_scatter(
        grid, wire, full, small, acc, out_c, in_c, out_p, in_p, out_z, in_z, s_out, s_in, extra,
        lambda b: full_copy(b).wait(), idle,
    )
    small_out[:SMALL_ROWS, :] = smalls
    small_out[SMALL_ROWS:, :] = jnp.zeros((40 - SMALL_ROWS, LANES), F32)
    flat[me] = total.astype(BF)
    gather_all(grid, wire, flat, "flat", idle)
    while duties:
        idle()

    def flat_block(block):
        height = flat.shape[1]
        pieces, at = [], block * D
        while at < (block + 1) * D:
            slot, row = at // height, at % height
            take = min((block + 1) * D - at, height - row)
            pieces.append(flat[slot, row : row + take, :])
            at += take
        return pieces[0] if len(pieces) == 1 else jnp.concatenate(pieces, axis=0)

    directions = {}
    for name in NAMES:
        height, width = HEIGHT[name], WIDTH[name]
        rows, padded = lay.rows[name], lay.padded[name]
        lhs = picks[name][...]
        if name in ("down", "pos"):
            both = None
            for block in range(height // LANES):
                part = nt(
                    lhs[:, block * LANES : (block + 1) * LANES], flat_block(STARTS[name] + block)
                )
                both = part if both is None else both + part
        else:
            both = jnp.concatenate(
                [nn(lhs, flat_block(STARTS[name] + i)) for i in range(width // LANES)], axis=1
            )
        keep(0, name, slice(0, width), both[padded : padded + rows])
        terms = split(both[:padded])
        for at in range(0, width, D):
            cols = slice(at, at + D)
            rotated = joined(nn(terms, rights[name][:, cols]))[:rows]
            first = DECAY * firsts[name][:, cols] + (1.0 - DECAY) * rotated
            second = DECAY * seconds[name][:, cols] + (1.0 - DECAY) * rotated * rotated
            keep(1, name, cols, first)
            keep(2, name, cols, second)
            direction = first / (jnp.sqrt(second) + ADAM_EPSILON)
            for i in range(D // LANES):
                directions[name, at // LANES + i] = direction[:, i * LANES : (i + 1) * LANES]
    for number, group in enumerate(groups.members):
        piece = jnp.concatenate([directions[member] for member in group], axis=0)
        steps[me, groups.span(number), :] = pad_rows(piece, groups.rows[number]).astype(BF)

    gather_all(grid, wire, steps, "steps")

    partway = {}
    for number, group in enumerate(groups.members):
        rows = groups.rows[number]
        piece = steps[:, groups.span(number), :].reshape(lay.count * rows, LANES)
        whole = nn(thins[groups.kind_of[number]][...], piece)
        at = 0
        for name, block in group:
            padded = lay.padded[name]
            partway[name, block] = joined(whole[at : at + 2 * padded])
            at += 2 * padded
    for name in NAMES:
        height, width = HEIGHT[name], WIDTH[name]
        terms = split(
            jnp.concatenate([partway[name, i] for i in range(width // LANES)], axis=1)
        )
        rate = height ** (-0.5)
        for at in range(0, width, D):
            cols = slice(at, at + D)
            update = joined(nt(terms, rights[name][cols, :]))[: lay.rows[name]]
            master = masters[name][:, cols] * (1.0 - rate * WEIGHT_DECAY) - rate * update
            keep(3, name, cols, master)
    wire.finish()


def finish_step(roles, sizes, lay, full, small, bases, rights, lefts, masters, firsts, seconds):
    slots, rows, _ = full.shape
    nz, ny, nx, nc = (roles[role][2] for role in ("z", "y", "x", "c"))
    count = reduce_copies(roles) + small_copies(roles) + 2 * gather_copies(roles)
    extra = {}
    for role in ("c", "y", "x", "z"):
        for offset in range(1, roles[role][2]):
            extra[(role, offset)] = len(extra)
    groups = Groups(lay)
    chunks = sum(WIDTH[name] // RIGHT_CHUNK for name in NAMES)
    anywhere = pl.BlockSpec(memory_space=pl.ANY)
    return pl.pallas_call(
        functools.partial(tail_kernel, roles, sizes, lay, groups, extra),
        out_shape=(
            jax.ShapeDtypeStruct((40, LANES), F32),
            jax.ShapeDtypeStruct((4, lay.padded["qkv"], 5 * D + 3 * D), F32),
            jax.ShapeDtypeStruct((4, lay.padded["down"], D), F32),
            jax.ShapeDtypeStruct((4, lay.padded["pos"], D), F32),
        ),
        in_specs=[anywhere, vmem(), anywhere] + [anywhere] * 5 + [vmem()] * 20,
        out_specs=tuple([vmem()] * 4),
        scratch_shapes=[
            pltpu.VMEM((slots, rows, LANES), F32),
            pltpu.VMEM((rows, LANES), F32),
            pltpu.VMEM((nc - 1, nz, ny, nx, rows, LANES), BF),
            pltpu.VMEM((nc - 1, nz, ny, nx, rows, LANES), BF),
            pltpu.VMEM((nz, ny, nx, rows, LANES), BF),
            pltpu.VMEM((nz, ny, nx, rows, LANES), BF),
            pltpu.VMEM((nz - 1, rows, LANES), BF),
            pltpu.VMEM((nz - 1, rows, LANES), BF),
            pltpu.VMEM((4, SMALL_ROWS, LANES), F32),
            pltpu.VMEM((len(extra), SMALL_ROWS, LANES), F32),
            pltpu.VMEM((slots, rows, LANES), BF),
            pltpu.VMEM((slots, groups.total, LANES), BF),
            pltpu.VMEM(bases.shape, BF),
            pltpu.VMEM((2, RIGHT_CHUNK, FF), F32),
        ]
        + [pltpu.VMEM((WIDTH[name], WIDTH[name]), BF) for name in NAMES]
        + [pltpu.VMEM((2 * lay.padded[name], HEIGHT[name]), BF) for name in NAMES]
        + [pltpu.VMEM(groups.thin(i), BF) for i in range(len(groups.kinds))]
        + [
            pltpu.SemaphoreType.DMA((count,)),
            pltpu.SemaphoreType.DMA((count,)),
            pltpu.SemaphoreType.DMA((nz,)),
            pltpu.SemaphoreType.DMA,
            pltpu.SemaphoreType.DMA((chunks,)),
        ],
        compiler_params=pltpu.CompilerParams(
            collective_id=1, has_side_effects=True, vmem_limit_bytes=VMEM_LIMIT
        ),
        name="finish_step",
    )(full, small, bases, *rights, *lefts, *masters, *firsts, *seconds)


AXES = ("dp", "fsdp")


def on_device(roles, sizes, tokens, centres, lengths, cotangent, smalls, *matrices):
    masters, firsts, seconds, lefts, rights = (matrices[5 * i : 5 * i + 5] for i in range(5))
    count = sizes["dp"] * sizes["fsdp"]
    heads = Layout(count, True)
    lay = Layout(count, False)
    *weights, small_rows, bases = gather_weights(roles, sizes, heads, masters, smalls, lefts)
    w_qkv, w_out, w_up, w_down, w_pos = weights
    whole_bases = lax.all_gather(bases, AXES, axis=0, tiled=True)
    layer_out, grad_tokens, full, small_grads = layer_pass(
        tokens, centres, lengths, cotangent, small_rows, w_qkv, w_out, w_up, w_down, w_pos
    )
    small_total, *packed = finish_step(
        roles,
        sizes,
        lay,
        full.reshape(count, FLAT_ROWS // count, LANES),
        small_grads,
        whole_bases.reshape(count, heads.base_rows, FF),
        rights,
        lefts,
        masters,
        firsts,
        seconds,
    )
    me = lax.axis_index("dp") * sizes["fsdp"] + lax.axis_index("fsdp")
    grad_smalls, *finished = hand_out(heads, me.reshape(1), small_total, packed)
    return (layer_out, grad_tokens, grad_smalls.reshape(heads.small_len), *finished)


def solution(mesh):
    sizes = {axis: mesh.shape[axis] for axis in AXES}
    rows, flat = P(AXES, None), P(AXES)
    return jax.shard_map(
        functools.partial(on_device, mesh_roles(mesh), sizes),
        mesh=mesh,
        in_specs=(rows, P(None, AXES), flat, rows, flat) + (rows,) * 20 + (P(),) * 5,
        out_specs=(rows, rows, flat) + (rows,) * 25,
        check_vma=False,
    )
```

```python
import functools
import jax
import jax.numpy as jnp
from jax import lax
from jax.experimental import pallas as pl
from jax.experimental.pallas import tpu as pltpu
from jax.sharding import PartitionSpec as P

D = 384
HEADS = 6
HEAD = 64
FF = 1536
PH = 128
LMAX = 256
LANES = 128
EPSILON = 1e-05
NEG_FILL = -1e30
HIGHEST = lax.Precision.HIGHEST
BF = jnp.bfloat16
F32 = jnp.float32

QKV_AT, UP_AT, OUT_AT, DOWN_AT, POS_AT, BLOCKS = 0, 9, 21, 24, 36, 37
FLAT_ROWS = 14336
SMALL_ROWS = 37


def nn(a, b):
    return jnp.dot(a, b, preferred_element_type=F32)


def nt(a, b):
    return lax.dot_general(a, b, (((1,), (1,)), ((), ())), preferred_element_type=F32)


def tn(a, b):
    return lax.dot_general(a, b, (((0,), (0,)), ((), ())), preferred_element_type=F32)


INV_SQRT2 = 0.7071067811865476
INV_SQRT_2PI = 0.3989422804014327


def gelu_pair(x):
    cdf = 0.5 * (1.0 + lax.erf(x * INV_SQRT2))
    pdf = jnp.exp(-0.5 * x * x) * INV_SQRT_2PI
    return x * cdf, cdf + x * pdf


def norm_parts(x):
    mean = jnp.mean(x, axis=-1, keepdims=True)
    centred = x - mean
    spread = jnp.mean(centred * centred, axis=-1, keepdims=True)
    inv = lax.rsqrt(spread + EPSILON)
    return centred * inv, inv


def col8(x):
    rows, cols = x.shape
    return jnp.sum(x.reshape(rows // 8, 8, cols), axis=0)


def layer_kernel(
    len_ref,
    tok_ref,
    cen_ref,
    cot_ref,
    small_ref,
    wqkv_ref,
    wout_ref,
    wup_ref,
    wdown_ref,
    wpos_ref,
    out_ref,
    gtok_ref,
    grad_ref,
    sgrad_ref,
    sacc,
    posh_s,
    emb_s,
    xh1_s,
    n1_s,
    qkv_s,
    p_s,
    att_s,
    bin_s,
    n2g_s,
    ff_s,
    qg_s,
    wide_s,
    ds_s,
    dq_s,
    ag_s,
    *,
    fc,
    group,
):
    step = pl.program_id(0)
    last = pl.num_programs(0) - 1

    @pl.when(step == 0)
    def _():
        grad_ref[...] = jnp.zeros_like(grad_ref)
        sacc[...] = jnp.zeros_like(sacc)

    rows = group * LMAX
    lengths = [len_ref[step * group + i] for i in range(group)]

    def live(width):
        return jnp.concatenate(
            [lax.broadcasted_iota(jnp.int32, (LMAX, width), 0) < length for length in lengths], axis=0
        )

    def vec(at, blocks):
        return jnp.concatenate([small_ref[at + i : at + i + 1, :] for i in range(blocks)], axis=1)

    def add_small(at, value):
        cols = value.shape[1]
        sacc[:, at * LANES : at * LANES + cols] += value

    def add_grad(block, value):
        for i in range(value.shape[1] // LANES):
            rows = slice((block + i) * D, (block + i + 1) * D)
            grad_ref[rows, :] += value[:, i * LANES : (i + 1) * LANES]

    gain_one, shift_one, gain_two, shift_two, attn_bias, down_bias, embed_bias = (
        vec(3 * i, 3) for i in range(7)
    )
    hidden_bias = small_ref[33:34, :]
    pos_first = small_ref[34:37, :]
    cen = cen_ref[...]

    pos_hidden = (
        lax.dot_general(
            cen, pos_first, (((0,), (0,)), ((), ())), precision=HIGHEST, preferred_element_type=F32
        )
        + hidden_bias
    )
    pos_act, pos_slope = gelu_pair(pos_hidden)
    pos_low = pos_act.astype(BF)
    posh_s[...] = pos_slope
    embedded = tok_ref[...].astype(F32) + nn(pos_low, wpos_ref[...]) + embed_bias
    emb_s[...] = embedded
    xhat_one, inv_one = norm_parts(embedded)
    xh1_s[...] = xhat_one
    n1 = (xhat_one * gain_one + shift_one).astype(BF)
    n1_s[...] = n1
    qkv_s[...] = nn(n1, wqkv_ref[...]).astype(BF)

    lane = lax.broadcasted_iota(jnp.int32, (1, LANES), 1)
    halves = [(lane < HEAD).astype(F32).astype(BF), (lane >= HEAD).astype(F32).astype(BF)]
    scale = HEAD ** (-0.5)
    scaled = [(h.astype(F32) * scale).astype(BF) for h in halves]

    key_live = [
        lax.broadcasted_iota(jnp.int32, (LMAX, LMAX), 0) < length for length in lengths
    ]
    spans = [slice(i * LMAX, (i + 1) * LMAX) for i in range(group)]

    heads = [(i, head) for head in range(HEADS) for i in range(group)]

    def lanes_of(which, i, head):
        at = which * D + head // 2 * LANES
        return qkv_s[spans[i], at : at + LANES]

    def staged(*stages):
        for turn in range(len(heads) + len(stages) - 1):
            for lag, stage in enumerate(stages):
                if 0 <= turn - lag < len(heads):
                    stage(turn - lag, *heads[turn - lag])

    def scores(number, i, head):
        wide_s[number % 3] = nt(lanes_of(1, i, head), lanes_of(0, i, head) * scaled[head % 2])

    def soften(number, i, head):
        s = jnp.where(key_live[i], wide_s[number % 3], NEG_FILL)
        e = jnp.exp(s - jnp.max(s, axis=0, keepdims=True))
        p_s[i * HEADS + head] = (e * (1.0 / jnp.sum(e, axis=0, keepdims=True))).astype(BF)

    def attend(number, i, head):
        at = head % 2 * HEAD
        o_t = nn(lanes_of(2, i, head).T[at : at + HEAD, :], p_s[i * HEADS + head])
        att_s[head * HEAD : (head + 1) * HEAD, spans[i]] = o_t.astype(BF)

    staged(scores, soften, attend)

    branch_in = emb_s[...] + tn(att_s[...], wout_ref[...]) + attn_bias
    bin_s[...] = branch_in
    xhat_two, inv_two = norm_parts(branch_in)
    n2 = (xhat_two * gain_two + shift_two).astype(BF)
    n2_t = n2.T
    gy = jnp.where(live(D), cot_ref[...].astype(F32), 0.0)
    gy_low = gy.astype(BF)
    gy_t = gy_low.T
    add_small(15, col8(gy))

    for c in range(FF // fc):
        cols = slice(c * fc, (c + 1) * fc)
        up_bias = vec(21 + c * (fc // LANES), fc // LANES)
        hidden = nn(n2, wup_ref[:, cols]) + up_bias
        act, slope = gelu_pair(hidden)
        act_low = act.astype(BF)
        part = nn(act_low, wdown_ref[cols, :])
        act_grad = nt(gy_low, wdown_ref[cols, :])
        hg = (act_grad * slope).astype(BF)
        add_small(21 + c * (fc // LANES), col8(hg.astype(F32)))
        back = nt(hg, wup_ref[:, cols])
        if c == 0:
            ff_s[...] = part
            n2g_s[...] = back
        else:
            ff_s[...] += part
            n2g_s[...] += back
        add_grad(UP_AT + c * (fc // LANES), nn(n2_t, hg))
        add_grad(DOWN_AT + c * (fc // LANES), nn(gy_t, act_low))

    out_ref[...] = (bin_s[...] + ff_s[...] + down_bias).astype(BF)

    n2g = n2g_s[...]
    add_small(6, col8(n2g * xhat_two))
    add_small(9, col8(n2g))
    u = n2g * gain_two
    bg = gy + inv_two * (
        u
        - jnp.mean(u, axis=-1, keepdims=True)
        - xhat_two * jnp.mean(u * xhat_two, axis=-1, keepdims=True)
    )
    bin_s[...] = bg
    add_small(12, col8(bg))
    bg_low = bg.astype(BF)
    add_grad(OUT_AT, nn(att_s[...], bg_low))
    ag = nt(bg_low, wout_ref[...]).astype(BF)

    ag_s[...] = ag
    dk, dv = {}, {}

    def ago_of(i, head):
        at = head // 2 * LANES
        return ag_s[spans[i], at : at + LANES] * halves[head % 2]

    def probs_back(number, i, head):
        wide_s[number % 3] = nt(lanes_of(2, i, head), ago_of(i, head))

    def scores_back(number, i, head):
        p = p_s[i * HEADS + head].astype(F32)
        dp = wide_s[number % 3]
        rd = jnp.sum(p * dp, axis=0, keepdims=True)
        ds_s[number % 2] = (p * (dp - rd)).astype(BF)

    def heads_back(number, i, head):
        ds = ds_s[number % 2]
        at = head % 2 * HEAD
        dv[i, head] = nn(p_s[i * HEADS + head], ago_of(i, head))
        dk[i, head] = nn(ds, lanes_of(0, i, head) * scaled[head % 2])
        dq_t = nn(lanes_of(1, i, head).T[at : at + HEAD, :], ds) * scale
        dq_s[head * HEAD : (head + 1) * HEAD, spans[i]] = dq_t.astype(BF)
        if head % 2:
            at = head // 2 * LANES
            qg_s[spans[i], at : at + LANES] = dq_s[at : at + LANES, spans[i]].T
            for which, terms in ((1, dk), (2, dv)):
                total = terms.pop((i, head - 1)) + terms.pop((i, head))
                qg_s[spans[i], which * D + at : which * D + at + LANES] = total.astype(BF)

    staged(probs_back, scores_back, heads_back)

    qg = qg_s[...]
    add_grad(QKV_AT, nn(n1_s[...].T, qg))
    n1g = nt(qg, wqkv_ref[...])
    xhat = xh1_s[...]
    add_small(0, col8(n1g * xhat))
    add_small(3, col8(n1g))
    u = n1g * gain_one
    eg = bin_s[...] + inv_one * (
        u
        - jnp.mean(u, axis=-1, keepdims=True)
        - xhat * jnp.mean(u * xhat, axis=-1, keepdims=True)
    )
    add_small(18, col8(eg))
    eg_low = eg.astype(BF)
    gtok_ref[...] = eg_low
    add_grad(POS_AT, tn(eg_low, pos_low))
    phg = nt(eg_low, wpos_ref[...]) * posh_s[...]
    add_small(33, col8(phg))
    pf_grad = jnp.dot(cen, phg, precision=HIGHEST, preferred_element_type=F32)
    for i in range(3):
        sacc[0:1, (34 + i) * LANES : (35 + i) * LANES] += pf_grad[i : i + 1, :]

    @pl.when(step == last)
    def _():
        for i in range(SMALL_ROWS):
            sgrad_ref[i : i + 1, :] = jnp.sum(
                sacc[:, i * LANES : (i + 1) * LANES], axis=0, keepdims=True
            )


def layer_pass(tokens, centres, lengths, cotangent, small_rows, wqkv, wout, wup, wdown, wpos, fc=768, group=2):
    clouds = lengths.shape[0]
    rows = clouds * LMAX
    span = group * LMAX
    whole = lambda shape: pl.BlockSpec(shape, lambda i, *_: (0, 0), pipeline_mode=pl.Buffered(1))
    tile = lambda: pl.BlockSpec((span, D), lambda i, *_: (i, 0))
    return pl.pallas_call(
        functools.partial(layer_kernel, fc=fc, group=group),
        out_shape=(
            jax.ShapeDtypeStruct((rows, D), BF),
            jax.ShapeDtypeStruct((rows, D), BF),
            jax.ShapeDtypeStruct((FLAT_ROWS, LANES), F32),
            jax.ShapeDtypeStruct((SMALL_ROWS, LANES), F32),
        ),
        grid_spec=pltpu.PrefetchScalarGridSpec(
            num_scalar_prefetch=1,
            grid=(clouds // group,),
            in_specs=[
                tile(),
                pl.BlockSpec((3, span), lambda i, *_: (0, i)),
                tile(),
                whole((SMALL_ROWS, LANES)),
                whole((D, 3 * D)),
                whole((D, D)),
                whole((D, FF)),
                whole((FF, D)),
                whole((PH, D)),
            ],
            out_specs=[
                tile(),
                tile(),
                whole((FLAT_ROWS, LANES)),
                whole((SMALL_ROWS, LANES)),
            ],
            scratch_shapes=[
                pltpu.VMEM((8, SMALL_ROWS * LANES), F32),
                pltpu.VMEM((span, PH), F32),
                pltpu.VMEM((span, D), F32),
                pltpu.VMEM((span, D), F32),
                pltpu.VMEM((span, D), BF),
                pltpu.VMEM((span, 3 * D), BF),
                pltpu.VMEM((group * HEADS, LMAX, LMAX), BF),
                pltpu.VMEM((D, span), BF),
                pltpu.VMEM((span, D), F32),
                pltpu.VMEM((span, D), F32),
                pltpu.VMEM((span, D), F32),
                pltpu.VMEM((span, 3 * D), BF),
                pltpu.VMEM((3, LMAX, LMAX), F32),
                pltpu.VMEM((2, LMAX, LMAX), BF),
                pltpu.VMEM((D, span), BF),
                pltpu.VMEM((span, D), BF),
            ],
        ),
        compiler_params=pltpu.CompilerParams(vmem_limit_bytes=60 * 1024 * 1024),
        name="layer",
    )(lengths, tokens, centres, cotangent, small_rows, wqkv, wout, wup, wdown, wpos)


MESH_ID = pl.DeviceIdType.MESH


def mesh_roles(mesh):
    dp, fs = mesh.shape["dp"], mesh.shape["fsdp"]
    if dp >= 32:
        return {
            "z": ("dp", dp // 4 // 2, 4) if dp == 32 else ("dp", 8, dp // 8),
            "y": ("dp", 2, 4),
            "c": ("dp", 1, 2),
            "x": ("fsdp", 1, fs),
        }
    return {
        "z": ("dp", 2, dp // 2),
        "y": ("dp", 1, 2),
        "x": ("fsdp", 2, fs // 2),
        "c": ("fsdp", 1, 2),
    }


def flipped(coord, offset, size):
    if offset == 0:
        return coord
    if size == 2:
        return 1 - coord
    return {1: coord + 1 - 2 * (coord % 2), 2: (coord + 2) % 4, 3: 3 - coord}[offset]


class Grid:
    def __init__(self, roles, sizes):
        self.roles, self.sizes = roles, sizes
        self.index = {axis: lax.axis_index(axis) for axis in sizes}
        self.coord = {
            role: (self.index[axis] // stride) % size
            for role, (axis, stride, size) in roles.items()
        }

        z = self.z = self.coord["z"]
        self.line = [z] + [self.by_z(*row) for row in ((1, 0, 1, 2), (2, 2, 3, 1), (3, 3, 0, 0))]
        self.came_by = [self.by_z(*row) for row in ((1, 0, 1, 2), (1, 2, 3, 2), (1, 2, 1, 2))]
        self.inbox = [self.by_z(*row) for row in ((1, 0, 0, 0), (3, 1, 1, 2), (4, 3, 2, 4))]
        self.inner = z // 2 + z % 2 == 1

    def by_z(self, *values):
        high, low = self.coord["z"] // 2, self.coord["z"] % 2
        return (1 - high) * ((1 - low) * values[0] + low * values[1]) + high * (
            (1 - low) * values[2] + low * values[3]
        )

    def at_z(self, coordinate):
        axis, stride, _ = self.roles["z"]
        return {**self.index, axis: self.index[axis] + (coordinate - self.z) * stride}

    def place(self, line=0, **offsets):
        at = self.at_z(self.line[line]) if line else dict(self.index)
        for role, offset in offsets.items():
            axis, stride, size = self.roles[role]
            other = flipped(self.coord[role], offset, size)
            at[axis] = at[axis] + (other - self.coord[role]) * stride
        return at

    def slot(self, **offsets):
        at = self.place(**offsets)
        return at["dp"] * self.sizes["fsdp"] + at["fsdp"]

    def size(self, role):
        return self.roles[role][2]

    def offsets(self, role):
        return range(1, self.size(role))


class Wire:
    def __init__(self, grid, send_sems, recv_sems):
        self.grid, self.send_sems, self.recv_sems = grid, send_sems, recv_sems
        self.count = 0
        self.copies = {}

    def reserve(self, count):
        self.count += count
        return self.count - count

    def make(self, number, into, source, target, place):
        return pltpu.make_async_remote_copy(
            src_ref=source,
            dst_ref=target,
            send_sem=self.send_sems.at[number],
            recv_sem=self.recv_sems.at[into],
            device_id=place,
            device_id_type=MESH_ID,
        )

    def send_to(self, key, number, into, source, target, place, when=None):
        make = functools.partial(self.make, number, into, source, target, place)
        if when is None:
            make().start()
        else:
            pl.when(when)(lambda: make().start())
        assert key not in self.copies
        self.copies[key] = (make, when)

    def send(self, key, source, target, **offsets):
        number = self.reserve(1)
        self.send_to(key, number, number, source, target, self.grid.place(**offsets))

    def arrived(self, key):
        self.copies[key][0]().wait_recv()

    def arrived_at(self, number, target):
        self.make(number, number, target, target, self.grid.place(c=1)).wait_recv()

    def finish(self):
        for make, when in self.copies.values():
            if when is None:
                make().wait_send()
            else:
                pl.when(when)(lambda make=make: make().wait_send())


def meet(grid):
    barrier = pltpu.get_barrier_semaphore()
    count = 0
    for role in ("z", "y", "x", "c"):
        for offset in grid.offsets(role):
            pl.semaphore_signal(
                barrier,
                inc=1,
                device_id=grid.place(**{role: offset}),
                device_id_type=MESH_ID,
            )
            count += 1
    pl.semaphore_wait(barrier, count)


def gather_copies(roles):
    nz, ny, nx, nc = (roles[role][2] for role in ("z", "y", "x", "c"))
    plane = (ny - 1) + (nx - 1) + 2 * (ny - 1) * (nx - 1)
    core = (nc - 1) * (1 + plane)
    return 5 + nz * (plane + core)


def nothing():
    pass


def gather_all(grid, wire, buf, tag, rows=None):
    start, rows = (0, buf.shape[1]) if rows is None else rows
    half = rows // 32 * 16
    parts = {
        None: pl.ds(start, rows),
        "a": pl.ds(start, half),
        "b": pl.ds(start + half, rows - half),
    }

    def pass_on(key, slot, part, **offsets):
        ref = buf.at[slot, parts[part]]
        wire.send((tag,) + key, ref, ref, **offsets)

    def arrived(*key):
        wire.arrived((tag,) + key)

    ys, xs, cs = ([*grid.offsets(role)] for role in ("y", "x", "c"))

    def to_core(key, slot, part=None):
        for c in cs:
            pass_on(("c", c) + key, slot, part, c=c)

    def have(b):
        slot = grid.slot(line=b)
        for y in ys:
            pass_on(("y", b, y), slot, None, y=y)
        for x in xs:
            pass_on(("x", b, x), slot, None, x=x)
        to_core((b, 0, 0, 0), slot)

    def relay(b):
        for y in ys:
            yield
            arrived("y", b, y)
            for x in xs:
                pass_on(("a", b, y, x), grid.slot(line=b, y=y), "a", x=x)
            to_core((b, y, 0, 0), grid.slot(line=b, y=y))
        for x in xs:
            yield
            arrived("x", b, x)
            for y in ys:
                pass_on(("b", b, y, x), grid.slot(line=b, x=x), "b", y=y)
            to_core((b, 0, x, 0), grid.slot(line=b, x=x))

    base = wire.reserve(5)
    z = grid.z

    def along(site, line, target, into, when):
        ref = buf.at[grid.slot(line=line), parts[None]]
        place = grid.at_z(target)
        wire.send_to((tag, "z", site), base + site, base + into, ref, ref, place, when)

    along(0, 0, z + 1, 0, z < 3)
    along(1, 0, z - 1, z // 2, z > 0)
    have(0)
    onward = ((z + 1, 3 - z), (z - 1, z), (3 * (z - 1), 2))
    for b in (1, 2, 3):
        yield
        wire.arrived_at(base + b - 1, buf.at[grid.slot(line=b), parts[None]])
        along(1 + b, b, *onward[b - 1], grid.inner)
        have(b)
        yield from relay(b - 1)
    yield from relay(3)
    for b in range(4):
        for y in ys:
            for x in xs:
                for part in ("a", "b"):
                    yield
                    arrived(part, b, y, x)
                    to_core((b, y, x, part), grid.slot(line=b, y=y, x=x), part)
    yield
    for key in list(wire.copies):
        if key[:2] == (tag, "c"):
            wire.arrived(key)


def together(*chains, idle=nothing):
    chains = list(chains)
    while chains:
        for chain in list(chains):
            try:
                next(chain)
            except StopIteration:
                chains.remove(chain)
        idle()


def reduce_copies(roles):
    nz, ny, nx, nc = (roles[role][2] for role in ("z", "y", "x", "c"))
    plane = (ny - 1) + (nx - 1) + 2 * (ny - 1) * (nx - 1)
    return (nc - 1) * nz * ny * nx + nz * plane + 5


def small_copies(roles):
    return sum(roles[role][2] - 1 for role in ("z", "y", "x", "c"))


def reduce_small(grid, wire, small, s_out, s_in, numbers, result):
    value = small[...]
    for stage, role in enumerate(("c", "y", "x", "z")):
        s_out[stage] = value
        for offset in grid.offsets(role):
            number = numbers[role, offset]
            wire.send(("s", role, offset), s_out.at[stage], s_in.at[number], **{role: offset})
        yield
        for offset in grid.offsets(role):
            wire.arrived(("s", role, offset))
            value = value + s_in[numbers[role, offset]]
    result[: value.shape[0], :] = value


def reduce_scatter(grid, wire, tag, take, out_c, in_c, out_p, in_p, out_z, in_z, acc, ready, done):
    rows = acc.shape[0]
    half = rows // 32 * 16
    first, second = pl.ds(0, half), pl.ds(half, rows - half)
    ys, xs, cs = ([*grid.offsets(role)] for role in ("y", "x", "c"))
    order = [3, 2, 1, 0]
    base = wire.reserve(5)

    def send(key, source, target, **offsets):
        wire.send((tag,) + key, source, target, **offsets)

    def arrived(*key):
        wire.arrived((tag,) + key)

    def core_sum(b, y, x):
        value = take(grid.slot(line=b, y=y, x=x))
        for c in cs:
            arrived("c", c, b, y, x)
            value = value + in_c[c - 1, b, y, x].astype(F32)
        return value

    def to_core(b):
        ready(b)
        for y in [*ys, 0]:
            for x in [*xs, 0]:
                for c in cs:
                    out_c[c - 1, b, y, x] = take(grid.slot(line=b, y=y, x=x, c=c)).astype(BF)
                    send(("c", c, b, y, x), out_c.at[c - 1, b, y, x], in_c.at[c - 1, b, y, x], c=c)

    def diagonal(b):
        for y in ys:
            for x in xs:
                out_p[b, y, x] = core_sum(b, y, x).astype(BF)
                send(("a", b, y, x), out_p.at[b, y, x, first], in_p.at[b, y, x, first], x=x)
                send(("b", b, y, x), out_p.at[b, y, x, second], in_p.at[b, y, x, second], y=y)

    def neighbour(b):
        for y in ys:
            acc[...] = core_sum(b, y, 0)
            for x in xs:
                arrived("a", b, y, x)
                acc[first, :] += in_p[b, y, x, first].astype(F32)
            out_p[b, y, 0] = acc[...].astype(BF)
            send(("y", b, y), out_p.at[b, y, 0], in_p.at[b, y, 0], y=y)
        for x in xs:
            acc[...] = core_sum(b, 0, x)
            for y in ys:
                arrived("b", b, y, x)
                acc[second, :] += in_p[b, y, x, second].astype(F32)
            out_p[b, 0, x] = acc[...].astype(BF)
            send(("x", b, x), out_p.at[b, 0, x], in_p.at[b, 0, x], x=x)

    def plane_sum(b):
        value = core_sum(b, 0, 0)
        for y in ys:
            arrived("y", b, y)
            value = value + in_p[b, y, 0].astype(F32)
        for x in xs:
            arrived("x", b, x)
            value = value + in_p[b, 0, x].astype(F32)
        return value

    def add_from(inbox):
        wire.arrived_at(base + inbox, in_z.at[inbox])
        acc[...] += in_z[inbox].astype(F32)

    for b in order:
        to_core(b)
        yield
    for turn in range(len(order) + 2):
        if turn < len(order):
            yield
            diagonal(order[turn])
        if 1 <= turn <= len(order):
            yield
            neighbour(order[turn - 1])
        if turn >= 2:
            yield
            b = order[turn - 2]
            acc[...] = plane_sum(b)
            if b:
                yield
                pl.when(grid.inner)(functools.partial(add_from, 1 + b))
                out_z[b - 1] = acc[...].astype(BF)
                inbox = grid.inbox[b - 1]
                wire.send_to(
                    (tag, "z", b), base + b - 1, base + inbox, out_z.at[b - 1], in_z.at[inbox],
                    grid.at_z(grid.came_by[b - 1]),
                )
    yield
    pl.when(grid.z < 3)(functools.partial(add_from, 0))
    pl.when(grid.z > 0)(functools.partial(add_from, 1))
    done(acc[...])


DECAY = 0.5
ADAM_EPSILON = 1e-08
WEIGHT_DECAY = 0.05
VMEM_LIMIT = 60 * 1024 * 1024
NAMES = ("qkv", "out", "up", "down", "pos")
HEIGHT = {"qkv": D, "out": D, "up": D, "down": FF, "pos": PH}
WIDTH = {"qkv": 3 * D, "out": D, "up": FF, "down": D, "pos": D}
SMALLS = SMALL_ROWS * LANES


def pad16(rows):
    return -(-rows // 16) * 16


class Layout:
    def __init__(self, count, smalls):
        self.count = count
        self.rows = {name: HEIGHT[name] // count for name in NAMES}
        self.padded = {name: pad16(self.rows[name]) for name in NAMES}
        self.start = {}
        at = 0
        for name in NAMES:
            self.start[name] = at
            at += self.padded[name] * (WIDTH[name] // LANES)
        self.small_at = at
        self.small_len = SMALLS // count
        if smalls:
            at += 16
        self.total = at

    @property
    def base_rows(self):
        return self.padded["down"] + 16

    def base_place(self, name):
        if name == "down":
            return slice(0, self.padded["down"]), slice(0, FF)
        at = {"qkv": 0, "out": D, "up": 2 * D, "pos": 3 * D}[name]
        return slice(self.padded["down"], self.base_rows), slice(at, at + HEIGHT[name])

    def span(self, name, block):
        at = self.start[name] + block * self.padded[name]
        return slice(at, at + self.padded[name])

    def spread(self, name):
        rows, padded = self.rows[name], self.padded[name]
        shape = (HEIGHT[name], self.count * padded)
        row = lax.broadcasted_iota(jnp.int32, shape, 0)
        col = lax.broadcasted_iota(jnp.int32, shape, 1)
        own, owner = col % padded, col // padded
        hit = (own < rows) & (owner * rows + own == row)
        return hit.astype(F32).astype(BF)


def pad_rows(value, rows):
    have = value.shape[0]
    if have == rows:
        return value
    return jnp.concatenate([value, jnp.zeros((rows - have, value.shape[1]), value.dtype)], axis=0)


def once(action):
    pending = [action]

    def run():
        if pending:
            pending.pop()()

    return run


def head_kernel(roles, sizes, lay, *refs):
    masters = dict(zip(NAMES, refs[:5]))
    small_ref = refs[5]
    lefts = dict(zip(NAMES, refs[6:11]))
    outs = dict(zip(NAMES, refs[11:16]))
    flat_ref, bases, buf, send_sems, recv_sems = refs[16:]
    grid = Grid(roles, sizes)
    wire = Wire(grid, send_sems, recv_sems)
    own = grid.slot()
    for name in NAMES:
        for block in range(WIDTH[name] // LANES):
            piece = masters[name][:, block * LANES : (block + 1) * LANES]
            buf[own, lay.span(name, block), :] = pad_rows(piece, lay.padded[name]).astype(BF)
    lines = []
    for at in range(0, lay.small_len, LANES):
        line = small_ref[:, at : min(at + LANES, lay.small_len)]
        if line.shape[1] < LANES:
            line = jnp.concatenate([line, jnp.zeros((1, LANES - line.shape[1]), F32)], axis=1)
        lines.append(line)
    lines = jnp.concatenate(lines, axis=0)
    buf[own, lay.small_at : lay.small_at + 16, :] = pad_rows(lines, 16).astype(BF)

    def pack_bases():
        bases[lay.padded["down"] :, :] = jnp.zeros((16, FF), BF)
        for name in NAMES:
            rows, cols = lay.base_place(name)
            bases[rows, cols] = pad_rows(lefts[name][...], rows.stop - rows.start).astype(BF)

    meet(grid)
    together(gather_all(grid, wire, buf, "w"), idle=once(pack_bases))
    for name in NAMES:
        spread = None if lay.rows[name] == lay.padded[name] else lay.spread(name)
        for block in range(WIDTH[name] // LANES):
            piece = buf[:, lay.span(name, block), :].reshape(lay.count * lay.padded[name], LANES)
            if spread is not None:
                piece = nn(spread, piece).astype(BF)
            outs[name][:, block * LANES : (block + 1) * LANES] = piece
    lane = lax.broadcasted_iota(jnp.int32, (1, LANES), 1)
    for row in range(SMALL_ROWS):
        line = jnp.zeros((1, LANES), F32)
        at = row * LANES
        while at < (row + 1) * LANES:
            owner, place = at // lay.small_len, at % lay.small_len
            source_row, source_lane = place // LANES, place % LANES
            take = min(
                (row + 1) * LANES - at, lay.small_len - place, LANES - source_lane
            )
            target = at - row * LANES
            piece = buf[owner, lay.small_at : lay.small_at + 16, :].astype(F32)
            piece = piece[source_row : source_row + 1, :]
            shift = (target - source_lane) % LANES
            if shift:
                piece = pltpu.roll(piece, shift, 1)
            line = jnp.where((lane >= target) & (lane < target + take), piece, line)
            at += take
        flat_ref[row : row + 1, :] = line
    wire.finish()


def vmem():
    return pl.BlockSpec(memory_space=pltpu.VMEM)


def gather_weights(roles, sizes, lay, masters, smalls, lefts):
    count = gather_copies(roles)
    return pl.pallas_call(
        functools.partial(head_kernel, roles, sizes, lay),
        out_shape=tuple(jax.ShapeDtypeStruct((HEIGHT[n], WIDTH[n]), BF) for n in NAMES)
        + (
            jax.ShapeDtypeStruct((SMALL_ROWS, LANES), F32),
            jax.ShapeDtypeStruct((lay.base_rows, FF), BF),
        ),
        in_specs=[vmem()] * 11,
        out_specs=tuple([vmem()] * 7),
        scratch_shapes=[
            pltpu.VMEM((lay.count, lay.total, LANES), BF),
            pltpu.SemaphoreType.DMA((count,)),
            pltpu.SemaphoreType.DMA((count,)),
        ],
        compiler_params=pltpu.CompilerParams(
            collective_id=0, has_side_effects=True, vmem_limit_bytes=VMEM_LIMIT
        ),
        name="gather_weights",
    )(*masters, smalls.reshape(1, lay.small_len), *lefts)


def split(value):
    high = value.astype(BF)
    return jnp.concatenate([high, (value - high.astype(F32)).astype(BF)], axis=0)


def joined(value):
    half = value.shape[0] // 2
    return value[:half] + value[half:]


class Groups:
    def __init__(self, lay):
        self.lay = lay
        wide = [(name, i) for name in ("qkv", "out", "up") for i in range(WIDTH[name] // LANES)]
        self.members = [wide[i : i + 4] for i in range(0, len(wide), 4)]
        self.members += [[("down", i)] for i in range(WIDTH["down"] // LANES)]
        self.members += [[("pos", i) for i in range(WIDTH["pos"] // LANES)]]
        self.rows = [pad16(sum(lay.rows[name] for name, _ in group)) for group in self.members]
        self.starts = [sum(self.rows[:i]) for i in range(len(self.rows))]
        self.total = sum(self.rows)
        self.kinds = []
        self.kind_of = []
        for group, rows in zip(self.members, self.rows):
            kind = (tuple(name for name, _ in group), rows)
            if kind not in self.kinds:
                self.kinds.append(kind)
            self.kind_of.append(self.kinds.index(kind))

    def span(self, number):
        return slice(self.starts[number], self.starts[number] + self.rows[number])

    def spread(self, name, rows, place):
        own_rows = self.lay.rows[name]
        shape = (HEIGHT[name], self.lay.count * rows)
        row = lax.broadcasted_iota(jnp.int32, shape, 0)
        col = lax.broadcasted_iota(jnp.int32, shape, 1)
        owner = col // rows
        own = col - owner * rows - place * own_rows
        hit = (own >= 0) & (own < own_rows) & (owner * own_rows + own == row)
        return hit.astype(F32).astype(BF)

    def thin(self, number):
        names, rows = self.kinds[number]
        return sum(2 * self.lay.padded[name] for name in names), self.lay.count * rows


RIGHT_CHUNK = 384
STARTS = {"qkv": QKV_AT, "up": UP_AT, "out": OUT_AT, "down": DOWN_AT, "pos": POS_AT}


WIDE_AT = {"qkv": 0, "out": 3 * D, "up": 4 * D}


def packed_place(packed, name):
    if name in WIDE_AT:
        return packed[0], WIDE_AT[name]
    return packed[1 if name == "down" else 2], 0


def hand_out_kernel(lay, index_ref, small, *refs):
    packed, small_out = refs[:3], refs[3]
    outs = [dict(zip(NAMES, refs[4 + 5 * i : 9 + 5 * i])) for i in range(5)]
    at = index_ref[0] * lay.small_len
    row, shift = at // LANES, at % LANES
    lane = lax.broadcasted_iota(jnp.int32, (1, LANES), 1)
    for start in range(0, lay.small_len, LANES):
        near, far = (
            pltpu.roll(small[pl.ds(row + start // LANES + i, 1), :], LANES - shift, 1)
            for i in range(2)
        )
        take = min(LANES, lay.small_len - start)
        line = jnp.where(lane < LANES - shift, near, far)
        small_out[:, start : start + take] = line[:, :take]
    for name in NAMES:
        source, at = packed_place(packed, name)
        for kind in range(4):
            value = source[kind, : lay.rows[name], at : at + WIDTH[name]]
            outs[kind][name][...] = value
            if kind == 3:
                outs[4][name][...] = value.astype(BF)


def hand_out(lay, index, small, packed):
    shapes = [(lay.rows[n], WIDTH[n]) for n in NAMES]
    return pl.pallas_call(
        functools.partial(hand_out_kernel, lay),
        out_shape=(jax.ShapeDtypeStruct((1, lay.small_len), F32),)
        + tuple(jax.ShapeDtypeStruct(s, F32) for s in shapes * 4)
        + tuple(jax.ShapeDtypeStruct(s, BF) for s in shapes),
        in_specs=[pl.BlockSpec(memory_space=pltpu.SMEM)] + [vmem()] * 4,
        out_specs=tuple([vmem()] * 26),
        name="hand_out",
    )(index, small, *packed)


def tail_kernel(roles, sizes, lay, groups, extra, full_hbm, small, bases_hbm, *refs):
    rights_hbm, lefts, masters, firsts, seconds = (
        dict(zip(NAMES, refs[5 * i : 5 * i + 5])) for i in range(5)
    )
    small_out = refs[25]
    packed = refs[26:29]
    rest = refs[29:]

    def keep(kind, name, cols, value):
        target, at = packed_place(packed, name)
        target[kind, : value.shape[0], at + cols.start : at + cols.stop] = value

    full, acc, out_c, in_c, out_p, in_p, out_z, in_z, s_out, s_in = rest[:10]
    flat, steps, bases, coarse = rest[10:14]
    rights = dict(zip(NAMES, rest[14:19]))
    picks = dict(zip(NAMES, rest[19:24]))
    thins = rest[24 : 24 + len(groups.kinds)]
    send_sems, recv_sems, full_sems, base_sem, right_sems = rest[24 + len(groups.kinds) :]
    grid = Grid(roles, sizes)
    wire = Wire(grid, send_sems, recv_sems)
    me = grid.slot()

    plane = lay.count // grid.size("z")

    def full_copy(b):
        at = pl.multiple_of(grid.line[b] * plane, plane)
        part = pl.ds(at, plane)
        return pltpu.make_async_copy(full_hbm.at[part], full.at[part], full_sems.at[b])

    for b in (3, 2, 1, 0):
        full_copy(b).start()
    base_copy = pltpu.make_async_copy(bases_hbm, bases, base_sem)
    base_copy.start()

    chunks = [(name, at) for name in NAMES for at in range(0, WIDTH[name], RIGHT_CHUNK)]

    def right_copy(number):
        name, at = chunks[number]
        return pltpu.make_async_copy(
            rights_hbm[name].at[pl.ds(at, RIGHT_CHUNK), :],
            coarse.at[number % 2, :, pl.ds(0, WIDTH[name])],
            right_sems.at[number],
        )

    right_copy(0).start()
    right_copy(1).start()

    def round_right(number):
        name, at = chunks[number]
        right_copy(number).wait()
        rights[name][at : at + RIGHT_CHUNK, :] = coarse[number % 2, :, : WIDTH[name]].astype(BF)
        if number + 2 < len(chunks):
            right_copy(number + 2).start()

    def make_pick(name):
        height, rows, padded = HEIGHT[name], lay.rows[name], lay.padded[name]
        row = lax.broadcasted_iota(jnp.int32, (padded, height), 0)
        col = lax.broadcasted_iota(jnp.int32, (padded, height), 1)
        pick = ((row < rows) & (col == me * rows + row)).astype(F32).astype(BF)
        base_rows, base_cols = lay.base_place(name)
        base = bases[:, base_rows, base_cols]
        left_rows = nt(pick, base.reshape(base.shape[0] * base.shape[1], height)).astype(BF)
        if rows != padded:
            left_rows = nt(left_rows, lay.spread(name)).astype(BF)
        picks[name][:padded, :] = left_rows
        picks[name][padded:, :] = pick

    def make_thin(number):
        names, rows = groups.kinds[number]
        at = 0
        for place, name in enumerate(names):
            padded = lay.padded[name]
            left = split(pad_rows(lefts[name][...], padded))
            if len(names) > 1 or rows != lay.rows[name]:
                left = nn(left, groups.spread(name, rows, place)).astype(BF)
            thins[number][at : at + 2 * padded, :] = left
            at += 2 * padded

    duties = [functools.partial(round_right, i) for i in range(len(chunks))]
    duties += [base_copy.wait]
    duties += [functools.partial(make_pick, name) for name in NAMES]
    duties += [functools.partial(make_thin, i) for i in range(len(groups.kinds))]

    def idle():
        if duties:
            duties.pop(0)()

    meet(grid)
    small_out[...] = jnp.zeros_like(small_out)

    def share():
        def done(total):
            flat[me] = total.astype(BF)

        yield from reduce_scatter(
            grid, wire, "sum", lambda slot: full[slot], out_c, in_c, out_p, in_p, out_z, in_z, acc,
            lambda b: full_copy(b).wait(), done,
        )
        yield from gather_all(grid, wire, flat, "flat")

    together(
        share(), reduce_small(grid, wire, small, s_out, s_in, extra, small_out), idle=idle
    )
    while duties:
        idle()

    def flat_block(block):
        height = flat.shape[1]
        pieces, at = [], block * D
        while at < (block + 1) * D:
            slot, row = at // height, at % height
            take = min((block + 1) * D - at, height - row)
            pieces.append(flat[slot, row : row + take, :])
            at += take
        return pieces[0] if len(pieces) == 1 else jnp.concatenate(pieces, axis=0)

    directions = {}
    for name in NAMES:
        height, width = HEIGHT[name], WIDTH[name]
        rows, padded = lay.rows[name], lay.padded[name]
        lhs = picks[name][...]
        if name in ("down", "pos"):
            both = None
            for block in range(height // LANES):
                part = nt(
                    lhs[:, block * LANES : (block + 1) * LANES], flat_block(STARTS[name] + block)
                )
                both = part if both is None else both + part
        else:
            both = jnp.concatenate(
                [nn(lhs, flat_block(STARTS[name] + i)) for i in range(width // LANES)], axis=1
            )
        keep(0, name, slice(0, width), both[padded : padded + rows])
        terms = split(both[:padded])
        for at in range(0, width, D):
            cols = slice(at, at + D)
            rotated = joined(nn(terms, rights[name][:, cols]))[:rows]
            first = DECAY * firsts[name][:, cols] + (1.0 - DECAY) * rotated
            second = DECAY * seconds[name][:, cols] + (1.0 - DECAY) * rotated * rotated
            keep(1, name, cols, first)
            keep(2, name, cols, second)
            direction = first / (jnp.sqrt(second) + ADAM_EPSILON)
            for i in range(D // LANES):
                directions[name, at // LANES + i] = direction[:, i * LANES : (i + 1) * LANES]
    for number, group in enumerate(groups.members):
        piece = jnp.concatenate([directions[member] for member in group], axis=0)
        steps[me, groups.span(number), :] = pad_rows(piece, groups.rows[number]).astype(BF)

    together(gather_all(grid, wire, steps, "steps"))

    partway = {}
    for number, group in enumerate(groups.members):
        rows = groups.rows[number]
        piece = steps[:, groups.span(number), :].reshape(lay.count * rows, LANES)
        whole = nn(thins[groups.kind_of[number]][...], piece)
        at = 0
        for name, block in group:
            padded = lay.padded[name]
            partway[name, block] = joined(whole[at : at + 2 * padded])
            at += 2 * padded
    for name in NAMES:
        height, width = HEIGHT[name], WIDTH[name]
        terms = split(
            jnp.concatenate([partway[name, i] for i in range(width // LANES)], axis=1)
        )
        rate = height ** (-0.5)
        for at in range(0, width, D):
            cols = slice(at, at + D)
            update = joined(nt(terms, rights[name][cols, :]))[: lay.rows[name]]
            master = masters[name][:, cols] * (1.0 - rate * WEIGHT_DECAY) - rate * update
            keep(3, name, cols, master)
    wire.finish()


def finish_step(roles, sizes, lay, full, small, bases, rights, lefts, masters, firsts, seconds):
    slots, rows, _ = full.shape
    nz, ny, nx, nc = (roles[role][2] for role in ("z", "y", "x", "c"))
    count = reduce_copies(roles) + small_copies(roles) + 2 * gather_copies(roles)
    extra = {}
    for role in ("c", "y", "x", "z"):
        for offset in range(1, roles[role][2]):
            extra[(role, offset)] = len(extra)
    groups = Groups(lay)
    chunks = sum(WIDTH[name] // RIGHT_CHUNK for name in NAMES)
    anywhere = pl.BlockSpec(memory_space=pl.ANY)
    return pl.pallas_call(
        functools.partial(tail_kernel, roles, sizes, lay, groups, extra),
        out_shape=(
            jax.ShapeDtypeStruct((40, LANES), F32),
            jax.ShapeDtypeStruct((4, lay.padded["qkv"], 5 * D + 3 * D), F32),
            jax.ShapeDtypeStruct((4, lay.padded["down"], D), F32),
            jax.ShapeDtypeStruct((4, lay.padded["pos"], D), F32),
        ),
        in_specs=[anywhere, vmem(), anywhere] + [anywhere] * 5 + [vmem()] * 20,
        out_specs=tuple([vmem()] * 4),
        scratch_shapes=[
            pltpu.VMEM((slots, rows, LANES), F32),
            pltpu.VMEM((rows, LANES), F32),
            pltpu.VMEM((nc - 1, nz, ny, nx, rows, LANES), BF),
            pltpu.VMEM((nc - 1, nz, ny, nx, rows, LANES), BF),
            pltpu.VMEM((nz, ny, nx, rows, LANES), BF),
            pltpu.VMEM((nz, ny, nx, rows, LANES), BF),
            pltpu.VMEM((nz - 1, rows, LANES), BF),
            pltpu.VMEM((5, rows, LANES), BF),
            pltpu.VMEM((4, SMALL_ROWS, LANES), F32),
            pltpu.VMEM((len(extra), SMALL_ROWS, LANES), F32),
            pltpu.VMEM((slots, rows, LANES), BF),
            pltpu.VMEM((slots, groups.total, LANES), BF),
            pltpu.VMEM(bases.shape, BF),
            pltpu.VMEM((2, RIGHT_CHUNK, FF), F32),
        ]
        + [pltpu.VMEM((WIDTH[name], WIDTH[name]), BF) for name in NAMES]
        + [pltpu.VMEM((2 * lay.padded[name], HEIGHT[name]), BF) for name in NAMES]
        + [pltpu.VMEM(groups.thin(i), BF) for i in range(len(groups.kinds))]
        + [
            pltpu.SemaphoreType.DMA((count,)),
            pltpu.SemaphoreType.DMA((count,)),
            pltpu.SemaphoreType.DMA((nz,)),
            pltpu.SemaphoreType.DMA,
            pltpu.SemaphoreType.DMA((chunks,)),
        ],
        compiler_params=pltpu.CompilerParams(
            collective_id=1, has_side_effects=True, vmem_limit_bytes=VMEM_LIMIT
        ),
        name="finish_step",
    )(full, small, bases, *rights, *lefts, *masters, *firsts, *seconds)


AXES = ("dp", "fsdp")


def on_device(roles, sizes, tokens, centres, lengths, cotangent, smalls, *matrices):
    masters, firsts, seconds, lefts, rights = (matrices[5 * i : 5 * i + 5] for i in range(5))
    count = sizes["dp"] * sizes["fsdp"]
    heads = Layout(count, True)
    lay = Layout(count, False)
    *weights, small_rows, bases = gather_weights(roles, sizes, heads, masters, smalls, lefts)
    w_qkv, w_out, w_up, w_down, w_pos = weights
    whole_bases = lax.all_gather(bases, AXES, axis=0, tiled=True)
    layer_out, grad_tokens, full, small_grads = layer_pass(
        tokens, centres, lengths, cotangent, small_rows, w_qkv, w_out, w_up, w_down, w_pos
    )
    small_total, *packed = finish_step(
        roles,
        sizes,
        lay,
        full.reshape(count, FLAT_ROWS // count, LANES),
        small_grads,
        whole_bases.reshape(count, heads.base_rows, FF),
        rights,
        lefts,
        masters,
        firsts,
        seconds,
    )
    me = lax.axis_index("dp") * sizes["fsdp"] + lax.axis_index("fsdp")
    grad_smalls, *finished = hand_out(heads, me.reshape(1), small_total, packed)
    return (layer_out, grad_tokens, grad_smalls.reshape(heads.small_len), *finished)


def solution(mesh):
    sizes = {axis: mesh.shape[axis] for axis in AXES}
    rows, flat = P(AXES, None), P(AXES)
    return jax.shard_map(
        functools.partial(on_device, mesh_roles(mesh), sizes),
        mesh=mesh,
        in_specs=(rows, P(None, AXES), flat, rows, flat) + (rows,) * 20 + (P(),) * 5,
        out_specs=(rows, rows, flat) + (rows,) * 25,
        check_vma=False,
    )
```

```python
import functools
import jax
import jax.numpy as jnp
from jax import lax
from jax.experimental import pallas as pl
from jax.experimental.pallas import tpu as pltpu
from jax.sharding import PartitionSpec as P

D = 384
HEADS = 6
HEAD = 64
FF = 1536
PH = 128
LMAX = 256
LANES = 128
EPSILON = 1e-05
NEG_FILL = -1e30
HIGHEST = lax.Precision.HIGHEST
BF = jnp.bfloat16
F32 = jnp.float32

QKV_AT, UP_AT, OUT_AT, DOWN_AT, POS_AT, BLOCKS = 0, 9, 21, 24, 36, 37
FLAT_ROWS = 14336
SMALL_ROWS = 37


def nn(a, b):
    return jnp.dot(a, b, preferred_element_type=F32)


def nt(a, b):
    return lax.dot_general(a, b, (((1,), (1,)), ((), ())), preferred_element_type=F32)


def tn(a, b):
    return lax.dot_general(a, b, (((0,), (0,)), ((), ())), preferred_element_type=F32)


INV_SQRT2 = 0.7071067811865476
INV_SQRT_2PI = 0.3989422804014327


def gelu_pair(x):
    cdf = 0.5 * (1.0 + lax.erf(x * INV_SQRT2))
    pdf = jnp.exp(-0.5 * x * x) * INV_SQRT_2PI
    return x * cdf, cdf + x * pdf


def norm_parts(x):
    mean = jnp.mean(x, axis=-1, keepdims=True)
    centred = x - mean
    spread = jnp.mean(centred * centred, axis=-1, keepdims=True)
    inv = lax.rsqrt(spread + EPSILON)
    return centred * inv, inv


def thirds(value):
    terms = []
    for _ in range(3):
        term = value.astype(BF)
        terms.append(term)
        value = value - term.astype(F32)
    return terms


def col8(x):
    rows, cols = x.shape
    return jnp.sum(x.reshape(rows // 8, 8, cols), axis=0)


def layer_kernel(
    len_ref,
    tok_ref,
    cen_ref,
    cot_ref,
    small_ref,
    wqkv_ref,
    wout_ref,
    wup_ref,
    wdown_ref,
    wpos_ref,
    out_ref,
    gtok_ref,
    grad_ref,
    sgrad_ref,
    sacc,
    posh_s,
    emb_s,
    xh1_s,
    n1_s,
    qkv_s,
    p_s,
    att_s,
    bin_s,
    n2g_s,
    ff_s,
    qg_s,
    wide_s,
    ds_s,
    dq_s,
    ag_s,
    hid_s,
    act_s,
    low_s,
    hg_s,
    inv_s,
    xh2_s,
    gy_s,
    bgl_s,
    *,
    fc,
    group,
):
    step = pl.program_id(0)
    last = pl.num_programs(0) - 1

    @pl.when(step == 0)
    def _():
        grad_ref[...] = jnp.zeros_like(grad_ref)
        sacc[...] = jnp.zeros_like(sacc)

    rows = group * LMAX
    lengths = [len_ref[step * group + i] for i in range(group)]

    def live(width):
        return jnp.concatenate(
            [lax.broadcasted_iota(jnp.int32, (LMAX, width), 0) < length for length in lengths], axis=0
        )

    def vec(at, blocks):
        return jnp.concatenate([small_ref[at + i : at + i + 1, :] for i in range(blocks)], axis=1)

    def add_small(at, value):
        cols = value.shape[1]
        sacc[:, at * LANES : at * LANES + cols] += value

    def add_grad(block, value):
        for i in range(value.shape[1] // LANES):
            rows = slice((block + i) * D, (block + i + 1) * D)
            grad_ref[rows, :] += value[:, i * LANES : (i + 1) * LANES]

    gain_one, shift_one, gain_two, shift_two, attn_bias, down_bias, embed_bias = (
        vec(3 * i, 3) for i in range(7)
    )
    hidden_bias = small_ref[33:34, :]
    pos_first = small_ref[34:37, :]
    cen = cen_ref[...]

    cen_terms = jnp.concatenate(thirds(cen) + [jnp.zeros((7, rows), BF)], axis=0)
    first_terms = jnp.concatenate(
        [pos_first.astype(BF)] * 3 + [jnp.zeros((7, PH), BF)], axis=0
    )
    pos_hidden = tn(cen_terms, first_terms) + hidden_bias
    pos_act, pos_slope = gelu_pair(pos_hidden)
    pos_low = pos_act.astype(BF)
    posh_s[...] = pos_slope
    embedded = tok_ref[...].astype(F32) + nn(pos_low, wpos_ref[...]) + embed_bias
    emb_s[...] = embedded
    xhat_one, inv_one = norm_parts(embedded)
    xh1_s[...] = xhat_one
    n1 = (xhat_one * gain_one + shift_one).astype(BF)
    n1_s[...] = n1
    qkv_s[...] = nn(n1, wqkv_ref[...]).astype(BF)

    lane = lax.broadcasted_iota(jnp.int32, (1, LANES), 1)
    halves = [(lane < HEAD).astype(F32).astype(BF), (lane >= HEAD).astype(F32).astype(BF)]
    scale = HEAD ** (-0.5)
    scaled = [(h.astype(F32) * scale).astype(BF) for h in halves]

    key_live = [
        lax.broadcasted_iota(jnp.int32, (LMAX, LMAX), 0) < length for length in lengths
    ]
    spans = [slice(i * LMAX, (i + 1) * LMAX) for i in range(group)]

    heads = [(i, head) for head in range(HEADS) for i in range(group)]

    def lanes_of(which, i, head):
        at = which * D + head // 2 * LANES
        return qkv_s[spans[i], at : at + LANES]

    def staged(*stages):
        for turn in range(len(heads) + len(stages) - 1):
            for lag, stage in enumerate(stages):
                if 0 <= turn - lag < len(heads):
                    stage(turn - lag, *heads[turn - lag])

    def scores(number, i, head):
        wide_s[number % 3] = nt(lanes_of(1, i, head), lanes_of(0, i, head) * scaled[head % 2])

    def soften(number, i, head):
        s = jnp.where(key_live[i], wide_s[number % 3], NEG_FILL)
        e = jnp.exp(s - jnp.max(s, axis=0, keepdims=True))
        p_s[i * HEADS + head] = (e * (1.0 / jnp.sum(e, axis=0, keepdims=True))).astype(BF)

    def attend(number, i, head):
        at = head % 2 * HEAD
        o_t = nn(lanes_of(2, i, head).T[at : at + HEAD, :], p_s[i * HEADS + head])
        att_s[head * HEAD : (head + 1) * HEAD, spans[i]] = o_t.astype(BF)

    staged(scores, soften, attend)

    branch_in = emb_s[...] + tn(att_s[...], wout_ref[...]) + attn_bias
    bin_s[...] = branch_in
    xhat_two, inv_two = norm_parts(branch_in)
    xh2_s[...] = xhat_two
    n2 = (xhat_two * gain_two + shift_two).astype(BF)
    n2_t = n2.T
    gy = jnp.where(live(D), cot_ref[...].astype(F32), 0.0)
    gy_s[...] = gy
    gy_low = gy.astype(BF)
    gy_t = gy_low.T
    add_small(15, col8(gy))

    blocks = fc // LANES

    def widen(c):
        cols = slice(c * fc, (c + 1) * fc)
        hid_s[c % 2] = nn(n2, wup_ref[:, cols])
        act_s[c % 2] = nt(gy_low, wdown_ref[cols, :])

    def bend(c):
        cols = slice(c * fc, (c + 1) * fc)
        act, slope = gelu_pair(hid_s[c % 2] + vec(21 + c * blocks, blocks))
        low_s[:, cols] = act.astype(BF)
        hg = (act_s[c % 2] * slope).astype(BF)
        hg_s[:, cols] = hg
        add_small(21 + c * blocks, col8(hg.astype(F32)))

    def narrow(c):
        cols = slice(c * fc, (c + 1) * fc)
        add_grad(UP_AT + c * blocks, nn(n2_t, hg_s[:, cols]))
        add_grad(DOWN_AT + c * blocks, nn(gy_t, low_s[:, cols]))

    count = FF // fc
    for turn in range(count + 1):
        for lag, stage in enumerate((widen, bend)):
            if 0 <= turn - lag < count:
                stage(turn - lag)
    n2g_s[...] = nt(hg_s[...], wup_ref[...])
    ff_s[...] = nn(low_s[...], wdown_ref[...])

    out_ref[...] = (bin_s[...] + ff_s[...] + down_bias).astype(BF)

    inv_s[...] = inv_two
    parts = count
    height = rows // parts if rows % (16 * parts) == 0 else rows // 4
    for turn in range(max(count, rows // height)):
        if turn < rows // height:
            at = slice(turn * height, (turn + 1) * height)
            n2g = n2g_s[at, :]
            xhat_two = xh2_s[at, :]
            add_small(6, col8(n2g * xhat_two))
            add_small(9, col8(n2g))
            u = n2g * gain_two
            bg = gy_s[at, :] + inv_s[at, :] * (
                u
                - jnp.mean(u, axis=-1, keepdims=True)
                - xhat_two * jnp.mean(u * xhat_two, axis=-1, keepdims=True)
            )
            bin_s[at, :] = bg
            add_small(12, col8(bg))
            bgl_s[at, :] = bg.astype(BF)
        if turn < count:
            narrow(turn)
    bg_low = bgl_s[...]
    add_grad(OUT_AT, nn(att_s[...], bg_low))
    ag = nt(bg_low, wout_ref[...]).astype(BF)

    ag_s[...] = ag
    dk, dv = {}, {}

    def ago_of(i, head):
        at = head // 2 * LANES
        return ag_s[spans[i], at : at + LANES] * halves[head % 2]

    def probs_back(number, i, head):
        wide_s[number % 3] = nt(lanes_of(2, i, head), ago_of(i, head))

    def scores_back(number, i, head):
        p = p_s[i * HEADS + head].astype(F32)
        dp = wide_s[number % 3]
        rd = jnp.sum(p * dp, axis=0, keepdims=True)
        ds_s[number % 2] = (p * (dp - rd)).astype(BF)

    def heads_back(number, i, head):
        ds = ds_s[number % 2]
        at = head % 2 * HEAD
        dv[i, head] = nn(p_s[i * HEADS + head], ago_of(i, head))
        dk[i, head] = nn(ds, lanes_of(0, i, head) * scaled[head % 2])
        dq_t = nn(lanes_of(1, i, head).T[at : at + HEAD, :], ds) * scale
        dq_s[head * HEAD : (head + 1) * HEAD, spans[i]] = dq_t.astype(BF)
        if head % 2:
            at = head // 2 * LANES
            qg_s[spans[i], at : at + LANES] = dq_s[at : at + LANES, spans[i]].T
            for which, terms in ((1, dk), (2, dv)):
                total = terms.pop((i, head - 1)) + terms.pop((i, head))
                qg_s[spans[i], which * D + at : which * D + at + LANES] = total.astype(BF)

    staged(probs_back, scores_back, heads_back)

    qg = qg_s[...]
    n2g_s[...] = nt(qg, wqkv_ref[...])
    inv_s[...] = inv_one
    n1_t = n1_s[...].T
    height = rows // 4
    for turn in range(4):
        at = slice(turn * height, (turn + 1) * height)
        n1g = n2g_s[at, :]
        xhat = xh1_s[at, :]
        add_small(0, col8(n1g * xhat))
        add_small(3, col8(n1g))
        u = n1g * gain_one
        eg = bin_s[at, :] + inv_s[at, :] * (
            u
            - jnp.mean(u, axis=-1, keepdims=True)
            - xhat * jnp.mean(u * xhat, axis=-1, keepdims=True)
        )
        add_small(18, col8(eg))
        gtok_ref[at, :] = eg.astype(BF)
        if turn < 3:
            add_grad(QKV_AT + 3 * turn, nn(n1_t, qg_s[:, turn * D : (turn + 1) * D]))
    eg_low = gtok_ref[...]
    add_grad(POS_AT, tn(eg_low, pos_low))
    phg = nt(eg_low, wpos_ref[...]) * posh_s[...]
    add_small(33, col8(phg))
    products = nn(cen_terms, jnp.concatenate(thirds(phg), axis=1))
    pf_grad = products[:, :PH] + products[:, PH : 2 * PH] + products[:, 2 * PH :]
    for i in range(3):
        sacc[0:1, (34 + i) * LANES : (35 + i) * LANES] += (
            pf_grad[i : i + 1, :] + pf_grad[i + 3 : i + 4, :] + pf_grad[i + 6 : i + 7, :]
        )

    @pl.when(step == last)
    def _():
        for i in range(SMALL_ROWS):
            sgrad_ref[i : i + 1, :] = jnp.sum(
                sacc[:, i * LANES : (i + 1) * LANES], axis=0, keepdims=True
            )


def layer_pass(tokens, centres, lengths, cotangent, small_rows, wqkv, wout, wup, wdown, wpos, fc=256, group=2):
    clouds = lengths.shape[0]
    rows = clouds * LMAX
    span = group * LMAX
    whole = lambda shape: pl.BlockSpec(shape, lambda i, *_: (0, 0), pipeline_mode=pl.Buffered(1))
    tile = lambda: pl.BlockSpec((span, D), lambda i, *_: (i, 0))
    return pl.pallas_call(
        functools.partial(layer_kernel, fc=fc, group=group),
        out_shape=(
            jax.ShapeDtypeStruct((rows, D), BF),
            jax.ShapeDtypeStruct((rows, D), BF),
            jax.ShapeDtypeStruct((FLAT_ROWS, LANES), F32),
            jax.ShapeDtypeStruct((SMALL_ROWS, LANES), F32),
        ),
        grid_spec=pltpu.PrefetchScalarGridSpec(
            num_scalar_prefetch=1,
            grid=(clouds // group,),
            in_specs=[
                tile(),
                pl.BlockSpec((3, span), lambda i, *_: (0, i)),
                tile(),
                whole((SMALL_ROWS, LANES)),
                whole((D, 3 * D)),
                whole((D, D)),
                whole((D, FF)),
                whole((FF, D)),
                whole((PH, D)),
            ],
            out_specs=[
                tile(),
                tile(),
                whole((FLAT_ROWS, LANES)),
                whole((SMALL_ROWS, LANES)),
            ],
            scratch_shapes=[
                pltpu.VMEM((8, SMALL_ROWS * LANES), F32),
                pltpu.VMEM((span, PH), F32),
                pltpu.VMEM((span, D), F32),
                pltpu.VMEM((span, D), F32),
                pltpu.VMEM((span, D), BF),
                pltpu.VMEM((span, 3 * D), BF),
                pltpu.VMEM((group * HEADS, LMAX, LMAX), BF),
                pltpu.VMEM((D, span), BF),
                pltpu.VMEM((span, D), F32),
                pltpu.VMEM((span, D), F32),
                pltpu.VMEM((span, D), F32),
                pltpu.VMEM((span, 3 * D), BF),
                pltpu.VMEM((3, LMAX, LMAX), F32),
                pltpu.VMEM((2, LMAX, LMAX), BF),
                pltpu.VMEM((D, span), BF),
                pltpu.VMEM((span, D), BF),
                pltpu.VMEM((2, span, fc), F32),
                pltpu.VMEM((2, span, fc), F32),
                pltpu.VMEM((span, FF), BF),
                pltpu.VMEM((span, FF), BF),
                pltpu.VMEM((span, 1), F32),
                pltpu.VMEM((span, D), F32),
                pltpu.VMEM((span, D), F32),
                pltpu.VMEM((span, D), BF),
            ],
        ),
        compiler_params=pltpu.CompilerParams(vmem_limit_bytes=60 * 1024 * 1024),
        name="layer",
    )(lengths, tokens, centres, cotangent, small_rows, wqkv, wout, wup, wdown, wpos)


MESH_ID = pl.DeviceIdType.MESH


def mesh_roles(mesh):
    dp, fs = mesh.shape["dp"], mesh.shape["fsdp"]
    if dp >= 32:
        return {
            "z": ("dp", dp // 4 // 2, 4) if dp == 32 else ("dp", 8, dp // 8),
            "y": ("dp", 2, 4),
            "c": ("dp", 1, 2),
            "x": ("fsdp", 1, fs),
        }
    return {
        "z": ("dp", 2, dp // 2),
        "y": ("dp", 1, 2),
        "x": ("fsdp", 2, fs // 2),
        "c": ("fsdp", 1, 2),
    }


def flipped(coord, offset, size):
    if offset == 0:
        return coord
    if size == 2:
        return 1 - coord
    return {1: coord + 1 - 2 * (coord % 2), 2: (coord + 2) % 4, 3: 3 - coord}[offset]


class Grid:
    def __init__(self, roles, sizes):
        self.roles, self.sizes = roles, sizes
        self.index = {axis: lax.axis_index(axis) for axis in sizes}
        self.coord = {
            role: (self.index[axis] // stride) % size
            for role, (axis, stride, size) in roles.items()
        }

        z = self.z = self.coord["z"]
        self.line = [z] + [self.by_z(*row) for row in ((1, 0, 1, 2), (2, 2, 3, 1), (3, 3, 0, 0))]
        self.came_by = [self.by_z(*row) for row in ((1, 0, 1, 2), (1, 2, 3, 2), (1, 2, 1, 2))]
        self.inbox = [self.by_z(*row) for row in ((1, 0, 0, 0), (3, 1, 1, 2), (4, 3, 2, 4))]
        self.inner = z // 2 + z % 2 == 1

    def by_z(self, *values):
        high, low = self.coord["z"] // 2, self.coord["z"] % 2
        return (1 - high) * ((1 - low) * values[0] + low * values[1]) + high * (
            (1 - low) * values[2] + low * values[3]
        )

    def at_z(self, coordinate):
        axis, stride, _ = self.roles["z"]
        return {**self.index, axis: self.index[axis] + (coordinate - self.z) * stride}

    def place(self, line=0, **offsets):
        at = self.at_z(self.line[line]) if line else dict(self.index)
        for role, offset in offsets.items():
            axis, stride, size = self.roles[role]
            other = flipped(self.coord[role], offset, size)
            at[axis] = at[axis] + (other - self.coord[role]) * stride
        return at

    def slot(self, **offsets):
        at = self.place(**offsets)
        return at["dp"] * self.sizes["fsdp"] + at["fsdp"]

    def size(self, role):
        return self.roles[role][2]

    def offsets(self, role):
        return range(1, self.size(role))


class Wire:
    def __init__(self, grid, send_sems, recv_sems):
        self.grid, self.send_sems, self.recv_sems = grid, send_sems, recv_sems
        self.count = 0
        self.copies = {}

    def reserve(self, count):
        self.count += count
        return self.count - count

    def make(self, number, into, source, target, place):
        return pltpu.make_async_remote_copy(
            src_ref=source,
            dst_ref=target,
            send_sem=self.send_sems.at[number],
            recv_sem=self.recv_sems.at[into],
            device_id=place,
            device_id_type=MESH_ID,
        )

    def send_to(self, key, number, into, source, target, place, when=None):
        make = functools.partial(self.make, number, into, source, target, place)
        if when is None:
            make().start()
        else:
            pl.when(when)(lambda: make().start())
        assert key not in self.copies
        self.copies[key] = (make, when)

    def send(self, key, source, target, **offsets):
        number = self.reserve(1)
        self.send_to(key, number, number, source, target, self.grid.place(**offsets))

    def arrived(self, key):
        self.copies[key][0]().wait_recv()

    def arrived_at(self, number, target):
        self.make(number, number, target, target, self.grid.place(c=1)).wait_recv()

    def finish(self):
        for make, when in self.copies.values():
            if when is None:
                make().wait_send()
            else:
                pl.when(when)(lambda make=make: make().wait_send())


def meet(grid):
    barrier = pltpu.get_barrier_semaphore()
    count = 0
    for role in ("z", "y", "x", "c"):
        for offset in grid.offsets(role):
            pl.semaphore_signal(
                barrier,
                inc=1,
                device_id=grid.place(**{role: offset}),
                device_id_type=MESH_ID,
            )
            count += 1
    pl.semaphore_wait(barrier, count)


def gather_copies(roles):
    nz, ny, nx, nc = (roles[role][2] for role in ("z", "y", "x", "c"))
    plane = (ny - 1) + (nx - 1) + 2 * (ny - 1) * (nx - 1)
    core = (nc - 1) * (1 + plane)
    return 5 + nz * (plane + core)


def nothing():
    pass


def gather_all(grid, wire, buf, tag, rows=None):
    start, rows = (0, buf.shape[1]) if rows is None else rows
    half = rows // 32 * 16
    parts = {
        None: pl.ds(start, rows),
        "a": pl.ds(start, half),
        "b": pl.ds(start + half, rows - half),
    }

    def pass_on(key, slot, part, **offsets):
        ref = buf.at[slot, parts[part]]
        wire.send((tag,) + key, ref, ref, **offsets)

    def arrived(*key):
        wire.arrived((tag,) + key)

    ys, xs, cs = ([*grid.offsets(role)] for role in ("y", "x", "c"))

    def to_core(key, slot, part=None):
        for c in cs:
            pass_on(("c", c) + key, slot, part, c=c)

    def have(b):
        slot = grid.slot(line=b)
        for y in ys:
            pass_on(("y", b, y), slot, None, y=y)
        for x in xs:
            pass_on(("x", b, x), slot, None, x=x)
        to_core((b, 0, 0, 0), slot)

    def relay(b):
        for y in ys:
            yield
            arrived("y", b, y)
            for x in xs:
                pass_on(("a", b, y, x), grid.slot(line=b, y=y), "a", x=x)
            to_core((b, y, 0, 0), grid.slot(line=b, y=y))
        for x in xs:
            yield
            arrived("x", b, x)
            for y in ys:
                pass_on(("b", b, y, x), grid.slot(line=b, x=x), "b", y=y)
            to_core((b, 0, x, 0), grid.slot(line=b, x=x))

    base = wire.reserve(5)
    z = grid.z

    def along(site, line, target, into, when):
        ref = buf.at[grid.slot(line=line), parts[None]]
        place = grid.at_z(target)
        wire.send_to((tag, "z", site), base + site, base + into, ref, ref, place, when)

    along(0, 0, z + 1, 0, z < 3)
    along(1, 0, z - 1, z // 2, z > 0)
    have(0)
    onward = ((z + 1, 3 - z), (z - 1, z), (3 * (z - 1), 2))
    for b in (1, 2, 3):
        yield
        wire.arrived_at(base + b - 1, buf.at[grid.slot(line=b), parts[None]])
        along(1 + b, b, *onward[b - 1], grid.inner)
        have(b)
        yield from relay(b - 1)
    yield from relay(3)
    for b in range(4):
        for y in ys:
            for x in xs:
                for part in ("a", "b"):
                    yield
                    arrived(part, b, y, x)
                    to_core((b, y, x, part), grid.slot(line=b, y=y, x=x), part)
    yield
    for key in list(wire.copies):
        if key[:2] == (tag, "c"):
            wire.arrived(key)


def together(*chains, idle=nothing, quiet=0):
    chains = [chain if isinstance(chain, tuple) else (chain, 1) for chain in chains]
    turn = 0
    while chains:
        for chain in list(chains):
            if turn % chain[1] == 0 or len(chains) == 1:
                try:
                    next(chain[0])
                except StopIteration:
                    chains.remove(chain)
        if turn >= quiet:
            idle()
        turn += 1


def exchange_copies(roles):
    return sum(roles[role][2] - 1 for role in ("c", "x", "y", "z"))


def exchange_all(grid, wire, tag, blocks, pack):
    pack()
    for stage, role in enumerate(("c", "x", "y", "z")):
        source, target = blocks[stage], blocks[stage + 1]
        coord, size = grid.coord[role], grid.size(role)
        for offset in grid.offsets(role):
            part = source.at[:, :, :, flipped(coord, offset, size)]
            wire.send((tag, role, offset), part, target.at[offset], **{role: offset})
        target[0] = source[:, :, :, coord]
        yield
        for offset in grid.offsets(role):
            wire.arrived((tag, role, offset))


def reduce_copies(roles):
    nz, ny, nx, nc = (roles[role][2] for role in ("z", "y", "x", "c"))
    plane = (ny - 1) + (nx - 1) + 2 * (ny - 1) * (nx - 1)
    return (nc - 1) * nz * ny * nx + nz * plane + 5


def small_copies(roles):
    return sum(roles[role][2] - 1 for role in ("z", "y", "x", "c"))


def reduce_small(grid, wire, small, s_out, s_in, numbers, result):
    value = small[...]
    for stage, role in enumerate(("c", "y", "x", "z")):
        s_out[stage] = value
        for offset in grid.offsets(role):
            number = numbers[role, offset]
            wire.send(("s", role, offset), s_out.at[stage], s_in.at[number], **{role: offset})
        yield
        for offset in grid.offsets(role):
            wire.arrived(("s", role, offset))
            value = value + s_in[numbers[role, offset]]
    result[: value.shape[0], :] = value


def reduce_scatter(grid, wire, tag, take, out_c, in_c, out_p, in_p, out_z, in_z, acc, ready, done):
    rows = acc.shape[0]
    half = rows // 32 * 16
    first, second = pl.ds(0, half), pl.ds(half, rows - half)
    zs, ys, xs, cs = ([*grid.offsets(role)] for role in ("z", "y", "x", "c"))
    order = zs + [0]

    def send(key, source, target, **offsets):
        wire.send((tag,) + key, source, target, **offsets)

    def arrived(*key):
        wire.arrived((tag,) + key)

    def core_sum(b, y, x):
        value = take(grid.slot(z=b, y=y, x=x))
        for c in cs:
            arrived("c", c, b, y, x)
            value = value + in_c[c - 1, b, y, x].astype(F32)
        return value

    def to_core(b):
        ready(b)
        for y in [*ys, 0]:
            for x in [*xs, 0]:
                for c in cs:
                    out_c[c - 1, b, y, x] = take(grid.slot(z=b, y=y, x=x, c=c)).astype(BF)
                    send(("c", c, b, y, x), out_c.at[c - 1, b, y, x], in_c.at[c - 1, b, y, x], c=c)

    def diagonal(b):
        for y in ys:
            for x in xs:
                out_p[b, y, x] = core_sum(b, y, x).astype(BF)
                send(("a", b, y, x), out_p.at[b, y, x, first], in_p.at[b, y, x, first], x=x)
                send(("b", b, y, x), out_p.at[b, y, x, second], in_p.at[b, y, x, second], y=y)

    def neighbour(b):
        for y in ys:
            acc[...] = core_sum(b, y, 0)
            for x in xs:
                arrived("a", b, y, x)
                acc[first, :] += in_p[b, y, x, first].astype(F32)
            out_p[b, y, 0] = acc[...].astype(BF)
            send(("y", b, y), out_p.at[b, y, 0], in_p.at[b, y, 0], y=y)
        for x in xs:
            acc[...] = core_sum(b, 0, x)
            for y in ys:
                arrived("b", b, y, x)
                acc[second, :] += in_p[b, y, x, second].astype(F32)
            out_p[b, 0, x] = acc[...].astype(BF)
            send(("x", b, x), out_p.at[b, 0, x], in_p.at[b, 0, x], x=x)

    def plane_sum(b):
        value = core_sum(b, 0, 0)
        for y in ys:
            arrived("y", b, y)
            value = value + in_p[b, y, 0].astype(F32)
        for x in xs:
            arrived("x", b, x)
            value = value + in_p[b, 0, x].astype(F32)
        return value

    for b in order:
        to_core(b)
        yield
    for turn in range(len(order) + 2):
        if turn < len(order):
            yield
            diagonal(order[turn])
        if 1 <= turn <= len(order):
            yield
            neighbour(order[turn - 1])
        if turn >= 2:
            yield
            b = order[turn - 2]
            value = plane_sum(b)
            if b:
                out_z[b - 1] = value.astype(BF)
                send(("z", b), out_z.at[b - 1], in_z.at[b - 1], z=b)
            else:
                acc[...] = value
    yield
    for b in zs:
        arrived("z", b)
        acc[...] += in_z[b - 1].astype(F32)
    done(acc[...])


DECAY = 0.5
ADAM_EPSILON = 1e-08
WEIGHT_DECAY = 0.05
VMEM_LIMIT = 60 * 1024 * 1024
NAMES = ("qkv", "out", "up", "down", "pos")
BASE_LANES = {"qkv": 64, "out": 80, "up": 96, "pos": 112}
HEIGHT = {"qkv": D, "out": D, "up": D, "down": FF, "pos": PH}
WIDTH = {"qkv": 3 * D, "out": D, "up": FF, "down": D, "pos": D}
SMALLS = SMALL_ROWS * LANES


def pad16(rows):
    return -(-rows // 16) * 16


class Layout:
    def __init__(self, count, smalls):
        self.count = count
        self.rows = {name: HEIGHT[name] // count for name in NAMES}
        self.padded = {name: pad16(self.rows[name]) for name in NAMES}
        self.start = {}
        at = 0
        for name in NAMES:
            self.start[name] = at
            at += self.padded[name] * (WIDTH[name] // LANES)
        self.small_at = at
        self.small_len = SMALLS // count
        if smalls:
            at += 16
        self.total = at

    def span(self, name, block):
        at = self.start[name] + block * self.padded[name]
        return slice(at, at + self.padded[name])

    def spread(self, name):
        rows, padded = self.rows[name], self.padded[name]
        shape = (HEIGHT[name], self.count * padded)
        row = lax.broadcasted_iota(jnp.int32, shape, 0)
        col = lax.broadcasted_iota(jnp.int32, shape, 1)
        own, owner = col % padded, col // padded
        hit = (own < rows) & (owner * rows + own == row)
        return hit.astype(F32).astype(BF)


def pad_rows(value, rows):
    have = value.shape[0]
    if have == rows:
        return value
    return jnp.concatenate([value, jnp.zeros((rows - have, value.shape[1]), value.dtype)], axis=0)


def once(action):
    pending = [action]

    def run():
        if pending:
            pending.pop()()

    return run


def head_kernel(roles, sizes, lay, *refs):
    masters = dict(zip(NAMES, refs[:5]))
    small_ref = refs[5]
    lefts = dict(zip(NAMES, refs[6:11]))
    outs = dict(zip(NAMES, refs[11:16]))
    flat_ref, bases, buf = refs[16:19]
    blocks, (send_sems, recv_sems) = refs[19:24], refs[24:]
    grid = Grid(roles, sizes)
    wire = Wire(grid, send_sems, recv_sems)
    own = grid.slot()
    for name in NAMES:
        for block in range(WIDTH[name] // LANES):
            piece = masters[name][:, block * LANES : (block + 1) * LANES]
            buf[own, lay.span(name, block), :] = pad_rows(piece, lay.padded[name]).astype(BF)
    lines = []
    for at in range(0, lay.small_len, LANES):
        line = small_ref[:, at : min(at + LANES, lay.small_len)]
        if line.shape[1] < LANES:
            line = jnp.concatenate([line, jnp.zeros((1, LANES - line.shape[1]), F32)], axis=1)
        lines.append(line)
    lines = jnp.concatenate(lines, axis=0)
    buf[own, lay.small_at : lay.small_at + 16, :] = pad_rows(lines, 16).astype(BF)

    def pack_bases():
        lane = lax.broadcasted_iota(jnp.int32, (1, LANES), 1)

        def piece(name, owner, target):
            width = lay.rows[name]
            at = owner * width
            tile, place = at // LANES * LANES, at % LANES
            value = lefts[name][:, tile : tile + LANES]
            shift = (target - place) % LANES
            value = pltpu.roll(value, shift, 1) if shift else value
            if place + width > LANES:
                after = lefts[name][:, tile + LANES : tile + 2 * LANES]
                after = pltpu.roll(after, shift, 1) if shift else after
                value = jnp.where(lane < target + LANES - place, value, after)
            value = jnp.where((lane >= target) & (lane < target + width), value, 0.0)
            return pad_rows(value, lay.padded["down"])

        for owner in range(lay.count):
            index = {"dp": owner // sizes["fsdp"], "fsdp": owner % sizes["fsdp"]}
            z, y, x, core = (
                index[axis] // stride % size
                for axis, stride, size in (roles[role] for role in ("z", "y", "x", "c"))
            )
            value = piece("down", owner, 0)
            for name, target in BASE_LANES.items():
                value = value + piece(name, owner, target)
            blocks[0][z, y, x, core] = value.astype(BF)

    meet(grid)
    together(
        gather_all(grid, wire, buf, "w"),
        (exchange_all(grid, wire, "e", blocks, pack_bases), 4),
    )
    nz, ny, nx, nc = (grid.size(role) for role in ("z", "y", "x", "c"))
    for z in range(nz):
        for y in range(ny):
            for x in range(nx):
                for core in range(nc):
                    bases[grid.slot(z=z, y=y, x=x, c=core)] = blocks[4][z, y, x, core]
    for name in NAMES:
        spread = None if lay.rows[name] == lay.padded[name] else lay.spread(name)
        for block in range(WIDTH[name] // LANES):
            piece = buf[:, lay.span(name, block), :].reshape(lay.count * lay.padded[name], LANES)
            if spread is not None:
                piece = nn(spread, piece).astype(BF)
            outs[name][:, block * LANES : (block + 1) * LANES] = piece
    lane = lax.broadcasted_iota(jnp.int32, (1, LANES), 1)
    for row in range(SMALL_ROWS):
        line = jnp.zeros((1, LANES), F32)
        at = row * LANES
        while at < (row + 1) * LANES:
            owner, place = at // lay.small_len, at % lay.small_len
            source_row, source_lane = place // LANES, place % LANES
            take = min(
                (row + 1) * LANES - at, lay.small_len - place, LANES - source_lane
            )
            target = at - row * LANES
            piece = buf[owner, lay.small_at : lay.small_at + 16, :].astype(F32)
            piece = piece[source_row : source_row + 1, :]
            shift = (target - source_lane) % LANES
            if shift:
                piece = pltpu.roll(piece, shift, 1)
            line = jnp.where((lane >= target) & (lane < target + take), piece, line)
            at += take
        flat_ref[row : row + 1, :] = line
    wire.finish()


def vmem():
    return pl.BlockSpec(memory_space=pltpu.VMEM)


def gather_weights(roles, sizes, lay, masters, smalls, lefts):
    count = gather_copies(roles) + exchange_copies(roles)
    nz, ny, nx, nc = (roles[role][2] for role in ("z", "y", "x", "c"))
    block = (lay.padded["down"], LANES)
    return pl.pallas_call(
        functools.partial(head_kernel, roles, sizes, lay),
        out_shape=tuple(jax.ShapeDtypeStruct((HEIGHT[n], WIDTH[n]), BF) for n in NAMES)
        + (
            jax.ShapeDtypeStruct((SMALL_ROWS, LANES), F32),
            jax.ShapeDtypeStruct((lay.count,) + block, BF),
        ),
        in_specs=[vmem()] * 11,
        out_specs=tuple([vmem()] * 7),
        scratch_shapes=[
            pltpu.VMEM((lay.count, lay.total, LANES), BF),
            pltpu.VMEM((nz, ny, nx, nc) + block, BF),
            pltpu.VMEM((nc, nz, ny, nx) + block, BF),
            pltpu.VMEM((nx, nc, nz, ny) + block, BF),
            pltpu.VMEM((ny, nx, nc, nz) + block, BF),
            pltpu.VMEM((nz, ny, nx, nc) + block, BF),
            pltpu.SemaphoreType.DMA((count,)),
            pltpu.SemaphoreType.DMA((count,)),
        ],
        compiler_params=pltpu.CompilerParams(
            collective_id=0, has_side_effects=True, vmem_limit_bytes=VMEM_LIMIT
        ),
        name="gather_weights",
    )(*masters, smalls.reshape(1, lay.small_len), *lefts)


def split(value):
    high = value.astype(BF)
    return jnp.concatenate([high, (value - high.astype(F32)).astype(BF)], axis=0)


def joined(value):
    half = value.shape[0] // 2
    return value[:half] + value[half:]


class Groups:
    def __init__(self, lay):
        self.lay = lay
        wide = [(name, i) for name in ("qkv", "out", "up") for i in range(WIDTH[name] // LANES)]
        self.members = [wide[i : i + 4] for i in range(0, len(wide), 4)]
        self.members += [[("down", i)] for i in range(WIDTH["down"] // LANES)]
        self.members += [[("pos", i) for i in range(WIDTH["pos"] // LANES)]]
        self.rows = [pad16(sum(lay.rows[name] for name, _ in group)) for group in self.members]
        self.starts = [sum(self.rows[:i]) for i in range(len(self.rows))]
        self.total = sum(self.rows)
        self.kinds = []
        self.kind_of = []
        for group, rows in zip(self.members, self.rows):
            kind = (tuple(name for name, _ in group), rows)
            if kind not in self.kinds:
                self.kinds.append(kind)
            self.kind_of.append(self.kinds.index(kind))

    def span(self, number):
        return slice(self.starts[number], self.starts[number] + self.rows[number])

    def spread(self, name, rows, place):
        own_rows = self.lay.rows[name]
        shape = (HEIGHT[name], self.lay.count * rows)
        row = lax.broadcasted_iota(jnp.int32, shape, 0)
        col = lax.broadcasted_iota(jnp.int32, shape, 1)
        owner = col // rows
        own = col - owner * rows - place * own_rows
        hit = (own >= 0) & (own < own_rows) & (owner * own_rows + own == row)
        return hit.astype(F32).astype(BF)

    def thin(self, number):
        names, rows = self.kinds[number]
        return sum(2 * self.lay.padded[name] for name in names), self.lay.count * rows


RIGHT_CHUNK = 384
STARTS = {"qkv": QKV_AT, "up": UP_AT, "out": OUT_AT, "down": DOWN_AT, "pos": POS_AT}


WIDE_AT = {"qkv": 0, "out": 3 * D, "up": 4 * D}


def packed_place(packed, name):
    if name in WIDE_AT:
        return packed[0], WIDE_AT[name]
    return packed[1 if name == "down" else 2], 0


def hand_out_kernel(lay, index_ref, small, *refs):
    packed, small_out = refs[:3], refs[3]
    outs = [dict(zip(NAMES, refs[4 + 5 * i : 9 + 5 * i])) for i in range(5)]
    at = index_ref[0] * lay.small_len
    row, shift = at // LANES, at % LANES
    lane = lax.broadcasted_iota(jnp.int32, (1, LANES), 1)
    for start in range(0, lay.small_len, LANES):
        near, far = (
            pltpu.roll(small[pl.ds(row + start // LANES + i, 1), :], LANES - shift, 1)
            for i in range(2)
        )
        take = min(LANES, lay.small_len - start)
        line = jnp.where(lane < LANES - shift, near, far)
        small_out[:, start : start + take] = line[:, :take]
    for name in NAMES:
        source, at = packed_place(packed, name)
        for kind in range(4):
            value = source[kind, : lay.rows[name], at : at + WIDTH[name]]
            outs[kind][name][...] = value
            if kind == 3:
                outs[4][name][...] = value.astype(BF)


def hand_out(lay, index, small, packed):
    shapes = [(lay.rows[n], WIDTH[n]) for n in NAMES]
    return pl.pallas_call(
        functools.partial(hand_out_kernel, lay),
        out_shape=(jax.ShapeDtypeStruct((1, lay.small_len), F32),)
        + tuple(jax.ShapeDtypeStruct(s, F32) for s in shapes * 4)
        + tuple(jax.ShapeDtypeStruct(s, BF) for s in shapes),
        in_specs=[pl.BlockSpec(memory_space=pltpu.SMEM)] + [vmem()] * 4,
        out_specs=tuple([vmem()] * 26),
        name="hand_out",
    )(index, small, *packed)


def tail_kernel(roles, sizes, lay, groups, extra, full_hbm, small, bases, *refs):
    rights_hbm, lefts, masters, firsts, seconds = (
        dict(zip(NAMES, refs[5 * i : 5 * i + 5])) for i in range(5)
    )
    small_out = refs[25]
    packed = refs[26:29]
    rest = refs[29:]

    def keep(kind, name, cols, value):
        target, at = packed_place(packed, name)
        target[kind, : value.shape[0], at + cols.start : at + cols.stop] = value

    full, acc, out_c, in_c, out_p, in_p, out_z, in_z, s_out, s_in = rest[:10]
    flat, steps, coarse = rest[10:13]
    rights = dict(zip(NAMES, rest[13:18]))
    picks = dict(zip(NAMES, rest[18:23]))
    thins = rest[23 : 23 + len(groups.kinds)]
    send_sems, recv_sems, full_sems, right_sems = rest[23 + len(groups.kinds) :]
    grid = Grid(roles, sizes)
    wire = Wire(grid, send_sems, recv_sems)
    me = grid.slot()

    plane = lay.count // grid.size("z")

    def full_copy(b):
        at = pl.multiple_of(flipped(grid.coord["z"], b, grid.size("z")) * plane, plane)
        part = pl.ds(at, plane)
        return pltpu.make_async_copy(full_hbm.at[part], full.at[part], full_sems.at[b])

    for b in (1, 2, 3, 0):
        full_copy(b).start()

    chunks = [(name, at) for name in NAMES for at in range(0, WIDTH[name], RIGHT_CHUNK)]

    def right_copy(number):
        name, at = chunks[number]
        return pltpu.make_async_copy(
            rights_hbm[name].at[pl.ds(at, RIGHT_CHUNK), :],
            coarse.at[number % 2, :, pl.ds(0, WIDTH[name])],
            right_sems.at[number],
        )

    def begin():
        right_copy(0).start()
        right_copy(1).start()

    def round_right(number):
        name, at = chunks[number]
        right_copy(number).wait()
        rights[name][at : at + RIGHT_CHUNK, :] = coarse[number % 2, :, : WIDTH[name]].astype(BF)
        if number + 2 < len(chunks):
            right_copy(number + 2).start()

    def make_pick(name):
        height, rows, padded = HEIGHT[name], lay.rows[name], lay.padded[name]
        row = lax.broadcasted_iota(jnp.int32, (padded, height), 0)
        col = lax.broadcasted_iota(jnp.int32, (padded, height), 1)
        pick = ((row < rows) & (col == me * rows + row)).astype(F32).astype(BF)
        at = BASE_LANES.get(name, 0)
        base = bases[:, :padded, :].reshape(lay.count * padded, LANES).T
        left_rows = base[at : at + padded, :]
        if rows != padded:
            left_rows = nt(left_rows, lay.spread(name)).astype(BF)
        picks[name][:padded, :] = left_rows
        picks[name][padded:, :] = pick

    def make_thin(number):
        names, rows = groups.kinds[number]
        at = 0
        for place, name in enumerate(names):
            padded = lay.padded[name]
            left = split(pad_rows(lefts[name][...], padded))
            if len(names) > 1 or rows != lay.rows[name]:
                left = nn(left, groups.spread(name, rows, place)).astype(BF)
            thins[number][at : at + 2 * padded, :] = left
            at += 2 * padded

    duties = [begin] + [functools.partial(round_right, i) for i in range(len(chunks))]
    duties += [functools.partial(make_pick, name) for name in NAMES]
    duties += [functools.partial(make_thin, i) for i in range(len(groups.kinds))]

    def idle():
        if duties:
            duties.pop(0)()

    meet(grid)
    small_out[...] = jnp.zeros_like(small_out)

    def share():
        def done(total):
            flat[me] = total.astype(BF)

        yield from reduce_scatter(
            grid, wire, "sum", lambda slot: full[slot], out_c, in_c, out_p, in_p, out_z, in_z, acc,
            lambda b: full_copy(b).wait(), done,
        )
        yield from gather_all(grid, wire, flat, "flat")

    smalls = reduce_small(grid, wire, small, s_out, s_in, extra, small_out)
    together(share(), (smalls, 6), idle=idle, quiet=5)
    while duties:
        idle()

    def flat_block(block):
        height = flat.shape[1]
        pieces, at = [], block * D
        while at < (block + 1) * D:
            slot, row = at // height, at % height
            take = min((block + 1) * D - at, height - row)
            pieces.append(flat[slot, row : row + take, :])
            at += take
        return pieces[0] if len(pieces) == 1 else jnp.concatenate(pieces, axis=0)

    directions = {}
    for name in NAMES:
        height, width = HEIGHT[name], WIDTH[name]
        rows, padded = lay.rows[name], lay.padded[name]
        lhs = picks[name][...]
        if name in ("down", "pos"):
            both = None
            for block in range(height // LANES):
                part = nt(
                    lhs[:, block * LANES : (block + 1) * LANES], flat_block(STARTS[name] + block)
                )
                both = part if both is None else both + part
        else:
            both = jnp.concatenate(
                [nn(lhs, flat_block(STARTS[name] + i)) for i in range(width // LANES)], axis=1
            )
        keep(0, name, slice(0, width), both[padded : padded + rows])
        terms = split(both[:padded])
        for at in range(0, width, D):
            cols = slice(at, at + D)
            rotated = joined(nn(terms, rights[name][:, cols]))[:rows]
            first = DECAY * firsts[name][:, cols] + (1.0 - DECAY) * rotated
            second = DECAY * seconds[name][:, cols] + (1.0 - DECAY) * rotated * rotated
            keep(1, name, cols, first)
            keep(2, name, cols, second)
            direction = first / (jnp.sqrt(second) + ADAM_EPSILON)
            for i in range(D // LANES):
                directions[name, at // LANES + i] = direction[:, i * LANES : (i + 1) * LANES]
    for number, group in enumerate(groups.members):
        piece = jnp.concatenate([directions[member] for member in group], axis=0)
        steps[me, groups.span(number), :] = pad_rows(piece, groups.rows[number]).astype(BF)

    together(gather_all(grid, wire, steps, "steps"))

    partway = {}
    for number, group in enumerate(groups.members):
        rows = groups.rows[number]
        piece = steps[:, groups.span(number), :].reshape(lay.count * rows, LANES)
        whole = nn(thins[groups.kind_of[number]][...], piece)
        at = 0
        for name, block in group:
            padded = lay.padded[name]
            partway[name, block] = joined(whole[at : at + 2 * padded])
            at += 2 * padded
    for name in NAMES:
        height, width = HEIGHT[name], WIDTH[name]
        terms = split(
            jnp.concatenate([partway[name, i] for i in range(width // LANES)], axis=1)
        )
        rate = height ** (-0.5)
        for at in range(0, width, D):
            cols = slice(at, at + D)
            update = joined(nt(terms, rights[name][cols, :]))[: lay.rows[name]]
            master = masters[name][:, cols] * (1.0 - rate * WEIGHT_DECAY) - rate * update
            keep(3, name, cols, master)
    wire.finish()


def finish_step(roles, sizes, lay, full, small, bases, rights, lefts, masters, firsts, seconds):
    slots, rows, _ = full.shape
    nz, ny, nx, nc = (roles[role][2] for role in ("z", "y", "x", "c"))
    count = reduce_copies(roles) + small_copies(roles) + 2 * gather_copies(roles)
    extra = {}
    for role in ("c", "y", "x", "z"):
        for offset in range(1, roles[role][2]):
            extra[(role, offset)] = len(extra)
    groups = Groups(lay)
    chunks = sum(WIDTH[name] // RIGHT_CHUNK for name in NAMES)
    anywhere = pl.BlockSpec(memory_space=pl.ANY)
    return pl.pallas_call(
        functools.partial(tail_kernel, roles, sizes, lay, groups, extra),
        out_shape=(
            jax.ShapeDtypeStruct((40, LANES), F32),
            jax.ShapeDtypeStruct((4, lay.padded["qkv"], 5 * D + 3 * D), F32),
            jax.ShapeDtypeStruct((4, lay.padded["down"], D), F32),
            jax.ShapeDtypeStruct((4, lay.padded["pos"], D), F32),
        ),
        in_specs=[anywhere, vmem(), vmem()] + [anywhere] * 5 + [vmem()] * 20,
        out_specs=tuple([vmem()] * 4),
        scratch_shapes=[
            pltpu.VMEM((slots, rows, LANES), F32),
            pltpu.VMEM((rows, LANES), F32),
            pltpu.VMEM((nc - 1, nz, ny, nx, rows, LANES), BF),
            pltpu.VMEM((nc - 1, nz, ny, nx, rows, LANES), BF),
            pltpu.VMEM((nz, ny, nx, rows, LANES), BF),
            pltpu.VMEM((nz, ny, nx, rows, LANES), BF),
            pltpu.VMEM((nz - 1, rows, LANES), BF),
            pltpu.VMEM((nz - 1, rows, LANES), BF),
            pltpu.VMEM((4, SMALL_ROWS, LANES), F32),
            pltpu.VMEM((len(extra), SMALL_ROWS, LANES), F32),
            pltpu.VMEM((slots, rows, LANES), BF),
            pltpu.VMEM((slots, groups.total, LANES), BF),
            pltpu.VMEM((2, RIGHT_CHUNK, FF), F32),
        ]
        + [pltpu.VMEM((WIDTH[name], WIDTH[name]), BF) for name in NAMES]
        + [pltpu.VMEM((2 * lay.padded[name], HEIGHT[name]), BF) for name in NAMES]
        + [pltpu.VMEM(groups.thin(i), BF) for i in range(len(groups.kinds))]
        + [
            pltpu.SemaphoreType.DMA((count,)),
            pltpu.SemaphoreType.DMA((count,)),
            pltpu.SemaphoreType.DMA((nz,)),
            pltpu.SemaphoreType.DMA((chunks,)),
        ],
        compiler_params=pltpu.CompilerParams(
            collective_id=1, has_side_effects=True, vmem_limit_bytes=VMEM_LIMIT
        ),
        name="finish_step",
    )(full, small, bases, *rights, *lefts, *masters, *firsts, *seconds)


AXES = ("dp", "fsdp")


def on_device(roles, sizes, tokens, centres, lengths, cotangent, smalls, *matrices):
    masters, firsts, seconds, lefts, rights = (matrices[5 * i : 5 * i + 5] for i in range(5))
    count = sizes["dp"] * sizes["fsdp"]
    heads = Layout(count, True)
    lay = Layout(count, False)
    *weights, small_rows, bases = gather_weights(roles, sizes, heads, masters, smalls, lefts)
    w_qkv, w_out, w_up, w_down, w_pos = weights
    layer_out, grad_tokens, full, small_grads = layer_pass(
        tokens, centres, lengths, cotangent, small_rows, w_qkv, w_out, w_up, w_down, w_pos
    )
    small_total, *packed = finish_step(
        roles,
        sizes,
        lay,
        full.reshape(count, FLAT_ROWS // count, LANES),
        small_grads,
        bases,
        rights,
        lefts,
        masters,
        firsts,
        seconds,
    )
    me = lax.axis_index("dp") * sizes["fsdp"] + lax.axis_index("fsdp")
    grad_smalls, *finished = hand_out(heads, me.reshape(1), small_total, packed)
    return (layer_out, grad_tokens, grad_smalls.reshape(heads.small_len), *finished)


def solution(mesh):
    sizes = {axis: mesh.shape[axis] for axis in AXES}
    rows, flat = P(AXES, None), P(AXES)
    return jax.shard_map(
        functools.partial(on_device, mesh_roles(mesh), sizes),
        mesh=mesh,
        in_specs=(rows, P(None, AXES), flat, rows, flat) + (rows,) * 20 + (P(),) * 5,
        out_specs=(rows, rows, flat) + (rows,) * 25,
        check_vma=False,
    )
```

```python
import functools
import jax
import jax.numpy as jnp
from jax import lax
from jax.experimental import pallas as pl
from jax.experimental.pallas import tpu as pltpu
from jax.sharding import PartitionSpec as P

D = 384
HEADS = 6
HEAD = 64
FF = 1536
PH = 128
LMAX = 256
LANES = 128
EPSILON = 1e-05
NEG_FILL = -1e30
HIGHEST = lax.Precision.HIGHEST
BF = jnp.bfloat16
F32 = jnp.float32

QKV_AT, UP_AT, OUT_AT, DOWN_AT, POS_AT, BLOCKS = 0, 9, 21, 24, 36, 37
FLAT_ROWS = 14336
SMALL_ROWS = 37


def nn(a, b):
    return jnp.dot(a, b, preferred_element_type=F32)


def nt(a, b):
    return lax.dot_general(a, b, (((1,), (1,)), ((), ())), preferred_element_type=F32)


def tn(a, b):
    return lax.dot_general(a, b, (((0,), (0,)), ((), ())), preferred_element_type=F32)


INV_SQRT2 = 0.7071067811865476
INV_SQRT_2PI = 0.3989422804014327


def gelu_pair(x):
    cdf = 0.5 * (1.0 + lax.erf(x * INV_SQRT2))
    pdf = jnp.exp(-0.5 * x * x) * INV_SQRT_2PI
    return x * cdf, cdf + x * pdf


def norm_parts(x):
    mean = jnp.mean(x, axis=-1, keepdims=True)
    centred = x - mean
    spread = jnp.mean(centred * centred, axis=-1, keepdims=True)
    inv = lax.rsqrt(spread + EPSILON)
    return centred * inv, inv


def thirds(value):
    terms = []
    for _ in range(3):
        term = value.astype(BF)
        terms.append(term)
        value = value - term.astype(F32)
    return terms


def col8(x):
    rows, cols = x.shape
    return jnp.sum(x.reshape(rows // 8, 8, cols), axis=0)


def layer_kernel(
    len_ref,
    tok_ref,
    cen_ref,
    cot_ref,
    small_ref,
    wqkv_ref,
    wout_ref,
    wup_ref,
    wdown_ref,
    wpos_ref,
    out_ref,
    gtok_ref,
    grad_ref,
    sgrad_ref,
    sacc,
    posh_s,
    emb_s,
    xh1_s,
    n1_s,
    qkv_s,
    p_s,
    att_s,
    bin_s,
    n2g_s,
    ff_s,
    qg_s,
    wide_s,
    ds_s,
    dq_s,
    ag_s,
    hid_s,
    act_s,
    low_s,
    hg_s,
    inv_s,
    xh2_s,
    gy_s,
    bgl_s,
    *,
    fc,
    group,
):
    step = pl.program_id(0)
    last = pl.num_programs(0) - 1

    @pl.when(step == 0)
    def _():
        grad_ref[...] = jnp.zeros_like(grad_ref)
        sacc[...] = jnp.zeros_like(sacc)

    rows = group * LMAX
    lengths = [len_ref[step * group + i] for i in range(group)]

    def live(width):
        return jnp.concatenate(
            [lax.broadcasted_iota(jnp.int32, (LMAX, width), 0) < length for length in lengths], axis=0
        )

    def vec(at, blocks):
        return jnp.concatenate([small_ref[at + i : at + i + 1, :] for i in range(blocks)], axis=1)

    def add_small(at, value):
        cols = value.shape[1]
        sacc[:, at * LANES : at * LANES + cols] += value

    def add_grad(block, value):
        for i in range(value.shape[1] // LANES):
            rows = slice((block + i) * D, (block + i + 1) * D)
            grad_ref[rows, :] += value[:, i * LANES : (i + 1) * LANES]

    gain_one, shift_one, gain_two, shift_two, attn_bias, down_bias, embed_bias = (
        vec(3 * i, 3) for i in range(7)
    )
    hidden_bias = small_ref[33:34, :]
    pos_first = small_ref[34:37, :]
    cen = cen_ref[...]

    cen_terms = jnp.concatenate(thirds(cen) + [jnp.zeros((7, rows), BF)], axis=0)
    first_terms = jnp.concatenate(
        [pos_first.astype(BF)] * 3 + [jnp.zeros((7, PH), BF)], axis=0
    )
    pos_hidden = tn(cen_terms, first_terms) + hidden_bias
    pos_act, pos_slope = gelu_pair(pos_hidden)
    pos_low = pos_act.astype(BF)
    posh_s[...] = pos_slope
    embedded = tok_ref[...].astype(F32) + nn(pos_low, wpos_ref[...]) + embed_bias
    emb_s[...] = embedded
    xhat_one, inv_one = norm_parts(embedded)
    xh1_s[...] = xhat_one
    n1 = (xhat_one * gain_one + shift_one).astype(BF)
    n1_s[...] = n1
    qkv_s[...] = nn(n1, wqkv_ref[...]).astype(BF)

    lane = lax.broadcasted_iota(jnp.int32, (1, LANES), 1)
    halves = [(lane < HEAD).astype(F32).astype(BF), (lane >= HEAD).astype(F32).astype(BF)]
    scale = HEAD ** (-0.5)
    scaled = [(h.astype(F32) * scale).astype(BF) for h in halves]

    key_live = [
        lax.broadcasted_iota(jnp.int32, (LMAX, LMAX), 0) < length for length in lengths
    ]
    spans = [slice(i * LMAX, (i + 1) * LMAX) for i in range(group)]

    heads = [(i, head) for head in range(HEADS) for i in range(group)]

    def lanes_of(which, i, head):
        at = which * D + head // 2 * LANES
        return qkv_s[spans[i], at : at + LANES]

    def staged(*stages):
        for turn in range(len(heads) + len(stages) - 1):
            for lag, stage in enumerate(stages):
                if 0 <= turn - lag < len(heads):
                    stage(turn - lag, *heads[turn - lag])

    def scores(number, i, head):
        wide_s[number % 3] = nt(lanes_of(1, i, head), lanes_of(0, i, head) * scaled[head % 2])

    def soften(number, i, head):
        s = jnp.where(key_live[i], wide_s[number % 3], NEG_FILL)
        e = jnp.exp(s - jnp.max(s, axis=0, keepdims=True))
        p_s[i * HEADS + head] = (e * (1.0 / jnp.sum(e, axis=0, keepdims=True))).astype(BF)

    def attend(number, i, head):
        at = head % 2 * HEAD
        o_t = nn(lanes_of(2, i, head).T[at : at + HEAD, :], p_s[i * HEADS + head])
        att_s[head * HEAD : (head + 1) * HEAD, spans[i]] = o_t.astype(BF)

    staged(scores, soften, attend)

    branch_in = emb_s[...] + tn(att_s[...], wout_ref[...]) + attn_bias
    bin_s[...] = branch_in
    xhat_two, inv_two = norm_parts(branch_in)
    xh2_s[...] = xhat_two
    n2 = (xhat_two * gain_two + shift_two).astype(BF)
    n2_t = n2.T
    gy = jnp.where(live(D), cot_ref[...].astype(F32), 0.0)
    gy_s[...] = gy
    gy_low = gy.astype(BF)
    gy_t = gy_low.T
    add_small(15, col8(gy))

    blocks = fc // LANES

    def widen(c):
        cols = slice(c * fc, (c + 1) * fc)
        hid_s[c % 2] = nn(n2, wup_ref[:, cols])
        act_s[c % 2] = nt(gy_low, wdown_ref[cols, :])

    def bend(c):
        cols = slice(c * fc, (c + 1) * fc)
        act, slope = gelu_pair(hid_s[c % 2] + vec(21 + c * blocks, blocks))
        low_s[:, cols] = act.astype(BF)
        hg = (act_s[c % 2] * slope).astype(BF)
        hg_s[:, cols] = hg
        add_small(21 + c * blocks, col8(hg.astype(F32)))

    def narrow(c):
        cols = slice(c * fc, (c + 1) * fc)
        add_grad(UP_AT + c * blocks, nn(n2_t, hg_s[:, cols]))
        add_grad(DOWN_AT + c * blocks, nn(gy_t, low_s[:, cols]))

    count = FF // fc
    for turn in range(count + 1):
        for lag, stage in enumerate((widen, bend)):
            if 0 <= turn - lag < count:
                stage(turn - lag)
    n2g_s[...] = nt(hg_s[...], wup_ref[...])
    ff_s[...] = nn(low_s[...], wdown_ref[...])

    out_ref[...] = (bin_s[...] + ff_s[...] + down_bias).astype(BF)

    inv_s[...] = inv_two
    parts = count
    height = rows // parts if rows % (16 * parts) == 0 else rows // 4
    for turn in range(max(count, rows // height)):
        if turn < rows // height:
            at = slice(turn * height, (turn + 1) * height)
            n2g = n2g_s[at, :]
            xhat_two = xh2_s[at, :]
            add_small(6, col8(n2g * xhat_two))
            add_small(9, col8(n2g))
            u = n2g * gain_two
            bg = gy_s[at, :] + inv_s[at, :] * (
                u
                - jnp.mean(u, axis=-1, keepdims=True)
                - xhat_two * jnp.mean(u * xhat_two, axis=-1, keepdims=True)
            )
            bin_s[at, :] = bg
            add_small(12, col8(bg))
            bgl_s[at, :] = bg.astype(BF)
        if turn < count:
            narrow(turn)
    bg_low = bgl_s[...]
    add_grad(OUT_AT, nn(att_s[...], bg_low))
    ag = nt(bg_low, wout_ref[...]).astype(BF)

    ag_s[...] = ag
    dk, dv = {}, {}

    def ago_of(i, head):
        at = head // 2 * LANES
        return ag_s[spans[i], at : at + LANES] * halves[head % 2]

    def probs_back(number, i, head):
        wide_s[number % 3] = nt(lanes_of(2, i, head), ago_of(i, head))

    def scores_back(number, i, head):
        p = p_s[i * HEADS + head].astype(F32)
        dp = wide_s[number % 3]
        rd = jnp.sum(p * dp, axis=0, keepdims=True)
        ds_s[number % 2] = (p * (dp - rd)).astype(BF)

    def heads_back(number, i, head):
        ds = ds_s[number % 2]
        at = head % 2 * HEAD
        dv[i, head] = nn(p_s[i * HEADS + head], ago_of(i, head))
        dk[i, head] = nn(ds, lanes_of(0, i, head) * scaled[head % 2])
        dq_t = nn(lanes_of(1, i, head).T[at : at + HEAD, :], ds) * scale
        dq_s[head * HEAD : (head + 1) * HEAD, spans[i]] = dq_t.astype(BF)
        if head % 2:
            at = head // 2 * LANES
            qg_s[spans[i], at : at + LANES] = dq_s[at : at + LANES, spans[i]].T
            for which, terms in ((1, dk), (2, dv)):
                total = terms.pop((i, head - 1)) + terms.pop((i, head))
                qg_s[spans[i], which * D + at : which * D + at + LANES] = total.astype(BF)

    staged(probs_back, scores_back, heads_back)

    qg = qg_s[...]
    n2g_s[...] = nt(qg, wqkv_ref[...])
    inv_s[...] = inv_one
    n1_t = n1_s[...].T
    height = rows // 4
    for turn in range(4):
        at = slice(turn * height, (turn + 1) * height)
        n1g = n2g_s[at, :]
        xhat = xh1_s[at, :]
        add_small(0, col8(n1g * xhat))
        add_small(3, col8(n1g))
        u = n1g * gain_one
        eg = bin_s[at, :] + inv_s[at, :] * (
            u
            - jnp.mean(u, axis=-1, keepdims=True)
            - xhat * jnp.mean(u * xhat, axis=-1, keepdims=True)
        )
        add_small(18, col8(eg))
        gtok_ref[at, :] = eg.astype(BF)
        if turn < 3:
            add_grad(QKV_AT + 3 * turn, nn(n1_t, qg_s[:, turn * D : (turn + 1) * D]))
    eg_low = gtok_ref[...]
    add_grad(POS_AT, tn(eg_low, pos_low))
    phg = nt(eg_low, wpos_ref[...]) * posh_s[...]
    add_small(33, col8(phg))
    products = nn(cen_terms, jnp.concatenate(thirds(phg), axis=1))
    pf_grad = products[:, :PH] + products[:, PH : 2 * PH] + products[:, 2 * PH :]
    for i in range(3):
        sacc[0:1, (34 + i) * LANES : (35 + i) * LANES] += (
            pf_grad[i : i + 1, :] + pf_grad[i + 3 : i + 4, :] + pf_grad[i + 6 : i + 7, :]
        )

    @pl.when(step == last)
    def _():
        for i in range(SMALL_ROWS):
            sgrad_ref[i : i + 1, :] = jnp.sum(
                sacc[:, i * LANES : (i + 1) * LANES], axis=0, keepdims=True
            )


def layer_pass(tokens, centres, lengths, cotangent, small_rows, wqkv, wout, wup, wdown, wpos, fc=256, group=2):
    clouds = lengths.shape[0]
    rows = clouds * LMAX
    span = group * LMAX
    whole = lambda shape: pl.BlockSpec(shape, lambda i, *_: (0, 0), pipeline_mode=pl.Buffered(1))
    tile = lambda: pl.BlockSpec((span, D), lambda i, *_: (i, 0))
    return pl.pallas_call(
        functools.partial(layer_kernel, fc=fc, group=group),
        out_shape=(
            jax.ShapeDtypeStruct((rows, D), BF),
            jax.ShapeDtypeStruct((rows, D), BF),
            jax.ShapeDtypeStruct((FLAT_ROWS, LANES), F32),
            jax.ShapeDtypeStruct((SMALL_ROWS, LANES), F32),
        ),
        grid_spec=pltpu.PrefetchScalarGridSpec(
            num_scalar_prefetch=1,
            grid=(clouds // group,),
            in_specs=[
                tile(),
                pl.BlockSpec((3, span), lambda i, *_: (0, i)),
                tile(),
                whole((SMALL_ROWS, LANES)),
                whole((D, 3 * D)),
                whole((D, D)),
                whole((D, FF)),
                whole((FF, D)),
                whole((PH, D)),
            ],
            out_specs=[
                tile(),
                tile(),
                whole((FLAT_ROWS, LANES)),
                whole((SMALL_ROWS, LANES)),
            ],
            scratch_shapes=[
                pltpu.VMEM((8, SMALL_ROWS * LANES), F32),
                pltpu.VMEM((span, PH), F32),
                pltpu.VMEM((span, D), F32),
                pltpu.VMEM((span, D), F32),
                pltpu.VMEM((span, D), BF),
                pltpu.VMEM((span, 3 * D), BF),
                pltpu.VMEM((group * HEADS, LMAX, LMAX), BF),
                pltpu.VMEM((D, span), BF),
                pltpu.VMEM((span, D), F32),
                pltpu.VMEM((span, D), F32),
                pltpu.VMEM((span, D), F32),
                pltpu.VMEM((span, 3 * D), BF),
                pltpu.VMEM((3, LMAX, LMAX), F32),
                pltpu.VMEM((2, LMAX, LMAX), BF),
                pltpu.VMEM((D, span), BF),
                pltpu.VMEM((span, D), BF),
                pltpu.VMEM((2, span, fc), F32),
                pltpu.VMEM((2, span, fc), F32),
                pltpu.VMEM((span, FF), BF),
                pltpu.VMEM((span, FF), BF),
                pltpu.VMEM((span, 1), F32),
                pltpu.VMEM((span, D), F32),
                pltpu.VMEM((span, D), F32),
                pltpu.VMEM((span, D), BF),
            ],
        ),
        compiler_params=pltpu.CompilerParams(vmem_limit_bytes=60 * 1024 * 1024),
        name="layer",
    )(lengths, tokens, centres, cotangent, small_rows, wqkv, wout, wup, wdown, wpos)


MESH_ID = pl.DeviceIdType.MESH


def mesh_roles(mesh):
    dp, fs = mesh.shape["dp"], mesh.shape["fsdp"]
    if dp >= 32:
        return {
            "z": ("dp", dp // 4 // 2, 4) if dp == 32 else ("dp", 8, dp // 8),
            "y": ("dp", 2, 4),
            "c": ("dp", 1, 2),
            "x": ("fsdp", 1, fs),
        }
    return {
        "z": ("dp", 2, dp // 2),
        "y": ("dp", 1, 2),
        "x": ("fsdp", 2, fs // 2),
        "c": ("fsdp", 1, 2),
    }


def flipped(coord, offset, size):
    if offset == 0:
        return coord
    if size == 2:
        return 1 - coord
    return {1: coord + 1 - 2 * (coord % 2), 2: (coord + 2) % 4, 3: 3 - coord}[offset]


class Grid:
    def __init__(self, roles, sizes):
        self.roles, self.sizes = roles, sizes
        self.index = {axis: lax.axis_index(axis) for axis in sizes}
        self.coord = {
            role: (self.index[axis] // stride) % size
            for role, (axis, stride, size) in roles.items()
        }

        z = self.z = self.coord["z"]
        self.line = [z] + [self.by_z(*row) for row in ((1, 0, 1, 2), (2, 2, 3, 1), (3, 3, 0, 0))]
        self.came_by = [self.by_z(*row) for row in ((1, 0, 1, 2), (1, 2, 3, 2), (1, 2, 1, 2))]
        self.inbox = [self.by_z(*row) for row in ((1, 0, 0, 0), (3, 1, 1, 2), (4, 3, 2, 4))]
        self.inner = z // 2 + z % 2 == 1

    def by_z(self, *values):
        high, low = self.coord["z"] // 2, self.coord["z"] % 2
        return (1 - high) * ((1 - low) * values[0] + low * values[1]) + high * (
            (1 - low) * values[2] + low * values[3]
        )

    def at_z(self, coordinate):
        axis, stride, _ = self.roles["z"]
        return {**self.index, axis: self.index[axis] + (coordinate - self.z) * stride}

    def place(self, line=0, **offsets):
        at = self.at_z(self.line[line]) if line else dict(self.index)
        for role, offset in offsets.items():
            axis, stride, size = self.roles[role]
            other = flipped(self.coord[role], offset, size)
            at[axis] = at[axis] + (other - self.coord[role]) * stride
        return at

    def slot(self, **offsets):
        at = self.place(**offsets)
        return at["dp"] * self.sizes["fsdp"] + at["fsdp"]

    def size(self, role):
        return self.roles[role][2]

    def offsets(self, role):
        return range(1, self.size(role))


class Wire:
    def __init__(self, grid, send_sems, recv_sems):
        self.grid, self.send_sems, self.recv_sems = grid, send_sems, recv_sems
        self.count = 0
        self.copies = {}

    def reserve(self, count):
        self.count += count
        return self.count - count

    def make(self, number, into, source, target, place):
        return pltpu.make_async_remote_copy(
            src_ref=source,
            dst_ref=target,
            send_sem=self.send_sems.at[number],
            recv_sem=self.recv_sems.at[into],
            device_id=place,
            device_id_type=MESH_ID,
        )

    def send_to(self, key, number, into, source, target, place, when=None):
        make = functools.partial(self.make, number, into, source, target, place)
        if when is None:
            make().start()
        else:
            pl.when(when)(lambda: make().start())
        assert key not in self.copies
        self.copies[key] = (make, when)

    def send(self, key, source, target, **offsets):
        number = self.reserve(1)
        self.send_to(key, number, number, source, target, self.grid.place(**offsets))

    def arrived(self, key):
        self.copies[key][0]().wait_recv()

    def arrived_at(self, number, target):
        self.make(number, number, target, target, self.grid.place(c=1)).wait_recv()

    def finish(self):
        for make, when in self.copies.values():
            if when is None:
                make().wait_send()
            else:
                pl.when(when)(lambda make=make: make().wait_send())


def meet(grid):
    barrier = pltpu.get_barrier_semaphore()
    count = 0
    for role in ("z", "y", "x", "c"):
        for offset in grid.offsets(role):
            pl.semaphore_signal(
                barrier,
                inc=1,
                device_id=grid.place(**{role: offset}),
                device_id_type=MESH_ID,
            )
            count += 1
    pl.semaphore_wait(barrier, count)


def gather_copies(roles):
    nz, ny, nx, nc = (roles[role][2] for role in ("z", "y", "x", "c"))
    plane = (ny - 1) + (nx - 1) + 2 * (ny - 1) * (nx - 1)
    core = (nc - 1) * (1 + plane)
    return 5 + nz * (plane + core)


def nothing():
    pass


def gather_all(grid, wire, buf, tag, rows=None):
    start, rows = (0, buf.shape[1]) if rows is None else rows
    half = rows // 32 * 16
    parts = {
        None: pl.ds(start, rows),
        "a": pl.ds(start, half),
        "b": pl.ds(start + half, rows - half),
    }

    def pass_on(key, slot, part, **offsets):
        ref = buf.at[slot, parts[part]]
        wire.send((tag,) + key, ref, ref, **offsets)

    def arrived(*key):
        wire.arrived((tag,) + key)

    ys, xs, cs = ([*grid.offsets(role)] for role in ("y", "x", "c"))

    def to_core(key, slot, part=None):
        for c in cs:
            pass_on(("c", c) + key, slot, part, c=c)

    def have(b):
        slot = grid.slot(line=b)
        for y in ys:
            pass_on(("y", b, y), slot, None, y=y)
        for x in xs:
            pass_on(("x", b, x), slot, None, x=x)
        to_core((b, 0, 0, 0), slot)

    def relay(b):
        for y in ys:
            yield
            arrived("y", b, y)
            for x in xs:
                pass_on(("a", b, y, x), grid.slot(line=b, y=y), "a", x=x)
            to_core((b, y, 0, 0), grid.slot(line=b, y=y))
        for x in xs:
            yield
            arrived("x", b, x)
            for y in ys:
                pass_on(("b", b, y, x), grid.slot(line=b, x=x), "b", y=y)
            to_core((b, 0, x, 0), grid.slot(line=b, x=x))

    base = wire.reserve(5)
    z = grid.z

    def along(site, line, target, into, when):
        ref = buf.at[grid.slot(line=line), parts[None]]
        place = grid.at_z(target)
        wire.send_to((tag, "z", site), base + site, base + into, ref, ref, place, when)

    along(0, 0, z + 1, 0, z < 3)
    along(1, 0, z - 1, z // 2, z > 0)
    have(0)
    onward = ((z + 1, 3 - z), (z - 1, z), (3 * (z - 1), 2))
    for b in (1, 2, 3):
        yield
        wire.arrived_at(base + b - 1, buf.at[grid.slot(line=b), parts[None]])
        along(1 + b, b, *onward[b - 1], grid.inner)
        have(b)
        yield from relay(b - 1)
    yield from relay(3)
    for b in range(4):
        for y in ys:
            for x in xs:
                for part in ("a", "b"):
                    yield
                    arrived(part, b, y, x)
                    to_core((b, y, x, part), grid.slot(line=b, y=y, x=x), part)
    yield
    for key in list(wire.copies):
        if key[:2] == (tag, "c"):
            wire.arrived(key)


def together(*chains, idle=nothing, quiet=0):
    chains = [chain if isinstance(chain, tuple) else (chain, 1) for chain in chains]
    turn = 0
    while chains:
        for chain in list(chains):
            if turn % chain[1] == 0 or len(chains) == 1:
                try:
                    next(chain[0])
                except StopIteration:
                    chains.remove(chain)
        if turn >= quiet:
            idle()
        turn += 1


def exchange_copies(roles):
    return sum(roles[role][2] - 1 for role in ("c", "x", "y", "z"))


def exchange_all(grid, wire, tag, blocks, pack):
    pack()
    for stage, role in enumerate(("c", "x", "y", "z")):
        source, target = blocks[stage], blocks[stage + 1]
        coord, size = grid.coord[role], grid.size(role)
        for offset in grid.offsets(role):
            part = source.at[:, :, :, flipped(coord, offset, size)]
            wire.send((tag, role, offset), part, target.at[offset], **{role: offset})
        target[0] = source[:, :, :, coord]
        yield
        for offset in grid.offsets(role):
            wire.arrived((tag, role, offset))


def reduce_copies(roles):
    nz, ny, nx, nc = (roles[role][2] for role in ("z", "y", "x", "c"))
    plane = (ny - 1) + (nx - 1) + 2 * (ny - 1) * (nx - 1)
    return (nc - 1) * nz * ny * nx + nz * plane + 5


def small_copies(roles):
    return sum(roles[role][2] - 1 for role in ("z", "y", "x", "c"))


def reduce_small(grid, wire, small, s_out, s_in, numbers, result):
    value = small[...]
    for stage, role in enumerate(("c", "y", "x", "z")):
        s_out[stage] = value
        for offset in grid.offsets(role):
            number = numbers[role, offset]
            wire.send(("s", role, offset), s_out.at[stage], s_in.at[number], **{role: offset})
        yield
        for offset in grid.offsets(role):
            wire.arrived(("s", role, offset))
            value = value + s_in[numbers[role, offset]]
    result[: value.shape[0], :] = value


def reduce_scatter(grid, wire, tag, take, out_c, in_c, out_p, in_p, out_z, in_z, acc, ready, done):
    rows = acc.shape[0]
    half = rows // 32 * 16
    first, second = pl.ds(0, half), pl.ds(half, rows - half)
    zs, ys, xs, cs = ([*grid.offsets(role)] for role in ("z", "y", "x", "c"))
    order = zs + [0]

    def send(key, source, target, **offsets):
        wire.send((tag,) + key, source, target, **offsets)

    def arrived(*key):
        wire.arrived((tag,) + key)

    def core_sum(b, y, x):
        value = take(grid.slot(z=b, y=y, x=x))
        for c in cs:
            arrived("c", c, b, y, x)
            value = value + in_c[c - 1, b, y, x].astype(F32)
        return value

    def to_core(b):
        ready(b)
        for y in [*ys, 0]:
            for x in [*xs, 0]:
                for c in cs:
                    out_c[c - 1, b, y, x] = take(grid.slot(z=b, y=y, x=x, c=c)).astype(BF)
                    send(("c", c, b, y, x), out_c.at[c - 1, b, y, x], in_c.at[c - 1, b, y, x], c=c)

    def diagonal(b):
        for y in ys:
            for x in xs:
                out_p[b, y, x] = core_sum(b, y, x).astype(BF)
                send(("a", b, y, x), out_p.at[b, y, x, first], in_p.at[b, y, x, first], x=x)
                send(("b", b, y, x), out_p.at[b, y, x, second], in_p.at[b, y, x, second], y=y)

    def neighbour(b):
        for y in ys:
            acc[...] = core_sum(b, y, 0)
            for x in xs:
                arrived("a", b, y, x)
                acc[first, :] += in_p[b, y, x, first].astype(F32)
            out_p[b, y, 0] = acc[...].astype(BF)
            send(("y", b, y), out_p.at[b, y, 0], in_p.at[b, y, 0], y=y)
        for x in xs:
            acc[...] = core_sum(b, 0, x)
            for y in ys:
                arrived("b", b, y, x)
                acc[second, :] += in_p[b, y, x, second].astype(F32)
            out_p[b, 0, x] = acc[...].astype(BF)
            send(("x", b, x), out_p.at[b, 0, x], in_p.at[b, 0, x], x=x)

    def plane_sum(b):
        value = core_sum(b, 0, 0)
        for y in ys:
            arrived("y", b, y)
            value = value + in_p[b, y, 0].astype(F32)
        for x in xs:
            arrived("x", b, x)
            value = value + in_p[b, 0, x].astype(F32)
        return value

    for b in order:
        to_core(b)
        yield
    for turn in range(len(order) + 2):
        if turn < len(order):
            yield
            diagonal(order[turn])
        if 1 <= turn <= len(order):
            yield
            neighbour(order[turn - 1])
        if turn >= 2:
            yield
            b = order[turn - 2]
            value = plane_sum(b)
            if b:
                out_z[b - 1] = value.astype(BF)
                send(("z", b), out_z.at[b - 1], in_z.at[b - 1], z=b)
            else:
                acc[...] = value
    yield
    for b in zs:
        arrived("z", b)
        acc[...] += in_z[b - 1].astype(F32)
    done(acc[...])


DECAY = 0.5
ADAM_EPSILON = 1e-08
WEIGHT_DECAY = 0.05
VMEM_LIMIT = 60 * 1024 * 1024
NAMES = ("qkv", "out", "up", "down", "pos")
BASE_PLACE = {"qkv": (0, 96), "out": (0, 112), "up": (16, 96), "pos": (16, 112)}
BASE_ROWS = 32
HEIGHT = {"qkv": D, "out": D, "up": D, "down": FF, "pos": PH}
WIDTH = {"qkv": 3 * D, "out": D, "up": FF, "down": D, "pos": D}
SMALLS = SMALL_ROWS * LANES


def pad16(rows):
    return -(-rows // 16) * 16


class Layout:
    def __init__(self, count, smalls):
        self.count = count
        self.rows = {name: HEIGHT[name] // count for name in NAMES}
        self.padded = {name: pad16(self.rows[name]) for name in NAMES}
        self.start = {}
        at = 0
        for name in NAMES:
            self.start[name] = at
            at += self.padded[name] * (WIDTH[name] // LANES)
        self.small_at = at
        self.small_len = SMALLS // count
        if smalls:
            at += 16
        self.total = at

    def span(self, name, block):
        at = self.start[name] + block * self.padded[name]
        return slice(at, at + self.padded[name])

    def spread(self, name):
        rows, padded = self.rows[name], self.padded[name]
        shape = (HEIGHT[name], self.count * padded)
        row = lax.broadcasted_iota(jnp.int32, shape, 0)
        col = lax.broadcasted_iota(jnp.int32, shape, 1)
        own, owner = col % padded, col // padded
        hit = (own < rows) & (owner * rows + own == row)
        return hit.astype(F32).astype(BF)


def pad_rows(value, rows):
    have = value.shape[0]
    if have == rows:
        return value
    return jnp.concatenate([value, jnp.zeros((rows - have, value.shape[1]), value.dtype)], axis=0)


def once(action):
    pending = [action]

    def run():
        if pending:
            pending.pop()()

    return run


def head_kernel(roles, sizes, lay, *refs):
    masters = dict(zip(NAMES, refs[:5]))
    small_ref = refs[5]
    lefts = dict(zip(NAMES, refs[6:11]))
    outs = dict(zip(NAMES, refs[11:16]))
    flat_ref, bases, buf = refs[16:19]
    blocks, (send_sems, recv_sems) = refs[19:24], refs[24:]
    grid = Grid(roles, sizes)
    wire = Wire(grid, send_sems, recv_sems)
    own = grid.slot()
    for name in NAMES:
        for block in range(WIDTH[name] // LANES):
            piece = masters[name][:, block * LANES : (block + 1) * LANES]
            buf[own, lay.span(name, block), :] = pad_rows(piece, lay.padded[name]).astype(BF)
    lines = []
    for at in range(0, lay.small_len, LANES):
        line = small_ref[:, at : min(at + LANES, lay.small_len)]
        if line.shape[1] < LANES:
            line = jnp.concatenate([line, jnp.zeros((1, LANES - line.shape[1]), F32)], axis=1)
        lines.append(line)
    lines = jnp.concatenate(lines, axis=0)
    buf[own, lay.small_at : lay.small_at + 16, :] = pad_rows(lines, 16).astype(BF)

    def pack_bases():
        lane = lax.broadcasted_iota(jnp.int32, (1, LANES), 1)

        def piece(name, owner, target):
            width = lay.rows[name]
            at = owner * width
            tile, place = at // LANES * LANES, at % LANES
            value = lefts[name][:, tile : tile + LANES]
            shift = (target - place) % LANES
            value = pltpu.roll(value, shift, 1) if shift else value
            if place + width > LANES:
                after = lefts[name][:, tile + LANES : tile + 2 * LANES]
                after = pltpu.roll(after, shift, 1) if shift else after
                value = jnp.where(lane < target + LANES - place, value, after)
            value = jnp.where((lane >= target) & (lane < target + width), value, 0.0)
            return value

        for owner in range(lay.count):
            index = {"dp": owner // sizes["fsdp"], "fsdp": owner % sizes["fsdp"]}
            z, y, x, core = (
                index[axis] // stride % size
                for axis, stride, size in (roles[role] for role in ("z", "y", "x", "c"))
            )
            half = lay.rows["down"] // 2
            value = pad_rows(
                piece("down", owner, 0)[:half] + piece("down", owner, 48)[half:], BASE_ROWS
            )
            for name, (top, target) in BASE_PLACE.items():
                below = piece(name, owner, target)
                if top:
                    below = jnp.concatenate([jnp.zeros((top, LANES), F32), below], axis=0)
                value = value + pad_rows(below, BASE_ROWS)
            blocks[0][z, y, x, core] = value.astype(BF)

    meet(grid)
    together(
        gather_all(grid, wire, buf, "w"),
        (exchange_all(grid, wire, "e", blocks, pack_bases), 4),
    )
    nz, ny, nx, nc = (grid.size(role) for role in ("z", "y", "x", "c"))
    for z in range(nz):
        for y in range(ny):
            for x in range(nx):
                for core in range(nc):
                    bases[grid.slot(z=z, y=y, x=x, c=core)] = blocks[4][z, y, x, core]
    for name in NAMES:
        spread = None if lay.rows[name] == lay.padded[name] else lay.spread(name)
        for block in range(WIDTH[name] // LANES):
            piece = buf[:, lay.span(name, block), :].reshape(lay.count * lay.padded[name], LANES)
            if spread is not None:
                piece = nn(spread, piece).astype(BF)
            outs[name][:, block * LANES : (block + 1) * LANES] = piece
    lane = lax.broadcasted_iota(jnp.int32, (1, LANES), 1)
    for row in range(SMALL_ROWS):
        line = jnp.zeros((1, LANES), F32)
        at = row * LANES
        while at < (row + 1) * LANES:
            owner, place = at // lay.small_len, at % lay.small_len
            source_row, source_lane = place // LANES, place % LANES
            take = min(
                (row + 1) * LANES - at, lay.small_len - place, LANES - source_lane
            )
            target = at - row * LANES
            piece = buf[owner, lay.small_at : lay.small_at + 16, :].astype(F32)
            piece = piece[source_row : source_row + 1, :]
            shift = (target - source_lane) % LANES
            if shift:
                piece = pltpu.roll(piece, shift, 1)
            line = jnp.where((lane >= target) & (lane < target + take), piece, line)
            at += take
        flat_ref[row : row + 1, :] = line
    wire.finish()


def vmem():
    return pl.BlockSpec(memory_space=pltpu.VMEM)


def gather_weights(roles, sizes, lay, masters, smalls, lefts):
    count = gather_copies(roles) + exchange_copies(roles)
    nz, ny, nx, nc = (roles[role][2] for role in ("z", "y", "x", "c"))
    block = (BASE_ROWS, LANES)
    return pl.pallas_call(
        functools.partial(head_kernel, roles, sizes, lay),
        out_shape=tuple(jax.ShapeDtypeStruct((HEIGHT[n], WIDTH[n]), BF) for n in NAMES)
        + (
            jax.ShapeDtypeStruct((SMALL_ROWS, LANES), F32),
            jax.ShapeDtypeStruct((lay.count,) + block, BF),
        ),
        in_specs=[vmem()] * 11,
        out_specs=tuple([vmem()] * 7),
        scratch_shapes=[
            pltpu.VMEM((lay.count, lay.total, LANES), BF),
            pltpu.VMEM((nz, ny, nx, nc) + block, BF),
            pltpu.VMEM((nc, nz, ny, nx) + block, BF),
            pltpu.VMEM((nx, nc, nz, ny) + block, BF),
            pltpu.VMEM((ny, nx, nc, nz) + block, BF),
            pltpu.VMEM((nz, ny, nx, nc) + block, BF),
            pltpu.SemaphoreType.DMA((count,)),
            pltpu.SemaphoreType.DMA((count,)),
        ],
        compiler_params=pltpu.CompilerParams(
            collective_id=0, has_side_effects=True, vmem_limit_bytes=VMEM_LIMIT
        ),
        name="gather_weights",
    )(*masters, smalls.reshape(1, lay.small_len), *lefts)


def split(value):
    high = value.astype(BF)
    return jnp.concatenate([high, (value - high.astype(F32)).astype(BF)], axis=0)


def joined(value):
    half = value.shape[0] // 2
    return value[:half] + value[half:]


class Groups:
    def __init__(self, lay):
        self.lay = lay
        wide = [(name, i) for name in ("qkv", "out", "up") for i in range(WIDTH[name] // LANES)]
        self.members = [wide[i : i + 4] for i in range(0, len(wide), 4)]
        self.members += [[("down", i)] for i in range(WIDTH["down"] // LANES)]
        self.members += [[("pos", i) for i in range(WIDTH["pos"] // LANES)]]
        self.rows = [pad16(sum(lay.rows[name] for name, _ in group)) for group in self.members]
        self.starts = [sum(self.rows[:i]) for i in range(len(self.rows))]
        self.total = sum(self.rows)
        self.kinds = []
        self.kind_of = []
        for group, rows in zip(self.members, self.rows):
            kind = (tuple(name for name, _ in group), rows)
            if kind not in self.kinds:
                self.kinds.append(kind)
            self.kind_of.append(self.kinds.index(kind))

    def span(self, number):
        return slice(self.starts[number], self.starts[number] + self.rows[number])

    def spread(self, name, rows, place):
        own_rows = self.lay.rows[name]
        shape = (HEIGHT[name], self.lay.count * rows)
        row = lax.broadcasted_iota(jnp.int32, shape, 0)
        col = lax.broadcasted_iota(jnp.int32, shape, 1)
        owner = col // rows
        own = col - owner * rows - place * own_rows
        hit = (own >= 0) & (own < own_rows) & (owner * own_rows + own == row)
        return hit.astype(F32).astype(BF)

    def thin(self, number):
        names, rows = self.kinds[number]
        return sum(2 * self.lay.padded[name] for name in names), self.lay.count * rows


RIGHT_CHUNK = 384
STARTS = {"qkv": QKV_AT, "up": UP_AT, "out": OUT_AT, "down": DOWN_AT, "pos": POS_AT}


WIDE_AT = {"qkv": 0, "out": 3 * D, "up": 4 * D}


def packed_place(packed, name):
    if name in WIDE_AT:
        return packed[0], WIDE_AT[name]
    return packed[1 if name == "down" else 2], 0


def hand_out_kernel(lay, index_ref, small, *refs):
    packed, small_out = refs[:3], refs[3]
    outs = [dict(zip(NAMES, refs[4 + 5 * i : 9 + 5 * i])) for i in range(5)]
    at = index_ref[0] * lay.small_len
    row, shift = at // LANES, at % LANES
    lane = lax.broadcasted_iota(jnp.int32, (1, LANES), 1)
    for start in range(0, lay.small_len, LANES):
        near, far = (
            pltpu.roll(small[pl.ds(row + start // LANES + i, 1), :], LANES - shift, 1)
            for i in range(2)
        )
        take = min(LANES, lay.small_len - start)
        line = jnp.where(lane < LANES - shift, near, far)
        small_out[:, start : start + take] = line[:, :take]
    for name in NAMES:
        source, at = packed_place(packed, name)
        for kind in range(4):
            value = source[kind, : lay.rows[name], at : at + WIDTH[name]]
            outs[kind][name][...] = value
            if kind == 3:
                outs[4][name][...] = value.astype(BF)


def hand_out(lay, index, small, packed):
    shapes = [(lay.rows[n], WIDTH[n]) for n in NAMES]
    return pl.pallas_call(
        functools.partial(hand_out_kernel, lay),
        out_shape=(jax.ShapeDtypeStruct((1, lay.small_len), F32),)
        + tuple(jax.ShapeDtypeStruct(s, F32) for s in shapes * 4)
        + tuple(jax.ShapeDtypeStruct(s, BF) for s in shapes),
        in_specs=[pl.BlockSpec(memory_space=pltpu.SMEM)] + [vmem()] * 4,
        out_specs=tuple([vmem()] * 26),
        name="hand_out",
    )(index, small, *packed)


def tail_kernel(roles, sizes, lay, groups, extra, full_hbm, small, bases, *refs):
    rights_hbm, lefts, masters, firsts, seconds = (
        dict(zip(NAMES, refs[5 * i : 5 * i + 5])) for i in range(5)
    )
    small_out = refs[25]
    packed = refs[26:29]
    rest = refs[29:]

    def keep(kind, name, cols, value):
        target, at = packed_place(packed, name)
        target[kind, : value.shape[0], at + cols.start : at + cols.stop] = value

    full, acc, out_c, in_c, out_p, in_p, out_z, in_z, s_out, s_in = rest[:10]
    flat, steps, coarse = rest[10:13]
    rights = dict(zip(NAMES, rest[13:18]))
    picks = dict(zip(NAMES, rest[18:23]))
    thins = rest[23 : 23 + len(groups.kinds)]
    send_sems, recv_sems, full_sems, right_sems = rest[23 + len(groups.kinds) :]
    grid = Grid(roles, sizes)
    wire = Wire(grid, send_sems, recv_sems)
    me = grid.slot()

    plane = lay.count // grid.size("z")

    def full_copy(b):
        at = pl.multiple_of(flipped(grid.coord["z"], b, grid.size("z")) * plane, plane)
        part = pl.ds(at, plane)
        return pltpu.make_async_copy(full_hbm.at[part], full.at[part], full_sems.at[b])

    for b in (1, 2, 3, 0):
        full_copy(b).start()

    chunks = [(name, at) for name in NAMES for at in range(0, WIDTH[name], RIGHT_CHUNK)]

    def right_copy(number):
        name, at = chunks[number]
        return pltpu.make_async_copy(
            rights_hbm[name].at[pl.ds(at, RIGHT_CHUNK), :],
            coarse.at[number % 2, :, pl.ds(0, WIDTH[name])],
            right_sems.at[number],
        )

    def begin():
        right_copy(0).start()
        right_copy(1).start()

    def round_right(number):
        name, at = chunks[number]
        right_copy(number).wait()
        rights[name][at : at + RIGHT_CHUNK, :] = coarse[number % 2, :, : WIDTH[name]].astype(BF)
        if number + 2 < len(chunks):
            right_copy(number + 2).start()

    def make_pick(name):
        height, rows, padded = HEIGHT[name], lay.rows[name], lay.padded[name]
        row = lax.broadcasted_iota(jnp.int32, (padded, height), 0)
        col = lax.broadcasted_iota(jnp.int32, (padded, height), 1)
        pick = ((row < rows) & (col == me * rows + row)).astype(F32).astype(BF)
        base = bases[...].reshape(lay.count * BASE_ROWS, LANES).T
        places = [(*BASE_PLACE[name], rows, 0)] if name in BASE_PLACE else [
            (0, half * 48, rows // 2, half * (rows // 2)) for half in range(2)
        ]
        left_rows = None
        for top, at, height_part, first_row in places:
            shape = (height, lay.count * BASE_ROWS)
            to = lax.broadcasted_iota(jnp.int32, shape, 0)
            col = lax.broadcasted_iota(jnp.int32, shape, 1)
            owner = col // BASE_ROWS
            own = col - owner * BASE_ROWS - top
            hit = (own >= 0) & (own < height_part) & (owner * rows + first_row + own == to)
            term = nt(base[at : at + padded, :], hit.astype(F32).astype(BF))
            left_rows = term if left_rows is None else left_rows + term
        left_rows = left_rows.astype(BF)
        picks[name][:padded, :] = left_rows
        picks[name][padded:, :] = pick

    def make_thin(number):
        names, rows = groups.kinds[number]
        at = 0
        for place, name in enumerate(names):
            padded = lay.padded[name]
            left = split(pad_rows(lefts[name][...], padded))
            if len(names) > 1 or rows != lay.rows[name]:
                left = nn(left, groups.spread(name, rows, place)).astype(BF)
            thins[number][at : at + 2 * padded, :] = left
            at += 2 * padded

    duties = [begin] + [functools.partial(round_right, i) for i in range(len(chunks))]
    duties += [functools.partial(make_pick, name) for name in NAMES]
    duties += [functools.partial(make_thin, i) for i in range(len(groups.kinds))]

    def idle():
        if duties:
            duties.pop(0)()

    meet(grid)
    small_out[...] = jnp.zeros_like(small_out)

    def share():
        def done(total):
            flat[me] = total.astype(BF)

        yield from reduce_scatter(
            grid, wire, "sum", lambda slot: full[slot], out_c, in_c, out_p, in_p, out_z, in_z, acc,
            lambda b: full_copy(b).wait(), done,
        )
        yield from gather_all(grid, wire, flat, "flat")

    smalls = reduce_small(grid, wire, small, s_out, s_in, extra, small_out)
    together(share(), (smalls, 6), idle=idle, quiet=5)
    while duties:
        idle()

    def flat_block(block):
        height = flat.shape[1]
        pieces, at = [], block * D
        while at < (block + 1) * D:
            slot, row = at // height, at % height
            take = min((block + 1) * D - at, height - row)
            pieces.append(flat[slot, row : row + take, :])
            at += take
        return pieces[0] if len(pieces) == 1 else jnp.concatenate(pieces, axis=0)

    def step(tag, names):
        numbers = [
            (number, group)
            for number, group in enumerate(groups.members)
            if group[0][0] in names
        ]
        start = groups.starts[numbers[0][0]]
        end = groups.starts[numbers[-1][0]] + groups.rows[numbers[-1][0]]
        directions, partway = {}, {}
        for name in names:
            height, width = HEIGHT[name], WIDTH[name]
            rows, padded = lay.rows[name], lay.padded[name]
            lhs = picks[name][...]
            if name in ("down", "pos"):
                both = None
                for block in range(height // LANES):
                    part = nt(
                        lhs[:, block * LANES : (block + 1) * LANES], flat_block(STARTS[name] + block)
                    )
                    both = part if both is None else both + part
            else:
                both = jnp.concatenate(
                    [nn(lhs, flat_block(STARTS[name] + i)) for i in range(width // LANES)], axis=1
                )
            keep(0, name, slice(0, width), both[padded : padded + rows])
            terms = split(both[:padded])
            for at in range(0, width, D):
                cols = slice(at, at + D)
                rotated = joined(nn(terms, rights[name][:, cols]))[:rows]
                first = DECAY * firsts[name][:, cols] + (1.0 - DECAY) * rotated
                second = DECAY * seconds[name][:, cols] + (1.0 - DECAY) * rotated * rotated
                keep(1, name, cols, first)
                keep(2, name, cols, second)
                direction = first / (jnp.sqrt(second) + ADAM_EPSILON)
                for i in range(D // LANES):
                    directions[name, at // LANES + i] = direction[:, i * LANES : (i + 1) * LANES]
        for number, group in numbers:
            piece = jnp.concatenate([directions[member] for member in group], axis=0)
            steps[me, groups.span(number), :] = pad_rows(piece, groups.rows[number]).astype(BF)
        yield from gather_all(grid, wire, steps, tag, (start, end - start))
        for number, group in numbers:
            rows = groups.rows[number]
            piece = steps[:, groups.span(number), :].reshape(lay.count * rows, LANES)
            whole = nn(thins[groups.kind_of[number]][...], piece)
            at = 0
            for name, block in group:
                padded = lay.padded[name]
                partway[name, block] = joined(whole[at : at + 2 * padded])
                at += 2 * padded
        for name in names:
            height, width = HEIGHT[name], WIDTH[name]
            terms = split(
                jnp.concatenate([partway[name, i] for i in range(width // LANES)], axis=1)
            )
            rate = height ** (-0.5)
            for at in range(0, width, D):
                cols = slice(at, at + D)
                update = joined(nt(terms, rights[name][cols, :]))[: lay.rows[name]]
                master = masters[name][:, cols] * (1.0 - rate * WEIGHT_DECAY) - rate * update
                keep(3, name, cols, master)

    together(step("down steps", ("down", "pos")), step("wide steps", ("qkv", "out", "up")))
    wire.finish()


def finish_step(roles, sizes, lay, full, small, bases, rights, lefts, masters, firsts, seconds):
    slots, rows, _ = full.shape
    nz, ny, nx, nc = (roles[role][2] for role in ("z", "y", "x", "c"))
    count = reduce_copies(roles) + small_copies(roles) + 3 * gather_copies(roles)
    extra = {}
    for role in ("c", "y", "x", "z"):
        for offset in range(1, roles[role][2]):
            extra[(role, offset)] = len(extra)
    groups = Groups(lay)
    chunks = sum(WIDTH[name] // RIGHT_CHUNK for name in NAMES)
    anywhere = pl.BlockSpec(memory_space=pl.ANY)
    return pl.pallas_call(
        functools.partial(tail_kernel, roles, sizes, lay, groups, extra),
        out_shape=(
            jax.ShapeDtypeStruct((40, LANES), F32),
            jax.ShapeDtypeStruct((4, lay.padded["qkv"], 5 * D + 3 * D), F32),
            jax.ShapeDtypeStruct((4, lay.padded["down"], D), F32),
            jax.ShapeDtypeStruct((4, lay.padded["pos"], D), F32),
        ),
        in_specs=[anywhere, vmem(), vmem()] + [anywhere] * 5 + [vmem()] * 20,
        out_specs=tuple([vmem()] * 4),
        scratch_shapes=[
            pltpu.VMEM((slots, rows, LANES), F32),
            pltpu.VMEM((rows, LANES), F32),
            pltpu.VMEM((nc - 1, nz, ny, nx, rows, LANES), BF),
            pltpu.VMEM((nc - 1, nz, ny, nx, rows, LANES), BF),
            pltpu.VMEM((nz, ny, nx, rows, LANES), BF),
            pltpu.VMEM((nz, ny, nx, rows, LANES), BF),
            pltpu.VMEM((nz - 1, rows, LANES), BF),
            pltpu.VMEM((nz - 1, rows, LANES), BF),
            pltpu.VMEM((4, SMALL_ROWS, LANES), F32),
            pltpu.VMEM((len(extra), SMALL_ROWS, LANES), F32),
            pltpu.VMEM((slots, rows, LANES), BF),
            pltpu.VMEM((slots, groups.total, LANES), BF),
            pltpu.VMEM((2, RIGHT_CHUNK, FF), F32),
        ]
        + [pltpu.VMEM((WIDTH[name], WIDTH[name]), BF) for name in NAMES]
        + [pltpu.VMEM((2 * lay.padded[name], HEIGHT[name]), BF) for name in NAMES]
        + [pltpu.VMEM(groups.thin(i), BF) for i in range(len(groups.kinds))]
        + [
            pltpu.SemaphoreType.DMA((count,)),
            pltpu.SemaphoreType.DMA((count,)),
            pltpu.SemaphoreType.DMA((nz,)),
            pltpu.SemaphoreType.DMA((chunks,)),
        ],
        compiler_params=pltpu.CompilerParams(
            collective_id=1, has_side_effects=True, vmem_limit_bytes=VMEM_LIMIT
        ),
        name="finish_step",
    )(full, small, bases, *rights, *lefts, *masters, *firsts, *seconds)


AXES = ("dp", "fsdp")


def on_device(roles, sizes, tokens, centres, lengths, cotangent, smalls, *matrices):
    masters, firsts, seconds, lefts, rights = (matrices[5 * i : 5 * i + 5] for i in range(5))
    count = sizes["dp"] * sizes["fsdp"]
    heads = Layout(count, True)
    lay = Layout(count, False)
    *weights, small_rows, bases = gather_weights(roles, sizes, heads, masters, smalls, lefts)
    w_qkv, w_out, w_up, w_down, w_pos = weights
    layer_out, grad_tokens, full, small_grads = layer_pass(
        tokens, centres, lengths, cotangent, small_rows, w_qkv, w_out, w_up, w_down, w_pos
    )
    small_total, *packed = finish_step(
        roles,
        sizes,
        lay,
        full.reshape(count, FLAT_ROWS // count, LANES),
        small_grads,
        bases,
        rights,
        lefts,
        masters,
        firsts,
        seconds,
    )
    me = lax.axis_index("dp") * sizes["fsdp"] + lax.axis_index("fsdp")
    grad_smalls, *finished = hand_out(heads, me.reshape(1), small_total, packed)
    return (layer_out, grad_tokens, grad_smalls.reshape(heads.small_len), *finished)


def solution(mesh):
    sizes = {axis: mesh.shape[axis] for axis in AXES}
    rows, flat = P(AXES, None), P(AXES)
    return jax.shard_map(
        functools.partial(on_device, mesh_roles(mesh), sizes),
        mesh=mesh,
        in_specs=(rows, P(None, AXES), flat, rows, flat) + (rows,) * 20 + (P(),) * 5,
        out_specs=(rows, rows, flat) + (rows,) * 25,
        check_vma=False,
    )
```

```python
import functools
import jax
import jax.numpy as jnp
from jax import lax
from jax.experimental import pallas as pl
from jax.experimental.pallas import tpu as pltpu
from jax.sharding import PartitionSpec as P

D = 384
HEADS = 6
HEAD = 64
FF = 1536
PH = 128
LMAX = 256
LANES = 128
EPSILON = 1e-05
NEG_FILL = -1e30
HIGHEST = lax.Precision.HIGHEST
BF = jnp.bfloat16
F32 = jnp.float32

QKV_AT, UP_AT, OUT_AT, DOWN_AT, POS_AT, BLOCKS = 0, 9, 21, 24, 36, 37
FLAT_ROWS = 14336
SMALL_ROWS = 37


def nn(a, b):
    return jnp.dot(a, b, preferred_element_type=F32)


def nt(a, b):
    return lax.dot_general(a, b, (((1,), (1,)), ((), ())), preferred_element_type=F32)


def tn(a, b):
    return lax.dot_general(a, b, (((0,), (0,)), ((), ())), preferred_element_type=F32)


INV_SQRT2 = 0.7071067811865476
INV_SQRT_2PI = 0.3989422804014327


def gelu_pair(x):
    cdf = 0.5 * (1.0 + lax.erf(x * INV_SQRT2))
    pdf = jnp.exp(-0.5 * x * x) * INV_SQRT_2PI
    return x * cdf, cdf + x * pdf


def norm_parts(x):
    mean = jnp.mean(x, axis=-1, keepdims=True)
    centred = x - mean
    spread = jnp.mean(centred * centred, axis=-1, keepdims=True)
    inv = lax.rsqrt(spread + EPSILON)
    return centred * inv, inv


def thirds(value):
    terms = []
    for _ in range(3):
        term = value.astype(BF)
        terms.append(term)
        value = value - term.astype(F32)
    return terms


def col8(x):
    rows, cols = x.shape
    return jnp.sum(x.reshape(rows // 8, 8, cols), axis=0)


def layer_kernel(
    len_ref,
    tok_ref,
    cen_ref,
    cot_ref,
    small_ref,
    wqkv_ref,
    wout_ref,
    wup_ref,
    wdown_ref,
    wpos_ref,
    out_ref,
    gtok_ref,
    grad_ref,
    sgrad_ref,
    sacc,
    posh_s,
    emb_s,
    xh1_s,
    n1_s,
    qkv_s,
    p_s,
    att_s,
    bin_s,
    n2g_s,
    ff_s,
    qg_s,
    wide_s,
    ds_s,
    dq_s,
    ag_s,
    hid_s,
    act_s,
    low_s,
    hg_s,
    inv_s,
    xh2_s,
    gy_s,
    bgl_s,
    *,
    fc,
    group,
):
    step = pl.program_id(0)
    last = pl.num_programs(0) - 1

    @pl.when(step == 0)
    def _():
        grad_ref[...] = jnp.zeros_like(grad_ref)
        sacc[...] = jnp.zeros_like(sacc)

    rows = group * LMAX
    lengths = [len_ref[step * group + i] for i in range(group)]

    def live(width):
        return jnp.concatenate(
            [lax.broadcasted_iota(jnp.int32, (LMAX, width), 0) < length for length in lengths], axis=0
        )

    def vec(at, blocks):
        return jnp.concatenate([small_ref[at + i : at + i + 1, :] for i in range(blocks)], axis=1)

    def add_small(at, value):
        cols = value.shape[1]
        sacc[:, at * LANES : at * LANES + cols] += value

    def add_grad(block, value):
        for i in range(value.shape[1] // LANES):
            rows = slice((block + i) * D, (block + i + 1) * D)
            grad_ref[rows, :] += value[:, i * LANES : (i + 1) * LANES]

    gain_one, shift_one, gain_two, shift_two, attn_bias, down_bias, embed_bias = (
        vec(3 * i, 3) for i in range(7)
    )
    hidden_bias = small_ref[33:34, :]
    pos_first = small_ref[34:37, :]
    cen = cen_ref[...]

    cen_terms = jnp.concatenate(thirds(cen) + [jnp.zeros((7, rows), BF)], axis=0)
    first_terms = jnp.concatenate(
        [pos_first.astype(BF)] * 3 + [jnp.zeros((7, PH), BF)], axis=0
    )
    pos_hidden = tn(cen_terms, first_terms) + hidden_bias
    pos_act, pos_slope = gelu_pair(pos_hidden)
    pos_low = pos_act.astype(BF)
    posh_s[...] = pos_slope
    embedded = tok_ref[...].astype(F32) + nn(pos_low, wpos_ref[...]) + embed_bias
    emb_s[...] = embedded
    xhat_one, inv_one = norm_parts(embedded)
    xh1_s[...] = xhat_one
    n1 = (xhat_one * gain_one + shift_one).astype(BF)
    n1_s[...] = n1
    qkv_s[...] = nn(n1, wqkv_ref[...]).astype(BF)

    lane = lax.broadcasted_iota(jnp.int32, (1, LANES), 1)
    halves = [(lane < HEAD).astype(F32).astype(BF), (lane >= HEAD).astype(F32).astype(BF)]
    scale = HEAD ** (-0.5)
    scaled = [(h.astype(F32) * scale).astype(BF) for h in halves]

    key_live = [
        lax.broadcasted_iota(jnp.int32, (LMAX, LMAX), 0) < length for length in lengths
    ]
    spans = [slice(i * LMAX, (i + 1) * LMAX) for i in range(group)]

    heads = [(i, head) for head in range(HEADS) for i in range(group)]

    def lanes_of(which, i, head):
        at = which * D + head // 2 * LANES
        return qkv_s[spans[i], at : at + LANES]

    def staged(*stages):
        for turn in range(len(heads) + len(stages) - 1):
            for lag, stage in enumerate(stages):
                if 0 <= turn - lag < len(heads):
                    stage(turn - lag, *heads[turn - lag])

    def scores(number, i, head):
        wide_s[number % 3] = nt(lanes_of(1, i, head), lanes_of(0, i, head) * scaled[head % 2])

    def soften(number, i, head):
        s = jnp.where(key_live[i], wide_s[number % 3], NEG_FILL)
        e = jnp.exp(s - jnp.max(s, axis=0, keepdims=True))
        p_s[i * HEADS + head] = (e * (1.0 / jnp.sum(e, axis=0, keepdims=True))).astype(BF)

    def attend(number, i, head):
        at = head % 2 * HEAD
        o_t = nn(lanes_of(2, i, head).T[at : at + HEAD, :], p_s[i * HEADS + head])
        att_s[head * HEAD : (head + 1) * HEAD, spans[i]] = o_t.astype(BF)

    staged(scores, soften, attend)

    branch_in = emb_s[...] + tn(att_s[...], wout_ref[...]) + attn_bias
    bin_s[...] = branch_in
    xhat_two, inv_two = norm_parts(branch_in)
    xh2_s[...] = xhat_two
    n2 = (xhat_two * gain_two + shift_two).astype(BF)
    n2_t = n2.T
    gy = jnp.where(live(D), cot_ref[...].astype(F32), 0.0)
    gy_s[...] = gy
    gy_low = gy.astype(BF)
    gy_t = gy_low.T
    add_small(15, col8(gy))

    blocks = fc // LANES

    def widen(c):
        cols = slice(c * fc, (c + 1) * fc)
        hid_s[c % 2] = nn(n2, wup_ref[:, cols])
        act_s[c % 2] = nt(gy_low, wdown_ref[cols, :])

    def bend(c):
        cols = slice(c * fc, (c + 1) * fc)
        act, slope = gelu_pair(hid_s[c % 2] + vec(21 + c * blocks, blocks))
        low_s[:, cols] = act.astype(BF)
        hg = (act_s[c % 2] * slope).astype(BF)
        hg_s[:, cols] = hg
        add_small(21 + c * blocks, col8(hg.astype(F32)))

    def narrow(c):
        cols = slice(c * fc, (c + 1) * fc)
        add_grad(UP_AT + c * blocks, nn(n2_t, hg_s[:, cols]))
        add_grad(DOWN_AT + c * blocks, nn(gy_t, low_s[:, cols]))

    count = FF // fc
    for turn in range(count + 1):
        for lag, stage in enumerate((widen, bend)):
            if 0 <= turn - lag < count:
                stage(turn - lag)
    n2g_s[...] = nt(hg_s[...], wup_ref[...])
    ff_s[...] = nn(low_s[...], wdown_ref[...])

    out_ref[...] = (bin_s[...] + ff_s[...] + down_bias).astype(BF)

    inv_s[...] = inv_two
    parts = count
    height = rows // parts if rows % (16 * parts) == 0 else rows // 4
    for turn in range(max(count, rows // height)):
        if turn < rows // height:
            at = slice(turn * height, (turn + 1) * height)
            n2g = n2g_s[at, :]
            xhat_two = xh2_s[at, :]
            add_small(6, col8(n2g * xhat_two))
            add_small(9, col8(n2g))
            u = n2g * gain_two
            bg = gy_s[at, :] + inv_s[at, :] * (
                u
                - jnp.mean(u, axis=-1, keepdims=True)
                - xhat_two * jnp.mean(u * xhat_two, axis=-1, keepdims=True)
            )
            bin_s[at, :] = bg
            add_small(12, col8(bg))
            bgl_s[at, :] = bg.astype(BF)
        if turn < count:
            narrow(turn)
    bg_low = bgl_s[...]
    add_grad(OUT_AT, nn(att_s[...], bg_low))
    ag = nt(bg_low, wout_ref[...]).astype(BF)

    ag_s[...] = ag
    dk, dv = {}, {}

    def ago_of(i, head):
        at = head // 2 * LANES
        return ag_s[spans[i], at : at + LANES] * halves[head % 2]

    def probs_back(number, i, head):
        wide_s[number % 3] = nt(lanes_of(2, i, head), ago_of(i, head))

    def scores_back(number, i, head):
        p = p_s[i * HEADS + head].astype(F32)
        dp = wide_s[number % 3]
        rd = jnp.sum(p * dp, axis=0, keepdims=True)
        ds_s[number % 2] = (p * (dp - rd)).astype(BF)

    def heads_back(number, i, head):
        ds = ds_s[number % 2]
        at = head % 2 * HEAD
        dv[i, head] = nn(p_s[i * HEADS + head], ago_of(i, head))
        dk[i, head] = nn(ds, lanes_of(0, i, head) * scaled[head % 2])
        dq_t = nn(lanes_of(1, i, head).T[at : at + HEAD, :], ds) * scale
        dq_s[head * HEAD : (head + 1) * HEAD, spans[i]] = dq_t.astype(BF)
        if head % 2:
            at = head // 2 * LANES
            qg_s[spans[i], at : at + LANES] = dq_s[at : at + LANES, spans[i]].T
            for which, terms in ((1, dk), (2, dv)):
                total = terms.pop((i, head - 1)) + terms.pop((i, head))
                qg_s[spans[i], which * D + at : which * D + at + LANES] = total.astype(BF)

    staged(probs_back, scores_back, heads_back)

    qg = qg_s[...]
    n2g_s[...] = nt(qg, wqkv_ref[...])
    inv_s[...] = inv_one
    n1_t = n1_s[...].T
    height = rows // 4
    for turn in range(4):
        at = slice(turn * height, (turn + 1) * height)
        n1g = n2g_s[at, :]
        xhat = xh1_s[at, :]
        add_small(0, col8(n1g * xhat))
        add_small(3, col8(n1g))
        u = n1g * gain_one
        eg = bin_s[at, :] + inv_s[at, :] * (
            u
            - jnp.mean(u, axis=-1, keepdims=True)
            - xhat * jnp.mean(u * xhat, axis=-1, keepdims=True)
        )
        add_small(18, col8(eg))
        gtok_ref[at, :] = eg.astype(BF)
        if turn < 3:
            add_grad(QKV_AT + 3 * turn, nn(n1_t, qg_s[:, turn * D : (turn + 1) * D]))
    eg_low = gtok_ref[...]
    add_grad(POS_AT, tn(eg_low, pos_low))
    phg = nt(eg_low, wpos_ref[...]) * posh_s[...]
    add_small(33, col8(phg))
    products = nn(cen_terms, jnp.concatenate(thirds(phg), axis=1))
    pf_grad = products[:, :PH] + products[:, PH : 2 * PH] + products[:, 2 * PH :]
    for i in range(3):
        sacc[0:1, (34 + i) * LANES : (35 + i) * LANES] += (
            pf_grad[i : i + 1, :] + pf_grad[i + 3 : i + 4, :] + pf_grad[i + 6 : i + 7, :]
        )

    @pl.when(step == last)
    def _():
        for i in range(SMALL_ROWS):
            sgrad_ref[i : i + 1, :] = jnp.sum(
                sacc[:, i * LANES : (i + 1) * LANES], axis=0, keepdims=True
            )


def layer_pass(tokens, centres, lengths, cotangent, small_rows, wqkv, wout, wup, wdown, wpos, fc=256, group=2):
    clouds = lengths.shape[0]
    rows = clouds * LMAX
    span = group * LMAX
    whole = lambda shape: pl.BlockSpec(shape, lambda i, *_: (0, 0), pipeline_mode=pl.Buffered(1))
    tile = lambda: pl.BlockSpec((span, D), lambda i, *_: (i, 0))
    return pl.pallas_call(
        functools.partial(layer_kernel, fc=fc, group=group),
        out_shape=(
            jax.ShapeDtypeStruct((rows, D), BF),
            jax.ShapeDtypeStruct((rows, D), BF),
            jax.ShapeDtypeStruct((FLAT_ROWS, LANES), F32),
            jax.ShapeDtypeStruct((SMALL_ROWS, LANES), F32),
        ),
        grid_spec=pltpu.PrefetchScalarGridSpec(
            num_scalar_prefetch=1,
            grid=(clouds // group,),
            in_specs=[
                tile(),
                pl.BlockSpec((3, span), lambda i, *_: (0, i)),
                tile(),
                whole((SMALL_ROWS, LANES)),
                whole((D, 3 * D)),
                whole((D, D)),
                whole((D, FF)),
                whole((FF, D)),
                whole((PH, D)),
            ],
            out_specs=[
                tile(),
                tile(),
                whole((FLAT_ROWS, LANES)),
                whole((SMALL_ROWS, LANES)),
            ],
            scratch_shapes=[
                pltpu.VMEM((8, SMALL_ROWS * LANES), F32),
                pltpu.VMEM((span, PH), F32),
                pltpu.VMEM((span, D), F32),
                pltpu.VMEM((span, D), F32),
                pltpu.VMEM((span, D), BF),
                pltpu.VMEM((span, 3 * D), BF),
                pltpu.VMEM((group * HEADS, LMAX, LMAX), BF),
                pltpu.VMEM((D, span), BF),
                pltpu.VMEM((span, D), F32),
                pltpu.VMEM((span, D), F32),
                pltpu.VMEM((span, D), F32),
                pltpu.VMEM((span, 3 * D), BF),
                pltpu.VMEM((3, LMAX, LMAX), F32),
                pltpu.VMEM((2, LMAX, LMAX), BF),
                pltpu.VMEM((D, span), BF),
                pltpu.VMEM((span, D), BF),
                pltpu.VMEM((2, span, fc), F32),
                pltpu.VMEM((2, span, fc), F32),
                pltpu.VMEM((span, FF), BF),
                pltpu.VMEM((span, FF), BF),
                pltpu.VMEM((span, 1), F32),
                pltpu.VMEM((span, D), F32),
                pltpu.VMEM((span, D), F32),
                pltpu.VMEM((span, D), BF),
            ],
        ),
        compiler_params=pltpu.CompilerParams(vmem_limit_bytes=60 * 1024 * 1024),
        name="layer",
    )(lengths, tokens, centres, cotangent, small_rows, wqkv, wout, wup, wdown, wpos)


MESH_ID = pl.DeviceIdType.MESH


def mesh_roles(mesh):
    dp, fs = mesh.shape["dp"], mesh.shape["fsdp"]
    if dp >= 32:
        return {
            "z": ("dp", dp // 4 // 2, 4) if dp == 32 else ("dp", 8, dp // 8),
            "y": ("dp", 2, 4),
            "c": ("dp", 1, 2),
            "x": ("fsdp", 1, fs),
        }
    return {
        "z": ("dp", 2, dp // 2),
        "y": ("dp", 1, 2),
        "x": ("fsdp", 2, fs // 2),
        "c": ("fsdp", 1, 2),
    }


def flipped(coord, offset, size):
    if offset == 0:
        return coord
    if size == 2:
        return 1 - coord
    return {1: coord + 1 - 2 * (coord % 2), 2: (coord + 2) % 4, 3: 3 - coord}[offset]


class Grid:
    def __init__(self, roles, sizes):
        self.roles, self.sizes = roles, sizes
        self.index = {axis: lax.axis_index(axis) for axis in sizes}
        self.coord = {
            role: (self.index[axis] // stride) % size
            for role, (axis, stride, size) in roles.items()
        }

        z = self.z = self.coord["z"]
        self.line = [z] + [self.by_z(*row) for row in ((1, 0, 1, 2), (2, 2, 3, 1), (3, 3, 0, 0))]
        self.came_by = [self.by_z(*row) for row in ((1, 0, 1, 2), (1, 2, 3, 2), (1, 2, 1, 2))]
        self.inbox = [self.by_z(*row) for row in ((1, 0, 0, 0), (3, 1, 1, 2), (4, 3, 2, 4))]
        self.inner = z // 2 + z % 2 == 1

    def by_z(self, *values):
        high, low = self.coord["z"] // 2, self.coord["z"] % 2
        return (1 - high) * ((1 - low) * values[0] + low * values[1]) + high * (
            (1 - low) * values[2] + low * values[3]
        )

    def at_z(self, coordinate):
        axis, stride, _ = self.roles["z"]
        return {**self.index, axis: self.index[axis] + (coordinate - self.z) * stride}

    def place(self, line=0, **offsets):
        at = self.at_z(self.line[line]) if line else dict(self.index)
        for role, offset in offsets.items():
            axis, stride, size = self.roles[role]
            other = flipped(self.coord[role], offset, size)
            at[axis] = at[axis] + (other - self.coord[role]) * stride
        return at

    def slot(self, **offsets):
        at = self.place(**offsets)
        return at["dp"] * self.sizes["fsdp"] + at["fsdp"]

    def size(self, role):
        return self.roles[role][2]

    def offsets(self, role):
        return range(1, self.size(role))


class Wire:
    def __init__(self, grid, send_sems, recv_sems):
        self.grid, self.send_sems, self.recv_sems = grid, send_sems, recv_sems
        self.count = 0
        self.copies = {}

    def reserve(self, count):
        self.count += count
        return self.count - count

    def make(self, number, into, source, target, place):
        return pltpu.make_async_remote_copy(
            src_ref=source,
            dst_ref=target,
            send_sem=self.send_sems.at[number],
            recv_sem=self.recv_sems.at[into],
            device_id=place,
            device_id_type=MESH_ID,
        )

    def send_to(self, key, number, into, source, target, place, when=None):
        make = functools.partial(self.make, number, into, source, target, place)
        if when is None:
            make().start()
        else:
            pl.when(when)(lambda: make().start())
        assert key not in self.copies
        self.copies[key] = (make, when)

    def send(self, key, source, target, **offsets):
        number = self.reserve(1)
        self.send_to(key, number, number, source, target, self.grid.place(**offsets))

    def arrived(self, key):
        self.copies[key][0]().wait_recv()

    def arrived_at(self, number, target):
        self.make(number, number, target, target, self.grid.place(c=1)).wait_recv()

    def finish(self):
        for make, when in self.copies.values():
            if when is None:
                make().wait_send()
            else:
                pl.when(when)(lambda make=make: make().wait_send())


def meet(grid):
    barrier = pltpu.get_barrier_semaphore()
    count = 0
    for role in ("z", "y", "x", "c"):
        for offset in grid.offsets(role):
            pl.semaphore_signal(
                barrier,
                inc=1,
                device_id=grid.place(**{role: offset}),
                device_id_type=MESH_ID,
            )
            count += 1
    pl.semaphore_wait(barrier, count)


def gather_copies(roles):
    nz, ny, nx, nc = (roles[role][2] for role in ("z", "y", "x", "c"))
    plane = (ny - 1) + (nx - 1) + 2 * (ny - 1) * (nx - 1)
    core = (nc - 1) * (1 + plane)
    return 5 + nz * (plane + core)


def nothing():
    pass


def gather_all(grid, wire, buf, tag, rows=None):
    start, rows = (0, buf.shape[1]) if rows is None else rows
    half = rows // 32 * 16
    parts = {
        None: pl.ds(start, rows),
        "a": pl.ds(start, half),
        "b": pl.ds(start + half, rows - half),
    }

    def pass_on(key, slot, part, **offsets):
        ref = buf.at[slot, parts[part]]
        wire.send((tag,) + key, ref, ref, **offsets)

    def arrived(*key):
        wire.arrived((tag,) + key)

    ys, xs, cs = ([*grid.offsets(role)] for role in ("y", "x", "c"))

    def to_core(key, slot, part=None):
        for c in cs:
            pass_on(("c", c) + key, slot, part, c=c)

    def have(b):
        slot = grid.slot(line=b)
        for y in ys:
            pass_on(("y", b, y), slot, None, y=y)
        for x in xs:
            pass_on(("x", b, x), slot, None, x=x)
        to_core((b, 0, 0, 0), slot)

    def relay(b):
        for y in ys:
            yield
            arrived("y", b, y)
            for x in xs:
                pass_on(("a", b, y, x), grid.slot(line=b, y=y), "a", x=x)
            to_core((b, y, 0, 0), grid.slot(line=b, y=y))
        for x in xs:
            yield
            arrived("x", b, x)
            for y in ys:
                pass_on(("b", b, y, x), grid.slot(line=b, x=x), "b", y=y)
            to_core((b, 0, x, 0), grid.slot(line=b, x=x))

    base = wire.reserve(5)
    z = grid.z

    def along(site, line, target, into, when):
        ref = buf.at[grid.slot(line=line), parts[None]]
        place = grid.at_z(target)
        wire.send_to((tag, "z", site), base + site, base + into, ref, ref, place, when)

    along(0, 0, z + 1, 0, z < 3)
    along(1, 0, z - 1, z // 2, z > 0)
    have(0)
    onward = ((z + 1, 3 - z), (z - 1, z), (3 * (z - 1), 2))
    for b in (1, 2, 3):
        yield
        wire.arrived_at(base + b - 1, buf.at[grid.slot(line=b), parts[None]])
        along(1 + b, b, *onward[b - 1], grid.inner)
        have(b)
        yield from relay(b - 1)
    yield from relay(3)
    for b in range(4):
        for y in ys:
            for x in xs:
                for part in ("a", "b"):
                    yield
                    arrived(part, b, y, x)
                    to_core((b, y, x, part), grid.slot(line=b, y=y, x=x), part)
    yield
    for key in list(wire.copies):
        if key[:2] == (tag, "c"):
            wire.arrived(key)


def together(*chains, idle=nothing, quiet=0):
    chains = [chain if isinstance(chain, tuple) else (chain, 1) for chain in chains]
    turn = 0
    while chains:
        for chain in list(chains):
            if turn % chain[1] == 0 or len(chains) == 1:
                try:
                    next(chain[0])
                except StopIteration:
                    chains.remove(chain)
        if turn >= quiet:
            idle()
        turn += 1


def exchange_copies(roles):
    return sum(roles[role][2] - 1 for role in ("c", "x", "y", "z"))


def exchange_all(grid, wire, tag, blocks, pack):
    pack()
    for stage, role in enumerate(("c", "x", "y", "z")):
        source, target = blocks[stage], blocks[stage + 1]
        coord, size = grid.coord[role], grid.size(role)
        for offset in grid.offsets(role):
            part = source.at[:, :, :, flipped(coord, offset, size)]
            wire.send((tag, role, offset), part, target.at[offset], **{role: offset})
        target[0] = source[:, :, :, coord]
        yield
        for offset in grid.offsets(role):
            wire.arrived((tag, role, offset))


def reduce_copies(roles):
    nz, ny, nx, nc = (roles[role][2] for role in ("z", "y", "x", "c"))
    plane = (ny - 1) + (nx - 1) + 2 * (ny - 1) * (nx - 1)
    return (nc - 1) * nz * ny * nx + nz * plane + 5


def small_copies(roles):
    return sum(roles[role][2] - 1 for role in ("z", "y", "x", "c"))


def reduce_small(grid, wire, small, s_out, s_in, numbers, result):
    value = small[...]
    for stage, role in enumerate(("c", "y", "x", "z")):
        s_out[stage] = value
        for offset in grid.offsets(role):
            number = numbers[role, offset]
            wire.send(("s", role, offset), s_out.at[stage], s_in.at[number], **{role: offset})
        yield
        for offset in grid.offsets(role):
            wire.arrived(("s", role, offset))
            value = value + s_in[numbers[role, offset]]
    result[: value.shape[0], :] = value


def reduce_scatter(grid, wire, tag, take, out_c, in_c, out_p, in_p, out_z, in_z, acc, ready, done):
    rows = acc.shape[0]
    half = rows // 32 * 16
    first, second = pl.ds(0, half), pl.ds(half, rows - half)
    zs, ys, xs, cs = ([*grid.offsets(role)] for role in ("z", "y", "x", "c"))
    order = zs + [0]

    def send(key, source, target, **offsets):
        wire.send((tag,) + key, source, target, **offsets)

    def arrived(*key):
        wire.arrived((tag,) + key)

    def core_sum(b, y, x):
        value = take(grid.slot(z=b, y=y, x=x))
        for c in cs:
            arrived("c", c, b, y, x)
            value = value + in_c[c - 1, b, y, x].astype(F32)
        return value

    def to_core(b):
        ready(b)
        for y in [*ys, 0]:
            for x in [*xs, 0]:
                for c in cs:
                    out_c[c - 1, b, y, x] = take(grid.slot(z=b, y=y, x=x, c=c)).astype(BF)
                    send(("c", c, b, y, x), out_c.at[c - 1, b, y, x], in_c.at[c - 1, b, y, x], c=c)

    def diagonal(b):
        for y in ys:
            for x in xs:
                out_p[b, y, x] = core_sum(b, y, x).astype(BF)
                send(("a", b, y, x), out_p.at[b, y, x, first], in_p.at[b, y, x, first], x=x)
                send(("b", b, y, x), out_p.at[b, y, x, second], in_p.at[b, y, x, second], y=y)

    def neighbour(b):
        for y in ys:
            acc[...] = core_sum(b, y, 0)
            for x in xs:
                arrived("a", b, y, x)
                acc[first, :] += in_p[b, y, x, first].astype(F32)
            out_p[b, y, 0] = acc[...].astype(BF)
            send(("y", b, y), out_p.at[b, y, 0], in_p.at[b, y, 0], y=y)
        for x in xs:
            acc[...] = core_sum(b, 0, x)
            for y in ys:
                arrived("b", b, y, x)
                acc[second, :] += in_p[b, y, x, second].astype(F32)
            out_p[b, 0, x] = acc[...].astype(BF)
            send(("x", b, x), out_p.at[b, 0, x], in_p.at[b, 0, x], x=x)

    def plane_sum(b):
        value = core_sum(b, 0, 0)
        for y in ys:
            arrived("y", b, y)
            value = value + in_p[b, y, 0].astype(F32)
        for x in xs:
            arrived("x", b, x)
            value = value + in_p[b, 0, x].astype(F32)
        return value

    for b in order:
        to_core(b)
        yield
    for turn in range(len(order) + 2):
        if turn < len(order):
            yield
            diagonal(order[turn])
        if 1 <= turn <= len(order):
            yield
            neighbour(order[turn - 1])
        if turn >= 2:
            yield
            b = order[turn - 2]
            value = plane_sum(b)
            if b:
                out_z[b - 1] = value.astype(BF)
                send(("z", b), out_z.at[b - 1], in_z.at[b - 1], z=b)
            else:
                acc[...] = value
    yield
    for b in zs:
        arrived("z", b)
        acc[...] += in_z[b - 1].astype(F32)
    done(acc[...])


DECAY = 0.5
ADAM_EPSILON = 1e-08
WEIGHT_DECAY = 0.05
VMEM_LIMIT = 60 * 1024 * 1024
NAMES = ("qkv", "out", "up", "down", "pos")
BASE_PLACE = {"qkv": (0, 96), "out": (0, 112), "up": (16, 96), "pos": (16, 112)}
BASE_ROWS = 32
HEIGHT = {"qkv": D, "out": D, "up": D, "down": FF, "pos": PH}
WIDTH = {"qkv": 3 * D, "out": D, "up": FF, "down": D, "pos": D}
SMALLS = SMALL_ROWS * LANES


def pad16(rows):
    return -(-rows // 16) * 16


class Layout:
    def __init__(self, count, smalls):
        self.count = count
        self.rows = {name: HEIGHT[name] // count for name in NAMES}
        self.padded = {name: pad16(self.rows[name]) for name in NAMES}
        self.start = {}
        at = 0
        for name in NAMES:
            self.start[name] = at
            at += self.padded[name] * (WIDTH[name] // LANES)
        self.small_at = at
        self.small_len = SMALLS // count
        if smalls:
            at += 16
        self.total = at

    def span(self, name, block):
        at = self.start[name] + block * self.padded[name]
        return slice(at, at + self.padded[name])

    def spread(self, name):
        rows, padded = self.rows[name], self.padded[name]
        shape = (HEIGHT[name], self.count * padded)
        row = lax.broadcasted_iota(jnp.int32, shape, 0)
        col = lax.broadcasted_iota(jnp.int32, shape, 1)
        own, owner = col % padded, col // padded
        hit = (own < rows) & (owner * rows + own == row)
        return hit.astype(F32).astype(BF)


def pad_rows(value, rows):
    have = value.shape[0]
    if have == rows:
        return value
    return jnp.concatenate([value, jnp.zeros((rows - have, value.shape[1]), value.dtype)], axis=0)


def once(action):
    pending = [action]

    def run():
        if pending:
            pending.pop()()

    return run


def head_kernel(roles, sizes, lay, *refs):
    masters = dict(zip(NAMES, refs[:5]))
    small_ref = refs[5]
    lefts = dict(zip(NAMES, refs[6:11]))
    outs = dict(zip(NAMES, refs[11:16]))
    flat_ref, bases, buf = refs[16:19]
    blocks, (send_sems, recv_sems) = refs[19:24], refs[24:]
    grid = Grid(roles, sizes)
    wire = Wire(grid, send_sems, recv_sems)
    own = grid.slot()
    for name in NAMES:
        for block in range(WIDTH[name] // LANES):
            piece = masters[name][:, block * LANES : (block + 1) * LANES]
            buf[own, lay.span(name, block), :] = pad_rows(piece, lay.padded[name]).astype(BF)
    lines = []
    for at in range(0, lay.small_len, LANES):
        line = small_ref[:, at : min(at + LANES, lay.small_len)]
        if line.shape[1] < LANES:
            line = jnp.concatenate([line, jnp.zeros((1, LANES - line.shape[1]), F32)], axis=1)
        lines.append(line)
    lines = jnp.concatenate(lines, axis=0)
    buf[own, lay.small_at : lay.small_at + 16, :] = pad_rows(lines, 16).astype(BF)

    def pack_bases():
        lane = lax.broadcasted_iota(jnp.int32, (1, LANES), 1)

        def piece(name, owner, target):
            width = lay.rows[name]
            at = owner * width
            tile, place = at // LANES * LANES, at % LANES
            value = lefts[name][:, tile : tile + LANES]
            shift = (target - place) % LANES
            value = pltpu.roll(value, shift, 1) if shift else value
            if place + width > LANES:
                after = lefts[name][:, tile + LANES : tile + 2 * LANES]
                after = pltpu.roll(after, shift, 1) if shift else after
                value = jnp.where(lane < target + LANES - place, value, after)
            value = jnp.where((lane >= target) & (lane < target + width), value, 0.0)
            return value

        for owner in range(lay.count):
            index = {"dp": owner // sizes["fsdp"], "fsdp": owner % sizes["fsdp"]}
            z, y, x, core = (
                index[axis] // stride % size
                for axis, stride, size in (roles[role] for role in ("z", "y", "x", "c"))
            )
            half = lay.rows["down"] // 2
            value = pad_rows(
                piece("down", owner, 0)[:half] + piece("down", owner, 48)[half:], BASE_ROWS
            )
            for name, (top, target) in BASE_PLACE.items():
                below = piece(name, owner, target)
                if top:
                    below = jnp.concatenate([jnp.zeros((top, LANES), F32), below], axis=0)
                value = value + pad_rows(below, BASE_ROWS)
            blocks[0][z, y, x, core] = value.astype(BF)

    meet(grid)
    together(
        gather_all(grid, wire, buf, "w"),
        (exchange_all(grid, wire, "e", blocks, pack_bases), 3),
    )
    nz, ny, nx, nc = (grid.size(role) for role in ("z", "y", "x", "c"))
    for z in range(nz):
        for y in range(ny):
            for x in range(nx):
                for core in range(nc):
                    bases[grid.slot(z=z, y=y, x=x, c=core)] = blocks[4][z, y, x, core]
    for name in NAMES:
        spread = None if lay.rows[name] == lay.padded[name] else lay.spread(name)
        for block in range(WIDTH[name] // LANES):
            piece = buf[:, lay.span(name, block), :].reshape(lay.count * lay.padded[name], LANES)
            if spread is not None:
                piece = nn(spread, piece).astype(BF)
            outs[name][:, block * LANES : (block + 1) * LANES] = piece
    lane = lax.broadcasted_iota(jnp.int32, (1, LANES), 1)
    for row in range(SMALL_ROWS):
        line = jnp.zeros((1, LANES), F32)
        at = row * LANES
        while at < (row + 1) * LANES:
            owner, place = at // lay.small_len, at % lay.small_len
            source_row, source_lane = place // LANES, place % LANES
            take = min(
                (row + 1) * LANES - at, lay.small_len - place, LANES - source_lane
            )
            target = at - row * LANES
            piece = buf[owner, lay.small_at : lay.small_at + 16, :].astype(F32)
            piece = piece[source_row : source_row + 1, :]
            shift = (target - source_lane) % LANES
            if shift:
                piece = pltpu.roll(piece, shift, 1)
            line = jnp.where((lane >= target) & (lane < target + take), piece, line)
            at += take
        flat_ref[row : row + 1, :] = line
    wire.finish()


def vmem():
    return pl.BlockSpec(memory_space=pltpu.VMEM)


def gather_weights(roles, sizes, lay, masters, smalls, lefts):
    count = gather_copies(roles) + exchange_copies(roles)
    nz, ny, nx, nc = (roles[role][2] for role in ("z", "y", "x", "c"))
    block = (BASE_ROWS, LANES)
    return pl.pallas_call(
        functools.partial(head_kernel, roles, sizes, lay),
        out_shape=tuple(jax.ShapeDtypeStruct((HEIGHT[n], WIDTH[n]), BF) for n in NAMES)
        + (
            jax.ShapeDtypeStruct((SMALL_ROWS, LANES), F32),
            jax.ShapeDtypeStruct((lay.count,) + block, BF),
        ),
        in_specs=[vmem()] * 11,
        out_specs=tuple([vmem()] * 7),
        scratch_shapes=[
            pltpu.VMEM((lay.count, lay.total, LANES), BF),
            pltpu.VMEM((nz, ny, nx, nc) + block, BF),
            pltpu.VMEM((nc, nz, ny, nx) + block, BF),
            pltpu.VMEM((nx, nc, nz, ny) + block, BF),
            pltpu.VMEM((ny, nx, nc, nz) + block, BF),
            pltpu.VMEM((nz, ny, nx, nc) + block, BF),
            pltpu.SemaphoreType.DMA((count,)),
            pltpu.SemaphoreType.DMA((count,)),
        ],
        compiler_params=pltpu.CompilerParams(
            collective_id=0, has_side_effects=True, vmem_limit_bytes=VMEM_LIMIT
        ),
        name="gather_weights",
    )(*masters, smalls.reshape(1, lay.small_len), *lefts)


def split(value):
    high = value.astype(BF)
    return jnp.concatenate([high, (value - high.astype(F32)).astype(BF)], axis=0)


def joined(value):
    half = value.shape[0] // 2
    return value[:half] + value[half:]


class Groups:
    def __init__(self, lay):
        self.lay = lay
        wide = [(name, i) for name in ("qkv", "out", "up") for i in range(WIDTH[name] // LANES)]
        self.members = [wide[i : i + 4] for i in range(0, len(wide), 4)]
        self.members += [[("down", i)] for i in range(WIDTH["down"] // LANES)]
        self.members += [[("pos", i) for i in range(WIDTH["pos"] // LANES)]]
        self.rows = [pad16(sum(lay.rows[name] for name, _ in group)) for group in self.members]
        self.starts = [sum(self.rows[:i]) for i in range(len(self.rows))]
        self.total = sum(self.rows)
        self.kinds = []
        self.kind_of = []
        for group, rows in zip(self.members, self.rows):
            kind = (tuple(name for name, _ in group), rows)
            if kind not in self.kinds:
                self.kinds.append(kind)
            self.kind_of.append(self.kinds.index(kind))

    def span(self, number):
        return slice(self.starts[number], self.starts[number] + self.rows[number])

    def spread(self, name, rows, place):
        own_rows = self.lay.rows[name]
        shape = (HEIGHT[name], self.lay.count * rows)
        row = lax.broadcasted_iota(jnp.int32, shape, 0)
        col = lax.broadcasted_iota(jnp.int32, shape, 1)
        owner = col // rows
        own = col - owner * rows - place * own_rows
        hit = (own >= 0) & (own < own_rows) & (owner * own_rows + own == row)
        return hit.astype(F32).astype(BF)

    def thin(self, number):
        names, rows = self.kinds[number]
        return sum(2 * self.lay.padded[name] for name in names), self.lay.count * rows


RIGHT_CHUNK = 384
STARTS = {"qkv": QKV_AT, "up": UP_AT, "out": OUT_AT, "down": DOWN_AT, "pos": POS_AT}


WIDE_AT = {"qkv": 0, "out": 3 * D, "up": 4 * D}


def packed_place(packed, name):
    if name in WIDE_AT:
        return packed[0], WIDE_AT[name]
    return packed[1 if name == "down" else 2], 0


def hand_out_kernel(lay, index_ref, small, *refs):
    packed, small_out = refs[:3], refs[3]
    outs = [dict(zip(NAMES, refs[4 + 5 * i : 9 + 5 * i])) for i in range(5)]
    at = index_ref[0] * lay.small_len
    row, shift = at // LANES, at % LANES
    lane = lax.broadcasted_iota(jnp.int32, (1, LANES), 1)
    for start in range(0, lay.small_len, LANES):
        near, far = (
            pltpu.roll(small[pl.ds(row + start // LANES + i, 1), :], LANES - shift, 1)
            for i in range(2)
        )
        take = min(LANES, lay.small_len - start)
        line = jnp.where(lane < LANES - shift, near, far)
        small_out[:, start : start + take] = line[:, :take]
    for name in NAMES:
        source, at = packed_place(packed, name)
        for kind in range(4):
            value = source[kind, : lay.rows[name], at : at + WIDTH[name]]
            outs[kind][name][...] = value
            if kind == 3:
                outs[4][name][...] = value.astype(BF)


def hand_out(lay, index, small, packed):
    shapes = [(lay.rows[n], WIDTH[n]) for n in NAMES]
    return pl.pallas_call(
        functools.partial(hand_out_kernel, lay),
        out_shape=(jax.ShapeDtypeStruct((1, lay.small_len), F32),)
        + tuple(jax.ShapeDtypeStruct(s, F32) for s in shapes * 4)
        + tuple(jax.ShapeDtypeStruct(s, BF) for s in shapes),
        in_specs=[pl.BlockSpec(memory_space=pltpu.SMEM)] + [vmem()] * 4,
        out_specs=tuple([vmem()] * 26),
        name="hand_out",
    )(index, small, *packed)


def tail_kernel(roles, sizes, lay, groups, extra, full_hbm, small, bases, *refs):
    rights_hbm, lefts, masters, firsts, seconds = (
        dict(zip(NAMES, refs[5 * i : 5 * i + 5])) for i in range(5)
    )
    small_out = refs[25]
    packed = refs[26:29]
    rest = refs[29:]

    def keep(kind, name, cols, value):
        target, at = packed_place(packed, name)
        target[kind, : value.shape[0], at + cols.start : at + cols.stop] = value

    full, acc, out_c, in_c, out_p, in_p, out_z, in_z, s_out, s_in = rest[:10]
    flat, steps, coarse = rest[10:13]
    rights = dict(zip(NAMES, rest[13:18]))
    picks = dict(zip(NAMES, rest[18:23]))
    thins = rest[23 : 23 + len(groups.kinds)]
    send_sems, recv_sems, full_sems, right_sems = rest[23 + len(groups.kinds) :]
    grid = Grid(roles, sizes)
    wire = Wire(grid, send_sems, recv_sems)
    me = grid.slot()

    plane = lay.count // grid.size("z")

    def full_copy(b):
        at = pl.multiple_of(flipped(grid.coord["z"], b, grid.size("z")) * plane, plane)
        part = pl.ds(at, plane)
        return pltpu.make_async_copy(full_hbm.at[part], full.at[part], full_sems.at[b])

    for b in (1, 2, 3, 0):
        full_copy(b).start()

    chunks = [(name, at) for name in NAMES for at in range(0, WIDTH[name], RIGHT_CHUNK)]

    def right_copy(number):
        name, at = chunks[number]
        return pltpu.make_async_copy(
            rights_hbm[name].at[pl.ds(at, RIGHT_CHUNK), :],
            coarse.at[number % 2, :, pl.ds(0, WIDTH[name])],
            right_sems.at[number],
        )

    def begin():
        right_copy(0).start()
        right_copy(1).start()

    def round_right(number):
        name, at = chunks[number]
        right_copy(number).wait()
        rights[name][at : at + RIGHT_CHUNK, :] = coarse[number % 2, :, : WIDTH[name]].astype(BF)
        if number + 2 < len(chunks):
            right_copy(number + 2).start()

    def make_pick(name):
        height, rows, padded = HEIGHT[name], lay.rows[name], lay.padded[name]
        row = lax.broadcasted_iota(jnp.int32, (padded, height), 0)
        col = lax.broadcasted_iota(jnp.int32, (padded, height), 1)
        pick = ((row < rows) & (col == me * rows + row)).astype(F32).astype(BF)
        base = bases[...].reshape(lay.count * BASE_ROWS, LANES).T
        places = [(*BASE_PLACE[name], rows, 0)] if name in BASE_PLACE else [
            (0, half * 48, rows // 2, half * (rows // 2)) for half in range(2)
        ]
        left_rows = None
        for top, at, height_part, first_row in places:
            shape = (height, lay.count * BASE_ROWS)
            to = lax.broadcasted_iota(jnp.int32, shape, 0)
            col = lax.broadcasted_iota(jnp.int32, shape, 1)
            owner = col // BASE_ROWS
            own = col - owner * BASE_ROWS - top
            hit = (own >= 0) & (own < height_part) & (owner * rows + first_row + own == to)
            term = nt(base[at : at + padded, :], hit.astype(F32).astype(BF))
            left_rows = term if left_rows is None else left_rows + term
        left_rows = left_rows.astype(BF)
        picks[name][:padded, :] = left_rows
        picks[name][padded:, :] = pick

    def make_thin(number):
        names, rows = groups.kinds[number]
        at = 0
        for place, name in enumerate(names):
            padded = lay.padded[name]
            left = split(pad_rows(lefts[name][...], padded))
            if len(names) > 1 or rows != lay.rows[name]:
                left = nn(left, groups.spread(name, rows, place)).astype(BF)
            thins[number][at : at + 2 * padded, :] = left
            at += 2 * padded

    duties = [begin] + [functools.partial(round_right, i) for i in range(len(chunks))]
    duties += [functools.partial(make_pick, name) for name in NAMES]
    duties += [functools.partial(make_thin, i) for i in range(len(groups.kinds))]

    def idle():
        if duties:
            duties.pop(0)()

    meet(grid)
    small_out[...] = jnp.zeros_like(small_out)

    def share():
        def done(total):
            flat[me] = total.astype(BF)

        yield from reduce_scatter(
            grid, wire, "sum", lambda slot: full[slot], out_c, in_c, out_p, in_p, out_z, in_z, acc,
            lambda b: full_copy(b).wait(), done,
        )
        yield from gather_all(grid, wire, flat, "flat")

    smalls = reduce_small(grid, wire, small, s_out, s_in, extra, small_out)
    together(share(), (smalls, 6), idle=idle, quiet=5)
    while duties:
        idle()

    def flat_block(block):
        height = flat.shape[1]
        pieces, at = [], block * D
        while at < (block + 1) * D:
            slot, row = at // height, at % height
            take = min((block + 1) * D - at, height - row)
            pieces.append(flat[slot, row : row + take, :])
            at += take
        return pieces[0] if len(pieces) == 1 else jnp.concatenate(pieces, axis=0)

    def step(tag, names):
        numbers = [
            (number, group)
            for number, group in enumerate(groups.members)
            if group[0][0] in names
        ]
        start = groups.starts[numbers[0][0]]
        end = groups.starts[numbers[-1][0]] + groups.rows[numbers[-1][0]]
        directions, partway = {}, {}
        for name in names:
            height, width = HEIGHT[name], WIDTH[name]
            rows, padded = lay.rows[name], lay.padded[name]
            lhs = picks[name][...]
            if name in ("down", "pos"):
                both = None
                for block in range(height // LANES):
                    part = nt(
                        lhs[:, block * LANES : (block + 1) * LANES], flat_block(STARTS[name] + block)
                    )
                    both = part if both is None else both + part
            else:
                both = jnp.concatenate(
                    [nn(lhs, flat_block(STARTS[name] + i)) for i in range(width // LANES)], axis=1
                )
            keep(0, name, slice(0, width), both[padded : padded + rows])
            terms = split(both[:padded])
            for at in range(0, width, D):
                cols = slice(at, at + D)
                rotated = joined(nn(terms, rights[name][:, cols]))[:rows]
                first = DECAY * firsts[name][:, cols] + (1.0 - DECAY) * rotated
                second = DECAY * seconds[name][:, cols] + (1.0 - DECAY) * rotated * rotated
                keep(1, name, cols, first)
                keep(2, name, cols, second)
                direction = first / (jnp.sqrt(second) + ADAM_EPSILON)
                for i in range(D // LANES):
                    directions[name, at // LANES + i] = direction[:, i * LANES : (i + 1) * LANES]
        for number, group in numbers:
            piece = jnp.concatenate([directions[member] for member in group], axis=0)
            steps[me, groups.span(number), :] = pad_rows(piece, groups.rows[number]).astype(BF)
        yield from gather_all(grid, wire, steps, tag, (start, end - start))
        for number, group in numbers:
            rows = groups.rows[number]
            piece = steps[:, groups.span(number), :].reshape(lay.count * rows, LANES)
            whole = nn(thins[groups.kind_of[number]][...], piece)
            at = 0
            for name, block in group:
                padded = lay.padded[name]
                partway[name, block] = joined(whole[at : at + 2 * padded])
                at += 2 * padded
        for name in names:
            height, width = HEIGHT[name], WIDTH[name]
            terms = split(
                jnp.concatenate([partway[name, i] for i in range(width // LANES)], axis=1)
            )
            rate = height ** (-0.5)
            for at in range(0, width, D):
                cols = slice(at, at + D)
                update = joined(nt(terms, rights[name][cols, :]))[: lay.rows[name]]
                master = masters[name][:, cols] * (1.0 - rate * WEIGHT_DECAY) - rate * update
                keep(3, name, cols, master)

    together(step("down steps", ("down", "pos")), step("wide steps", ("qkv", "out", "up")))
    wire.finish()


def finish_step(roles, sizes, lay, full, small, bases, rights, lefts, masters, firsts, seconds):
    slots, rows, _ = full.shape
    nz, ny, nx, nc = (roles[role][2] for role in ("z", "y", "x", "c"))
    count = reduce_copies(roles) + small_copies(roles) + 3 * gather_copies(roles)
    extra = {}
    for role in ("c", "y", "x", "z"):
        for offset in range(1, roles[role][2]):
            extra[(role, offset)] = len(extra)
    groups = Groups(lay)
    chunks = sum(WIDTH[name] // RIGHT_CHUNK for name in NAMES)
    anywhere = pl.BlockSpec(memory_space=pl.ANY)
    return pl.pallas_call(
        functools.partial(tail_kernel, roles, sizes, lay, groups, extra),
        out_shape=(
            jax.ShapeDtypeStruct((40, LANES), F32),
            jax.ShapeDtypeStruct((4, lay.padded["qkv"], 5 * D + 3 * D), F32),
            jax.ShapeDtypeStruct((4, lay.padded["down"], D), F32),
            jax.ShapeDtypeStruct((4, lay.padded["pos"], D), F32),
        ),
        in_specs=[anywhere, vmem(), vmem()] + [anywhere] * 5 + [vmem()] * 20,
        out_specs=tuple([vmem()] * 4),
        scratch_shapes=[
            pltpu.VMEM((slots, rows, LANES), F32),
            pltpu.VMEM((rows, LANES), F32),
            pltpu.VMEM((nc - 1, nz, ny, nx, rows, LANES), BF),
            pltpu.VMEM((nc - 1, nz, ny, nx, rows, LANES), BF),
            pltpu.VMEM((nz, ny, nx, rows, LANES), BF),
            pltpu.VMEM((nz, ny, nx, rows, LANES), BF),
            pltpu.VMEM((nz - 1, rows, LANES), BF),
            pltpu.VMEM((nz - 1, rows, LANES), BF),
            pltpu.VMEM((4, SMALL_ROWS, LANES), F32),
            pltpu.VMEM((len(extra), SMALL_ROWS, LANES), F32),
            pltpu.VMEM((slots, rows, LANES), BF),
            pltpu.VMEM((slots, groups.total, LANES), BF),
            pltpu.VMEM((2, RIGHT_CHUNK, FF), F32),
        ]
        + [pltpu.VMEM((WIDTH[name], WIDTH[name]), BF) for name in NAMES]
        + [pltpu.VMEM((2 * lay.padded[name], HEIGHT[name]), BF) for name in NAMES]
        + [pltpu.VMEM(groups.thin(i), BF) for i in range(len(groups.kinds))]
        + [
            pltpu.SemaphoreType.DMA((count,)),
            pltpu.SemaphoreType.DMA((count,)),
            pltpu.SemaphoreType.DMA((nz,)),
            pltpu.SemaphoreType.DMA((chunks,)),
        ],
        compiler_params=pltpu.CompilerParams(
            collective_id=1, has_side_effects=True, vmem_limit_bytes=VMEM_LIMIT
        ),
        name="finish_step",
    )(full, small, bases, *rights, *lefts, *masters, *firsts, *seconds)


AXES = ("dp", "fsdp")


def on_device(roles, sizes, tokens, centres, lengths, cotangent, smalls, *matrices):
    masters, firsts, seconds, lefts, rights = (matrices[5 * i : 5 * i + 5] for i in range(5))
    count = sizes["dp"] * sizes["fsdp"]
    heads = Layout(count, True)
    lay = Layout(count, False)
    *weights, small_rows, bases = gather_weights(roles, sizes, heads, masters, smalls, lefts)
    w_qkv, w_out, w_up, w_down, w_pos = weights
    layer_out, grad_tokens, full, small_grads = layer_pass(
        tokens, centres, lengths, cotangent, small_rows, w_qkv, w_out, w_up, w_down, w_pos
    )
    small_total, *packed = finish_step(
        roles,
        sizes,
        lay,
        full.reshape(count, FLAT_ROWS // count, LANES),
        small_grads,
        bases,
        rights,
        lefts,
        masters,
        firsts,
        seconds,
    )
    me = lax.axis_index("dp") * sizes["fsdp"] + lax.axis_index("fsdp")
    grad_smalls, *finished = hand_out(heads, me.reshape(1), small_total, packed)
    return (layer_out, grad_tokens, grad_smalls.reshape(heads.small_len), *finished)


def solution(mesh):
    sizes = {axis: mesh.shape[axis] for axis in AXES}
    rows, flat = P(AXES, None), P(AXES)
    return jax.shard_map(
        functools.partial(on_device, mesh_roles(mesh), sizes),
        mesh=mesh,
        in_specs=(rows, P(None, AXES), flat, rows, flat) + (rows,) * 20 + (P(),) * 5,
        out_specs=(rows, rows, flat) + (rows,) * 25,
        check_vma=False,
    )
```
